32 devices in a mesh: rep: 8 (over z, core), fsdp: 4 (over y, x).
Axes of the slice: x: 2, y: 2, z: 4, core: 2. Of those that a mesh axis runs over, the one named last changes fastest.
Arguments:
- hidden_in: bfloat16 [10240, 1536], P(('rep', 'fsdp')), may hold values from -6 to 6
- out_grad: bfloat16 [10240, 1536], P(('rep', 'fsdp')), may hold values from -6 to 6
- doc_lengths: int32 [8, 8], P('rep'), may hold values from 1 to 1024, 1280 in all within a row
- piece_starts: int32 [8, 2], P('rep'), may hold values from 0 to 1024, as said below
- w_query: bfloat16 [1536, 1536], P('fsdp'), may hold values from -0.15625 to 0.15625
- b_query: bfloat16 [1536], P('fsdp'), may hold values from -3 to 3
- w_key: bfloat16 [1536, 256], P('fsdp'), may hold values from -0.15625 to 0.15625
- b_key: bfloat16 [256], P('fsdp'), may hold values from -3 to 3
- w_value: bfloat16 [1536, 256], P('fsdp'), may hold values from -0.15625 to 0.15625
- b_value: bfloat16 [256], P('fsdp'), may hold values from -3 to 3
- w_output: bfloat16 [1536, 1536], P('fsdp'), may hold values from -0.625 to 0.625
- gain_attn: bfloat16 [1536], P('fsdp'), may hold values from 0.5 to 1.5
- w_gate: bfloat16 [1536, 8960], P('fsdp'), may hold values from -0.15625 to 0.15625
- w_up: bfloat16 [1536, 8960], P('fsdp'), may hold values from -0.15625 to 0.15625
- w_down: bfloat16 [8960, 1536], P('fsdp'), may hold values from -0.0625 to 0.0625
- gain_mlp: bfloat16 [1536], P('fsdp'), may hold values from 0.5 to 1.5
Outputs:
- output: float32 [10240, 1536], P(('rep', 'fsdp'))
- grad_input: float32 [10240, 1536], P(('rep', 'fsdp'))
- grad_w_query: float32 [1536, 1536], P('fsdp')
- grad_b_query: float32 [1536], P('fsdp')
- grad_w_key: float32 [1536, 256], P('fsdp')
- grad_b_key: float32 [256], P('fsdp')
- grad_w_value: float32 [1536, 256], P('fsdp')
- grad_b_value: float32 [256], P('fsdp')
- grad_w_output: float32 [1536, 1536], P('fsdp')
- grad_gain_attn: float32 [1536], P('fsdp')
- grad_w_gate: float32 [1536, 8960], P('fsdp')
- grad_w_up: float32 [1536, 8960], P('fsdp')
- grad_w_down: float32 [8960, 1536], P('fsdp')
- grad_gain_mlp: float32 [1536], P('fsdp')
The draws below stay inside these ranges and needn't reach their ends.
Inputs may be any that keep to these rules, and one draw needn't show every extreme that they name: `doc_lengths`: each row's 8 lengths sum to 1280, and the longest is exactly 1024. `piece_starts`: in each row the starts rise by 256 or more from piece to piece, so pieces never intersect; a piece may run over a document's end.
All inputs are finite; a program needn't handle non-finite values.
Results may differ from the reference program's by a relative error of at most 0.028.
Values may be sent and summed in bfloat16 or wider, within the bound.
A program may use at most 576 MiB of HBM per device.

```python
import math
import jax
import jax.numpy as jnp
import numpy as np
from jax import lax

D = 1536
HEADS = 12
KVH = 2
HDIM = 128
FF = 8960
MAXDOC = 1024
PIECE = 256
ROW = 1280
GROUPS = 8
TOKENS = 10240
NDOC = 8
NPIC = 2
KVW = 256


def draw_piece_starts(key, part):
    stride = ROW // NPIC
    offsets = jax.random.randint(key, (GROUPS, NPIC), 0, stride - PIECE + 1)
    offsets = offsets.at[0, 0].set(0)
    offsets = offsets.at[0, NPIC - 1].set(stride - PIECE)
    base = jnp.arange(NPIC, dtype=jnp.int32) * stride
    return (base[None, :] + offsets).astype(jnp.int32)


def levels(own_key, shape, split, low, largest):
    factor_of = 1.0
    for position, blocks in split:
        steps = jax.random.uniform(jax.random.fold_in(jax.random.fold_in(own_key, 6), position), (blocks,), jnp.float32, low / len(split), largest / len(split))
        factor_of = factor_of * jnp.repeat(jnp.exp(steps), shape[position] // blocks).reshape((-1,) + (1,) * (len(shape) - 1 - position))
    return factor_of


def profile(number_of, total, bound, skew):
    weights = [(1 << 20) // math.isqrt(grade ** skew) + 1 for grade in range(2, number_of + 1)]
    surplus, given = total - bound - (number_of - 1), [1] * (number_of - 1)
    while surplus > 0:
        candidates = [i for i in range(number_of - 1) if given[i] < bound]
        whole, remaining = sum([weights[i] for i in candidates]), surplus
        for i in candidates:
            more = min(bound - given[i], max(1, remaining * weights[i] // whole), surplus)
            given[i] = given[i] + more
            surplus = surplus - more
    return np.array([bound] + given)


def ragged(key, count, total, reach, slope):
    if count == 2:
        one = jax.random.randint(key, (), max(1, total - reach), min(reach, total - 1) + 1)
        return jnp.stack([one, total - one])
    sizes = jnp.asarray(profile(count, total, reach, slope), jnp.int32)
    twos = (count - 1) // 2
    donor, receiver = sizes[1:1 + 2 * twos:2], sizes[2:2 + 2 * twos:2]
    slack = jnp.minimum(donor - 1, reach - receiver)
    shifted = jax.random.randint(jax.random.fold_in(key, 1), (twos,), 0, 1 << 20) % (slack + 1)
    sizes = sizes.at[1:1 + 2 * twos:2].set(donor - shifted).at[2:2 + 2 * twos:2].set(receiver + shifted)
    return sizes[jax.random.permutation(jax.random.fold_in(key, 2), count)]


def noise(stream_key, dims, scale, bound, pieces=(), held_as=jnp.bfloat16):
    array = scale * jax.random.normal(stream_key, dims, jnp.float32)
    if pieces:
        array = array * levels(stream_key, dims, pieces, -0.22, 0.18)
    return jnp.clip(array, -bound, bound).astype(held_as)


def setup_inputs(seed: int = 0) -> dict:
    arg_keys = jax.random.split(jax.random.key(seed), 17)
    hidden_in = noise(arg_keys[0], (TOKENS, D), 1.0, 6.0, ((0, 32),))
    out_grad = noise(arg_keys[1], (TOKENS, D), 1.0, 6.0, ((0, 32),))
    doc_lengths = jax.vmap(lambda own: ragged(own, NDOC, ROW, MAXDOC, 2))(jax.random.split(arg_keys[2], GROUPS)).reshape((GROUPS, NDOC)).astype(jnp.int32)
    piece_starts = draw_piece_starts(jax.random.fold_in(arg_keys[16], 71), 0)
    w_query = noise(arg_keys[4], (D, D), D ** -0.5, 0.15625, ((0, 4),))
    b_query = noise(arg_keys[5], (D,), 0.5, 3.0, ((0, 4),))
    w_key = noise(arg_keys[6], (D, KVW), D ** -0.5, 0.15625, ((0, 4),))
    b_key = noise(arg_keys[7], (KVW,), 0.5, 3.0, ((0, 4),))
    w_value = noise(arg_keys[8], (D, KVW), D ** -0.5, 0.15625, ((0, 4),))
    b_value = noise(arg_keys[9], (KVW,), 0.5, 3.0, ((0, 4),))
    w_output = noise(arg_keys[10], (D, D), (D // 16) ** -0.5, 0.625, ((0, 4),))
    gain_attn = jnp.clip(1.0 + 0.1 * jax.random.normal(arg_keys[11], (D,), jnp.float32), 0.5, 1.5).astype(jnp.bfloat16)
    w_gate = noise(arg_keys[12], (D, FF), D ** -0.5, 0.15625, ((0, 4),))
    w_up = noise(arg_keys[13], (D, FF), D ** -0.5, 0.15625, ((0, 4),))
    w_down = noise(arg_keys[14], (FF, D), FF ** -0.5, 0.0625, ((0, 4),))
    gain_mlp = jnp.clip(1.0 + 0.1 * jax.random.normal(arg_keys[15], (D,), jnp.float32), 0.5, 1.5).astype(jnp.bfloat16)
    return dict(hidden_in=hidden_in, out_grad=out_grad, doc_lengths=doc_lengths, piece_starts=piece_starts, w_query=w_query, b_query=b_query, w_key=w_key, b_key=b_key, w_value=w_value, b_value=b_value, w_output=w_output, gain_attn=gain_attn, w_gate=w_gate, w_up=w_up, w_down=w_down, gain_mlp=gain_mlp)


epsilon = 1e-06
rope_base = 1000000.0

@jax.custom_vjp
def low(v):
    return lax.optimization_barrier(v.astype(jnp.bfloat16)).astype(jnp.float32)

@jax.custom_vjp
def low_back(v):
    return v

def low_keep(v):
    return (low(v), None)

def low_pass(kept, grad):
    return (grad,)

def back_keep(v):
    return (v, None)

def back_low(kept, grad):
    return (low(grad),)
low.defvjp(low_keep, low_pass)
low_back.defvjp(back_keep, back_low)

def row_layout(positions, lengths, starts, piece_len):
    doc_ends = jnp.cumsum(lengths).astype(jnp.int32)
    passed = positions[:, None] >= doc_ends[None, :]
    doc_ids = lax.optimization_barrier(jnp.sum(passed.astype(jnp.int32), axis=1, dtype=jnp.int32))
    offsets = lax.optimization_barrier(jnp.sum(jnp.where(passed, lengths[None, :], 0), axis=1, dtype=jnp.int32))
    inside = (positions[:, None] >= starts[None, :]) & (positions[:, None] < starts[None, :] + piece_len)
    labels = jnp.arange(1, starts.shape[0] + 1, dtype=jnp.int32)
    piece_ids = lax.optimization_barrier(jnp.sum(jnp.where(inside, labels[None, :], 0), axis=1, dtype=jnp.int32))
    return (doc_ids, (positions - offsets).astype(jnp.int32), piece_ids)

def visible_pairs(query_doc, query_pos, query_piece, key_doc, key_pos, key_piece):
    same_doc = query_doc[:, None] == key_doc[None, :]
    causal = key_pos[None, :] <= query_pos[:, None]
    same_piece = (query_piece[:, None] == key_piece[None, :]) & (query_piece[:, None] > 0)
    return same_doc & (causal | same_piece)

def rope_tables(relative, head_dim):
    halves = jnp.arange(0, head_dim, 2).astype(jnp.float32) / head_dim
    inverse = rope_base ** (-halves)
    angles = relative.astype(jnp.float32)[:, None] * inverse[None, :]
    angles = jnp.concatenate([angles, angles], axis=1)
    return (jnp.cos(angles), jnp.sin(angles))

def rotate(values, cosine, sine):
    half_dim = values.shape[-1] // 2
    turned = jnp.concatenate([-values[..., half_dim:], values[..., :half_dim]], axis=-1)
    return values * cosine[:, None, :] + turned * sine[:, None, :]

def mat_high(left, right):
    return jnp.dot(left, right, precision=lax.Precision.HIGHEST, preferred_element_type=jnp.float32)

def rms_unit(values):
    return values * lax.rsqrt(lax.optimization_barrier(jnp.mean(values * values, axis=1, keepdims=True)) + epsilon)

def reference(hidden_in, out_grad, doc_lengths, piece_starts, w_query, b_query, w_key, b_key, w_value, b_value, w_output, gain_attn, w_gate, w_up, w_down, gain_mlp):
    group_size = HEADS // KVH
    score_scale = 1.0 / HDIM ** 0.5
    row_pos = jnp.arange(ROW, dtype=jnp.int32)

    def row_of(lengths, starts):
        return row_layout(row_pos, lengths, starts, PIECE)
    doc_ids, relative, piece_ids = jax.vmap(row_of)(doc_lengths, piece_starts)
    cosine, sine = rope_tables(relative.reshape(TOKENS), HDIM)

    def row_attention(inputs):
        query_row, key_row, value_row, doc_row, piece_row = inputs
        allowed = visible_pairs(doc_row, row_pos, piece_row, doc_row, row_pos, piece_row)
        raw_scores = jnp.einsum('tgjd,rgd->gjtr', query_row.reshape(ROW, KVH, group_size, HDIM), key_row, precision=lax.Precision.HIGHEST)
        scores = jnp.where(allowed[None, None], low_back(raw_scores * score_scale), -1e+30)
        row_peak = lax.optimization_barrier(jnp.max(scores, axis=3, keepdims=True))
        expo_vals = jnp.exp(scores - row_peak)
        soft_probs = low(expo_vals / lax.optimization_barrier(jnp.sum(expo_vals, axis=3, keepdims=True)))
        mixed = jnp.einsum('gjtr,rgd->tgjd', soft_probs, value_row, precision=lax.Precision.HIGHEST)
        return mixed.reshape(ROW, D)

    def forward(x_float, query_w, query_b, key_w, key_b, value_w, value_b, output_w, first_gain, gate_w, up_w, down_w, second_gain):
        normed_first = low(rms_unit(x_float) * first_gain)
        query_pre = low_back(mat_high(normed_first, query_w) + query_b)
        key_pre = low_back(mat_high(normed_first, key_w) + key_b)
        value_low = low(low_back(mat_high(normed_first, value_w) + value_b))
        query_rot = low(rotate(query_pre.reshape(TOKENS, HEADS, HDIM), cosine, sine))
        key_rot = low(rotate(key_pre.reshape(TOKENS, KVH, HDIM), cosine, sine))
        mixed = lax.map(jax.checkpoint(row_attention), (query_rot.reshape(GROUPS, ROW, HEADS, HDIM), key_rot.reshape(GROUPS, ROW, KVH, HDIM), value_low.reshape(GROUPS, ROW, KVH, HDIM), doc_ids, piece_ids))
        attn_low = low(low_back(mixed.reshape(TOKENS, D)))
        mid_state = x_float + low_back(mat_high(attn_low, output_w))
        normed_second = low(rms_unit(mid_state) * second_gain)
        gate_val = low_back(mat_high(normed_second, gate_w))
        up_val = low_back(mat_high(normed_second, up_w))
        act_low = low(jax.nn.silu(gate_val) * up_val)
        return mid_state + mat_high(act_low, down_w)
    result, pull_back = jax.vjp(forward, hidden_in.astype(jnp.float32), w_query.astype(jnp.float32), b_query.astype(jnp.float32), w_key.astype(jnp.float32), b_key.astype(jnp.float32), w_value.astype(jnp.float32), b_value.astype(jnp.float32), w_output.astype(jnp.float32), gain_attn.astype(jnp.float32), w_gate.astype(jnp.float32), w_up.astype(jnp.float32), w_down.astype(jnp.float32), gain_mlp.astype(jnp.float32))
    grads = pull_back(out_grad.astype(jnp.float32))
    return (result, grads[0], grads[1], grads[2], grads[3], grads[4], grads[5], grads[6], grads[7], grads[8], grads[9], grads[10], grads[11], grads[12])
```

```python
import jax
import jax.numpy as jnp
from jax import lax
from jax.sharding import PartitionSpec as P

HEADS = 12
KVH = 2
HDIM = 128
PIECE = 256


epsilon = 1e-06
rope_base = 1000000.0


def row_layout(positions, lengths, starts, piece_len):
    doc_ends = jnp.cumsum(lengths)
    passed = positions[:, None] >= doc_ends[None, :]
    doc_ids = jnp.sum(passed.astype(jnp.int32), axis=1, dtype=jnp.int32)
    offsets = jnp.sum(jnp.where(passed, lengths[None, :], 0), axis=1, dtype=jnp.int32)
    inside = (positions[:, None] >= starts[None, :]) & (
        positions[:, None] < starts[None, :] + piece_len
    )
    labels = jnp.arange(1, starts.shape[0] + 1, dtype=jnp.int32)
    piece_ids = jnp.sum(jnp.where(inside, labels[None, :], 0), axis=1, dtype=jnp.int32)
    return (doc_ids, positions - offsets, piece_ids)


def visible_pairs(query_doc, query_pos, query_piece, key_doc, key_pos, key_piece):
    same_doc = query_doc[:, None] == key_doc[None, :]
    causal = key_pos[None, :] <= query_pos[:, None]
    same_piece = (query_piece[:, None] == key_piece[None, :]) & (query_piece[:, None] > 0)
    return same_doc & (causal | same_piece)


def rope_tables(relative, head_dim):
    halves = jnp.arange(0, head_dim, 2).astype(jnp.float32) / head_dim
    inverse = rope_base ** (-halves)
    angles = relative.astype(jnp.float32)[:, None] * inverse[None, :]
    angles = jnp.concatenate([angles, angles], axis=1)
    return (jnp.cos(angles), jnp.sin(angles))


def rotate(values, cosine, sine):
    half_dim = values.shape[-1] // 2
    turned = jnp.concatenate([-values[..., half_dim:], values[..., :half_dim]], axis=-1)
    return values * cosine[:, None, :] + turned * sine[:, None, :]


def unrotate(grads, cosine, sine):
    half_dim = grads.shape[-1] // 2
    spun = grads * sine[:, None, :]
    turned_back = jnp.concatenate([spun[..., half_dim:], -spun[..., :half_dim]], axis=-1)
    return grads * cosine[:, None, :] + turned_back


def mat_dot(left, right):
    return jnp.dot(left, right, preferred_element_type=jnp.float32)


def dot_right_t(left, right):
    return lax.dot_general(
        left, right, (((1,), (1,)), ((), ())), preferred_element_type=jnp.float32
    )


def dot_left_t(left, right):
    return lax.dot_general(
        left, right, (((0,), (0,)), ((), ())), preferred_element_type=jnp.float32
    )


def xor_pairs(count, bit):
    return [(i, i ^ bit) for i in range(count)]


def bits_of(count):
    return [1 << k for k in range(count.bit_length() - 1)]


def gather_relative(block, axis):
    count = lax.axis_size(axis)
    bits = bits_of(count)
    half = block.shape[0] // 2
    halves = []
    for part, order in ((block[:half], bits), (block[half:], bits[::-1])):
        have = {0: part}
        for bit in order:
            fresh = {
                d ^ bit: lax.ppermute(piece, axis, xor_pairs(count, bit))
                for d, piece in have.items()
            }
            have.update(fresh)
        halves.append(have)
    return [(halves[0][d], halves[1][d]) for d in range(count)]


def scatter_relative(pieces, axis):
    count = lax.axis_size(axis)
    bits = bits_of(count)
    half = pieces[0].shape[0] // 2
    sums = []
    for lo, hi, order in ((0, half, bits[::-1]), (half, 2 * half, bits)):
        have = {d: pieces[d][lo:hi] for d in range(count)}
        for bit in order:
            come = {
                d ^ bit: lax.ppermute(have[d].astype(jnp.bfloat16), axis, xor_pairs(count, bit))
                for d in have
                if d & bit
            }
            have = {d: have[d].astype(jnp.float32) + come[d].astype(jnp.float32) for d in come}
        sums.append(have[0])
    return jnp.concatenate(sums, axis=0)


def core_swap(block):
    return lax.ppermute(block, "rep", xor_pairs(lax.axis_size("rep"), 1))


def line_pairs(lows, way):
    return [(2 * i + c, 2 * (i + way) + c) for i in lows for c in range(2)]


def pick(array, index):
    return lax.dynamic_index_in_dim(array, index, 0, keepdims=False)


def line_scatter(parts):
    count = lax.axis_size("rep") // 2
    here = lax.axis_index("rep") // 2
    arrived = [None, None]
    for step in range(1, count):
        sends = [
            pick(parts, jnp.clip(count - step + here, 0, count - 1)),
            pick(parts, jnp.clip(here - count + step, 0, count - 1)),
        ]
        for way in range(2):
            if arrived[way] is not None:
                sends[way] = (
                    sends[way].astype(jnp.float32) + arrived[way].astype(jnp.float32)
                ).astype(jnp.bfloat16)
        arrived = [
            lax.ppermute(sends[0], "rep", line_pairs(range(step), 1)),
            lax.ppermute(sends[1], "rep", line_pairs(range(count - step, count), -1)),
        ]
    own = pick(parts, here).astype(jnp.float32)
    return own + arrived[0].astype(jnp.float32) + arrived[1].astype(jnp.float32)


def line_gather(block):
    count = lax.axis_size("rep") // 2
    here = lax.axis_index("rep") // 2
    below, above = [block], [block]
    for step in range(1, count):
        below.append(lax.ppermute(below[-1], "rep", line_pairs(range(step - 1, count - 1), 1)))
        above.append(lax.ppermute(above[-1], "rep", line_pairs(range(1, count - step + 1), -1)))
    stacked = jnp.stack(below[:0:-1] + above)
    return lax.dynamic_slice_in_dim(stacked, count - 1 - here, count, 0)


def core_halves(mine, other, core):
    return jnp.where(core == 0, jnp.stack([mine, other]), jnp.stack([other, mine]))


def place(pieces, here):
    count = len(pieces)
    stacked = jnp.stack(pieces)
    return jnp.stack([pick(stacked, here ^ j) for j in range(count)])


def local(
    hidden_in,
    out_grad,
    doc_lengths,
    piece_starts,
    w_query,
    b_query,
    w_key,
    b_key,
    w_value,
    b_value,
    w_output,
    gain_attn,
    w_gate,
    w_up,
    w_down,
    gain_mlp,
):
    tok_rows = hidden_in.shape[0]
    model_width = hidden_in.shape[1]
    shard_count = lax.axis_size("fsdp")
    row_len = tok_rows * shard_count
    group_size = HEADS // KVH
    kv_width = KVH * HDIM
    ff_width = w_gate.shape[1]
    score_scale = 1.0 / HDIM**0.5
    local_pos = lax.axis_index("fsdp") * tok_rows + jnp.arange(tok_rows, dtype=jnp.int32)
    row_pos = jnp.arange(row_len, dtype=jnp.int32)
    lengths = doc_lengths[0]
    starts = piece_starts[0]
    query_doc, query_rel, query_piece = row_layout(local_pos, lengths, starts, PIECE)
    key_doc, unused_rel, key_piece = row_layout(row_pos, lengths, starts, PIECE)
    allowed = visible_pairs(query_doc, local_pos, query_piece, key_doc, row_pos, key_piece)
    cosine, sine = rope_tables(query_rel, HDIM)
    here = lax.axis_index("fsdp")
    core = lax.axis_index("rep") % 2
    line = lax.axis_size("rep") // 2
    low = jnp.bfloat16

    def gather_rows(weight):
        half = weight.shape[0] // 2
        mine = lax.dynamic_slice_in_dim(weight, core * half, half, 0)
        mine = jnp.stack([jnp.concatenate(p, axis=0) for p in gather_relative(mine, "fsdp")])
        both = core_halves(mine, core_swap(mine), core)
        rows = place([both[:, d] for d in range(shard_count)], here)
        return rows.reshape(2 * half * shard_count, weight.shape[1])

    qkv_full = gather_rows(jnp.concatenate([w_query, w_key, w_value], axis=1))
    query_full = qkv_full[:, :model_width]
    key_full = qkv_full[:, model_width : model_width + kv_width]
    value_full = qkv_full[:, model_width + kv_width :]
    output_full = gather_rows(w_output)
    vectors = lax.all_gather(
        jnp.concatenate([b_query, b_key, b_value, gain_attn, gain_mlp]), "fsdp", axis=0
    )
    cuts = [0]
    for vector in (b_query, b_key, b_value, gain_attn, gain_mlp):
        cuts.append(cuts[-1] + vector.shape[0])
    query_bias, key_bias, value_bias, attn_gain, mlp_gain = (
        vectors[:, cuts[i] : cuts[i + 1]].reshape(-1) for i in range(5)
    )

    part = ff_width // shard_count

    def exchange_columns(weight):
        half = weight.shape[0] // 2
        mine = lax.dynamic_slice_in_dim(weight, core * half, half, 0)
        got = []
        for d in range(shard_count):
            piece = lax.dynamic_slice_in_dim(mine, (here ^ d) * part, part, 1)
            got.append(piece if d == 0 else lax.ppermute(piece, "fsdp", xor_pairs(shard_count, d)))
        got = jnp.stack(got)
        both = core_halves(got, core_swap(got), core)
        rows = place([both[:, d] for d in range(shard_count)], here)
        return rows.reshape(2 * half * shard_count, part)

    gate_part = exchange_columns(w_gate)
    up_part = exchange_columns(w_up)
    cot_all = jnp.concatenate([h for p in gather_relative(out_grad, "fsdp") for h in p], axis=0)
    x_float = hidden_in.astype(jnp.float32)
    inv_first = lax.rsqrt(jnp.mean(x_float * x_float, axis=1, keepdims=True) + epsilon)
    unit_first = x_float * inv_first
    gain_first = attn_gain.astype(jnp.float32)
    normed_first = (unit_first * gain_first).astype(jnp.bfloat16)
    query_pre = mat_dot(normed_first, query_full) + query_bias.astype(jnp.float32)
    key_pre = mat_dot(normed_first, key_full) + key_bias.astype(jnp.float32)
    value_pre = mat_dot(normed_first, value_full) + value_bias.astype(jnp.float32)
    query_rot = rotate(query_pre.reshape(tok_rows, HEADS, HDIM), cosine, sine).astype(jnp.bfloat16)
    key_rot = (
        rotate(key_pre.reshape(tok_rows, KVH, HDIM), cosine, sine)
        .astype(jnp.bfloat16)
        .reshape(tok_rows, kv_width)
    )
    value_low = value_pre.astype(jnp.bfloat16)
    keys_row, values_row = (
        lax.all_gather(key_rot, "fsdp", axis=0, tiled=True),
        lax.all_gather(value_low, "fsdp", axis=0, tiled=True),
    )
    query_grouped = query_rot.reshape(tok_rows, KVH, group_size, HDIM)
    keys_grouped = keys_row.reshape(row_len, KVH, HDIM)
    values_grouped = values_row.reshape(row_len, KVH, HDIM)

    def masked_scores():
        raw_scores = (
            jnp.einsum(
                "tgjd,rgd->gjtr", query_grouped, keys_grouped, preferred_element_type=jnp.float32
            )
            * score_scale
        )
        return jnp.where(allowed[None, None], raw_scores, -1e30)

    scores = masked_scores()
    row_peak = jnp.max(scores, axis=3, keepdims=True)
    expo_vals = jnp.exp(scores - row_peak)
    row_total = jnp.sum(expo_vals, axis=3, keepdims=True)
    soft_probs = expo_vals / row_total
    log_total = row_peak + jnp.log(row_total)
    attn_heads = jnp.einsum(
        "gjtr,rgd->tgjd",
        soft_probs.astype(jnp.bfloat16),
        values_grouped,
        preferred_element_type=jnp.float32,
    )
    attn_low = attn_heads.reshape(tok_rows, model_width).astype(jnp.bfloat16)
    mid_state = x_float + mat_dot(attn_low, output_full)
    inv_second = lax.rsqrt(jnp.mean(mid_state * mid_state, axis=1, keepdims=True) + epsilon)
    unit_second = mid_state * inv_second
    gain_second = mlp_gain.astype(jnp.float32)
    normed_second = (unit_second * gain_second).astype(jnp.bfloat16)
    cot_float = out_grad.astype(jnp.float32)
    normed_all = jnp.concatenate([h for p in gather_relative(normed_second, "fsdp") for h in p], axis=0)
    gate_val = mat_dot(normed_all, gate_part)
    up_val = mat_dot(normed_all, up_part)
    sig_gate = jax.nn.sigmoid(gate_val)
    silu_gate = gate_val * sig_gate
    act_low = (silu_gate * up_val).astype(low)
    d_act = dot_right_t(cot_all, w_down)
    d_gate = (d_act * up_val * sig_gate * (1.0 + gate_val * (1.0 - sig_gate))).astype(low)
    d_up = (d_act * silu_gate).astype(low)
    mlp_part = mat_dot(act_low, w_down).reshape(shard_count, tok_rows, model_width)
    mlp_out = scatter_relative([mlp_part[d] for d in range(shard_count)], "fsdp")
    norm_part = (dot_right_t(d_gate, gate_part) + dot_right_t(d_up, up_part)).reshape(
        shard_count, tok_rows, model_width
    )
    partial_value = scatter_relative([norm_part[d] for d in range(shard_count)], "fsdp")

    def keep_half(grad):
        mine = lax.dynamic_index_in_dim(grad, core, 1, keepdims=False)
        other = lax.dynamic_index_in_dim(grad, 1 - core, 1, keepdims=False)
        return (mine.astype(jnp.float32) + core_swap(other).astype(jnp.float32)).astype(low)

    def both_cores(half):
        return core_halves(half, core_swap(half), core)

    down_grad = dot_left_t(act_low, cot_all).astype(low)
    half = part // 2
    down_half = keep_half(down_grad.reshape(1, 2, half, model_width))[0]
    wide = model_width // line
    down_parts = jnp.stack([down_half[:, q * wide : (q + 1) * wide] for q in range(line)])
    down_own = line_scatter(down_parts).astype(low)
    down_rows = line_gather(down_own)
    down_rows = jnp.concatenate([down_rows[q] for q in range(line)], axis=1)
    down_sums = both_cores(down_rows).reshape(part, model_width).astype(jnp.float32)

    rows = model_width // shard_count
    thin = rows // 2 // line

    def column_grad(d_value):
        grad = dot_left_t(normed_all, d_value).astype(low)
        kept = keep_half(grad.reshape(shard_count, 2, rows // 2, part))
        kept = kept.reshape(shard_count, line, thin, part).transpose(1, 0, 2, 3)
        own = line_scatter(kept).astype(low)
        got = []
        for d in range(shard_count):
            piece = pick(own, here ^ d)
            got.append(piece if d == 0 else lax.ppermute(piece, "fsdp", xor_pairs(shard_count, d)))
        got = place(got, here).transpose(1, 0, 2).reshape(thin, ff_width)
        full = line_gather(got).reshape(rows // 2, ff_width)
        return both_cores(full).reshape(rows, ff_width).astype(jnp.float32)

    grad_gate = column_grad(d_gate)
    grad_up = column_grad(d_up)
    output = mid_state + mlp_out
    d_gain_second = jnp.sum(partial_value * unit_second, axis=0)
    scaled_second = partial_value * gain_second
    d_mid = cot_float + inv_second * (
        scaled_second - unit_second * jnp.mean(scaled_second * unit_second, axis=1, keepdims=True)
    )
    d_branch_low = d_mid.astype(jnp.bfloat16)
    d_attn_low = dot_right_t(d_branch_low, output_full).astype(jnp.bfloat16)
    d_attn_grouped = d_attn_low.reshape(tok_rows, KVH, group_size, HDIM)
    scores = masked_scores()
    soft_back = jnp.exp(scores - log_total)
    probs_low = soft_back.astype(jnp.bfloat16)
    prob_grad = jnp.einsum(
        "tgjd,rgd->gjtr", d_attn_grouped, values_grouped, preferred_element_type=jnp.float32
    )
    row_delta = jnp.sum(soft_back * prob_grad, axis=3, keepdims=True)
    score_grad = (soft_back * (prob_grad - row_delta)).astype(jnp.bfloat16)
    dquery_rot = (
        jnp.einsum("gjtr,rgd->tgjd", score_grad, keys_grouped, preferred_element_type=jnp.float32)
        * score_scale
    )
    dquery_low = (
        unrotate(dquery_rot.reshape(tok_rows, HEADS, HDIM), cosine, sine)
        .reshape(tok_rows, model_width)
        .astype(jnp.bfloat16)
    )
    key_grad = (
        jnp.einsum("gjtr,tgjd->rgd", score_grad, query_grouped, preferred_element_type=jnp.float32)
        * score_scale
    )
    value_grad = jnp.einsum(
        "gjtr,tgjd->rgd", probs_low, d_attn_grouped, preferred_element_type=jnp.float32
    )
    kv_sums = lax.psum_scatter(
        jnp.concatenate(
            [
                key_grad.reshape(lax.axis_size("fsdp") * tok_rows, kv_width),
                value_grad.reshape(lax.axis_size("fsdp") * tok_rows, kv_width),
            ],
            axis=1,
        ).astype(jnp.bfloat16),
        "fsdp",
        scatter_dimension=0,
        tiled=True,
    ).astype(jnp.float32)
    dkey_low = (
        unrotate(kv_sums[:, :kv_width].reshape(tok_rows, KVH, HDIM), cosine, sine)
        .reshape(tok_rows, kv_width)
        .astype(jnp.bfloat16)
    )
    dvalue_low = kv_sums[:, kv_width:].astype(jnp.bfloat16)
    d_norm_first = (
        dot_right_t(dquery_low, query_full)
        + dot_right_t(dkey_low, key_full)
        + dot_right_t(dvalue_low, value_full)
    )
    attn_grads = jnp.concatenate(
        [
            dot_left_t(normed_first, dquery_low).astype(low),
            dot_left_t(normed_first, dkey_low).astype(low),
            dot_left_t(normed_first, dvalue_low).astype(low),
            dot_left_t(attn_low, d_branch_low).astype(low),
        ],
        axis=1,
    )
    attn_wide = attn_grads.shape[1]
    attn_kept = keep_half(attn_grads.reshape(shard_count, 2, rows // 2, attn_wide))
    attn_own = scatter_relative([pick(attn_kept, here ^ d) for d in range(shard_count)], "fsdp").astype(low)
    attn_own = line_scatter(attn_own.reshape(line, thin, attn_wide)).astype(low)
    attn_rows = line_gather(attn_own).reshape(rows // 2, attn_wide)
    attn_sums = both_cores(attn_rows).reshape(rows, attn_wide).astype(jnp.float32)
    d_gain_first = jnp.sum(d_norm_first * unit_first, axis=0)
    scaled_first = d_norm_first * gain_first
    grad_input = d_mid + inv_first * (
        scaled_first - unit_first * jnp.mean(scaled_first * unit_first, axis=1, keepdims=True)
    )
    bias_query = jnp.sum(dquery_low.astype(jnp.float32), axis=0)
    bias_key = jnp.sum(dkey_low.astype(jnp.float32), axis=0)
    bias_value = jnp.sum(dvalue_low.astype(jnp.float32), axis=0)
    small = (bias_query, bias_key, bias_value, d_gain_first, d_gain_second)
    summed = lax.psum(jnp.concatenate(small), ("rep", "fsdp"))
    outs = []
    at = 0
    for vector in small:
        size = vector.shape[0] // shard_count
        outs.append(lax.dynamic_slice_in_dim(summed, at + here * size, size, 0))
        at += vector.shape[0]
    bias_query, bias_key, bias_value, gain_first_sum, gain_second_sum = outs
    grad_query = attn_sums[:, :model_width]
    grad_key = attn_sums[:, model_width : model_width + kv_width]
    grad_value = attn_sums[:, model_width + kv_width : model_width + 2 * kv_width]
    grad_output = attn_sums[:, model_width + 2 * kv_width :]
    return (
        output,
        grad_input,
        grad_query,
        bias_query,
        grad_key,
        bias_key,
        grad_value,
        bias_value,
        grad_output,
        gain_first_sum,
        grad_gate,
        grad_up,
        down_sums,
        gain_second_sum,
    )


def solution(mesh):
    placed = (
        P(("rep", "fsdp"), None),
        P(("rep", "fsdp"), None),
        P("rep", None),
        P("rep", None),
        P("fsdp", None),
        P("fsdp"),
        P("fsdp", None),
        P("fsdp"),
        P("fsdp", None),
        P("fsdp"),
        P("fsdp", None),
        P("fsdp"),
        P("fsdp", None),
        P("fsdp", None),
        P("fsdp", None),
        P("fsdp"),
    )
    return jax.shard_map(
        local,
        mesh=mesh,
        in_specs=placed,
        out_specs=(
            P(("rep", "fsdp"), None),
            P(("rep", "fsdp"), None),
            P("fsdp", None),
            P("fsdp"),
            P("fsdp", None),
            P("fsdp"),
            P("fsdp", None),
            P("fsdp"),
            P("fsdp", None),
            P("fsdp"),
            P("fsdp", None),
            P("fsdp", None),
            P("fsdp", None),
            P("fsdp"),
        ),
        check_vma=False,
    )
```

```python
import jax
import jax.numpy as jnp
from jax import lax
from jax.experimental import pallas as pl
from jax.experimental.pallas import tpu as pltpu
from jax.sharding import PartitionSpec as P

HEADS = 12
KVH = 2
HDIM = 128
PIECE = 256


epsilon = 1e-06
rope_base = 1000000.0


def row_layout(positions, lengths, starts, piece_len):
    doc_ends = jnp.cumsum(lengths)
    passed = positions[:, None] >= doc_ends[None, :]
    doc_ids = jnp.sum(passed.astype(jnp.int32), axis=1, dtype=jnp.int32)
    offsets = jnp.sum(jnp.where(passed, lengths[None, :], 0), axis=1, dtype=jnp.int32)
    inside = (positions[:, None] >= starts[None, :]) & (
        positions[:, None] < starts[None, :] + piece_len
    )
    labels = jnp.arange(1, starts.shape[0] + 1, dtype=jnp.int32)
    piece_ids = jnp.sum(jnp.where(inside, labels[None, :], 0), axis=1, dtype=jnp.int32)
    return (doc_ids, positions - offsets, piece_ids)


def visible_pairs(query_doc, query_pos, query_piece, key_doc, key_pos, key_piece):
    same_doc = query_doc[:, None] == key_doc[None, :]
    causal = key_pos[None, :] <= query_pos[:, None]
    same_piece = (query_piece[:, None] == key_piece[None, :]) & (query_piece[:, None] > 0)
    return same_doc & (causal | same_piece)


def rope_tables(relative, head_dim):
    halves = jnp.arange(0, head_dim, 2).astype(jnp.float32) / head_dim
    inverse = rope_base ** (-halves)
    angles = relative.astype(jnp.float32)[:, None] * inverse[None, :]
    angles = jnp.concatenate([angles, angles], axis=1)
    return (jnp.cos(angles), jnp.sin(angles))


def rotate(values, cosine, sine):
    half_dim = values.shape[-1] // 2
    turned = jnp.concatenate([-values[..., half_dim:], values[..., :half_dim]], axis=-1)
    return values * cosine[:, None, :] + turned * sine[:, None, :]


def unrotate(grads, cosine, sine):
    half_dim = grads.shape[-1] // 2
    spun = grads * sine[:, None, :]
    turned_back = jnp.concatenate([spun[..., half_dim:], -spun[..., :half_dim]], axis=-1)
    return grads * cosine[:, None, :] + turned_back


def mat_dot(left, right):
    return jnp.dot(left, right, preferred_element_type=jnp.float32)


def dot_right_t(left, right):
    return lax.dot_general(
        left, right, (((1,), (1,)), ((), ())), preferred_element_type=jnp.float32
    )


def dot_left_t(left, right):
    return lax.dot_general(
        left, right, (((0,), (0,)), ((), ())), preferred_element_type=jnp.float32
    )


def xor_pairs(count, bit):
    return [(i, i ^ bit) for i in range(count)]


def bits_of(count):
    return [1 << k for k in range(count.bit_length() - 1)]


def gather_relative(block, axis):
    count = lax.axis_size(axis)
    bits = bits_of(count)
    half = block.shape[0] // 2
    halves = []
    for part, order in ((block[:half], bits), (block[half:], bits[::-1])):
        have = {0: part}
        for bit in order:
            fresh = {
                d ^ bit: lax.ppermute(piece, axis, xor_pairs(count, bit))
                for d, piece in have.items()
            }
            have.update(fresh)
        halves.append(have)
    return [(halves[0][d], halves[1][d]) for d in range(count)]


def scatter_relative(pieces, axis):
    count = lax.axis_size(axis)
    bits = bits_of(count)
    half = pieces[0].shape[0] // 2
    sums = []
    for lo, hi, order in ((0, half, bits[::-1]), (half, 2 * half, bits)):
        have = {d: pieces[d][lo:hi] for d in range(count)}
        for bit in order:
            come = {
                d ^ bit: lax.ppermute(have[d].astype(jnp.bfloat16), axis, xor_pairs(count, bit))
                for d in have
                if d & bit
            }
            have = {d: have[d].astype(jnp.float32) + come[d].astype(jnp.float32) for d in come}
        sums.append(have[0])
    return jnp.concatenate(sums, axis=0)


def core_swap(block):
    return lax.ppermute(block, "rep", xor_pairs(lax.axis_size("rep"), 1))


def line_pairs(lows, way):
    return [(2 * i + c, 2 * (i + way) + c) for i in lows for c in range(2)]


def pick(array, index):
    return lax.dynamic_index_in_dim(array, index, 0, keepdims=False)


def line_scatter(parts):
    count = lax.axis_size("rep") // 2
    here = lax.axis_index("rep") // 2
    arrived = [None, None]
    for step in range(1, count):
        sends = [
            pick(parts, jnp.clip(count - step + here, 0, count - 1)),
            pick(parts, jnp.clip(here - count + step, 0, count - 1)),
        ]
        for way in range(2):
            if arrived[way] is not None:
                sends[way] = (
                    sends[way].astype(jnp.float32) + arrived[way].astype(jnp.float32)
                ).astype(jnp.bfloat16)
        arrived = [
            lax.ppermute(sends[0], "rep", line_pairs(range(step), 1)),
            lax.ppermute(sends[1], "rep", line_pairs(range(count - step, count), -1)),
        ]
    own = pick(parts, here).astype(jnp.float32)
    return own + arrived[0].astype(jnp.float32) + arrived[1].astype(jnp.float32)


def line_gather(block):
    count = lax.axis_size("rep") // 2
    here = lax.axis_index("rep") // 2
    below, above = [block], [block]
    for step in range(1, count):
        below.append(lax.ppermute(below[-1], "rep", line_pairs(range(step - 1, count - 1), 1)))
        above.append(lax.ppermute(above[-1], "rep", line_pairs(range(1, count - step + 1), -1)))
    stacked = jnp.stack(below[:0:-1] + above)
    return lax.dynamic_slice_in_dim(stacked, count - 1 - here, count, 0)


def core_halves(mine, other, core):
    return jnp.where(core == 0, jnp.stack([mine, other]), jnp.stack([other, mine]))


def place(pieces, here):
    count = len(pieces)
    stacked = jnp.stack(pieces)
    return jnp.stack([pick(stacked, here ^ j) for j in range(count)])


MESH = pl.DeviceIdType.MESH
MASKED = -1e30


def dot_f32(left, right, dims=((1,), (0,))):
    return lax.dot_general(left, right, (dims, ((), ())), preferred_element_type=jnp.float32)


def layout_of(positions, lengths_ref, starts_ref):
    end = jnp.int32(0)
    doc = jnp.zeros_like(positions)
    before = jnp.zeros_like(positions)
    piece = jnp.zeros_like(positions)
    for i in range(lengths_ref.shape[1]):
        end = end + lengths_ref[0, i]
        passed = positions >= end
        doc = doc + jnp.where(passed, 1, 0)
        before = before + jnp.where(passed, lengths_ref[0, i], 0)
    for i in range(starts_ref.shape[1]):
        first = starts_ref[0, i]
        inside = (positions >= first) & (positions < first + PIECE)
        piece = piece + jnp.where(inside, i + 1, 0)
    return doc, positions - before, piece


def mask_bias(here, rows, row_len, lengths_ref, starts_ref):
    query_pos = here * rows + lax.broadcasted_iota(jnp.int32, (rows, 1), 0)
    key_pos = lax.broadcasted_iota(jnp.int32, (1, row_len), 1)
    query_doc, query_rel, query_piece = layout_of(query_pos, lengths_ref, starts_ref)
    key_doc, unused, key_piece = layout_of(key_pos, lengths_ref, starts_ref)
    allowed = (query_doc == key_doc) & (
        (key_pos <= query_pos) | ((query_piece == key_piece) & (query_piece > 0))
    )
    return jnp.where(allowed, 0.0, MASKED), query_rel


class Links:
    def __init__(self):
        self.here = lax.axis_index("fsdp")
        self.rep = lax.axis_index("rep")
        self.core = lax.rem(self.rep, 2)
        self.line = self.rep // 2
        reps = lax.axis_size("rep")
        here = self.here
        self.near = [here, here + 1 - 2 * lax.rem(here, 2), lax.rem(here + 2, 4), 3 - here]
        self.plane = [{"fsdp": index} for index in self.near]
        self.partner = {"rep": self.rep + 1 - 2 * self.core}
        self.up = {"rep": lax.rem(self.rep + 2, reps)}
        self.down = {"rep": lax.rem(self.rep + reps - 2, reps)}

    def greet(self, line=True):
        barrier = pltpu.get_barrier_semaphore()
        others = self.plane[1:] + ([self.partner, self.up, self.down] if line else [])
        for other in others:
            pl.semaphore_signal(barrier, inc=1, device_id=other, device_id_type=MESH)
        pl.semaphore_wait(barrier, len(others))


def remote(src, dst, sems, index, device):
    return pltpu.make_async_remote_copy(
        src_ref=src,
        dst_ref=dst,
        send_sem=sems.at[0, index],
        recv_sem=sems.at[1, index],
        device_id=device,
        device_id_type=MESH,
    )


class PlaneGather:
    def __init__(self, links, own, slot, rows, sems):
        x, y = links.plane[1], links.plane[2]
        here, near_x, near_y, far = links.near
        half = rows // 2

        def part(index, lo):
            return slot(index).at[pl.ds(lo, half)]

        self.first = [
            remote(own, slot(here), sems, 0, x),
            remote(own, slot(here), sems, 1, y),
        ]
        self.second = [
            remote(part(near_x, 0), part(near_x, 0), sems, 2, y),
            remote(part(near_y, half), part(near_y, half), sems, 3, x),
        ]
        self.come = [
            remote(slot(near_x), slot(near_x), sems, 0, x),
            remote(slot(near_y), slot(near_y), sems, 1, y),
            remote(part(far, 0), part(far, 0), sems, 2, y),
            remote(part(far, half), part(far, half), sems, 3, x),
        ]

    def start(self):
        for copy in self.first:
            copy.start()

    def hand_on(self):
        for i in range(2):
            self.come[i].wait_recv()
            self.second[i].start()

    def finish(self):
        for i in (2, 3):
            self.come[i].wait_recv()

    def drain(self):
        for copy in self.first + self.second:
            copy.wait_send()


def prologue_kernel(
    lengths_ref,
    starts_ref,
    x_ref,
    cot_ref,
    vec_ref,
    inverse_ref,
    wqkv_ref,
    wo_ref,
    gu_ref,
    normed_all,
    cot_all,
    wgu,
    wqkv_full,
    wo_full,
    kv_full,
    mid_ref,
    normed_first_ref,
    query_ref,
    attn_ref,
    lse_ref,
    trig_ref,
    gains_ref,
    vec_all,
    wqkv_buf,
    wo_buf,
    kv_buf,
    normed_buf,
    bias_ref,
    local_sems,
    vec_sems,
    qkv_sems,
    qkv_core,
    wo_sems,
    wo_core,
    kv_sems,
    cot_sems,
    norm_sems,
    gu_sems,
    up_sems,
    down_sems,
    own_core,
    up_core,
    down_core,
):
    links = Links()
    here, core, line = links.here, links.core, links.line
    count = lax.axis_size("rep") // 2
    rows, width = x_ref.shape
    shard = wqkv_ref.shape[0]
    half = shard // 2
    links.greet()

    def shard_rows(ref, index):
        return ref.at[pl.ds(pl.multiple_of(index * shard, shard), shard)]

    own_copies = [
        pltpu.make_async_copy(wqkv_ref, shard_rows(wqkv_buf, here), local_sems.at[0]),
        pltpu.make_async_copy(wo_ref, shard_rows(wo_buf, here), local_sems.at[1]),
        pltpu.make_async_copy(cot_ref, cot_all.at[here], local_sems.at[2]),
        pltpu.make_async_copy(vec_ref, vec_all.at[here], local_sems.at[3]),
    ]

    vec_sends = [remote(vec_ref, vec_all.at[here], vec_sems, d - 1, links.plane[d]) for d in (1, 2, 3)]
    vec_comes = [
        remote(vec_ref, vec_all.at[links.near[d]], vec_sems, d - 1, links.plane[d]) for d in (1, 2, 3)
    ]

    def half_rows(ref, index, which):
        return ref.at[pl.ds(pl.multiple_of(index * shard + which * half, half), half)]

    def weight_gather(src, buf, sems, core_sems):
        gather = PlaneGather(
            links,
            src.at[pl.ds(pl.multiple_of(core * half, half), half)],
            lambda index: half_rows(buf, index, core),
            half,
            sems,
        )
        swaps = [
            remote(
                half_rows(buf, links.near[d], core),
                half_rows(buf, links.near[d], core),
                core_sems,
                d - 1,
                links.partner,
            )
            for d in (1, 2, 3)
        ]
        comes = [
            remote(
                half_rows(buf, links.near[d], 1 - core),
                half_rows(buf, links.near[d], 1 - core),
                core_sems,
                d - 1,
                links.partner,
            )
            for d in (1, 2, 3)
        ]
        return gather, swaps, comes

    qkv_gather, qkv_swaps, qkv_comes = weight_gather(wqkv_ref, wqkv_buf, qkv_sems, qkv_core)
    wo_gather, wo_swaps, wo_comes = weight_gather(wo_ref, wo_buf, wo_sems, wo_core)
    cot_gather = PlaneGather(links, cot_ref, lambda index: cot_all.at[index], rows, cot_sems)
    norm_gather = PlaneGather(links, normed_buf, lambda index: normed_all.at[index], rows, norm_sems)

    gu_sends = [
        remote(gu_ref.at[links.near[d]], wgu.at[core, line, d - 1], gu_sems, d - 1, links.plane[d])
        for d in (1, 2, 3)
    ]
    own_block = wgu.at[core, line]
    own_swap = remote(own_block, own_block, own_core, 0, links.partner)
    own_come = remote(wgu.at[1 - core, line], wgu.at[1 - core, line], own_core, 0, links.partner)

    class Hop:
        def __init__(self, k, way):
            sems = up_sems if way > 0 else down_sems
            core_sems = up_core if way > 0 else down_core
            device = links.up if way > 0 else links.down
            back = links.down if way > 0 else links.up
            sent = jnp.clip(line - way * (k - 1), 0, count - 1)
            come = jnp.clip(line - way * k, 0, count - 1)
            if way > 0:
                self.sends = (line <= count - 2) & (line >= k - 1)
                self.comes = line >= k
            else:
                self.sends = (line >= 1) & (line + k - 1 <= count - 1)
                self.comes = line + k <= count - 1
            self.send = remote(wgu.at[core, sent], wgu.at[core, sent], sems, k - 1, device)
            self.recv = remote(wgu.at[core, come], wgu.at[core, come], sems, k - 1, back)
            self.swap = remote(wgu.at[core, come], wgu.at[core, come], core_sems, k - 1, links.partner)
            self.swap_come = remote(
                wgu.at[1 - core, come], wgu.at[1 - core, come], core_sems, k - 1, links.partner
            )

    hops = [(Hop(k, 1), Hop(k, -1)) for k in range(1, count)]

    def start_hop(k):
        for hop in hops[k - 1]:
            pl.when(hop.sends)(hop.send.start)

    def take_hop(k):
        for hop in hops[k - 1]:

            @pl.when(hop.comes)
            def _():
                hop.recv.wait_recv()
                hop.swap.start()

    for copy in vec_sends:
        copy.start()
    qkv_gather.start()
    for copy in gu_sends:
        copy.start()
    for copy in own_copies:
        copy.start()
    wo_gather.start()

    bias, query_rel = mask_bias(here, rows, kv_buf.shape[0] * rows, lengths_ref, starts_ref)
    bias_ref[...] = bias
    angles = query_rel.astype(jnp.float32) * inverse_ref[0:1, :]
    lanes = lax.broadcasted_iota(jnp.int32, (1, HDIM), 1)
    cosine = jnp.cos(angles)
    sine = jnp.sin(angles) * jnp.where(lanes < HDIM // 2, -1.0, 1.0)
    trig_ref[0] = cosine
    trig_ref[1] = sine

    x_float = x_ref[...].astype(jnp.float32)
    unit = x_float * lax.rsqrt(jnp.mean(x_float * x_float, axis=1, keepdims=True) + epsilon)
    own_copies[3].wait()
    for copy in vec_comes:
        copy.wait_recv()
    gains_ref[...] = vec_all[0] + vec_all[1] + vec_all[2] + vec_all[3]
    normed_first_ref[...] = (unit * gains_ref[1:2, :]).astype(jnp.bfloat16)

    qkv_gather.hand_on()
    for swap in qkv_swaps[:2]:
        swap.start()
    for copy in gu_sends:
        copy.wait_recv()
    start_hop(1)
    own_swap.start()
    qkv_gather.finish()
    qkv_swaps[2].start()
    cot_gather.start()
    own_copies[0].wait()
    for copy in qkv_comes:
        copy.wait_recv()

    full_copy = pltpu.make_async_copy(wqkv_buf, wqkv_full, local_sems.at[4])
    full_copy.start()

    def rope(value):
        return value * trig_ref[0] + pltpu.roll(value, HDIM // 2, 1) * trig_ref[1]

    def project(first, bias_row):
        columns = pl.ds(pl.multiple_of(first, 2 * HDIM), 2 * HDIM)
        return dot_f32(normed_first_ref[...], wqkv_buf[:, columns]) + bias_row

    keys = project(width, gains_ref[3:4, 0 : 2 * HDIM])
    own_kv = kv_buf.at[here]
    for h in range(2):
        kv_buf[here, :, h * HDIM : (h + 1) * HDIM] = rope(keys[:, h * HDIM : (h + 1) * HDIM]).astype(
            jnp.bfloat16
        )
    values = project(width + 2 * HDIM, gains_ref[3:4, 2 * HDIM : 4 * HDIM])
    kv_buf[here, :, 2 * HDIM : 4 * HDIM] = values.astype(jnp.bfloat16)
    kv_sends = [remote(own_kv, own_kv, kv_sems, d - 1, links.plane[d]) for d in (1, 2, 3)]
    kv_comes = [
        remote(kv_buf.at[links.near[d]], kv_buf.at[links.near[d]], kv_sems, d - 1, links.plane[d])
        for d in (1, 2, 3)
    ]
    for copy in kv_sends:
        copy.start()

    def query_pair(pair, carry):
        columns = pl.ds(pl.multiple_of(pair * 2 * HDIM, 2 * HDIM), 2 * HDIM)
        got = project(pair * 2 * HDIM, gains_ref[0:1, columns])
        for h in range(2):
            where = pl.ds(pl.multiple_of(pair * 2 * HDIM + h * HDIM, HDIM), HDIM)
            query_ref[:, where] = rope(got[:, h * HDIM : (h + 1) * HDIM]).astype(jnp.bfloat16)
        return carry

    lax.fori_loop(0, HEADS // 2, query_pair, 0)
    wo_gather.hand_on()
    for swap in wo_swaps[:2]:
        swap.start()
    for copy in kv_comes:
        copy.wait_recv()
    kv_copy = pltpu.make_async_copy(kv_buf, kv_full, local_sems.at[5])
    kv_copy.start()

    group = HEADS // KVH
    row_len = kv_buf.shape[0] * rows
    head_lane = lax.broadcasted_iota(jnp.int32, (1, HDIM), 1)

    def head_step(h, lse):
        columns = pl.ds(pl.multiple_of(h * HDIM, HDIM), HDIM)
        shared = h // group
        key = kv_buf[:, :, pl.ds(pl.multiple_of(shared * HDIM, HDIM), HDIM)].reshape(row_len, HDIM)
        value = kv_buf[:, :, pl.ds(pl.multiple_of((KVH + shared) * HDIM, HDIM), HDIM)].reshape(
            row_len, HDIM
        )
        scores = dot_f32(query_ref[:, columns], key, ((1,), (1,))) * (1.0 / HDIM**0.5) + bias_ref[...]
        peak = jnp.max(scores, axis=1, keepdims=True)
        expo = jnp.exp(scores - peak)
        total = jnp.sum(expo, axis=1, keepdims=True)
        mixed = dot_f32(expo.astype(jnp.bfloat16), value) / total
        attn_ref[:, columns] = mixed.astype(jnp.bfloat16)
        return jnp.where(head_lane == h, peak + jnp.log(total), lse)

    lse = lax.fori_loop(0, HEADS // 2, head_step, jnp.zeros((rows, HDIM), jnp.float32))
    wo_gather.finish()
    wo_swaps[2].start()
    take_hop(1)
    start_hop(2)
    lse_ref[...] = lax.fori_loop(HEADS // 2, HEADS, head_step, lse)
    cot_gather.hand_on()
    take_hop(2)
    start_hop(3)
    own_copies[1].wait()
    for copy in wo_comes:
        copy.wait_recv()
    wo_copy = pltpu.make_async_copy(wo_buf, wo_full, local_sems.at[6])
    wo_copy.start()

    def out_columns(i, carry):
        columns = pl.ds(pl.multiple_of(i * 256, 256), 256)
        mid_ref[:, columns] = x_ref[:, columns].astype(jnp.float32) + dot_f32(
            attn_ref[...], wo_buf[:, columns]
        )
        return carry

    lax.fori_loop(0, width // 256, out_columns, 0)
    mid = mid_ref[...]
    unit = mid * lax.rsqrt(jnp.mean(mid * mid, axis=1, keepdims=True) + epsilon)
    normed_buf[...] = (unit * gains_ref[2:3, :]).astype(jnp.bfloat16)
    norm_gather.start()
    norm_copy = pltpu.make_async_copy(normed_buf, normed_all.at[here], local_sems.at[7])
    norm_copy.start()
    norm_gather.hand_on()
    cot_gather.finish()
    take_hop(3)
    norm_gather.finish()

    own_copies[2].wait()
    full_copy.wait()
    kv_copy.wait()
    wo_copy.wait()
    norm_copy.wait()
    for copy in vec_sends + gu_sends + qkv_swaps + wo_swaps + kv_sends + [own_swap]:
        copy.wait_send()
    own_come.wait_recv()
    for copy in wo_comes[:0]:
        copy.wait_recv()
    for gather in (qkv_gather, wo_gather, cot_gather, norm_gather):
        gather.drain()
    for pair in hops:
        for hop in pair:
            pl.when(hop.sends)(hop.send.wait_send)

            @pl.when(hop.comes)
            def _():
                hop.swap.wait_send()
                hop.swap_come.wait_recv()


def prologue(lengths, starts, x, cot, vec, inverse, wqkv, wo, pieces):
    rows, width = x.shape
    shards = lax.axis_size("fsdp")
    count = lax.axis_size("rep") // 2
    thin, part = pieces.shape[2:]
    bf16, f32 = jnp.bfloat16, jnp.float32
    any_space = pl.BlockSpec(memory_space=pl.ANY)
    vmem = pl.BlockSpec(memory_space=pltpu.VMEM)
    smem = pl.BlockSpec(memory_space=pltpu.SMEM)
    shape = jax.ShapeDtypeStruct

    def sems(n):
        return pltpu.SemaphoreType.DMA((2, n))

    return pl.pallas_call(
        prologue_kernel,
        name="prologue",
        out_shape=(
            shape((shards, rows, width), bf16),
            shape((shards, rows, width), bf16),
            shape((2, count, shards - 1, 2, thin, part), bf16),
            shape((width, wqkv.shape[1]), bf16),
            shape((width, width), bf16),
            shape((shards, rows, 4 * HDIM), bf16),
            shape((rows, width), f32),
            shape((rows, width), bf16),
            shape((rows, width), bf16),
            shape((rows, width), bf16),
            shape((rows, HDIM), f32),
            shape((2, rows, HDIM), f32),
            shape((8, width), f32),
        ),
        in_specs=[smem, smem, vmem, vmem, vmem, vmem, any_space, any_space, any_space],
        out_specs=[any_space] * 6 + [vmem] * 7,
        scratch_shapes=[
            pltpu.VMEM((shards, 8, width), f32),
            pltpu.VMEM((width, wqkv.shape[1]), bf16),
            pltpu.VMEM((width, width), bf16),
            pltpu.VMEM((shards, rows, 4 * HDIM), bf16),
            pltpu.VMEM((rows, width), bf16),
            pltpu.VMEM((rows, shards * rows), f32),
            pltpu.SemaphoreType.DMA((8,)),
            sems(3),
            sems(4),
            sems(3),
            sems(4),
            sems(3),
            sems(3),
            sems(4),
            sems(4),
            sems(3),
            sems(count - 1),
            sems(count - 1),
            sems(1),
            sems(count - 1),
            sems(count - 1),
        ],
        compiler_params=pltpu.CompilerParams(
            collective_id=0, has_side_effects=True, vmem_limit_bytes=60 * 2**20
        ),
    )(lengths, starts, x, cot, vec, inverse, wqkv, wo, pieces)


def local(
    hidden_in,
    out_grad,
    doc_lengths,
    piece_starts,
    w_query,
    b_query,
    w_key,
    b_key,
    w_value,
    b_value,
    w_output,
    gain_attn,
    w_gate,
    w_up,
    w_down,
    gain_mlp,
):
    tok_rows = hidden_in.shape[0]
    model_width = hidden_in.shape[1]
    shard_count = lax.axis_size("fsdp")
    row_len = tok_rows * shard_count
    group_size = HEADS // KVH
    kv_width = KVH * HDIM
    ff_width = w_gate.shape[1]
    score_scale = 1.0 / HDIM**0.5
    local_pos = lax.axis_index("fsdp") * tok_rows + jnp.arange(tok_rows, dtype=jnp.int32)
    row_pos = jnp.arange(row_len, dtype=jnp.int32)
    lengths = doc_lengths[0]
    starts = piece_starts[0]
    query_doc, query_rel, query_piece = row_layout(local_pos, lengths, starts, PIECE)
    key_doc, unused_rel, key_piece = row_layout(row_pos, lengths, starts, PIECE)
    allowed = visible_pairs(query_doc, local_pos, query_piece, key_doc, row_pos, key_piece)
    cosine, sine = rope_tables(query_rel, HDIM)
    here = lax.axis_index("fsdp")
    core = lax.axis_index("rep") % 2
    line = lax.axis_size("rep") // 2
    low = jnp.bfloat16

    def gather_rows(weight):
        half = weight.shape[0] // 2
        mine = lax.dynamic_slice_in_dim(weight, core * half, half, 0)
        mine = jnp.stack([jnp.concatenate(p, axis=0) for p in gather_relative(mine, "fsdp")])
        both = core_halves(mine, core_swap(mine), core)
        rows = place([both[:, d] for d in range(shard_count)], here)
        return rows.reshape(2 * half * shard_count, weight.shape[1])

    qkv_full = gather_rows(jnp.concatenate([w_query, w_key, w_value], axis=1))
    query_full = qkv_full[:, :model_width]
    key_full = qkv_full[:, model_width : model_width + kv_width]
    value_full = qkv_full[:, model_width + kv_width :]
    output_full = gather_rows(w_output)
    vectors = lax.all_gather(
        jnp.concatenate([b_query, b_key, b_value, gain_attn, gain_mlp]), "fsdp", axis=0
    )
    cuts = [0]
    for vector in (b_query, b_key, b_value, gain_attn, gain_mlp):
        cuts.append(cuts[-1] + vector.shape[0])
    query_bias, key_bias, value_bias, attn_gain, mlp_gain = (
        vectors[:, cuts[i] : cuts[i + 1]].reshape(-1) for i in range(5)
    )

    part = ff_width // shard_count

    def exchange_columns(weight):
        half = weight.shape[0] // 2
        mine = lax.dynamic_slice_in_dim(weight, core * half, half, 0)
        got = []
        for d in range(shard_count):
            piece = lax.dynamic_slice_in_dim(mine, (here ^ d) * part, part, 1)
            got.append(piece if d == 0 else lax.ppermute(piece, "fsdp", xor_pairs(shard_count, d)))
        got = jnp.stack(got)
        both = core_halves(got, core_swap(got), core)
        rows = place([both[:, d] for d in range(shard_count)], here)
        return rows.reshape(2 * half * shard_count, part)

    gate_part = exchange_columns(w_gate)
    up_part = exchange_columns(w_up)
    cot_all = jnp.concatenate([h for p in gather_relative(out_grad, "fsdp") for h in p], axis=0)
    x_float = hidden_in.astype(jnp.float32)
    inv_first = lax.rsqrt(jnp.mean(x_float * x_float, axis=1, keepdims=True) + epsilon)
    unit_first = x_float * inv_first
    gain_first = attn_gain.astype(jnp.float32)
    normed_first = (unit_first * gain_first).astype(jnp.bfloat16)
    query_pre = mat_dot(normed_first, query_full) + query_bias.astype(jnp.float32)
    key_pre = mat_dot(normed_first, key_full) + key_bias.astype(jnp.float32)
    value_pre = mat_dot(normed_first, value_full) + value_bias.astype(jnp.float32)
    query_rot = rotate(query_pre.reshape(tok_rows, HEADS, HDIM), cosine, sine).astype(jnp.bfloat16)
    key_rot = (
        rotate(key_pre.reshape(tok_rows, KVH, HDIM), cosine, sine)
        .astype(jnp.bfloat16)
        .reshape(tok_rows, kv_width)
    )
    value_low = value_pre.astype(jnp.bfloat16)
    keys_row, values_row = (
        lax.all_gather(key_rot, "fsdp", axis=0, tiled=True),
        lax.all_gather(value_low, "fsdp", axis=0, tiled=True),
    )
    query_grouped = query_rot.reshape(tok_rows, KVH, group_size, HDIM)
    keys_grouped = keys_row.reshape(row_len, KVH, HDIM)
    values_grouped = values_row.reshape(row_len, KVH, HDIM)

    def masked_scores():
        raw_scores = (
            jnp.einsum(
                "tgjd,rgd->gjtr", query_grouped, keys_grouped, preferred_element_type=jnp.float32
            )
            * score_scale
        )
        return jnp.where(allowed[None, None], raw_scores, -1e30)

    scores = masked_scores()
    row_peak = jnp.max(scores, axis=3, keepdims=True)
    expo_vals = jnp.exp(scores - row_peak)
    row_total = jnp.sum(expo_vals, axis=3, keepdims=True)
    soft_probs = expo_vals / row_total
    log_total = row_peak + jnp.log(row_total)
    attn_heads = jnp.einsum(
        "gjtr,rgd->tgjd",
        soft_probs.astype(jnp.bfloat16),
        values_grouped,
        preferred_element_type=jnp.float32,
    )
    attn_low = attn_heads.reshape(tok_rows, model_width).astype(jnp.bfloat16)
    mid_state = x_float + mat_dot(attn_low, output_full)
    inv_second = lax.rsqrt(jnp.mean(mid_state * mid_state, axis=1, keepdims=True) + epsilon)
    unit_second = mid_state * inv_second
    gain_second = mlp_gain.astype(jnp.float32)
    normed_second = (unit_second * gain_second).astype(jnp.bfloat16)
    cot_float = out_grad.astype(jnp.float32)
    normed_all = jnp.concatenate([h for p in gather_relative(normed_second, "fsdp") for h in p], axis=0)
    gate_val = mat_dot(normed_all, gate_part)
    up_val = mat_dot(normed_all, up_part)
    sig_gate = jax.nn.sigmoid(gate_val)
    silu_gate = gate_val * sig_gate
    act_low = (silu_gate * up_val).astype(low)
    d_act = dot_right_t(cot_all, w_down)
    d_gate = (d_act * up_val * sig_gate * (1.0 + gate_val * (1.0 - sig_gate))).astype(low)
    d_up = (d_act * silu_gate).astype(low)
    mlp_part = mat_dot(act_low, w_down).reshape(shard_count, tok_rows, model_width)
    mlp_out = scatter_relative([mlp_part[d] for d in range(shard_count)], "fsdp")
    norm_part = (dot_right_t(d_gate, gate_part) + dot_right_t(d_up, up_part)).reshape(
        shard_count, tok_rows, model_width
    )
    partial_value = scatter_relative([norm_part[d] for d in range(shard_count)], "fsdp")

    def keep_half(grad):
        mine = lax.dynamic_index_in_dim(grad, core, 1, keepdims=False)
        other = lax.dynamic_index_in_dim(grad, 1 - core, 1, keepdims=False)
        return (mine.astype(jnp.float32) + core_swap(other).astype(jnp.float32)).astype(low)

    def both_cores(half):
        return core_halves(half, core_swap(half), core)

    down_grad = dot_left_t(act_low, cot_all).astype(low)
    half = part // 2
    down_half = keep_half(down_grad.reshape(1, 2, half, model_width))[0]
    wide = model_width // line
    down_parts = jnp.stack([down_half[:, q * wide : (q + 1) * wide] for q in range(line)])
    down_own = line_scatter(down_parts).astype(low)
    down_rows = line_gather(down_own)
    down_rows = jnp.concatenate([down_rows[q] for q in range(line)], axis=1)
    down_sums = both_cores(down_rows).reshape(part, model_width).astype(jnp.float32)

    rows = model_width // shard_count
    thin = rows // 2 // line

    def column_grad(d_value):
        grad = dot_left_t(normed_all, d_value).astype(low)
        kept = keep_half(grad.reshape(shard_count, 2, rows // 2, part))
        kept = kept.reshape(shard_count, line, thin, part).transpose(1, 0, 2, 3)
        own = line_scatter(kept).astype(low)
        got = []
        for d in range(shard_count):
            piece = pick(own, here ^ d)
            got.append(piece if d == 0 else lax.ppermute(piece, "fsdp", xor_pairs(shard_count, d)))
        got = place(got, here).transpose(1, 0, 2).reshape(thin, ff_width)
        full = line_gather(got).reshape(rows // 2, ff_width)
        return both_cores(full).reshape(rows, ff_width).astype(jnp.float32)

    grad_gate = column_grad(d_gate)
    grad_up = column_grad(d_up)
    output = mid_state + mlp_out
    d_gain_second = jnp.sum(partial_value * unit_second, axis=0)
    scaled_second = partial_value * gain_second
    d_mid = cot_float + inv_second * (
        scaled_second - unit_second * jnp.mean(scaled_second * unit_second, axis=1, keepdims=True)
    )
    d_branch_low = d_mid.astype(jnp.bfloat16)
    d_attn_low = dot_right_t(d_branch_low, output_full).astype(jnp.bfloat16)
    d_attn_grouped = d_attn_low.reshape(tok_rows, KVH, group_size, HDIM)
    scores = masked_scores()
    soft_back = jnp.exp(scores - log_total)
    probs_low = soft_back.astype(jnp.bfloat16)
    prob_grad = jnp.einsum(
        "tgjd,rgd->gjtr", d_attn_grouped, values_grouped, preferred_element_type=jnp.float32
    )
    row_delta = jnp.sum(soft_back * prob_grad, axis=3, keepdims=True)
    score_grad = (soft_back * (prob_grad - row_delta)).astype(jnp.bfloat16)
    dquery_rot = (
        jnp.einsum("gjtr,rgd->tgjd", score_grad, keys_grouped, preferred_element_type=jnp.float32)
        * score_scale
    )
    dquery_low = (
        unrotate(dquery_rot.reshape(tok_rows, HEADS, HDIM), cosine, sine)
        .reshape(tok_rows, model_width)
        .astype(jnp.bfloat16)
    )
    key_grad = (
        jnp.einsum("gjtr,tgjd->rgd", score_grad, query_grouped, preferred_element_type=jnp.float32)
        * score_scale
    )
    value_grad = jnp.einsum(
        "gjtr,tgjd->rgd", probs_low, d_attn_grouped, preferred_element_type=jnp.float32
    )
    kv_sums = lax.psum_scatter(
        jnp.concatenate(
            [
                key_grad.reshape(lax.axis_size("fsdp") * tok_rows, kv_width),
                value_grad.reshape(lax.axis_size("fsdp") * tok_rows, kv_width),
            ],
            axis=1,
        ).astype(jnp.bfloat16),
        "fsdp",
        scatter_dimension=0,
        tiled=True,
    ).astype(jnp.float32)
    dkey_low = (
        unrotate(kv_sums[:, :kv_width].reshape(tok_rows, KVH, HDIM), cosine, sine)
        .reshape(tok_rows, kv_width)
        .astype(jnp.bfloat16)
    )
    dvalue_low = kv_sums[:, kv_width:].astype(jnp.bfloat16)
    d_norm_first = (
        dot_right_t(dquery_low, query_full)
        + dot_right_t(dkey_low, key_full)
        + dot_right_t(dvalue_low, value_full)
    )
    attn_grads = jnp.concatenate(
        [
            dot_left_t(normed_first, dquery_low).astype(low),
            dot_left_t(normed_first, dkey_low).astype(low),
            dot_left_t(normed_first, dvalue_low).astype(low),
            dot_left_t(attn_low, d_branch_low).astype(low),
        ],
        axis=1,
    )
    attn_wide = attn_grads.shape[1]
    attn_kept = keep_half(attn_grads.reshape(shard_count, 2, rows // 2, attn_wide))
    attn_own = scatter_relative([pick(attn_kept, here ^ d) for d in range(shard_count)], "fsdp").astype(low)
    attn_own = line_scatter(attn_own.reshape(line, thin, attn_wide)).astype(low)
    attn_rows = line_gather(attn_own).reshape(rows // 2, attn_wide)
    attn_sums = both_cores(attn_rows).reshape(rows, attn_wide).astype(jnp.float32)
    d_gain_first = jnp.sum(d_norm_first * unit_first, axis=0)
    scaled_first = d_norm_first * gain_first
    grad_input = d_mid + inv_first * (
        scaled_first - unit_first * jnp.mean(scaled_first * unit_first, axis=1, keepdims=True)
    )
    bias_query = jnp.sum(dquery_low.astype(jnp.float32), axis=0)
    bias_key = jnp.sum(dkey_low.astype(jnp.float32), axis=0)
    bias_value = jnp.sum(dvalue_low.astype(jnp.float32), axis=0)
    small = (bias_query, bias_key, bias_value, d_gain_first, d_gain_second)
    summed = lax.psum(jnp.concatenate(small), ("rep", "fsdp"))
    outs = []
    at = 0
    for vector in small:
        size = vector.shape[0] // shard_count
        outs.append(lax.dynamic_slice_in_dim(summed, at + here * size, size, 0))
        at += vector.shape[0]
    bias_query, bias_key, bias_value, gain_first_sum, gain_second_sum = outs
    grad_query = attn_sums[:, :model_width]
    grad_key = attn_sums[:, model_width : model_width + kv_width]
    grad_value = attn_sums[:, model_width + kv_width : model_width + 2 * kv_width]
    grad_output = attn_sums[:, model_width + 2 * kv_width :]
    return (
        output,
        grad_input,
        grad_query,
        bias_query,
        grad_key,
        bias_key,
        grad_value,
        bias_value,
        grad_output,
        gain_first_sum,
        grad_gate,
        grad_up,
        down_sums,
        gain_second_sum,
    )


def local_fast(
    hidden_in,
    out_grad,
    doc_lengths,
    piece_starts,
    w_query,
    b_query,
    w_key,
    b_key,
    w_value,
    b_value,
    w_output,
    gain_attn,
    w_gate,
    w_up,
    w_down,
    gain_mlp,
):
    tok_rows = hidden_in.shape[0]
    model_width = hidden_in.shape[1]
    shard_count = lax.axis_size("fsdp")
    row_len = tok_rows * shard_count
    group_size = HEADS // KVH
    kv_width = KVH * HDIM
    ff_width = w_gate.shape[1]
    score_scale = 1.0 / HDIM**0.5
    row_pos = jnp.arange(row_len, dtype=jnp.int32)
    lengths = doc_lengths[0]
    starts = piece_starts[0]
    here = lax.axis_index("fsdp")
    core = lax.axis_index("rep") % 2
    line = lax.axis_size("rep") // 2
    line_pos = lax.axis_index("rep") // 2
    low = jnp.bfloat16
    part = ff_width // shard_count
    shard_rows = model_width // shard_count
    thin = shard_rows // 2 // line
    halves = jnp.arange(0, HDIM, 2).astype(jnp.float32) / HDIM
    inverse = rope_base ** (-halves)
    inverse = jnp.broadcast_to(jnp.concatenate([inverse, inverse])[None], (8, HDIM))

    def spread(vector, first, size):
        zeros = jnp.zeros((1, size), jnp.float32)
        return lax.dynamic_update_slice(
            zeros, vector.astype(jnp.float32)[None], (0, first + here * vector.shape[0])
        )

    kv_bias = spread(b_key, 0, model_width) + spread(b_value, kv_width, model_width)
    vec = jnp.concatenate(
        [
            spread(b_query, 0, model_width),
            spread(gain_attn, 0, model_width),
            spread(gain_mlp, 0, model_width),
            kv_bias,
            jnp.zeros((4, model_width), jnp.float32),
        ]
    )
    first_row = core * (shard_rows // 2) + line_pos * thin

    def cut(weight):
        piece = lax.dynamic_slice_in_dim(weight, first_row, thin, 0)
        return jnp.stack([piece[:, t * part : (t + 1) * part] for t in range(shard_count)])

    pieces = jnp.stack([cut(w_gate), cut(w_up)], axis=1)
    (
        normed_all,
        cot_all,
        wgu,
        wqkv_full,
        output_full,
        kv_full,
        mid_state,
        normed_first,
        query_rot,
        attn_low,
        lse,
        trig,
        gains,
    ) = prologue(
        doc_lengths,
        piece_starts,
        hidden_in,
        out_grad,
        vec,
        inverse,
        jnp.concatenate([w_query, w_key, w_value], axis=1),
        w_output,
        pieces,
    )
    query_full = wqkv_full[:, :model_width]
    key_full = wqkv_full[:, model_width : model_width + kv_width]
    value_full = wqkv_full[:, model_width + kv_width :]
    cosine = trig[0]
    sine = trig[1] * jnp.where(jnp.arange(HDIM) < HDIM // 2, -1.0, 1.0)
    local_pos = here * tok_rows + jnp.arange(tok_rows, dtype=jnp.int32)
    query_doc, query_rel, query_piece = row_layout(local_pos, lengths, starts, PIECE)
    key_doc, unused_rel, key_piece = row_layout(row_pos, lengths, starts, PIECE)
    allowed = visible_pairs(query_doc, local_pos, query_piece, key_doc, row_pos, key_piece)
    x_float = hidden_in.astype(jnp.float32)
    inv_first = lax.rsqrt(jnp.mean(x_float * x_float, axis=1, keepdims=True) + epsilon)
    unit_first = x_float * inv_first
    gain_first = gains[1]
    gain_second = gains[2]
    inv_second = lax.rsqrt(jnp.mean(mid_state * mid_state, axis=1, keepdims=True) + epsilon)
    unit_second = mid_state * inv_second
    kv_rows = kv_full.reshape(row_len, 2 * kv_width)
    query_grouped = query_rot.reshape(tok_rows, KVH, group_size, HDIM)
    keys_grouped = kv_rows[:, :kv_width].reshape(row_len, KVH, HDIM)
    values_grouped = kv_rows[:, kv_width:].reshape(row_len, KVH, HDIM)
    log_total = lse[:, :HEADS].T.reshape(KVH, group_size, tok_rows, 1)

    def masked_scores():
        raw_scores = (
            jnp.einsum(
                "tgjd,rgd->gjtr", query_grouped, keys_grouped, preferred_element_type=jnp.float32
            )
            * score_scale
        )
        return jnp.where(allowed[None, None], raw_scores, -1e30)

    def whole(which, weight):
        mine = lax.dynamic_slice_in_dim(weight, here * part, part, 1)
        other = wgu[:, :, :, which].transpose(2, 0, 1, 3, 4).reshape(
            shard_count - 1, shard_rows, part
        )
        rows = place([mine] + [other[d] for d in range(shard_count - 1)], here)
        return rows.reshape(model_width, part)

    gate_part = whole(0, w_gate)
    up_part = whole(1, w_up)
    cot_float = out_grad.astype(jnp.float32)
    cot_all = cot_all.reshape(row_len, model_width)
    normed_all = normed_all.reshape(row_len, model_width)
    gate_val = mat_dot(normed_all, gate_part)
    up_val = mat_dot(normed_all, up_part)
    sig_gate = jax.nn.sigmoid(gate_val)
    silu_gate = gate_val * sig_gate
    act_low = (silu_gate * up_val).astype(low)
    d_act = dot_right_t(cot_all, w_down)
    d_gate = (d_act * up_val * sig_gate * (1.0 + gate_val * (1.0 - sig_gate))).astype(low)
    d_up = (d_act * silu_gate).astype(low)
    mlp_part = mat_dot(act_low, w_down).reshape(shard_count, tok_rows, model_width)
    mlp_out = scatter_relative([pick(mlp_part, here ^ d) for d in range(shard_count)], "fsdp")
    norm_part = (dot_right_t(d_gate, gate_part) + dot_right_t(d_up, up_part)).reshape(
        shard_count, tok_rows, model_width
    )
    partial_value = scatter_relative([pick(norm_part, here ^ d) for d in range(shard_count)], "fsdp")

    def keep_half(grad):
        mine = lax.dynamic_index_in_dim(grad, core, 1, keepdims=False)
        other = lax.dynamic_index_in_dim(grad, 1 - core, 1, keepdims=False)
        return (mine.astype(jnp.float32) + core_swap(other).astype(jnp.float32)).astype(low)

    def both_cores(half):
        return core_halves(half, core_swap(half), core)

    down_grad = dot_left_t(act_low, cot_all).astype(low)
    half = part // 2
    down_half = keep_half(down_grad.reshape(1, 2, half, model_width))[0]
    wide = model_width // line
    down_parts = jnp.stack([down_half[:, q * wide : (q + 1) * wide] for q in range(line)])
    down_own = line_scatter(down_parts).astype(low)
    down_rows = line_gather(down_own)
    down_rows = jnp.concatenate([down_rows[q] for q in range(line)], axis=1)
    down_sums = both_cores(down_rows).reshape(part, model_width).astype(jnp.float32)

    rows = model_width // shard_count
    thin = rows // 2 // line

    def column_grad(d_value):
        grad = dot_left_t(normed_all, d_value).astype(low)
        kept = keep_half(grad.reshape(shard_count, 2, rows // 2, part))
        kept = kept.reshape(shard_count, line, thin, part).transpose(1, 0, 2, 3)
        own = line_scatter(kept).astype(low)
        got = []
        for d in range(shard_count):
            piece = pick(own, here ^ d)
            got.append(piece if d == 0 else lax.ppermute(piece, "fsdp", xor_pairs(shard_count, d)))
        got = place(got, here).transpose(1, 0, 2).reshape(thin, ff_width)
        full = line_gather(got).reshape(rows // 2, ff_width)
        return both_cores(full).reshape(rows, ff_width).astype(jnp.float32)

    grad_gate = column_grad(d_gate)
    grad_up = column_grad(d_up)
    output = mid_state + mlp_out
    d_gain_second = jnp.sum(partial_value * unit_second, axis=0)
    scaled_second = partial_value * gain_second
    d_mid = cot_float + inv_second * (
        scaled_second - unit_second * jnp.mean(scaled_second * unit_second, axis=1, keepdims=True)
    )
    d_branch_low = d_mid.astype(jnp.bfloat16)
    d_attn_low = dot_right_t(d_branch_low, output_full).astype(jnp.bfloat16)
    d_attn_grouped = d_attn_low.reshape(tok_rows, KVH, group_size, HDIM)
    scores = masked_scores()
    soft_back = jnp.exp(scores - log_total)
    probs_low = soft_back.astype(jnp.bfloat16)
    prob_grad = jnp.einsum(
        "tgjd,rgd->gjtr", d_attn_grouped, values_grouped, preferred_element_type=jnp.float32
    )
    row_delta = jnp.sum(soft_back * prob_grad, axis=3, keepdims=True)
    score_grad = (soft_back * (prob_grad - row_delta)).astype(jnp.bfloat16)
    dquery_rot = (
        jnp.einsum("gjtr,rgd->tgjd", score_grad, keys_grouped, preferred_element_type=jnp.float32)
        * score_scale
    )
    dquery_low = (
        unrotate(dquery_rot.reshape(tok_rows, HEADS, HDIM), cosine, sine)
        .reshape(tok_rows, model_width)
        .astype(jnp.bfloat16)
    )
    key_grad = (
        jnp.einsum("gjtr,tgjd->rgd", score_grad, query_grouped, preferred_element_type=jnp.float32)
        * score_scale
    )
    value_grad = jnp.einsum(
        "gjtr,tgjd->rgd", probs_low, d_attn_grouped, preferred_element_type=jnp.float32
    )
    kv_sums = lax.psum_scatter(
        jnp.concatenate(
            [
                key_grad.reshape(lax.axis_size("fsdp") * tok_rows, kv_width),
                value_grad.reshape(lax.axis_size("fsdp") * tok_rows, kv_width),
            ],
            axis=1,
        ).astype(jnp.bfloat16),
        "fsdp",
        scatter_dimension=0,
        tiled=True,
    ).astype(jnp.float32)
    dkey_low = (
        unrotate(kv_sums[:, :kv_width].reshape(tok_rows, KVH, HDIM), cosine, sine)
        .reshape(tok_rows, kv_width)
        .astype(jnp.bfloat16)
    )
    dvalue_low = kv_sums[:, kv_width:].astype(jnp.bfloat16)
    d_norm_first = (
        dot_right_t(dquery_low, query_full)
        + dot_right_t(dkey_low, key_full)
        + dot_right_t(dvalue_low, value_full)
    )
    attn_grads = jnp.concatenate(
        [
            dot_left_t(normed_first, dquery_low).astype(low),
            dot_left_t(normed_first, dkey_low).astype(low),
            dot_left_t(normed_first, dvalue_low).astype(low),
            dot_left_t(attn_low, d_branch_low).astype(low),
        ],
        axis=1,
    )
    attn_wide = attn_grads.shape[1]
    attn_kept = keep_half(attn_grads.reshape(shard_count, 2, rows // 2, attn_wide))
    attn_own = scatter_relative([pick(attn_kept, here ^ d) for d in range(shard_count)], "fsdp").astype(low)
    attn_own = line_scatter(attn_own.reshape(line, thin, attn_wide)).astype(low)
    attn_rows = line_gather(attn_own).reshape(rows // 2, attn_wide)
    attn_sums = both_cores(attn_rows).reshape(rows, attn_wide).astype(jnp.float32)
    d_gain_first = jnp.sum(d_norm_first * unit_first, axis=0)
    scaled_first = d_norm_first * gain_first
    grad_input = d_mid + inv_first * (
        scaled_first - unit_first * jnp.mean(scaled_first * unit_first, axis=1, keepdims=True)
    )
    bias_query = jnp.sum(dquery_low.astype(jnp.float32), axis=0)
    bias_key = jnp.sum(dkey_low.astype(jnp.float32), axis=0)
    bias_value = jnp.sum(dvalue_low.astype(jnp.float32), axis=0)
    small = (bias_query, bias_key, bias_value, d_gain_first, d_gain_second)
    summed = lax.psum(jnp.concatenate(small), ("rep", "fsdp"))
    outs = []
    at = 0
    for vector in small:
        size = vector.shape[0] // shard_count
        outs.append(lax.dynamic_slice_in_dim(summed, at + here * size, size, 0))
        at += vector.shape[0]
    bias_query, bias_key, bias_value, gain_first_sum, gain_second_sum = outs
    grad_query = attn_sums[:, :model_width]
    grad_key = attn_sums[:, model_width : model_width + kv_width]
    grad_value = attn_sums[:, model_width + kv_width : model_width + 2 * kv_width]
    grad_output = attn_sums[:, model_width + 2 * kv_width :]
    return (
        output,
        grad_input,
        grad_query,
        bias_query,
        grad_key,
        bias_key,
        grad_value,
        bias_value,
        grad_output,
        gain_first_sum,
        grad_gate,
        grad_up,
        down_sums,
        gain_second_sum,
    )


def solution(mesh):
    body = local_fast if mesh.shape["fsdp"] == 4 and mesh.shape["rep"] == 8 else local
    placed = (
        P(("rep", "fsdp"), None),
        P(("rep", "fsdp"), None),
        P("rep", None),
        P("rep", None),
        P("fsdp", None),
        P("fsdp"),
        P("fsdp", None),
        P("fsdp"),
        P("fsdp", None),
        P("fsdp"),
        P("fsdp", None),
        P("fsdp"),
        P("fsdp", None),
        P("fsdp", None),
        P("fsdp", None),
        P("fsdp"),
    )
    return jax.shard_map(
        body,
        mesh=mesh,
        in_specs=placed,
        out_specs=(
            P(("rep", "fsdp"), None),
            P(("rep", "fsdp"), None),
            P("fsdp", None),
            P("fsdp"),
            P("fsdp", None),
            P("fsdp"),
            P("fsdp", None),
            P("fsdp"),
            P("fsdp", None),
            P("fsdp"),
            P("fsdp", None),
            P("fsdp", None),
            P("fsdp", None),
            P("fsdp"),
        ),
        check_vma=False,
    )
```

```python
import jax
import jax.numpy as jnp
from jax import lax
from jax.experimental import pallas as pl
from jax.experimental.pallas import tpu as pltpu
from jax.sharding import PartitionSpec as P

HEADS = 12
KVH = 2
HDIM = 128
PIECE = 256


epsilon = 1e-06
rope_base = 1000000.0


def row_layout(positions, lengths, starts, piece_len):
    doc_ends = jnp.cumsum(lengths)
    passed = positions[:, None] >= doc_ends[None, :]
    doc_ids = jnp.sum(passed.astype(jnp.int32), axis=1, dtype=jnp.int32)
    offsets = jnp.sum(jnp.where(passed, lengths[None, :], 0), axis=1, dtype=jnp.int32)
    inside = (positions[:, None] >= starts[None, :]) & (
        positions[:, None] < starts[None, :] + piece_len
    )
    labels = jnp.arange(1, starts.shape[0] + 1, dtype=jnp.int32)
    piece_ids = jnp.sum(jnp.where(inside, labels[None, :], 0), axis=1, dtype=jnp.int32)
    return (doc_ids, positions - offsets, piece_ids)


def visible_pairs(query_doc, query_pos, query_piece, key_doc, key_pos, key_piece):
    same_doc = query_doc[:, None] == key_doc[None, :]
    causal = key_pos[None, :] <= query_pos[:, None]
    same_piece = (query_piece[:, None] == key_piece[None, :]) & (query_piece[:, None] > 0)
    return same_doc & (causal | same_piece)


def rope_tables(relative, head_dim):
    halves = jnp.arange(0, head_dim, 2).astype(jnp.float32) / head_dim
    inverse = rope_base ** (-halves)
    angles = relative.astype(jnp.float32)[:, None] * inverse[None, :]
    angles = jnp.concatenate([angles, angles], axis=1)
    return (jnp.cos(angles), jnp.sin(angles))


def rotate(values, cosine, sine):
    half_dim = values.shape[-1] // 2
    turned = jnp.concatenate([-values[..., half_dim:], values[..., :half_dim]], axis=-1)
    return values * cosine[:, None, :] + turned * sine[:, None, :]


def unrotate(grads, cosine, sine):
    half_dim = grads.shape[-1] // 2
    spun = grads * sine[:, None, :]
    turned_back = jnp.concatenate([spun[..., half_dim:], -spun[..., :half_dim]], axis=-1)
    return grads * cosine[:, None, :] + turned_back


def mat_dot(left, right):
    return jnp.dot(left, right, preferred_element_type=jnp.float32)


def dot_right_t(left, right):
    return lax.dot_general(
        left, right, (((1,), (1,)), ((), ())), preferred_element_type=jnp.float32
    )


def dot_left_t(left, right):
    return lax.dot_general(
        left, right, (((0,), (0,)), ((), ())), preferred_element_type=jnp.float32
    )


def xor_pairs(count, bit):
    return [(i, i ^ bit) for i in range(count)]


def bits_of(count):
    return [1 << k for k in range(count.bit_length() - 1)]


def gather_relative(block, axis):
    count = lax.axis_size(axis)
    bits = bits_of(count)
    half = block.shape[0] // 2
    halves = []
    for part, order in ((block[:half], bits), (block[half:], bits[::-1])):
        have = {0: part}
        for bit in order:
            fresh = {
                d ^ bit: lax.ppermute(piece, axis, xor_pairs(count, bit))
                for d, piece in have.items()
            }
            have.update(fresh)
        halves.append(have)
    return [(halves[0][d], halves[1][d]) for d in range(count)]


def scatter_relative(pieces, axis):
    count = lax.axis_size(axis)
    bits = bits_of(count)
    half = pieces[0].shape[0] // 2
    sums = []
    for lo, hi, order in ((0, half, bits[::-1]), (half, 2 * half, bits)):
        have = {d: pieces[d][lo:hi] for d in range(count)}
        for bit in order:
            come = {
                d ^ bit: lax.ppermute(have[d].astype(jnp.bfloat16), axis, xor_pairs(count, bit))
                for d in have
                if d & bit
            }
            have = {d: have[d].astype(jnp.float32) + come[d].astype(jnp.float32) for d in come}
        sums.append(have[0])
    return jnp.concatenate(sums, axis=0)


def core_swap(block):
    return lax.ppermute(block, "rep", xor_pairs(lax.axis_size("rep"), 1))


def line_pairs(lows, way):
    return [(2 * i + c, 2 * (i + way) + c) for i in lows for c in range(2)]


def pick(array, index):
    return lax.dynamic_index_in_dim(array, index, 0, keepdims=False)


def line_scatter(parts):
    count = lax.axis_size("rep") // 2
    here = lax.axis_index("rep") // 2
    arrived = [None, None]
    for step in range(1, count):
        sends = [
            pick(parts, jnp.clip(count - step + here, 0, count - 1)),
            pick(parts, jnp.clip(here - count + step, 0, count - 1)),
        ]
        for way in range(2):
            if arrived[way] is not None:
                sends[way] = (
                    sends[way].astype(jnp.float32) + arrived[way].astype(jnp.float32)
                ).astype(jnp.bfloat16)
        arrived = [
            lax.ppermute(sends[0], "rep", line_pairs(range(step), 1)),
            lax.ppermute(sends[1], "rep", line_pairs(range(count - step, count), -1)),
        ]
    own = pick(parts, here).astype(jnp.float32)
    return own + arrived[0].astype(jnp.float32) + arrived[1].astype(jnp.float32)


def line_gather(block):
    count = lax.axis_size("rep") // 2
    here = lax.axis_index("rep") // 2
    below, above = [block], [block]
    for step in range(1, count):
        below.append(lax.ppermute(below[-1], "rep", line_pairs(range(step - 1, count - 1), 1)))
        above.append(lax.ppermute(above[-1], "rep", line_pairs(range(1, count - step + 1), -1)))
    stacked = jnp.stack(below[:0:-1] + above)
    return lax.dynamic_slice_in_dim(stacked, count - 1 - here, count, 0)


def core_halves(mine, other, core):
    return jnp.where(core == 0, jnp.stack([mine, other]), jnp.stack([other, mine]))


def place(pieces, here):
    count = len(pieces)
    stacked = jnp.stack(pieces)
    return jnp.stack([pick(stacked, here ^ j) for j in range(count)])


MESH = pl.DeviceIdType.MESH
MASKED = -1e30


def dot_f32(left, right, dims=((1,), (0,))):
    return lax.dot_general(left, right, (dims, ((), ())), preferred_element_type=jnp.float32)


def layout_of(positions, lengths_ref, starts_ref):
    end = jnp.int32(0)
    doc = jnp.zeros_like(positions)
    before = jnp.zeros_like(positions)
    piece = jnp.zeros_like(positions)
    for i in range(lengths_ref.shape[1]):
        end = end + lengths_ref[0, i]
        passed = positions >= end
        doc = doc + jnp.where(passed, 1, 0)
        before = before + jnp.where(passed, lengths_ref[0, i], 0)
    for i in range(starts_ref.shape[1]):
        first = starts_ref[0, i]
        inside = (positions >= first) & (positions < first + PIECE)
        piece = piece + jnp.where(inside, i + 1, 0)
    return doc, positions - before, piece


def mask_bias(here, rows, row_len, lengths_ref, starts_ref):
    query_pos = here * rows + lax.broadcasted_iota(jnp.int32, (rows, 1), 0)
    key_pos = lax.broadcasted_iota(jnp.int32, (1, row_len), 1)
    query_doc, query_rel, query_piece = layout_of(query_pos, lengths_ref, starts_ref)
    key_doc, unused, key_piece = layout_of(key_pos, lengths_ref, starts_ref)
    allowed = (query_doc == key_doc) & (
        (key_pos <= query_pos) | ((query_piece == key_piece) & (query_piece > 0))
    )
    return jnp.where(allowed, 0.0, MASKED), query_rel


class Links:
    def __init__(self):
        self.here = lax.axis_index("fsdp")
        self.rep = lax.axis_index("rep")
        self.core = lax.rem(self.rep, 2)
        self.line = self.rep // 2
        reps = lax.axis_size("rep")
        here = self.here
        self.near = [here, here + 1 - 2 * lax.rem(here, 2), lax.rem(here + 2, 4), 3 - here]
        self.plane = [{"fsdp": index} for index in self.near]
        self.partner = {"rep": self.rep + 1 - 2 * self.core}
        self.up = {"rep": lax.rem(self.rep + 2, reps)}
        self.down = {"rep": lax.rem(self.rep + reps - 2, reps)}

    def greet(self, line=True):
        barrier = pltpu.get_barrier_semaphore()
        others = self.plane[1:] + ([self.partner, self.up, self.down] if line else [])
        for other in others:
            pl.semaphore_signal(barrier, inc=1, device_id=other, device_id_type=MESH)
        pl.semaphore_wait(barrier, len(others))


def remote(src, dst, sems, index, device):
    return pltpu.make_async_remote_copy(
        src_ref=src,
        dst_ref=dst,
        send_sem=sems.at[0, index],
        recv_sem=sems.at[1, index],
        device_id=device,
        device_id_type=MESH,
    )


class PlaneGather:
    def __init__(self, links, own, slot, rows, sems):
        x, y = links.plane[1], links.plane[2]
        here, near_x, near_y, far = links.near
        half = rows // 2

        def part(index, lo):
            return slot(index).at[pl.ds(lo, half)]

        self.first = [
            remote(own, slot(here), sems, 0, x),
            remote(own, slot(here), sems, 1, y),
        ]
        self.second = [
            remote(part(near_x, 0), part(near_x, 0), sems, 2, y),
            remote(part(near_y, half), part(near_y, half), sems, 3, x),
        ]
        self.come = [
            remote(slot(near_x), slot(near_x), sems, 0, x),
            remote(slot(near_y), slot(near_y), sems, 1, y),
            remote(part(far, 0), part(far, 0), sems, 2, y),
            remote(part(far, half), part(far, half), sems, 3, x),
        ]

    def start(self):
        for copy in self.first:
            copy.start()

    def hand_on(self):
        for i in range(2):
            self.come[i].wait_recv()
            self.second[i].start()

    def finish(self):
        for i in (2, 3):
            self.come[i].wait_recv()

    def drain(self):
        for copy in self.first + self.second:
            copy.wait_send()


def prologue_kernel(
    lengths_ref,
    starts_ref,
    x_ref,
    cot_ref,
    vec_ref,
    inverse_ref,
    wqkv_ref,
    wo_ref,
    gu_ref,
    normed_all,
    cot_all,
    wgu,
    wqkv_full,
    wo_full,
    kv_full,
    mid_ref,
    normed_first_ref,
    query_ref,
    attn_ref,
    lse_ref,
    trig_ref,
    gains_ref,
    vec_all,
    wqkv_buf,
    wo_buf,
    kv_buf,
    normed_buf,
    bias_ref,
    local_sems,
    vec_sems,
    qkv_sems,
    qkv_core,
    wo_sems,
    wo_core,
    kv_sems,
    cot_sems,
    norm_sems,
    gu_sems,
    up_sems,
    down_sems,
    own_core,
    up_core,
    down_core,
):
    links = Links()
    here, core, line = links.here, links.core, links.line
    count = lax.axis_size("rep") // 2
    rows, width = x_ref.shape
    shard = wqkv_ref.shape[0]
    half = shard // 2
    links.greet()

    def shard_rows(ref, index):
        return ref.at[pl.ds(pl.multiple_of(index * shard, shard), shard)]

    own_copies = [
        pltpu.make_async_copy(wqkv_ref, shard_rows(wqkv_buf, here), local_sems.at[0]),
        pltpu.make_async_copy(wo_ref, shard_rows(wo_buf, here), local_sems.at[1]),
        pltpu.make_async_copy(cot_ref, cot_all.at[here], local_sems.at[2]),
        pltpu.make_async_copy(vec_ref, vec_all.at[here], local_sems.at[3]),
    ]

    vec_sends = [remote(vec_ref, vec_all.at[here], vec_sems, d - 1, links.plane[d]) for d in (1, 2, 3)]
    vec_comes = [
        remote(vec_ref, vec_all.at[links.near[d]], vec_sems, d - 1, links.plane[d]) for d in (1, 2, 3)
    ]

    def half_rows(ref, index, which):
        return ref.at[pl.ds(pl.multiple_of(index * shard + which * half, half), half)]

    def weight_gather(src, buf, sems, core_sems):
        gather = PlaneGather(
            links,
            src.at[pl.ds(pl.multiple_of(core * half, half), half)],
            lambda index: half_rows(buf, index, core),
            half,
            sems,
        )
        swaps = [
            remote(
                half_rows(buf, links.near[d], core),
                half_rows(buf, links.near[d], core),
                core_sems,
                d - 1,
                links.partner,
            )
            for d in (1, 2, 3)
        ]
        comes = [
            remote(
                half_rows(buf, links.near[d], 1 - core),
                half_rows(buf, links.near[d], 1 - core),
                core_sems,
                d - 1,
                links.partner,
            )
            for d in (1, 2, 3)
        ]
        return gather, swaps, comes

    qkv_gather, qkv_swaps, qkv_comes = weight_gather(wqkv_ref, wqkv_buf, qkv_sems, qkv_core)
    wo_gather, wo_swaps, wo_comes = weight_gather(wo_ref, wo_buf, wo_sems, wo_core)
    cot_gather = PlaneGather(links, cot_ref, lambda index: cot_all.at[index], rows, cot_sems)
    norm_gather = PlaneGather(links, normed_buf, lambda index: normed_all.at[index], rows, norm_sems)

    gu_sends = [
        remote(gu_ref.at[links.near[d]], wgu.at[core, line, d - 1], gu_sems, d - 1, links.plane[d])
        for d in (1, 2, 3)
    ]
    own_block = wgu.at[core, line]
    own_swap = remote(own_block, own_block, own_core, 0, links.partner)
    own_come = remote(wgu.at[1 - core, line], wgu.at[1 - core, line], own_core, 0, links.partner)

    class Hop:
        def __init__(self, k, way):
            sems = up_sems if way > 0 else down_sems
            core_sems = up_core if way > 0 else down_core
            device = links.up if way > 0 else links.down
            back = links.down if way > 0 else links.up
            sent = jnp.clip(line - way * (k - 1), 0, count - 1)
            come = jnp.clip(line - way * k, 0, count - 1)
            if way > 0:
                self.sends = (line <= count - 2) & (line >= k - 1)
                self.comes = line >= k
            else:
                self.sends = (line >= 1) & (line + k - 1 <= count - 1)
                self.comes = line + k <= count - 1
            self.send = remote(wgu.at[core, sent], wgu.at[core, sent], sems, k - 1, device)
            self.recv = remote(wgu.at[core, come], wgu.at[core, come], sems, k - 1, back)
            self.swap = remote(wgu.at[core, come], wgu.at[core, come], core_sems, k - 1, links.partner)
            self.swap_come = remote(
                wgu.at[1 - core, come], wgu.at[1 - core, come], core_sems, k - 1, links.partner
            )

    hops = [(Hop(k, 1), Hop(k, -1)) for k in range(1, count)]

    def start_hop(k):
        for hop in hops[k - 1]:
            pl.when(hop.sends)(hop.send.start)

    def take_hop(k):
        for hop in hops[k - 1]:

            @pl.when(hop.comes)
            def _():
                hop.recv.wait_recv()
                hop.swap.start()

    for copy in vec_sends:
        copy.start()
    qkv_gather.start()
    for copy in gu_sends:
        copy.start()
    for copy in own_copies:
        copy.start()
    wo_gather.start()

    bias, query_rel = mask_bias(here, rows, kv_buf.shape[0] * rows, lengths_ref, starts_ref)
    bias_ref[...] = bias
    angles = query_rel.astype(jnp.float32) * inverse_ref[0:1, :]
    lanes = lax.broadcasted_iota(jnp.int32, (1, HDIM), 1)
    cosine = jnp.cos(angles)
    sine = jnp.sin(angles) * jnp.where(lanes < HDIM // 2, -1.0, 1.0)
    trig_ref[0] = cosine
    trig_ref[1] = sine

    x_float = x_ref[...].astype(jnp.float32)
    unit = x_float * lax.rsqrt(jnp.mean(x_float * x_float, axis=1, keepdims=True) + epsilon)
    own_copies[3].wait()
    for copy in vec_comes:
        copy.wait_recv()
    gains_ref[...] = vec_all[0] + vec_all[1] + vec_all[2] + vec_all[3]
    normed_first_ref[...] = (unit * gains_ref[1:2, :]).astype(jnp.bfloat16)

    qkv_gather.hand_on()
    for swap in qkv_swaps[:2]:
        swap.start()
    for copy in gu_sends:
        copy.wait_recv()
    start_hop(1)
    own_swap.start()
    qkv_gather.finish()
    qkv_swaps[2].start()
    cot_gather.start()
    own_copies[0].wait()
    for copy in qkv_comes:
        copy.wait_recv()

    full_copy = pltpu.make_async_copy(wqkv_buf, wqkv_full, local_sems.at[4])
    full_copy.start()

    def rope(value):
        return value * trig_ref[0] + pltpu.roll(value, HDIM // 2, 1) * trig_ref[1]

    def project(first, bias_row):
        columns = pl.ds(pl.multiple_of(first, 2 * HDIM), 2 * HDIM)
        return dot_f32(normed_first_ref[...], wqkv_buf[:, columns]) + bias_row

    keys = project(width, gains_ref[3:4, 0 : 2 * HDIM])
    own_kv = kv_buf.at[here]
    for h in range(2):
        kv_buf[here, :, h * HDIM : (h + 1) * HDIM] = rope(keys[:, h * HDIM : (h + 1) * HDIM]).astype(
            jnp.bfloat16
        )
    values = project(width + 2 * HDIM, gains_ref[3:4, 2 * HDIM : 4 * HDIM])
    kv_buf[here, :, 2 * HDIM : 4 * HDIM] = values.astype(jnp.bfloat16)
    kv_sends = [remote(own_kv, own_kv, kv_sems, d - 1, links.plane[d]) for d in (1, 2, 3)]
    kv_comes = [
        remote(kv_buf.at[links.near[d]], kv_buf.at[links.near[d]], kv_sems, d - 1, links.plane[d])
        for d in (1, 2, 3)
    ]
    for copy in kv_sends:
        copy.start()

    def query_pair(pair, carry):
        columns = pl.ds(pl.multiple_of(pair * 2 * HDIM, 2 * HDIM), 2 * HDIM)
        got = project(pair * 2 * HDIM, gains_ref[0:1, columns])
        for h in range(2):
            where = pl.ds(pl.multiple_of(pair * 2 * HDIM + h * HDIM, HDIM), HDIM)
            query_ref[:, where] = rope(got[:, h * HDIM : (h + 1) * HDIM]).astype(jnp.bfloat16)
        return carry

    lax.fori_loop(0, HEADS // 2, query_pair, 0)
    wo_gather.hand_on()
    for swap in wo_swaps[:2]:
        swap.start()
    for copy in kv_comes:
        copy.wait_recv()
    kv_copy = pltpu.make_async_copy(kv_buf, kv_full, local_sems.at[5])
    kv_copy.start()

    group = HEADS // KVH
    row_len = kv_buf.shape[0] * rows
    head_lane = lax.broadcasted_iota(jnp.int32, (1, HDIM), 1)

    def head_step(h, lse):
        columns = pl.ds(pl.multiple_of(h * HDIM, HDIM), HDIM)
        shared = h // group
        key = kv_buf[:, :, pl.ds(pl.multiple_of(shared * HDIM, HDIM), HDIM)].reshape(row_len, HDIM)
        value = kv_buf[:, :, pl.ds(pl.multiple_of((KVH + shared) * HDIM, HDIM), HDIM)].reshape(
            row_len, HDIM
        )
        scores = dot_f32(query_ref[:, columns], key, ((1,), (1,))) * (1.0 / HDIM**0.5) + bias_ref[...]
        peak = jnp.max(scores, axis=1, keepdims=True)
        expo = jnp.exp(scores - peak)
        total = jnp.sum(expo, axis=1, keepdims=True)
        mixed = dot_f32(expo.astype(jnp.bfloat16), value) / total
        attn_ref[:, columns] = mixed.astype(jnp.bfloat16)
        return jnp.where(head_lane == h, peak + jnp.log(total), lse)

    lse = lax.fori_loop(0, HEADS // 2, head_step, jnp.zeros((rows, HDIM), jnp.float32))
    wo_gather.finish()
    wo_swaps[2].start()
    take_hop(1)
    start_hop(2)
    lse_ref[...] = lax.fori_loop(HEADS // 2, HEADS, head_step, lse)
    cot_gather.hand_on()
    take_hop(2)
    start_hop(3)
    own_copies[1].wait()
    for copy in wo_comes:
        copy.wait_recv()
    wo_copy = pltpu.make_async_copy(wo_buf, wo_full, local_sems.at[6])
    wo_copy.start()

    def out_columns(i, carry):
        columns = pl.ds(pl.multiple_of(i * 256, 256), 256)
        mid_ref[:, columns] = x_ref[:, columns].astype(jnp.float32) + dot_f32(
            attn_ref[...], wo_buf[:, columns]
        )
        return carry

    lax.fori_loop(0, width // 256, out_columns, 0)
    mid = mid_ref[...]
    unit = mid * lax.rsqrt(jnp.mean(mid * mid, axis=1, keepdims=True) + epsilon)
    normed_buf[...] = (unit * gains_ref[2:3, :]).astype(jnp.bfloat16)
    norm_gather.start()
    norm_copy = pltpu.make_async_copy(normed_buf, normed_all.at[here], local_sems.at[7])
    norm_copy.start()
    norm_gather.hand_on()
    cot_gather.finish()
    take_hop(3)
    norm_gather.finish()

    own_copies[2].wait()
    full_copy.wait()
    kv_copy.wait()
    wo_copy.wait()
    norm_copy.wait()
    for copy in vec_sends + gu_sends + qkv_swaps + wo_swaps + kv_sends + [own_swap]:
        copy.wait_send()
    own_come.wait_recv()
    for copy in wo_comes[:0]:
        copy.wait_recv()
    for gather in (qkv_gather, wo_gather, cot_gather, norm_gather):
        gather.drain()
    for pair in hops:
        for hop in pair:
            pl.when(hop.sends)(hop.send.wait_send)

            @pl.when(hop.comes)
            def _():
                hop.swap.wait_send()
                hop.swap_come.wait_recv()


def prologue(lengths, starts, x, cot, vec, inverse, wqkv, wo, pieces):
    rows, width = x.shape
    shards = lax.axis_size("fsdp")
    count = lax.axis_size("rep") // 2
    thin, part = pieces.shape[2:]
    bf16, f32 = jnp.bfloat16, jnp.float32
    any_space = pl.BlockSpec(memory_space=pl.ANY)
    vmem = pl.BlockSpec(memory_space=pltpu.VMEM)
    smem = pl.BlockSpec(memory_space=pltpu.SMEM)
    shape = jax.ShapeDtypeStruct

    def sems(n):
        return pltpu.SemaphoreType.DMA((2, n))

    return pl.pallas_call(
        prologue_kernel,
        name="prologue",
        out_shape=(
            shape((shards, rows, width), bf16),
            shape((shards, rows, width), bf16),
            shape((2, count, shards - 1, 2, thin, part), bf16),
            shape((width, wqkv.shape[1]), bf16),
            shape((width, width), bf16),
            shape((shards, rows, 4 * HDIM), bf16),
            shape((rows, width), f32),
            shape((rows, width), bf16),
            shape((rows, width), bf16),
            shape((rows, width), bf16),
            shape((rows, HDIM), f32),
            shape((2, rows, HDIM), f32),
            shape((8, width), f32),
        ),
        in_specs=[smem, smem, vmem, vmem, vmem, vmem, any_space, any_space, any_space],
        out_specs=[any_space] * 6 + [vmem] * 7,
        scratch_shapes=[
            pltpu.VMEM((shards, 8, width), f32),
            pltpu.VMEM((width, wqkv.shape[1]), bf16),
            pltpu.VMEM((width, width), bf16),
            pltpu.VMEM((shards, rows, 4 * HDIM), bf16),
            pltpu.VMEM((rows, width), bf16),
            pltpu.VMEM((rows, shards * rows), f32),
            pltpu.SemaphoreType.DMA((8,)),
            sems(3),
            sems(4),
            sems(3),
            sems(4),
            sems(3),
            sems(3),
            sems(4),
            sems(4),
            sems(3),
            sems(count - 1),
            sems(count - 1),
            sems(1),
            sems(count - 1),
            sems(count - 1),
        ],
        compiler_params=pltpu.CompilerParams(
            collective_id=0, has_side_effects=True, vmem_limit_bytes=60 * 2**20
        ),
    )(lengths, starts, x, cot, vec, inverse, wqkv, wo, pieces)


class Stream:
    def __init__(self, links, pairs, size, own, land_end, land_mid, final, loads, stage, sems, local_sems, targets):
        self.links, self.pairs, self.size = links, pairs, size
        self.own, self.land_end, self.land_mid, self.final = own, land_end, land_mid, final
        self.loads, self.stage, self.sems, self.local_sems = loads, stage, sems, local_sems
        self.targets = targets
        self.near = links.line // 2
        self.far = 1 - self.near
        self.busy = {}

    def rows(self, kind, p):
        return pl.ds(pl.multiple_of((kind * self.pairs + p) * self.size, self.size), self.size)

    def copy(self, src, dst, p, index, device):
        return pltpu.make_async_remote_copy(
            src_ref=src,
            dst_ref=dst,
            send_sem=self.sems.at[0, p, index],
            recv_sem=self.sems.at[1, p, index],
            device_id=device,
            device_id_type=MESH,
        )

    def total(self, refs):
        copies = [
            pltpu.make_async_copy(ref, self.loads.at[i], self.local_sems.at[i]) for i, ref in enumerate(refs)
        ]
        for copy in copies:
            copy.start()
        for copy in copies:
            copy.wait()
        out = self.loads[0].astype(jnp.float32)
        for i in range(1, len(refs)):
            out = out + self.loads[i].astype(jnp.float32)
        return out.astype(jnp.bfloat16)

    def free(self, role, which, p):
        for copy in self.busy.pop((role, which, p % 2), list)():
            copy.wait_send()

    def hold(self, role, which, p, make):
        copies = make()
        for copy in copies:
            copy.start()
        self.busy[(role, which, p % 2)] = make

    def finals(self, p, which):
        links = self.links
        near, far = self.rows(self.near, p), self.rows(self.far, p)
        ref_near, ref_far = self.final(links.core, near), self.final(links.core, far)
        plans = (
            (ref_near, 3, links.away),
            (ref_near, 4, links.toward),
            (ref_far, 5, links.away),
            (ref_near, 6, links.partner),
            (ref_far, 7, links.partner),
        )
        return [
            self.copy(ref, ref, p, index, device)
            for i, (ref, index, device) in enumerate(plans)
            if i in which
        ]

    def end_send(self, p):
        for which, kind in ((0, self.far), (1, self.near)):
            self.free("end", which, p)
            self.stage[which, p % 2] = self.total(self.own(self.rows(kind, p)))
            self.hold(
                "end",
                which,
                p,
                lambda which=which: [
                    self.copy(
                        self.stage.at[which, p % 2], self.land_end.at[p, which], p, which, self.links.toward
                    )
                ],
            )

    def mid_pass(self, p):
        self.free("mid", 0, p)
        self.copy(self.land_end.at[p, 0], self.land_end.at[p, 0], p, 0, self.links.away).wait_recv()
        self.stage[0, p % 2] = self.total(self.own(self.rows(self.far, p)) + [self.land_end.at[p, 0]])
        self.hold(
            "mid",
            0,
            p,
            lambda: [self.copy(self.stage.at[0, p % 2], self.land_mid.at[p], p, 2, self.links.toward)],
        )

    def mid_sum(self, p):
        links = self.links
        self.free("mid", 1, p)
        self.copy(self.land_end.at[p, 1], self.land_end.at[p, 1], p, 1, links.away).wait_recv()
        self.copy(self.land_mid.at[p], self.land_mid.at[p], p, 2, links.toward).wait_recv()
        near = self.rows(self.near, p)
        self.stage[1, p % 2] = self.total(self.own(near) + [self.land_end.at[p, 1], self.land_mid.at[p]])
        self.own_copy(p).start()

        def sends():
            buf = self.stage.at[1, p % 2]
            near = self.rows(self.near, p)
            final = self.final(links.core, near)
            if self.targets:
                ref = self.target(links.core, near, links.here)
                return [
                    self.copy(buf.at[links.near[d]], ref, p, 7 + d, links.plane[d]) for d in (1, 2, 3)
                ]
            return [
                self.copy(buf, final, p, 3, links.away),
                self.copy(buf, final, p, 4, links.toward),
                self.copy(buf, final, p, 6, links.partner),
            ]

        self.hold("mid", 1, p, sends)

    def own_copy(self, p):
        links = self.links
        buf, near = self.stage.at[1, p % 2], self.rows(self.near, p)
        final = self.final(links.core, near)
        if self.targets:
            buf, final = buf.at[links.here], self.target(links.core, near, links.here)
        return pltpu.make_async_copy(buf, final, self.local_sems.at[6 + p % 2])

    def target(self, core, rows, source):
        return self.final(core, rows).at[source]

    def mid_out(self, p):
        links = self.links
        self.own_copy(p).wait()
        if not self.targets:
            return
        near = self.rows(self.near, p)
        for d in (1, 2, 3):
            ref = self.target(links.core, near, links.near[d])
            self.copy(ref, ref, p, 7 + d, links.plane[d]).wait_recv()
        for copy in self.finals(p, (0, 1, 3)):
            copy.start()

    def mid_far(self, p):
        far = self.final(self.links.core, self.rows(self.far, p))
        self.copy(far, far, p, 4, self.links.toward).wait_recv()
        for copy in self.finals(p, (2, 4)):
            copy.start()

    def end_take(self, p):
        for kind, index, out in ((self.near, 3, 3), (self.far, 5, 4)):
            ref = self.final(self.links.core, self.rows(kind, p))
            self.copy(ref, ref, p, index, self.links.toward).wait_recv()
            self.finals(p, (out,))[0].start()

    def close_mid(self):
        for key in [k for k in self.busy if k[0] == "mid"]:
            for copy in self.busy.pop(key)():
                copy.wait_send()
        for p in range(self.pairs):
            for copy in self.finals(p, (0, 1, 2, 3, 4) if self.targets else (2, 4)):
                copy.wait_send()

    def close_end(self):
        for key in [k for k in self.busy if k[0] == "end"]:
            for copy in self.busy.pop(key)():
                copy.wait_send()
        for p in range(self.pairs):
            for copy in self.finals(p, (3, 4)):
                copy.wait_send()

    def close_core(self):
        for p in range(self.pairs):
            for kind, index in ((self.near, 6), (self.far, 7)):
                ref = self.final(1 - self.links.core, self.rows(kind, p))
                self.copy(ref, ref, p, index, self.links.partner).wait_recv()


def epilogue_kernel(
    lengths_ref,
    starts_ref,
    query_ref,
    lse_ref,
    trig_ref,
    gains_ref,
    x_hbm,
    cot_hbm,
    mid_hbm,
    part_hbm,
    normed_hbm,
    attn_hbm,
    mlp_hbm,
    kv_hbm,
    wqkv_hbm,
    wo_hbm,
    down_part,
    gate_part,
    up_part,
    grad_input_ref,
    sums_ref,
    down_final,
    gate_final,
    up_final,
    attn_final,
    down_core,
    gate_core,
    up_core,
    attn_core,
    attn_own,
    mlp_land,
    down_end,
    down_mid,
    gate_end,
    gate_mid,
    up_end,
    up_mid,
    attn_end,
    attn_mid,
    kv_buf,
    key_turned,
    bias_ref,
    lse_turned,
    dmid_ref,
    branch_ref,
    dattn_ref,
    dqkv_ref,
    dkey_ref,
    dvalue_ref,
    kv_out,
    kv_land,
    normed_turned,
    attn_turned,
    half_buf,
    half_load,
    plane_first,
    plane_second,
    plane_send,
    vec_plane,
    vec_core,
    vec_line,
    vec_send,
    down_loads,
    down_stage,
    gu_loads,
    gate_stage,
    up_stage,
    attn_loads,
    attn_stage,
    local_sems,
    scope_sems,
    mlp_sems,
    load_sems,
    core_sems,
    kv_sems,
    half_sems,
    plane_sems,
    vec_sems,
    down_sems,
    gate_sems,
    up_sems,
    attn_sems,
):
    links = Links()
    here, core, line = links.here, links.core, links.line
    rows, width = x_hbm.shape
    scale = 1.0 / HDIM**0.5
    group = HEADS // KVH
    bf16, f32 = jnp.bfloat16, jnp.float32
    step = 2 - 4 * (line // 2)
    links.toward = {"rep": links.rep + step}
    links.away = {"rep": links.rep - step}
    is_end = (line == 0) | (line == 3)
    is_mid = (line == 1) | (line == 2)

    barrier = pltpu.get_barrier_semaphore()
    line_others = [{"rep": 2 * lax.rem(line + j, 4) + core} for j in (1, 2, 3)]
    others = links.plane[1:] + [links.partner] + line_others
    for other in others:
        pl.semaphore_signal(barrier, inc=1, device_id=other, device_id_type=MESH)
    pl.semaphore_wait(barrier, len(others))

    swaps = [
        remote(down_part.at[1 - core], down_core, core_sems, 0, links.partner),
        remote(gate_part.at[:, 1 - core], gate_core, core_sems, 1, links.partner),
        remote(up_part.at[:, 1 - core], up_core, core_sems, 2, links.partner),
    ]
    for swap in swaps:
        swap.start()
    fetches = [pltpu.make_async_copy(kv_hbm, kv_buf, local_sems.at[1])]
    mlp_sends = [
        remote(mlp_hbm.at[links.near[d]], mlp_land.at[d - 1], mlp_sems, d - 1, links.plane[d]) for d in (1, 2, 3)
    ]
    for copy in mlp_sends:
        copy.start()
    for fetch in fetches:
        fetch.start()

    def stream(size, total, own, end, mid, final, loads, stage, sems, targets=False):
        return Stream(
            links, total // (2 * size), size, own, end, mid, final, loads, stage, sems, load_sems, targets
        )

    down = stream(
        down_stage.shape[2],
        down_core.shape[0],
        lambda r: [down_part.at[core, r], down_core.at[r]],
        down_end,
        down_mid,
        lambda c, r: down_final.at[c, r],
        down_loads,
        down_stage,
        down_sems,
    )
    gate = stream(
        gate_stage.shape[3],
        gate_core.shape[1],
        lambda r: [gate_part.at[:, core, r], gate_core.at[:, r]],
        gate_end,
        gate_mid,
        lambda c, r: gate_final.at[c, :, r],
        gu_loads,
        gate_stage,
        gate_sems,
        True,
    )
    up = stream(
        up_stage.shape[3],
        up_core.shape[1],
        lambda r: [up_part.at[:, core, r], up_core.at[:, r]],
        up_end,
        up_mid,
        lambda c, r: up_final.at[c, :, r],
        gu_loads,
        up_stage,
        up_sems,
        True,
    )
    attn = stream(
        attn_stage.shape[2],
        attn_own.shape[0],
        lambda r: [attn_own.at[r]],
        attn_end,
        attn_mid,
        lambda c, r: attn_final.at[c, r],
        attn_loads,
        attn_stage,
        attn_sems,
    )
    pairs = [(s, p) for s in (down, gate, up, attn) for p in range(s.pairs)]

    def service(n):
        def at(back):
            return pairs[n - back] if 0 <= n - back < len(pairs) else None

        first = {0: down, down.pairs: gate, down.pairs + gate.pairs: up}
        if n in first:
            swaps[list(first).index(n)].wait_recv()

        @pl.when(is_end)
        def _():
            for back, action in ((7, "end_take"), (0, "end_send")):
                if at(back):
                    getattr(at(back)[0], action)(at(back)[1])

        @pl.when(is_mid)
        def _():
            for back, action in ((4, "mid_far"), (3, "mid_out"), (2, "mid_sum"), (1, "mid_pass")):
                if at(back):
                    getattr(at(back)[0], action)(at(back)[1])

    def scoped(refs, body):
        def inner(*bufs):
            copies = [pltpu.make_async_copy(r, b, scope_sems.at[i]) for i, (r, b) in enumerate(zip(refs, bufs))]
            for copy in copies:
                copy.start()
            for copy in copies:
                copy.wait()
            body(*bufs)

        pl.run_scoped(inner, *[pltpu.VMEM(r.shape, r.dtype) for r in refs])

    def norm_back():
        scoped((mid_hbm, part_hbm, cot_hbm), norm_body)

    def norm_body(mid_ref, part_ref, cot_ref):
        mid = mid_ref[...]
        inv = lax.rsqrt(jnp.mean(mid * mid, axis=1, keepdims=True) + epsilon)
        unit = mid * inv
        part = part_ref[...]
        vec_send[2:3, :] = jnp.sum(part * unit, axis=0, keepdims=True)
        scaled = part * gains_ref[2:3, :]
        d_mid = cot_ref[...].astype(f32) + inv * (
            scaled - unit * jnp.mean(scaled * unit, axis=1, keepdims=True)
        )
        dmid_ref[...] = d_mid
        branch_ref[...] = d_mid.astype(bf16)
        query_pos = here * rows + lax.broadcasted_iota(jnp.int32, (1, rows), 1)
        key_pos = lax.broadcasted_iota(jnp.int32, (4 * rows, 1), 0)
        query_doc, unused, query_piece = layout_of(query_pos, lengths_ref, starts_ref)
        key_doc, unused, key_piece = layout_of(key_pos, lengths_ref, starts_ref)
        allowed = (query_doc == key_doc) & (
            (key_pos <= query_pos) | ((query_piece == key_piece) & (query_piece > 0))
        )
        bias_ref[...] = jnp.where(allowed, 0.0, MASKED)
        lse_turned[...] = lse_ref[...].T

    def attn_back():
        scoped((wo_hbm,), attn_body)

    def attn_body(wo_buf):
        def tile(i, carry):
            columns = pl.ds(pl.multiple_of(i * 256, 256), 256)
            dattn_ref[:, columns] = dot_f32(branch_ref[...], wo_buf[columns, :], ((1,), (1,))).astype(bf16)
            return carry

        lax.fori_loop(0, width // 256, tile, 0)
        fetches[0].wait()
        for g in range(KVH):
            key_turned[g] = kv_buf[:, :, g * HDIM : (g + 1) * HDIM].reshape(4 * rows, HDIM).T
        dkey_ref[...] = jnp.zeros_like(dkey_ref)
        dvalue_ref[...] = jnp.zeros_like(dvalue_ref)

    def head_back(h, carry):
        columns = pl.ds(pl.multiple_of(h * HDIM, HDIM), HDIM)
        shared = h // group
        key = kv_buf[:, :, pl.ds(pl.multiple_of(shared * HDIM, HDIM), HDIM)].reshape(4 * rows, HDIM)
        value = kv_buf[:, :, pl.ds(pl.multiple_of((KVH + shared) * HDIM, HDIM), HDIM)].reshape(
            4 * rows, HDIM
        )
        query, d_out = query_ref[:, columns], dattn_ref[:, columns]
        scores = dot_f32(key, query, ((1,), (1,))) * scale + bias_ref[...]
        probs = jnp.exp(scores - lse_turned[pl.ds(h, 1), :])
        d_probs = dot_f32(value, d_out, ((1,), (1,)))
        delta = jnp.sum(probs * d_probs, axis=0, keepdims=True)
        d_scores = (probs * (d_probs - delta)).astype(bf16)
        dkey_ref[shared] += dot_f32(d_scores, query)
        dvalue_ref[shared] += dot_f32(probs.astype(bf16), d_out)
        d_query = dot_f32(key_turned[shared], d_scores).T * scale
        d_query = d_query * trig_ref[0] - pltpu.roll(d_query, HDIM // 2, 1) * trig_ref[1]
        dqkv_ref[:, columns] = d_query.astype(bf16)
        return carry

    kv_sends = [
        remote(kv_out.at[links.near[d]], kv_land.at[d - 1], kv_sems, d - 1, links.plane[d]) for d in (1, 2, 3)
    ]

    def kv_send():
        for g in range(KVH):
            kv_out[:, :, g * HDIM : (g + 1) * HDIM] = (
                (dkey_ref[g] * scale).astype(bf16).reshape(4, rows, HDIM)
            )
            kv_out[:, :, (KVH + g) * HDIM : (KVH + g + 1) * HDIM] = (
                dvalue_ref[g].astype(bf16).reshape(4, rows, HDIM)
            )
        for copy in kv_sends:
            copy.start()

    vec_copies = {
        "plane": [remote(vec_send, vec_plane.at[here], vec_sems, d - 1, links.plane[d]) for d in (1, 2, 3)],
        "core": [remote(vec_core.at[core], vec_core.at[core], vec_sems, 3, links.partner)],
        "line": [
            remote(vec_line.at[line], vec_line.at[line], vec_sems, 4 + j, line_others[j]) for j in range(3)
        ],
    }
    vec_comes = {
        "plane": [
            remote(vec_send, vec_plane.at[links.near[d]], vec_sems, d - 1, links.plane[d]) for d in (1, 2, 3)
        ],
        "core": [remote(vec_core.at[core], vec_core.at[1 - core], vec_sems, 3, links.partner)],
        "line": [
            remote(
                vec_line.at[line],
                vec_line.at[lax.rem(line + 3 - j, 4)],
                vec_sems,
                4 + j,
                line_others[2 - j],
            )
            for j in range(3)
        ],
    }

    def input_back():
        for d in (1, 2, 3):
            remote(kv_land.at[d - 1], kv_land.at[d - 1], kv_sems, d - 1, links.plane[d]).wait_recv()
        kv = kv_out[here].astype(f32)
        for d in range(3):
            kv = kv + kv_land[d].astype(f32)
        for g in range(KVH):
            d_key = kv[:, g * HDIM : (g + 1) * HDIM]
            d_key = d_key * trig_ref[0] - pltpu.roll(d_key, HDIM // 2, 1) * trig_ref[1]
            dqkv_ref[:, width + g * HDIM : width + (g + 1) * HDIM] = d_key.astype(bf16)
        dqkv_ref[:, width + KVH * HDIM :] = kv[:, KVH * HDIM :].astype(bf16)
        scoped((wqkv_hbm, x_hbm), input_body)
        scoped((normed_hbm, attn_hbm), turn_body)

    def turn_body(normed_ref, attn_ref):
        normed_turned[...] = normed_ref[...].T
        attn_turned[...] = attn_ref[...].T

    def input_body(wqkv_buf, x_ref):
        def tile(i, carry):
            columns = pl.ds(pl.multiple_of(i * 256, 256), 256)
            grad_input_ref[:, columns] = dot_f32(dqkv_ref[...], wqkv_buf[columns, :], ((1,), (1,)))
            return carry

        lax.fori_loop(0, width // 256, tile, 0)
        x = x_ref[...].astype(f32)
        inv = lax.rsqrt(jnp.mean(x * x, axis=1, keepdims=True) + epsilon)
        unit = x * inv
        part = grad_input_ref[...]
        vec_send[1:2, :] = jnp.sum(part * unit, axis=0, keepdims=True)
        scaled = part * gains_ref[1:2, :]
        grad_input_ref[...] = dmid_ref[...] + inv * (
            scaled - unit * jnp.mean(scaled * unit, axis=1, keepdims=True)
        )
        sums = jnp.sum(dqkv_ref[...].astype(f32), axis=0, keepdims=True)
        vec_send[0:1, :] = sums[:, :width]
        vec_send[3:4, 0 : 2 * KVH * HDIM] = sums[:, width:]
        vec_send[3:4, 2 * KVH * HDIM :] = jnp.zeros((1, width - 2 * KVH * HDIM), f32)
        vec_send[4:8, :] = jnp.zeros((4, width), f32)
        vec_plane[here] = vec_send[...]
        for copy in vec_copies["plane"]:
            copy.start()

    shard = width // 4
    half = shard // 2
    qkv_width = wqkv_hbm.shape[1]

    def half_grad(t, which):
        at = pl.ds(pl.multiple_of(t * shard + which * half, half), half)
        return (
            dot_f32(normed_turned[at, :], dqkv_ref[...]).astype(bf16),
            dot_f32(attn_turned[at, :], branch_ref[...]).astype(bf16),
        )

    half_sends = [remote(half_buf.at[t], attn_core.at[t], half_sems, t, links.partner) for t in range(4)]

    def other_half():
        def one(t, carry):
            left, right = half_grad(t, 1 - core)
            half_buf[t, :, :qkv_width] = left
            half_buf[t, :, qkv_width:] = right
            return carry

        lax.fori_loop(0, 4, one, 0)
        for copy in half_sends:
            copy.start()
        for copy in vec_comes["plane"]:
            copy.wait_recv()
        vec_core[core] = vec_plane[0] + vec_plane[1] + vec_plane[2] + vec_plane[3]
        vec_copies["core"][0].start()

    quarter = half // 2
    near_x, near_y, far = links.near[1:]

    def own_half():
        for copy in half_sends:
            copy.wait_send()
        for t in range(4):
            remote(attn_core.at[t], attn_core.at[t], half_sems, t, links.partner).wait_recv()
            load = pltpu.make_async_copy(attn_core.at[t], half_load, local_sems.at[3])
            load.start()
            left, right = half_grad(t, core)
            load.wait()
            half_buf[t, :, :qkv_width] = (left.astype(f32) + half_load[:, :qkv_width].astype(f32)).astype(bf16)
            half_buf[t, :, qkv_width:] = (right.astype(f32) + half_load[:, qkv_width:].astype(f32)).astype(bf16)
        for copy in first_sends:
            copy.start()
        vec_comes["core"][0].wait_recv()
        vec_line[line] = vec_core[0] + vec_core[1]
        for copy in vec_copies["line"]:
            copy.start()

    low_rows, high_rows = pl.ds(0, quarter), pl.ds(quarter, quarter)
    first_sends = [
        remote(half_buf.at[near_y, low_rows], plane_first.at[0], plane_sems, 0, links.plane[2]),
        remote(half_buf.at[far, low_rows], plane_first.at[1], plane_sems, 1, links.plane[2]),
        remote(half_buf.at[near_x, high_rows], plane_first.at[2], plane_sems, 2, links.plane[1]),
        remote(half_buf.at[far, high_rows], plane_first.at[3], plane_sems, 3, links.plane[1]),
    ]
    second_sends = [
        remote(plane_send.at[0], plane_second.at[0], plane_sems, 4, links.plane[1]),
        remote(plane_send.at[1], plane_second.at[1], plane_sems, 5, links.plane[2]),
    ]

    def plane_turn():
        for copy in first_sends:
            copy.wait_recv()
        plane_send[0] = (half_buf[near_x, 0:quarter].astype(f32) + plane_first[1].astype(f32)).astype(bf16)
        plane_send[1] = (
            half_buf[near_y, quarter : 2 * quarter].astype(f32) + plane_first[3].astype(f32)
        ).astype(bf16)
        for copy in second_sends:
            copy.start()

    def plane_end():
        for copy in second_sends + first_sends:
            copy.wait_send()
        for copy in second_sends:
            copy.wait_recv()
        for i in range(2):
            at = slice(i * quarter, (i + 1) * quarter)
            half_load[at, :] = (
                half_buf[here, at].astype(f32)
                + plane_first[2 * i].astype(f32)
                + plane_second[i].astype(f32)
            ).astype(bf16)
        store = pltpu.make_async_copy(half_load, attn_own, local_sems.at[3])
        store.start()
        for copy in vec_comes["line"]:
            copy.wait_recv()
        sums_ref[...] = vec_line[0] + vec_line[1] + vec_line[2] + vec_line[3]
        store.wait()

    def heads(lo, hi):
        return lambda: lax.fori_loop(lo, hi, head_back, 0)

    chain = [
        norm_back,
        attn_back,
        heads(0, 2),
        heads(2, 4),
        heads(4, 6),
        heads(6, 8),
        heads(8, 10),
        heads(10, 12),
        kv_send,
        input_back,
        other_half,
        own_half,
        None,
        plane_turn,
        None,
        plane_end,
    ]
    for n in range(len(pairs) + 8):
        service(n)
        if n < len(chain) and chain[n] is not None:
            chain[n]()

    for swap in swaps + kv_sends + mlp_sends:
        swap.wait_send()
    for copy in mlp_sends:
        copy.wait_recv()
    for name in vec_copies:
        for copy in vec_copies[name]:
            copy.wait_send()
    streams = (down, gate, up, attn)

    @pl.when(is_end)
    def _():
        for s in streams:
            s.close_end()

    @pl.when(is_mid)
    def _():
        for s in streams:
            s.close_mid()

    for s in streams:
        s.close_core()


def epilogue(
    lengths, starts, query, lse, trig, gains, x, cot, mid, part, normed, attn, mlp, kv, wqkv, wo, downs, gates, ups
):
    rows, width = x.shape
    bf16, f32 = jnp.bfloat16, jnp.float32
    any_space = pl.BlockSpec(memory_space=pl.ANY)
    vmem = pl.BlockSpec(memory_space=pltpu.VMEM)
    smem = pl.BlockSpec(memory_space=pltpu.SMEM)
    shape = jax.ShapeDtypeStruct
    wide = wqkv.shape[1] + width
    half = width // 8
    down_half = downs.shape[1]
    cols = gates.shape[3]
    down_size, gu_size, attn_size = 80, 16, 32
    down_pairs = down_half // (2 * down_size)
    gu_pairs = half // (2 * gu_size)
    attn_pairs = half // (2 * attn_size)
    down_chunk = (down_size, width)
    gu_chunk = (4, gu_size, cols)
    attn_chunk = (attn_size, wide)

    def line_buffers(pairs, chunk):
        return [shape((pairs, 2) + chunk, bf16), shape((pairs,) + chunk, bf16)]

    def sems(*n):
        return pltpu.SemaphoreType.DMA((2,) + n)

    outs = [
        shape((rows, width), f32),
        shape((8, width), f32),
        shape((2, down_half, width), bf16),
        shape((2, 4, half, cols), bf16),
        shape((2, 4, half, cols), bf16),
        shape((2, half, wide), bf16),
        shape((down_half, width), bf16),
        shape((4, half, cols), bf16),
        shape((4, half, cols), bf16),
        shape((4, half, wide), bf16),
        shape((half, wide), bf16),
        shape((3, rows, width), bf16),
    ]
    outs += line_buffers(down_pairs, down_chunk)
    outs += line_buffers(gu_pairs, gu_chunk) + line_buffers(gu_pairs, gu_chunk)
    outs += line_buffers(attn_pairs, attn_chunk)
    return pl.pallas_call(
        epilogue_kernel,
        name="epilogue",
        out_shape=tuple(outs),
        in_specs=[smem] * 2 + [vmem] * 4 + [any_space] * 13,
        out_specs=[vmem] * 2 + [any_space] * (len(outs) - 2),
        scratch_shapes=[
            pltpu.VMEM((4, rows, 4 * HDIM), bf16),
            pltpu.VMEM((KVH, HDIM, 4 * rows), bf16),
            pltpu.VMEM((4 * rows, rows), f32),
            pltpu.VMEM((HDIM, rows), f32),
            pltpu.VMEM((rows, width), f32),
            pltpu.VMEM((rows, width), bf16),
            pltpu.VMEM((rows, width), bf16),
            pltpu.VMEM((rows, wqkv.shape[1]), bf16),
            pltpu.VMEM((KVH, 4 * rows, HDIM), f32),
            pltpu.VMEM((KVH, 4 * rows, HDIM), f32),
            pltpu.VMEM((4, rows, 4 * HDIM), bf16),
            pltpu.VMEM((3, rows, 4 * HDIM), bf16),
            pltpu.VMEM((width, rows), bf16),
            pltpu.VMEM((width, rows), bf16),
            pltpu.VMEM((4, half, wide), bf16),
            pltpu.VMEM((half, wide), bf16),
            pltpu.VMEM((4, half // 2, wide), bf16),
            pltpu.VMEM((2, half // 2, wide), bf16),
            pltpu.VMEM((2, half // 2, wide), bf16),
            pltpu.VMEM((4, 8, width), f32),
            pltpu.VMEM((2, 8, width), f32),
            pltpu.VMEM((4, 8, width), f32),
            pltpu.VMEM((8, width), f32),
            pltpu.VMEM((4,) + down_chunk, bf16),
            pltpu.VMEM((2, 2) + down_chunk, bf16),
            pltpu.VMEM((4,) + gu_chunk, bf16),
            pltpu.VMEM((2, 2) + gu_chunk, bf16),
            pltpu.VMEM((2, 2) + gu_chunk, bf16),
            pltpu.VMEM((4,) + attn_chunk, bf16),
            pltpu.VMEM((2, 2) + attn_chunk, bf16),
            pltpu.SemaphoreType.DMA((4,)),
            pltpu.SemaphoreType.DMA((4,)),
            sems(3),
            pltpu.SemaphoreType.DMA((8,)),
            sems(3),
            sems(3),
            sems(4),
            sems(6),
            sems(7),
            sems(down_pairs, 11),
            sems(gu_pairs, 11),
            sems(gu_pairs, 11),
            sems(attn_pairs, 11),
        ],
        compiler_params=pltpu.CompilerParams(
            collective_id=1, has_side_effects=True, vmem_limit_bytes=63 * 2**20
        ),
    )(lengths, starts, query, lse, trig, gains, x, cot, mid, part, normed, attn, mlp, kv, wqkv, wo, downs, gates, ups)


def local(
    hidden_in,
    out_grad,
    doc_lengths,
    piece_starts,
    w_query,
    b_query,
    w_key,
    b_key,
    w_value,
    b_value,
    w_output,
    gain_attn,
    w_gate,
    w_up,
    w_down,
    gain_mlp,
):
    tok_rows = hidden_in.shape[0]
    model_width = hidden_in.shape[1]
    shard_count = lax.axis_size("fsdp")
    row_len = tok_rows * shard_count
    group_size = HEADS // KVH
    kv_width = KVH * HDIM
    ff_width = w_gate.shape[1]
    score_scale = 1.0 / HDIM**0.5
    local_pos = lax.axis_index("fsdp") * tok_rows + jnp.arange(tok_rows, dtype=jnp.int32)
    row_pos = jnp.arange(row_len, dtype=jnp.int32)
    lengths = doc_lengths[0]
    starts = piece_starts[0]
    query_doc, query_rel, query_piece = row_layout(local_pos, lengths, starts, PIECE)
    key_doc, unused_rel, key_piece = row_layout(row_pos, lengths, starts, PIECE)
    allowed = visible_pairs(query_doc, local_pos, query_piece, key_doc, row_pos, key_piece)
    cosine, sine = rope_tables(query_rel, HDIM)
    here = lax.axis_index("fsdp")
    core = lax.axis_index("rep") % 2
    line = lax.axis_size("rep") // 2
    low = jnp.bfloat16

    def gather_rows(weight):
        half = weight.shape[0] // 2
        mine = lax.dynamic_slice_in_dim(weight, core * half, half, 0)
        mine = jnp.stack([jnp.concatenate(p, axis=0) for p in gather_relative(mine, "fsdp")])
        both = core_halves(mine, core_swap(mine), core)
        rows = place([both[:, d] for d in range(shard_count)], here)
        return rows.reshape(2 * half * shard_count, weight.shape[1])

    qkv_full = gather_rows(jnp.concatenate([w_query, w_key, w_value], axis=1))
    query_full = qkv_full[:, :model_width]
    key_full = qkv_full[:, model_width : model_width + kv_width]
    value_full = qkv_full[:, model_width + kv_width :]
    output_full = gather_rows(w_output)
    vectors = lax.all_gather(
        jnp.concatenate([b_query, b_key, b_value, gain_attn, gain_mlp]), "fsdp", axis=0
    )
    cuts = [0]
    for vector in (b_query, b_key, b_value, gain_attn, gain_mlp):
        cuts.append(cuts[-1] + vector.shape[0])
    query_bias, key_bias, value_bias, attn_gain, mlp_gain = (
        vectors[:, cuts[i] : cuts[i + 1]].reshape(-1) for i in range(5)
    )

    part = ff_width // shard_count

    def exchange_columns(weight):
        half = weight.shape[0] // 2
        mine = lax.dynamic_slice_in_dim(weight, core * half, half, 0)
        got = []
        for d in range(shard_count):
            piece = lax.dynamic_slice_in_dim(mine, (here ^ d) * part, part, 1)
            got.append(piece if d == 0 else lax.ppermute(piece, "fsdp", xor_pairs(shard_count, d)))
        got = jnp.stack(got)
        both = core_halves(got, core_swap(got), core)
        rows = place([both[:, d] for d in range(shard_count)], here)
        return rows.reshape(2 * half * shard_count, part)

    gate_part = exchange_columns(w_gate)
    up_part = exchange_columns(w_up)
    cot_all = jnp.concatenate([h for p in gather_relative(out_grad, "fsdp") for h in p], axis=0)
    x_float = hidden_in.astype(jnp.float32)
    inv_first = lax.rsqrt(jnp.mean(x_float * x_float, axis=1, keepdims=True) + epsilon)
    unit_first = x_float * inv_first
    gain_first = attn_gain.astype(jnp.float32)
    normed_first = (unit_first * gain_first).astype(jnp.bfloat16)
    query_pre = mat_dot(normed_first, query_full) + query_bias.astype(jnp.float32)
    key_pre = mat_dot(normed_first, key_full) + key_bias.astype(jnp.float32)
    value_pre = mat_dot(normed_first, value_full) + value_bias.astype(jnp.float32)
    query_rot = rotate(query_pre.reshape(tok_rows, HEADS, HDIM), cosine, sine).astype(jnp.bfloat16)
    key_rot = (
        rotate(key_pre.reshape(tok_rows, KVH, HDIM), cosine, sine)
        .astype(jnp.bfloat16)
        .reshape(tok_rows, kv_width)
    )
    value_low = value_pre.astype(jnp.bfloat16)
    keys_row, values_row = (
        lax.all_gather(key_rot, "fsdp", axis=0, tiled=True),
        lax.all_gather(value_low, "fsdp", axis=0, tiled=True),
    )
    query_grouped = query_rot.reshape(tok_rows, KVH, group_size, HDIM)
    keys_grouped = keys_row.reshape(row_len, KVH, HDIM)
    values_grouped = values_row.reshape(row_len, KVH, HDIM)

    def masked_scores():
        raw_scores = (
            jnp.einsum(
                "tgjd,rgd->gjtr", query_grouped, keys_grouped, preferred_element_type=jnp.float32
            )
            * score_scale
        )
        return jnp.where(allowed[None, None], raw_scores, -1e30)

    scores = masked_scores()
    row_peak = jnp.max(scores, axis=3, keepdims=True)
    expo_vals = jnp.exp(scores - row_peak)
    row_total = jnp.sum(expo_vals, axis=3, keepdims=True)
    soft_probs = expo_vals / row_total
    log_total = row_peak + jnp.log(row_total)
    attn_heads = jnp.einsum(
        "gjtr,rgd->tgjd",
        soft_probs.astype(jnp.bfloat16),
        values_grouped,
        preferred_element_type=jnp.float32,
    )
    attn_low = attn_heads.reshape(tok_rows, model_width).astype(jnp.bfloat16)
    mid_state = x_float + mat_dot(attn_low, output_full)
    inv_second = lax.rsqrt(jnp.mean(mid_state * mid_state, axis=1, keepdims=True) + epsilon)
    unit_second = mid_state * inv_second
    gain_second = mlp_gain.astype(jnp.float32)
    normed_second = (unit_second * gain_second).astype(jnp.bfloat16)
    cot_float = out_grad.astype(jnp.float32)
    normed_all = jnp.concatenate([h for p in gather_relative(normed_second, "fsdp") for h in p], axis=0)
    gate_val = mat_dot(normed_all, gate_part)
    up_val = mat_dot(normed_all, up_part)
    sig_gate = jax.nn.sigmoid(gate_val)
    silu_gate = gate_val * sig_gate
    act_low = (silu_gate * up_val).astype(low)
    d_act = dot_right_t(cot_all, w_down)
    d_gate = (d_act * up_val * sig_gate * (1.0 + gate_val * (1.0 - sig_gate))).astype(low)
    d_up = (d_act * silu_gate).astype(low)
    mlp_part = mat_dot(act_low, w_down).reshape(shard_count, tok_rows, model_width)
    mlp_out = scatter_relative([mlp_part[d] for d in range(shard_count)], "fsdp")
    norm_part = (dot_right_t(d_gate, gate_part) + dot_right_t(d_up, up_part)).reshape(
        shard_count, tok_rows, model_width
    )
    partial_value = scatter_relative([norm_part[d] for d in range(shard_count)], "fsdp")

    def keep_half(grad):
        mine = lax.dynamic_index_in_dim(grad, core, 1, keepdims=False)
        other = lax.dynamic_index_in_dim(grad, 1 - core, 1, keepdims=False)
        return (mine.astype(jnp.float32) + core_swap(other).astype(jnp.float32)).astype(low)

    def both_cores(half):
        return core_halves(half, core_swap(half), core)

    down_grad = dot_left_t(act_low, cot_all).astype(low)
    half = part // 2
    down_half = keep_half(down_grad.reshape(1, 2, half, model_width))[0]
    wide = model_width // line
    down_parts = jnp.stack([down_half[:, q * wide : (q + 1) * wide] for q in range(line)])
    down_own = line_scatter(down_parts).astype(low)
    down_rows = line_gather(down_own)
    down_rows = jnp.concatenate([down_rows[q] for q in range(line)], axis=1)
    down_sums = both_cores(down_rows).reshape(part, model_width).astype(jnp.float32)

    rows = model_width // shard_count
    thin = rows // 2 // line

    def column_grad(d_value):
        grad = dot_left_t(normed_all, d_value).astype(low)
        kept = keep_half(grad.reshape(shard_count, 2, rows // 2, part))
        kept = kept.reshape(shard_count, line, thin, part).transpose(1, 0, 2, 3)
        own = line_scatter(kept).astype(low)
        got = []
        for d in range(shard_count):
            piece = pick(own, here ^ d)
            got.append(piece if d == 0 else lax.ppermute(piece, "fsdp", xor_pairs(shard_count, d)))
        got = place(got, here).transpose(1, 0, 2).reshape(thin, ff_width)
        full = line_gather(got).reshape(rows // 2, ff_width)
        return both_cores(full).reshape(rows, ff_width).astype(jnp.float32)

    grad_gate = column_grad(d_gate)
    grad_up = column_grad(d_up)
    output = mid_state + mlp_out
    d_gain_second = jnp.sum(partial_value * unit_second, axis=0)
    scaled_second = partial_value * gain_second
    d_mid = cot_float + inv_second * (
        scaled_second - unit_second * jnp.mean(scaled_second * unit_second, axis=1, keepdims=True)
    )
    d_branch_low = d_mid.astype(jnp.bfloat16)
    d_attn_low = dot_right_t(d_branch_low, output_full).astype(jnp.bfloat16)
    d_attn_grouped = d_attn_low.reshape(tok_rows, KVH, group_size, HDIM)
    scores = masked_scores()
    soft_back = jnp.exp(scores - log_total)
    probs_low = soft_back.astype(jnp.bfloat16)
    prob_grad = jnp.einsum(
        "tgjd,rgd->gjtr", d_attn_grouped, values_grouped, preferred_element_type=jnp.float32
    )
    row_delta = jnp.sum(soft_back * prob_grad, axis=3, keepdims=True)
    score_grad = (soft_back * (prob_grad - row_delta)).astype(jnp.bfloat16)
    dquery_rot = (
        jnp.einsum("gjtr,rgd->tgjd", score_grad, keys_grouped, preferred_element_type=jnp.float32)
        * score_scale
    )
    dquery_low = (
        unrotate(dquery_rot.reshape(tok_rows, HEADS, HDIM), cosine, sine)
        .reshape(tok_rows, model_width)
        .astype(jnp.bfloat16)
    )
    key_grad = (
        jnp.einsum("gjtr,tgjd->rgd", score_grad, query_grouped, preferred_element_type=jnp.float32)
        * score_scale
    )
    value_grad = jnp.einsum(
        "gjtr,tgjd->rgd", probs_low, d_attn_grouped, preferred_element_type=jnp.float32
    )
    kv_sums = lax.psum_scatter(
        jnp.concatenate(
            [
                key_grad.reshape(lax.axis_size("fsdp") * tok_rows, kv_width),
                value_grad.reshape(lax.axis_size("fsdp") * tok_rows, kv_width),
            ],
            axis=1,
        ).astype(jnp.bfloat16),
        "fsdp",
        scatter_dimension=0,
        tiled=True,
    ).astype(jnp.float32)
    dkey_low = (
        unrotate(kv_sums[:, :kv_width].reshape(tok_rows, KVH, HDIM), cosine, sine)
        .reshape(tok_rows, kv_width)
        .astype(jnp.bfloat16)
    )
    dvalue_low = kv_sums[:, kv_width:].astype(jnp.bfloat16)
    d_norm_first = (
        dot_right_t(dquery_low, query_full)
        + dot_right_t(dkey_low, key_full)
        + dot_right_t(dvalue_low, value_full)
    )
    attn_grads = jnp.concatenate(
        [
            dot_left_t(normed_first, dquery_low).astype(low),
            dot_left_t(normed_first, dkey_low).astype(low),
            dot_left_t(normed_first, dvalue_low).astype(low),
            dot_left_t(attn_low, d_branch_low).astype(low),
        ],
        axis=1,
    )
    attn_wide = attn_grads.shape[1]
    attn_kept = keep_half(attn_grads.reshape(shard_count, 2, rows // 2, attn_wide))
    attn_own = scatter_relative([pick(attn_kept, here ^ d) for d in range(shard_count)], "fsdp").astype(low)
    attn_own = line_scatter(attn_own.reshape(line, thin, attn_wide)).astype(low)
    attn_rows = line_gather(attn_own).reshape(rows // 2, attn_wide)
    attn_sums = both_cores(attn_rows).reshape(rows, attn_wide).astype(jnp.float32)
    d_gain_first = jnp.sum(d_norm_first * unit_first, axis=0)
    scaled_first = d_norm_first * gain_first
    grad_input = d_mid + inv_first * (
        scaled_first - unit_first * jnp.mean(scaled_first * unit_first, axis=1, keepdims=True)
    )
    bias_query = jnp.sum(dquery_low.astype(jnp.float32), axis=0)
    bias_key = jnp.sum(dkey_low.astype(jnp.float32), axis=0)
    bias_value = jnp.sum(dvalue_low.astype(jnp.float32), axis=0)
    small = (bias_query, bias_key, bias_value, d_gain_first, d_gain_second)
    summed = lax.psum(jnp.concatenate(small), ("rep", "fsdp"))
    outs = []
    at = 0
    for vector in small:
        size = vector.shape[0] // shard_count
        outs.append(lax.dynamic_slice_in_dim(summed, at + here * size, size, 0))
        at += vector.shape[0]
    bias_query, bias_key, bias_value, gain_first_sum, gain_second_sum = outs
    grad_query = attn_sums[:, :model_width]
    grad_key = attn_sums[:, model_width : model_width + kv_width]
    grad_value = attn_sums[:, model_width + kv_width : model_width + 2 * kv_width]
    grad_output = attn_sums[:, model_width + 2 * kv_width :]
    return (
        output,
        grad_input,
        grad_query,
        bias_query,
        grad_key,
        bias_key,
        grad_value,
        bias_value,
        grad_output,
        gain_first_sum,
        grad_gate,
        grad_up,
        down_sums,
        gain_second_sum,
    )


def local_fast(
    hidden_in,
    out_grad,
    doc_lengths,
    piece_starts,
    w_query,
    b_query,
    w_key,
    b_key,
    w_value,
    b_value,
    w_output,
    gain_attn,
    w_gate,
    w_up,
    w_down,
    gain_mlp,
):
    tok_rows = hidden_in.shape[0]
    model_width = hidden_in.shape[1]
    shard_count = lax.axis_size("fsdp")
    row_len = tok_rows * shard_count
    group_size = HEADS // KVH
    kv_width = KVH * HDIM
    ff_width = w_gate.shape[1]
    score_scale = 1.0 / HDIM**0.5
    row_pos = jnp.arange(row_len, dtype=jnp.int32)
    lengths = doc_lengths[0]
    starts = piece_starts[0]
    here = lax.axis_index("fsdp")
    core = lax.axis_index("rep") % 2
    line = lax.axis_size("rep") // 2
    line_pos = lax.axis_index("rep") // 2
    low = jnp.bfloat16
    part = ff_width // shard_count
    shard_rows = model_width // shard_count
    thin = shard_rows // 2 // line
    halves = jnp.arange(0, HDIM, 2).astype(jnp.float32) / HDIM
    inverse = rope_base ** (-halves)
    inverse = jnp.broadcast_to(jnp.concatenate([inverse, inverse])[None], (8, HDIM))

    def spread(vector, first, size):
        zeros = jnp.zeros((1, size), jnp.float32)
        return lax.dynamic_update_slice(
            zeros, vector.astype(jnp.float32)[None], (0, first + here * vector.shape[0])
        )

    kv_bias = spread(b_key, 0, model_width) + spread(b_value, kv_width, model_width)
    vec = jnp.concatenate(
        [
            spread(b_query, 0, model_width),
            spread(gain_attn, 0, model_width),
            spread(gain_mlp, 0, model_width),
            kv_bias,
            jnp.zeros((4, model_width), jnp.float32),
        ]
    )
    first_row = core * (shard_rows // 2) + line_pos * thin

    def cut(weight):
        piece = lax.dynamic_slice_in_dim(weight, first_row, thin, 0)
        return jnp.stack([piece[:, t * part : (t + 1) * part] for t in range(shard_count)])

    pieces = jnp.stack([cut(w_gate), cut(w_up)], axis=1)
    (
        normed_all,
        cot_all,
        wgu,
        wqkv_full,
        output_full,
        kv_full,
        mid_state,
        normed_first,
        query_rot,
        attn_low,
        lse,
        trig,
        gains,
    ) = prologue(
        doc_lengths,
        piece_starts,
        hidden_in,
        out_grad,
        vec,
        inverse,
        jnp.concatenate([w_query, w_key, w_value], axis=1),
        w_output,
        pieces,
    )
    def whole(which, weight):
        mine = lax.dynamic_slice_in_dim(weight, here * part, part, 1)
        other = wgu[:, :, :, which].transpose(2, 0, 1, 3, 4).reshape(
            shard_count - 1, shard_rows, part
        )
        rows = place([mine] + [other[d] for d in range(shard_count - 1)], here)
        return rows.reshape(model_width, part)

    gate_part = whole(0, w_gate)
    up_part = whole(1, w_up)
    cot_all = cot_all.reshape(row_len, model_width)
    normed_all = normed_all.reshape(row_len, model_width)
    gate_val = mat_dot(normed_all, gate_part)
    up_val = mat_dot(normed_all, up_part)
    sig_gate = jax.nn.sigmoid(gate_val)
    silu_gate = gate_val * sig_gate
    act_low = (silu_gate * up_val).astype(low)
    d_act = dot_right_t(cot_all, w_down)
    d_gate = (d_act * up_val * sig_gate * (1.0 + gate_val * (1.0 - sig_gate))).astype(low)
    d_up = (d_act * silu_gate).astype(low)
    norm_part = (dot_right_t(d_gate, gate_part) + dot_right_t(d_up, up_part)).astype(low)
    norm_part, act_low, d_gate, d_up = lax.optimization_barrier((norm_part, act_low, d_gate, d_up))
    norm_part = norm_part.reshape(shard_count, tok_rows, model_width)
    partial_value = scatter_relative([pick(norm_part, here ^ d) for d in range(shard_count)], "fsdp")
    down_part = dot_left_t(act_low, cot_all).astype(low).reshape(2, part // 2, model_width)
    gate_grads = [
        dot_left_t(normed_all, d_value).astype(low).reshape(shard_count, 2, shard_rows // 2, part)
        for d_value in (d_gate, d_up)
    ]
    mlp_part = mat_dot(act_low, w_down).astype(low).reshape(shard_count, tok_rows, model_width)
    results = epilogue(
        doc_lengths,
        piece_starts,
        query_rot,
        lse,
        trig,
        gains,
        hidden_in,
        out_grad,
        mid_state,
        partial_value,
        normed_first,
        attn_low,
        mlp_part,
        kv_full,
        wqkv_full,
        output_full,
        down_part,
        gate_grads[0],
        gate_grads[1],
    )
    grad_input, sums, down_final, gate_final, up_final, attn_final = results[:6]
    mlp_land = results[11]
    output = mid_state + pick(mlp_part, here).astype(jnp.float32)
    for d in range(shard_count - 1):
        output = output + mlp_land[d].astype(jnp.float32)
    down_sums = down_final.reshape(part, model_width).astype(jnp.float32)
    grad_gate, grad_up = (
        final.transpose(0, 2, 1, 3).reshape(shard_rows, ff_width).astype(jnp.float32)
        for final in (gate_final, up_final)
    )
    attn_sums = attn_final.reshape(shard_rows, -1).astype(jnp.float32)
    ends = [0, model_width, model_width + kv_width, model_width + 2 * kv_width, 2 * (model_width + kv_width)]
    grad_query, grad_key, grad_value, grad_output = (attn_sums[:, ends[i] : ends[i + 1]] for i in range(4))

    def shard_of(row, first, size):
        return lax.dynamic_slice(sums, (row, first + here * (size // shard_count)), (1, size // shard_count))[0]

    return (
        output,
        grad_input,
        grad_query,
        shard_of(0, 0, model_width),
        grad_key,
        shard_of(3, 0, kv_width),
        grad_value,
        shard_of(3, kv_width, kv_width),
        grad_output,
        shard_of(1, 0, model_width),
        grad_gate,
        grad_up,
        down_sums,
        shard_of(2, 0, model_width),
    )


def solution(mesh):
    body = local_fast if mesh.shape["fsdp"] == 4 and mesh.shape["rep"] == 8 else local
    placed = (
        P(("rep", "fsdp"), None),
        P(("rep", "fsdp"), None),
        P("rep", None),
        P("rep", None),
        P("fsdp", None),
        P("fsdp"),
        P("fsdp", None),
        P("fsdp"),
        P("fsdp", None),
        P("fsdp"),
        P("fsdp", None),
        P("fsdp"),
        P("fsdp", None),
        P("fsdp", None),
        P("fsdp", None),
        P("fsdp"),
    )
    return jax.shard_map(
        body,
        mesh=mesh,
        in_specs=placed,
        out_specs=(
            P(("rep", "fsdp"), None),
            P(("rep", "fsdp"), None),
            P("fsdp", None),
            P("fsdp"),
            P("fsdp", None),
            P("fsdp"),
            P("fsdp", None),
            P("fsdp"),
            P("fsdp", None),
            P("fsdp"),
            P("fsdp", None),
            P("fsdp", None),
            P("fsdp", None),
            P("fsdp"),
        ),
        check_vma=False,
    )
```

```python
import jax
import jax.numpy as jnp
from jax import lax
from jax.experimental import pallas as pl
from jax.experimental.pallas import tpu as pltpu
from jax.sharding import PartitionSpec as P

HEADS = 12
KVH = 2
HDIM = 128
PIECE = 256


epsilon = 1e-06
rope_base = 1000000.0


def row_layout(positions, lengths, starts, piece_len):
    doc_ends = jnp.cumsum(lengths)
    passed = positions[:, None] >= doc_ends[None, :]
    doc_ids = jnp.sum(passed.astype(jnp.int32), axis=1, dtype=jnp.int32)
    offsets = jnp.sum(jnp.where(passed, lengths[None, :], 0), axis=1, dtype=jnp.int32)
    inside = (positions[:, None] >= starts[None, :]) & (
        positions[:, None] < starts[None, :] + piece_len
    )
    labels = jnp.arange(1, starts.shape[0] + 1, dtype=jnp.int32)
    piece_ids = jnp.sum(jnp.where(inside, labels[None, :], 0), axis=1, dtype=jnp.int32)
    return (doc_ids, positions - offsets, piece_ids)


def visible_pairs(query_doc, query_pos, query_piece, key_doc, key_pos, key_piece):
    same_doc = query_doc[:, None] == key_doc[None, :]
    causal = key_pos[None, :] <= query_pos[:, None]
    same_piece = (query_piece[:, None] == key_piece[None, :]) & (query_piece[:, None] > 0)
    return same_doc & (causal | same_piece)


def rope_tables(relative, head_dim):
    halves = jnp.arange(0, head_dim, 2).astype(jnp.float32) / head_dim
    inverse = rope_base ** (-halves)
    angles = relative.astype(jnp.float32)[:, None] * inverse[None, :]
    angles = jnp.concatenate([angles, angles], axis=1)
    return (jnp.cos(angles), jnp.sin(angles))


def rotate(values, cosine, sine):
    half_dim = values.shape[-1] // 2
    turned = jnp.concatenate([-values[..., half_dim:], values[..., :half_dim]], axis=-1)
    return values * cosine[:, None, :] + turned * sine[:, None, :]


def unrotate(grads, cosine, sine):
    half_dim = grads.shape[-1] // 2
    spun = grads * sine[:, None, :]
    turned_back = jnp.concatenate([spun[..., half_dim:], -spun[..., :half_dim]], axis=-1)
    return grads * cosine[:, None, :] + turned_back


def mat_dot(left, right):
    return jnp.dot(left, right, preferred_element_type=jnp.float32)


def dot_right_t(left, right):
    return lax.dot_general(
        left, right, (((1,), (1,)), ((), ())), preferred_element_type=jnp.float32
    )


def dot_left_t(left, right):
    return lax.dot_general(
        left, right, (((0,), (0,)), ((), ())), preferred_element_type=jnp.float32
    )


def xor_pairs(count, bit):
    return [(i, i ^ bit) for i in range(count)]


def bits_of(count):
    return [1 << k for k in range(count.bit_length() - 1)]


def gather_relative(block, axis):
    count = lax.axis_size(axis)
    bits = bits_of(count)
    half = block.shape[0] // 2
    halves = []
    for part, order in ((block[:half], bits), (block[half:], bits[::-1])):
        have = {0: part}
        for bit in order:
            fresh = {
                d ^ bit: lax.ppermute(piece, axis, xor_pairs(count, bit))
                for d, piece in have.items()
            }
            have.update(fresh)
        halves.append(have)
    return [(halves[0][d], halves[1][d]) for d in range(count)]


def scatter_relative(pieces, axis):
    count = lax.axis_size(axis)
    bits = bits_of(count)
    half = pieces[0].shape[0] // 2
    sums = []
    for lo, hi, order in ((0, half, bits[::-1]), (half, 2 * half, bits)):
        have = {d: pieces[d][lo:hi] for d in range(count)}
        for bit in order:
            come = {
                d ^ bit: lax.ppermute(have[d].astype(jnp.bfloat16), axis, xor_pairs(count, bit))
                for d in have
                if d & bit
            }
            have = {d: have[d].astype(jnp.float32) + come[d].astype(jnp.float32) for d in come}
        sums.append(have[0])
    return jnp.concatenate(sums, axis=0)


def core_swap(block):
    return lax.ppermute(block, "rep", xor_pairs(lax.axis_size("rep"), 1))


def line_pairs(lows, way):
    return [(2 * i + c, 2 * (i + way) + c) for i in lows for c in range(2)]


def pick(array, index):
    return lax.dynamic_index_in_dim(array, index, 0, keepdims=False)


def line_scatter(parts):
    count = lax.axis_size("rep") // 2
    here = lax.axis_index("rep") // 2
    arrived = [None, None]
    for step in range(1, count):
        sends = [
            pick(parts, jnp.clip(count - step + here, 0, count - 1)),
            pick(parts, jnp.clip(here - count + step, 0, count - 1)),
        ]
        for way in range(2):
            if arrived[way] is not None:
                sends[way] = (
                    sends[way].astype(jnp.float32) + arrived[way].astype(jnp.float32)
                ).astype(jnp.bfloat16)
        arrived = [
            lax.ppermute(sends[0], "rep", line_pairs(range(step), 1)),
            lax.ppermute(sends[1], "rep", line_pairs(range(count - step, count), -1)),
        ]
    own = pick(parts, here).astype(jnp.float32)
    return own + arrived[0].astype(jnp.float32) + arrived[1].astype(jnp.float32)


def line_gather(block):
    count = lax.axis_size("rep") // 2
    here = lax.axis_index("rep") // 2
    below, above = [block], [block]
    for step in range(1, count):
        below.append(lax.ppermute(below[-1], "rep", line_pairs(range(step - 1, count - 1), 1)))
        above.append(lax.ppermute(above[-1], "rep", line_pairs(range(1, count - step + 1), -1)))
    stacked = jnp.stack(below[:0:-1] + above)
    return lax.dynamic_slice_in_dim(stacked, count - 1 - here, count, 0)


def core_halves(mine, other, core):
    return jnp.where(core == 0, jnp.stack([mine, other]), jnp.stack([other, mine]))


def place(pieces, here):
    count = len(pieces)
    stacked = jnp.stack(pieces)
    return jnp.stack([pick(stacked, here ^ j) for j in range(count)])


MESH = pl.DeviceIdType.MESH
MASKED = -1e30


def dot_f32(left, right, dims=((1,), (0,))):
    return lax.dot_general(left, right, (dims, ((), ())), preferred_element_type=jnp.float32)


def layout_of(positions, lengths_ref, starts_ref):
    end = jnp.int32(0)
    doc = jnp.zeros_like(positions)
    before = jnp.zeros_like(positions)
    piece = jnp.zeros_like(positions)
    for i in range(lengths_ref.shape[1]):
        end = end + lengths_ref[0, i]
        passed = positions >= end
        doc = doc + jnp.where(passed, 1, 0)
        before = before + jnp.where(passed, lengths_ref[0, i], 0)
    for i in range(starts_ref.shape[1]):
        first = starts_ref[0, i]
        inside = (positions >= first) & (positions < first + PIECE)
        piece = piece + jnp.where(inside, i + 1, 0)
    return doc, positions - before, piece


def mask_bias(here, rows, row_len, lengths_ref, starts_ref):
    query_pos = here * rows + lax.broadcasted_iota(jnp.int32, (rows, 1), 0)
    key_pos = lax.broadcasted_iota(jnp.int32, (1, row_len), 1)
    query_doc, query_rel, query_piece = layout_of(query_pos, lengths_ref, starts_ref)
    key_doc, unused, key_piece = layout_of(key_pos, lengths_ref, starts_ref)
    allowed = (query_doc == key_doc) & (
        (key_pos <= query_pos) | ((query_piece == key_piece) & (query_piece > 0))
    )
    return jnp.where(allowed, 0.0, MASKED), query_rel


class Links:
    def __init__(self):
        self.here = lax.axis_index("fsdp")
        self.rep = lax.axis_index("rep")
        self.core = lax.rem(self.rep, 2)
        self.line = self.rep // 2
        reps = lax.axis_size("rep")
        here = self.here
        self.near = [here, here + 1 - 2 * lax.rem(here, 2), lax.rem(here + 2, 4), 3 - here]
        self.plane = [{"fsdp": index} for index in self.near]
        self.partner = {"rep": self.rep + 1 - 2 * self.core}
        self.up = {"rep": lax.rem(self.rep + 2, reps)}
        self.down = {"rep": lax.rem(self.rep + reps - 2, reps)}

    def greet(self, line=True):
        barrier = pltpu.get_barrier_semaphore()
        others = self.plane[1:] + ([self.partner, self.up, self.down] if line else [])
        for other in others:
            pl.semaphore_signal(barrier, inc=1, device_id=other, device_id_type=MESH)
        pl.semaphore_wait(barrier, len(others))


def remote(src, dst, sems, index, device):
    return pltpu.make_async_remote_copy(
        src_ref=src,
        dst_ref=dst,
        send_sem=sems.at[0, index],
        recv_sem=sems.at[1, index],
        device_id=device,
        device_id_type=MESH,
    )


class PlaneGather:
    def __init__(self, links, own, slot, rows, sems):
        x, y = links.plane[1], links.plane[2]
        here, near_x, near_y, far = links.near
        half = rows // 2

        def part(index, lo):
            return slot(index).at[pl.ds(lo, half)]

        self.first = [
            remote(own, slot(here), sems, 0, x),
            remote(own, slot(here), sems, 1, y),
        ]
        self.second = [
            remote(part(near_x, 0), part(near_x, 0), sems, 2, y),
            remote(part(near_y, half), part(near_y, half), sems, 3, x),
        ]
        self.come = [
            remote(slot(near_x), slot(near_x), sems, 0, x),
            remote(slot(near_y), slot(near_y), sems, 1, y),
            remote(part(far, 0), part(far, 0), sems, 2, y),
            remote(part(far, half), part(far, half), sems, 3, x),
        ]

    def start(self):
        for copy in self.first:
            copy.start()

    def hand_on(self):
        for i in range(2):
            self.come[i].wait_recv()
            self.second[i].start()

    def finish(self):
        for i in (2, 3):
            self.come[i].wait_recv()

    def drain(self):
        for copy in self.first + self.second:
            copy.wait_send()


def prologue_kernel(
    lengths_ref,
    starts_ref,
    x_ref,
    cot_ref,
    vec_ref,
    inverse_ref,
    wqkv_ref,
    wo_ref,
    gate_ref,
    up_ref,
    normed_all,
    cot_all,
    wgu,
    own_gu,
    wqkv_full,
    wo_full,
    kv_full,
    mid_ref,
    normed_first_ref,
    query_ref,
    attn_ref,
    lse_ref,
    trig_ref,
    gains_ref,
    vec_all,
    wqkv_buf,
    wo_buf,
    kv_buf,
    normed_buf,
    bias_ref,
    thin_buf,
    gu_ref,
    wide_buf,
    own_buf,
    cut_sems,
    local_sems,
    vec_sems,
    qkv_sems,
    qkv_core,
    wo_sems,
    wo_core,
    kv_sems,
    cot_sems,
    norm_sems,
    gu_sems,
    up_sems,
    down_sems,
    own_core,
    up_core,
    down_core,
):
    links = Links()
    here, core, line = links.here, links.core, links.line
    count = lax.axis_size("rep") // 2
    rows, width = x_ref.shape
    shard = wqkv_ref.shape[0]
    half = shard // 2
    links.greet()

    def shard_rows(ref, index):
        return ref.at[pl.ds(pl.multiple_of(index * shard, shard), shard)]

    own_copies = [
        pltpu.make_async_copy(wqkv_ref, shard_rows(wqkv_buf, here), local_sems.at[0]),
        pltpu.make_async_copy(wo_ref, shard_rows(wo_buf, here), local_sems.at[1]),
        pltpu.make_async_copy(cot_ref, cot_all.at[here], local_sems.at[2]),
        pltpu.make_async_copy(vec_ref, vec_all.at[here], local_sems.at[3]),
    ]

    vec_sends = [remote(vec_ref, vec_all.at[here], vec_sems, d - 1, links.plane[d]) for d in (1, 2, 3)]
    vec_comes = [
        remote(vec_ref, vec_all.at[links.near[d]], vec_sems, d - 1, links.plane[d]) for d in (1, 2, 3)
    ]

    def half_rows(ref, index, which):
        return ref.at[pl.ds(pl.multiple_of(index * shard + which * half, half), half)]

    def weight_gather(src, buf, sems, core_sems):
        gather = PlaneGather(
            links,
            src.at[pl.ds(pl.multiple_of(core * half, half), half)],
            lambda index: half_rows(buf, index, core),
            half,
            sems,
        )
        swaps = [
            remote(
                half_rows(buf, links.near[d], core),
                half_rows(buf, links.near[d], core),
                core_sems,
                d - 1,
                links.partner,
            )
            for d in (1, 2, 3)
        ]
        comes = [
            remote(
                half_rows(buf, links.near[d], 1 - core),
                half_rows(buf, links.near[d], 1 - core),
                core_sems,
                d - 1,
                links.partner,
            )
            for d in (1, 2, 3)
        ]
        return gather, swaps, comes

    qkv_gather, qkv_swaps, qkv_comes = weight_gather(wqkv_ref, wqkv_buf, qkv_sems, qkv_core)
    wo_gather, wo_swaps, wo_comes = weight_gather(wo_ref, wo_buf, wo_sems, wo_core)
    cot_gather = PlaneGather(links, cot_ref, lambda index: cot_all.at[index], rows, cot_sems)
    norm_gather = PlaneGather(links, normed_buf, lambda index: normed_all.at[index], rows, norm_sems)

    gu_sends = [
        remote(gu_ref.at[links.near[d]], wgu.at[core, line, d - 1], gu_sems, d - 1, links.plane[d])
        for d in (1, 2, 3)
    ]
    own_block = wgu.at[core, line]
    own_swap = remote(own_block, own_block, own_core, 0, links.partner)
    own_come = remote(wgu.at[1 - core, line], wgu.at[1 - core, line], own_core, 0, links.partner)

    class Hop:
        def __init__(self, k, way):
            sems = up_sems if way > 0 else down_sems
            core_sems = up_core if way > 0 else down_core
            device = links.up if way > 0 else links.down
            back = links.down if way > 0 else links.up
            sent = jnp.clip(line - way * (k - 1), 0, count - 1)
            come = jnp.clip(line - way * k, 0, count - 1)
            if way > 0:
                self.sends = (line <= count - 2) & (line >= k - 1)
                self.comes = line >= k
            else:
                self.sends = (line >= 1) & (line + k - 1 <= count - 1)
                self.comes = line + k <= count - 1
            self.send = remote(wgu.at[core, sent], wgu.at[core, sent], sems, k - 1, device)
            self.recv = remote(wgu.at[core, come], wgu.at[core, come], sems, k - 1, back)
            self.swap = remote(wgu.at[core, come], wgu.at[core, come], core_sems, k - 1, links.partner)
            self.swap_come = remote(
                wgu.at[1 - core, come], wgu.at[1 - core, come], core_sems, k - 1, links.partner
            )

    hops = [(Hop(k, 1), Hop(k, -1)) for k in range(1, count)]

    def start_hop(k):
        for hop in hops[k - 1]:
            pl.when(hop.sends)(hop.send.start)

    def take_hop(k):
        for hop in hops[k - 1]:

            @pl.when(hop.comes)
            def _():
                hop.recv.wait_recv()
                hop.swap.start()

    thin, part = gu_ref.shape[2:]
    first_row = pl.multiple_of(core * half + line * thin, thin)
    cuts = [
        pltpu.make_async_copy(ref.at[pl.ds(first_row, thin)], thin_buf.at[i], cut_sems.at[i])
        for i, ref in enumerate((gate_ref, up_ref))
    ] + [
        pltpu.make_async_copy(ref, wide_buf.at[i], cut_sems.at[2 + i])
        for i, ref in enumerate((gate_ref, up_ref))
    ]
    for copy in vec_sends + cuts:
        copy.start()
    qkv_gather.start()
    for copy in cuts[:2]:
        copy.wait()
    for t in range(4):
        gu_ref[t] = thin_buf[:, :, t * part : (t + 1) * part]
    for copy in gu_sends:
        copy.start()
    for copy in own_copies:
        copy.start()
    wo_gather.start()

    bias, query_rel = mask_bias(here, rows, kv_buf.shape[0] * rows, lengths_ref, starts_ref)
    bias_ref[...] = bias
    angles = query_rel.astype(jnp.float32) * inverse_ref[0:1, :]
    lanes = lax.broadcasted_iota(jnp.int32, (1, HDIM), 1)
    cosine = jnp.cos(angles)
    sine = jnp.sin(angles) * jnp.where(lanes < HDIM // 2, -1.0, 1.0)
    trig_ref[0] = cosine
    trig_ref[1] = sine

    x_float = x_ref[...].astype(jnp.float32)
    unit = x_float * lax.rsqrt(jnp.mean(x_float * x_float, axis=1, keepdims=True) + epsilon)
    own_copies[3].wait()
    for copy in vec_comes:
        copy.wait_recv()
    gains_ref[...] = vec_all[0] + vec_all[1] + vec_all[2] + vec_all[3]
    normed_first_ref[...] = (unit * gains_ref[1:2, :]).astype(jnp.bfloat16)

    qkv_gather.hand_on()
    for swap in qkv_swaps[:2]:
        swap.start()
    for copy in gu_sends:
        copy.wait_recv()
    start_hop(1)
    own_swap.start()
    qkv_gather.finish()
    qkv_swaps[2].start()
    cot_gather.start()
    own_copies[0].wait()
    for copy in qkv_comes:
        copy.wait_recv()

    full_copy = pltpu.make_async_copy(wqkv_buf, wqkv_full, local_sems.at[4])
    full_copy.start()

    def rope(value):
        return value * trig_ref[0] + pltpu.roll(value, HDIM // 2, 1) * trig_ref[1]

    def project(first, bias_row):
        columns = pl.ds(pl.multiple_of(first, 2 * HDIM), 2 * HDIM)
        return dot_f32(normed_first_ref[...], wqkv_buf[:, columns]) + bias_row

    keys = project(width, gains_ref[3:4, 0 : 2 * HDIM])
    own_kv = kv_buf.at[here]
    for h in range(2):
        kv_buf[here, :, h * HDIM : (h + 1) * HDIM] = rope(keys[:, h * HDIM : (h + 1) * HDIM]).astype(
            jnp.bfloat16
        )
    values = project(width + 2 * HDIM, gains_ref[3:4, 2 * HDIM : 4 * HDIM])
    kv_buf[here, :, 2 * HDIM : 4 * HDIM] = values.astype(jnp.bfloat16)
    kv_sends = [remote(own_kv, own_kv, kv_sems, d - 1, links.plane[d]) for d in (1, 2, 3)]
    kv_comes = [
        remote(kv_buf.at[links.near[d]], kv_buf.at[links.near[d]], kv_sems, d - 1, links.plane[d])
        for d in (1, 2, 3)
    ]
    for copy in kv_sends:
        copy.start()

    def query_pair(pair, carry):
        columns = pl.ds(pl.multiple_of(pair * 2 * HDIM, 2 * HDIM), 2 * HDIM)
        got = project(pair * 2 * HDIM, gains_ref[0:1, columns])
        for h in range(2):
            where = pl.ds(pl.multiple_of(pair * 2 * HDIM + h * HDIM, HDIM), HDIM)
            query_ref[:, where] = rope(got[:, h * HDIM : (h + 1) * HDIM]).astype(jnp.bfloat16)
        return carry

    lax.fori_loop(0, HEADS // 2, query_pair, 0)
    for copy in cuts[2:]:
        copy.wait()
    for t in range(4):

        @pl.when(here == t)
        def _():
            own_buf[...] = wide_buf[:, :, t * part : (t + 1) * part]

    own_store = pltpu.make_async_copy(own_buf, own_gu, cut_sems.at[0])
    own_store.start()
    wo_gather.hand_on()
    for swap in wo_swaps[:2]:
        swap.start()
    for copy in kv_comes:
        copy.wait_recv()
    kv_copy = pltpu.make_async_copy(kv_buf, kv_full, local_sems.at[5])
    kv_copy.start()

    group = HEADS // KVH
    row_len = kv_buf.shape[0] * rows
    head_lane = lax.broadcasted_iota(jnp.int32, (1, HDIM), 1)

    def head_step(h, lse):
        columns = pl.ds(pl.multiple_of(h * HDIM, HDIM), HDIM)
        shared = h // group
        key = kv_buf[:, :, pl.ds(pl.multiple_of(shared * HDIM, HDIM), HDIM)].reshape(row_len, HDIM)
        value = kv_buf[:, :, pl.ds(pl.multiple_of((KVH + shared) * HDIM, HDIM), HDIM)].reshape(
            row_len, HDIM
        )
        scores = dot_f32(query_ref[:, columns], key, ((1,), (1,))) * (1.0 / HDIM**0.5) + bias_ref[...]
        peak = jnp.max(scores, axis=1, keepdims=True)
        expo = jnp.exp(scores - peak)
        total = jnp.sum(expo, axis=1, keepdims=True)
        mixed = dot_f32(expo.astype(jnp.bfloat16), value) / total
        attn_ref[:, columns] = mixed.astype(jnp.bfloat16)
        return jnp.where(head_lane == h, peak + jnp.log(total), lse)

    lse = lax.fori_loop(0, HEADS // 2, head_step, jnp.zeros((rows, HDIM), jnp.float32))
    wo_gather.finish()
    wo_swaps[2].start()
    take_hop(1)
    start_hop(2)
    lse_ref[...] = lax.fori_loop(HEADS // 2, HEADS, head_step, lse)
    cot_gather.hand_on()
    take_hop(2)
    start_hop(3)
    own_copies[1].wait()
    for copy in wo_comes:
        copy.wait_recv()
    wo_copy = pltpu.make_async_copy(wo_buf, wo_full, local_sems.at[6])
    wo_copy.start()

    def out_columns(i, carry):
        columns = pl.ds(pl.multiple_of(i * 256, 256), 256)
        mid_ref[:, columns] = x_ref[:, columns].astype(jnp.float32) + dot_f32(
            attn_ref[...], wo_buf[:, columns]
        )
        return carry

    lax.fori_loop(0, width // 256, out_columns, 0)
    mid = mid_ref[...]
    unit = mid * lax.rsqrt(jnp.mean(mid * mid, axis=1, keepdims=True) + epsilon)
    normed_buf[...] = (unit * gains_ref[2:3, :]).astype(jnp.bfloat16)
    norm_gather.start()
    norm_copy = pltpu.make_async_copy(normed_buf, normed_all.at[here], local_sems.at[7])
    norm_copy.start()
    norm_gather.hand_on()
    cot_gather.finish()
    take_hop(3)
    norm_gather.finish()

    own_copies[2].wait()
    own_store.wait()
    full_copy.wait()
    kv_copy.wait()
    wo_copy.wait()
    norm_copy.wait()
    for copy in vec_sends + gu_sends + qkv_swaps + wo_swaps + kv_sends + [own_swap]:
        copy.wait_send()
    own_come.wait_recv()
    for copy in wo_comes[:0]:
        copy.wait_recv()
    for gather in (qkv_gather, wo_gather, cot_gather, norm_gather):
        gather.drain()
    for pair in hops:
        for hop in pair:
            pl.when(hop.sends)(hop.send.wait_send)

            @pl.when(hop.comes)
            def _():
                hop.swap.wait_send()
                hop.swap_come.wait_recv()


def prologue(lengths, starts, x, cot, vec, inverse, wqkv, wo, gate, up):
    rows, width = x.shape
    shards = lax.axis_size("fsdp")
    count = lax.axis_size("rep") // 2
    shard = gate.shape[0]
    thin, part = shard // (2 * count), gate.shape[1] // shards
    bf16, f32 = jnp.bfloat16, jnp.float32
    any_space = pl.BlockSpec(memory_space=pl.ANY)
    vmem = pl.BlockSpec(memory_space=pltpu.VMEM)
    smem = pl.BlockSpec(memory_space=pltpu.SMEM)
    shape = jax.ShapeDtypeStruct

    def sems(n):
        return pltpu.SemaphoreType.DMA((2, n))

    return pl.pallas_call(
        prologue_kernel,
        name="prologue",
        out_shape=(
            shape((shards, rows, width), bf16),
            shape((shards, rows, width), bf16),
            shape((2, count, shards - 1, 2, thin, part), bf16),
            shape((2, shard, part), bf16),
            shape((width, wqkv.shape[1]), bf16),
            shape((width, width), bf16),
            shape((shards, rows, 4 * HDIM), bf16),
            shape((rows, width), f32),
            shape((rows, width), bf16),
            shape((rows, width), bf16),
            shape((rows, width), bf16),
            shape((rows, HDIM), f32),
            shape((2, rows, HDIM), f32),
            shape((8, width), f32),
        ),
        in_specs=[smem, smem, vmem, vmem, vmem, vmem] + [any_space] * 4,
        out_specs=[any_space] * 7 + [vmem] * 7,
        scratch_shapes=[
            pltpu.VMEM((shards, 8, width), f32),
            pltpu.VMEM((width, wqkv.shape[1]), bf16),
            pltpu.VMEM((width, width), bf16),
            pltpu.VMEM((shards, rows, 4 * HDIM), bf16),
            pltpu.VMEM((rows, width), bf16),
            pltpu.VMEM((rows, shards * rows), f32),
            pltpu.VMEM((2, thin, gate.shape[1]), bf16),
            pltpu.VMEM((shards, 2, thin, part), bf16),
            pltpu.VMEM((2, shard, gate.shape[1]), bf16),
            pltpu.VMEM((2, shard, part), bf16),
            pltpu.SemaphoreType.DMA((4,)),
            pltpu.SemaphoreType.DMA((8,)),
            sems(3),
            sems(4),
            sems(3),
            sems(4),
            sems(3),
            sems(3),
            sems(4),
            sems(4),
            sems(3),
            sems(count - 1),
            sems(count - 1),
            sems(1),
            sems(count - 1),
            sems(count - 1),
        ],
        compiler_params=pltpu.CompilerParams(
            collective_id=0, has_side_effects=True, vmem_limit_bytes=60 * 2**20
        ),
    )(lengths, starts, x, cot, vec, inverse, wqkv, wo, gate, up)


class Stream:
    def __init__(self, links, pairs, size, own, land_end, land_mid, final, loads, stage, sems, local_sems, targets):
        self.links, self.pairs, self.size = links, pairs, size
        self.own, self.land_end, self.land_mid, self.final = own, land_end, land_mid, final
        self.loads, self.stage, self.sems, self.local_sems = loads, stage, sems, local_sems
        self.targets = targets
        self.near = links.line // 2
        self.far = 1 - self.near
        self.busy = {}

    def rows(self, kind, p):
        return pl.ds(pl.multiple_of((kind * self.pairs + p) * self.size, self.size), self.size)

    def copy(self, src, dst, p, index, device):
        return pltpu.make_async_remote_copy(
            src_ref=src,
            dst_ref=dst,
            send_sem=self.sems.at[0, p, index],
            recv_sem=self.sems.at[1, p, index],
            device_id=device,
            device_id_type=MESH,
        )

    def total(self, refs):
        copies = [
            pltpu.make_async_copy(ref, self.loads.at[i], self.local_sems.at[i]) for i, ref in enumerate(refs)
        ]
        for copy in copies:
            copy.start()
        for copy in copies:
            copy.wait()
        out = self.loads[0].astype(jnp.float32)
        for i in range(1, len(refs)):
            out = out + self.loads[i].astype(jnp.float32)
        return out.astype(jnp.bfloat16)

    def free(self, role, which, p):
        for copy in self.busy.pop((role, which, p % 2), list)():
            copy.wait_send()

    def hold(self, role, which, p, make):
        copies = make()
        for copy in copies:
            copy.start()
        self.busy[(role, which, p % 2)] = make

    def finals(self, p, which):
        links = self.links
        near, far = self.rows(self.near, p), self.rows(self.far, p)
        ref_near, ref_far = self.final(links.core, near), self.final(links.core, far)
        plans = (
            (ref_near, 3, links.away),
            (ref_near, 4, links.toward),
            (ref_far, 5, links.away),
            (ref_near, 6, links.partner),
            (ref_far, 7, links.partner),
        )
        return [
            self.copy(ref, ref, p, index, device)
            for i, (ref, index, device) in enumerate(plans)
            if i in which
        ]

    def end_send(self, p):
        for which, kind in ((0, self.far), (1, self.near)):
            self.free("end", which, p)
            self.stage[which, p % 2] = self.total(self.own(self.rows(kind, p)))
            self.hold(
                "end",
                which,
                p,
                lambda which=which: [
                    self.copy(
                        self.stage.at[which, p % 2], self.land_end.at[p, which], p, which, self.links.toward
                    )
                ],
            )

    def mid_pass(self, p):
        self.free("mid", 0, p)
        self.copy(self.land_end.at[p, 0], self.land_end.at[p, 0], p, 0, self.links.away).wait_recv()
        self.stage[0, p % 2] = self.total(self.own(self.rows(self.far, p)) + [self.land_end.at[p, 0]])
        self.hold(
            "mid",
            0,
            p,
            lambda: [self.copy(self.stage.at[0, p % 2], self.land_mid.at[p], p, 2, self.links.toward)],
        )

    def mid_sum(self, p):
        links = self.links
        self.free("mid", 1, p)
        self.copy(self.land_end.at[p, 1], self.land_end.at[p, 1], p, 1, links.away).wait_recv()
        self.copy(self.land_mid.at[p], self.land_mid.at[p], p, 2, links.toward).wait_recv()
        near = self.rows(self.near, p)
        self.stage[1, p % 2] = self.total(self.own(near) + [self.land_end.at[p, 1], self.land_mid.at[p]])
        self.own_copy(p).start()

        def sends():
            buf = self.stage.at[1, p % 2]
            near = self.rows(self.near, p)
            final = self.final(links.core, near)
            if self.targets:
                ref = self.target(links.core, near, links.here)
                return [
                    self.copy(buf.at[links.near[d]], ref, p, 7 + d, links.plane[d]) for d in (1, 2, 3)
                ]
            return [
                self.copy(buf, final, p, 3, links.away),
                self.copy(buf, final, p, 4, links.toward),
                self.copy(buf, final, p, 6, links.partner),
            ]

        self.hold("mid", 1, p, sends)

    def own_copy(self, p):
        links = self.links
        buf, near = self.stage.at[1, p % 2], self.rows(self.near, p)
        final = self.final(links.core, near)
        if self.targets:
            buf, final = buf.at[links.here], self.target(links.core, near, links.here)
        return pltpu.make_async_copy(buf, final, self.local_sems.at[6 + p % 2])

    def target(self, core, rows, source):
        return self.final(core, rows).at[source]

    def mid_out(self, p):
        links = self.links
        self.own_copy(p).wait()
        if not self.targets:
            return
        near = self.rows(self.near, p)
        for d in (1, 2, 3):
            ref = self.target(links.core, near, links.near[d])
            self.copy(ref, ref, p, 7 + d, links.plane[d]).wait_recv()
        for copy in self.finals(p, (0, 1, 3)):
            copy.start()

    def mid_far(self, p):
        far = self.final(self.links.core, self.rows(self.far, p))
        self.copy(far, far, p, 4, self.links.toward).wait_recv()
        for copy in self.finals(p, (2, 4)):
            copy.start()

    def end_take(self, p):
        for kind, index, out in ((self.near, 3, 3), (self.far, 5, 4)):
            ref = self.final(self.links.core, self.rows(kind, p))
            self.copy(ref, ref, p, index, self.links.toward).wait_recv()
            self.finals(p, (out,))[0].start()

    def close_mid(self):
        for key in [k for k in self.busy if k[0] == "mid"]:
            for copy in self.busy.pop(key)():
                copy.wait_send()
        for p in range(self.pairs):
            for copy in self.finals(p, (0, 1, 2, 3, 4) if self.targets else (2, 4)):
                copy.wait_send()

    def close_end(self):
        for key in [k for k in self.busy if k[0] == "end"]:
            for copy in self.busy.pop(key)():
                copy.wait_send()
        for p in range(self.pairs):
            for copy in self.finals(p, (3, 4)):
                copy.wait_send()

    def close_core(self):
        for p in range(self.pairs):
            for kind, index in ((self.near, 6), (self.far, 7)):
                ref = self.final(1 - self.links.core, self.rows(kind, p))
                self.copy(ref, ref, p, index, self.links.partner).wait_recv()


def epilogue_kernel(
    lengths_ref,
    starts_ref,
    query_ref,
    lse_ref,
    trig_ref,
    gains_ref,
    x_hbm,
    cot_hbm,
    mid_hbm,
    part_hbm,
    normed_hbm,
    attn_hbm,
    mlp_hbm,
    kv_hbm,
    wqkv_hbm,
    wo_hbm,
    down_part,
    gate_part,
    up_part,
    grad_input_ref,
    sums_ref,
    down_final,
    gate_final,
    up_final,
    attn_final,
    down_core,
    gate_core,
    up_core,
    attn_core,
    attn_own,
    mlp_land,
    down_end,
    down_mid,
    gate_end,
    gate_mid,
    up_end,
    up_mid,
    attn_end,
    attn_mid,
    kv_buf,
    key_turned,
    bias_ref,
    lse_turned,
    dmid_ref,
    branch_ref,
    dattn_ref,
    dqkv_ref,
    dkey_ref,
    dvalue_ref,
    kv_out,
    kv_land,
    normed_turned,
    attn_turned,
    half_buf,
    half_load,
    plane_first,
    plane_second,
    plane_send,
    vec_plane,
    vec_core,
    vec_line,
    vec_send,
    down_loads,
    down_stage,
    gu_loads,
    gate_stage,
    up_stage,
    attn_loads,
    attn_stage,
    local_sems,
    scope_sems,
    mlp_sems,
    load_sems,
    core_sems,
    kv_sems,
    half_sems,
    plane_sems,
    vec_sems,
    down_sems,
    gate_sems,
    up_sems,
    attn_sems,
):
    links = Links()
    here, core, line = links.here, links.core, links.line
    rows, width = x_hbm.shape
    scale = 1.0 / HDIM**0.5
    group = HEADS // KVH
    bf16, f32 = jnp.bfloat16, jnp.float32
    step = 2 - 4 * (line // 2)
    links.toward = {"rep": links.rep + step}
    links.away = {"rep": links.rep - step}
    is_end = (line == 0) | (line == 3)
    is_mid = (line == 1) | (line == 2)

    barrier = pltpu.get_barrier_semaphore()
    line_others = [{"rep": 2 * lax.rem(line + j, 4) + core} for j in (1, 2, 3)]
    others = links.plane[1:] + [links.partner] + line_others
    for other in others:
        pl.semaphore_signal(barrier, inc=1, device_id=other, device_id_type=MESH)
    pl.semaphore_wait(barrier, len(others))

    swaps = [
        remote(down_part.at[1 - core], down_core, core_sems, 0, links.partner),
        remote(gate_part.at[:, 1 - core], gate_core, core_sems, 1, links.partner),
        remote(up_part.at[:, 1 - core], up_core, core_sems, 2, links.partner),
    ]
    for swap in swaps:
        swap.start()
    fetches = [pltpu.make_async_copy(kv_hbm, kv_buf, local_sems.at[1])]
    mlp_sends = [
        remote(mlp_hbm.at[links.near[d]], mlp_land.at[d - 1], mlp_sems, d - 1, links.plane[d]) for d in (1, 2, 3)
    ]
    for copy in mlp_sends:
        copy.start()
    for fetch in fetches:
        fetch.start()

    def stream(size, total, own, end, mid, final, loads, stage, sems, targets=False):
        return Stream(
            links, total // (2 * size), size, own, end, mid, final, loads, stage, sems, load_sems, targets
        )

    down = stream(
        down_stage.shape[2],
        down_core.shape[0],
        lambda r: [down_part.at[core, r], down_core.at[r]],
        down_end,
        down_mid,
        lambda c, r: down_final.at[c, r],
        down_loads,
        down_stage,
        down_sems,
    )
    gate = stream(
        gate_stage.shape[3],
        gate_core.shape[1],
        lambda r: [gate_part.at[:, core, r], gate_core.at[:, r]],
        gate_end,
        gate_mid,
        lambda c, r: gate_final.at[c, :, r],
        gu_loads,
        gate_stage,
        gate_sems,
        True,
    )
    up = stream(
        up_stage.shape[3],
        up_core.shape[1],
        lambda r: [up_part.at[:, core, r], up_core.at[:, r]],
        up_end,
        up_mid,
        lambda c, r: up_final.at[c, :, r],
        gu_loads,
        up_stage,
        up_sems,
        True,
    )
    attn = stream(
        attn_stage.shape[2],
        attn_own.shape[0],
        lambda r: [attn_own.at[r]],
        attn_end,
        attn_mid,
        lambda c, r: attn_final.at[c, r],
        attn_loads,
        attn_stage,
        attn_sems,
    )
    pairs = [(s, p) for s in (down, gate, up, attn) for p in range(s.pairs)]

    def service(n):
        def at(back):
            return pairs[n - back] if 0 <= n - back < len(pairs) else None

        first = {0: down, down.pairs: gate, down.pairs + gate.pairs: up}
        if n in first:
            swaps[list(first).index(n)].wait_recv()

        @pl.when(is_end)
        def _():
            for back, action in ((7, "end_take"), (0, "end_send")):
                if at(back):
                    getattr(at(back)[0], action)(at(back)[1])

        @pl.when(is_mid)
        def _():
            for back, action in ((4, "mid_far"), (3, "mid_out"), (2, "mid_sum"), (1, "mid_pass")):
                if at(back):
                    getattr(at(back)[0], action)(at(back)[1])

    def scoped(refs, body):
        def inner(*bufs):
            copies = [pltpu.make_async_copy(r, b, scope_sems.at[i]) for i, (r, b) in enumerate(zip(refs, bufs))]
            for copy in copies:
                copy.start()
            for copy in copies:
                copy.wait()
            body(*bufs)

        pl.run_scoped(inner, *[pltpu.VMEM(r.shape, r.dtype) for r in refs])

    def norm_back():
        scoped((mid_hbm, part_hbm, cot_hbm), norm_body)

    def norm_body(mid_ref, part_ref, cot_ref):
        mid = mid_ref[...]
        inv = lax.rsqrt(jnp.mean(mid * mid, axis=1, keepdims=True) + epsilon)
        unit = mid * inv
        part = part_ref[...]
        vec_send[2:3, :] = jnp.sum(part * unit, axis=0, keepdims=True)
        scaled = part * gains_ref[2:3, :]
        d_mid = cot_ref[...].astype(f32) + inv * (
            scaled - unit * jnp.mean(scaled * unit, axis=1, keepdims=True)
        )
        dmid_ref[...] = d_mid
        branch_ref[...] = d_mid.astype(bf16)
        query_pos = here * rows + lax.broadcasted_iota(jnp.int32, (1, rows), 1)
        key_pos = lax.broadcasted_iota(jnp.int32, (4 * rows, 1), 0)
        query_doc, unused, query_piece = layout_of(query_pos, lengths_ref, starts_ref)
        key_doc, unused, key_piece = layout_of(key_pos, lengths_ref, starts_ref)
        allowed = (query_doc == key_doc) & (
            (key_pos <= query_pos) | ((query_piece == key_piece) & (query_piece > 0))
        )
        bias_ref[...] = jnp.where(allowed, 0.0, MASKED)
        lse_turned[...] = lse_ref[...].T

    def attn_back():
        scoped((wo_hbm,), attn_body)

    def attn_body(wo_buf):
        def tile(i, carry):
            columns = pl.ds(pl.multiple_of(i * 256, 256), 256)
            dattn_ref[:, columns] = dot_f32(branch_ref[...], wo_buf[columns, :], ((1,), (1,))).astype(bf16)
            return carry

        lax.fori_loop(0, width // 256, tile, 0)
        fetches[0].wait()
        for g in range(KVH):
            key_turned[g] = kv_buf[:, :, g * HDIM : (g + 1) * HDIM].reshape(4 * rows, HDIM).T
        dkey_ref[...] = jnp.zeros_like(dkey_ref)
        dvalue_ref[...] = jnp.zeros_like(dvalue_ref)

    def head_back(h, carry):
        columns = pl.ds(pl.multiple_of(h * HDIM, HDIM), HDIM)
        shared = h // group
        key = kv_buf[:, :, pl.ds(pl.multiple_of(shared * HDIM, HDIM), HDIM)].reshape(4 * rows, HDIM)
        value = kv_buf[:, :, pl.ds(pl.multiple_of((KVH + shared) * HDIM, HDIM), HDIM)].reshape(
            4 * rows, HDIM
        )
        query, d_out = query_ref[:, columns], dattn_ref[:, columns]
        scores = dot_f32(key, query, ((1,), (1,))) * scale + bias_ref[...]
        probs = jnp.exp(scores - lse_turned[pl.ds(h, 1), :])
        d_probs = dot_f32(value, d_out, ((1,), (1,)))
        delta = jnp.sum(probs * d_probs, axis=0, keepdims=True)
        d_scores = (probs * (d_probs - delta)).astype(bf16)
        dkey_ref[shared] += dot_f32(d_scores, query)
        dvalue_ref[shared] += dot_f32(probs.astype(bf16), d_out)
        d_query = dot_f32(key_turned[shared], d_scores).T * scale
        d_query = d_query * trig_ref[0] - pltpu.roll(d_query, HDIM // 2, 1) * trig_ref[1]
        dqkv_ref[:, columns] = d_query.astype(bf16)
        return carry

    kv_sends = [
        remote(kv_out.at[links.near[d]], kv_land.at[d - 1], kv_sems, d - 1, links.plane[d]) for d in (1, 2, 3)
    ]

    def kv_send():
        for g in range(KVH):
            kv_out[:, :, g * HDIM : (g + 1) * HDIM] = (
                (dkey_ref[g] * scale).astype(bf16).reshape(4, rows, HDIM)
            )
            kv_out[:, :, (KVH + g) * HDIM : (KVH + g + 1) * HDIM] = (
                dvalue_ref[g].astype(bf16).reshape(4, rows, HDIM)
            )
        for copy in kv_sends:
            copy.start()

    vec_copies = {
        "plane": [remote(vec_send, vec_plane.at[here], vec_sems, d - 1, links.plane[d]) for d in (1, 2, 3)],
        "core": [remote(vec_core.at[core], vec_core.at[core], vec_sems, 3, links.partner)],
        "line": [
            remote(vec_line.at[line], vec_line.at[line], vec_sems, 4 + j, line_others[j]) for j in range(3)
        ],
    }
    vec_comes = {
        "plane": [
            remote(vec_send, vec_plane.at[links.near[d]], vec_sems, d - 1, links.plane[d]) for d in (1, 2, 3)
        ],
        "core": [remote(vec_core.at[core], vec_core.at[1 - core], vec_sems, 3, links.partner)],
        "line": [
            remote(
                vec_line.at[line],
                vec_line.at[lax.rem(line + 3 - j, 4)],
                vec_sems,
                4 + j,
                line_others[2 - j],
            )
            for j in range(3)
        ],
    }

    def input_back():
        for d in (1, 2, 3):
            remote(kv_land.at[d - 1], kv_land.at[d - 1], kv_sems, d - 1, links.plane[d]).wait_recv()
        kv = kv_out[here].astype(f32)
        for d in range(3):
            kv = kv + kv_land[d].astype(f32)
        for g in range(KVH):
            d_key = kv[:, g * HDIM : (g + 1) * HDIM]
            d_key = d_key * trig_ref[0] - pltpu.roll(d_key, HDIM // 2, 1) * trig_ref[1]
            dqkv_ref[:, width + g * HDIM : width + (g + 1) * HDIM] = d_key.astype(bf16)
        dqkv_ref[:, width + KVH * HDIM :] = kv[:, KVH * HDIM :].astype(bf16)
        scoped((wqkv_hbm, x_hbm), input_body)
        scoped((normed_hbm, attn_hbm), turn_body)

    def turn_body(normed_ref, attn_ref):
        normed_turned[...] = normed_ref[...].T
        attn_turned[...] = attn_ref[...].T

    def input_body(wqkv_buf, x_ref):
        def tile(i, carry):
            columns = pl.ds(pl.multiple_of(i * 256, 256), 256)
            grad_input_ref[:, columns] = dot_f32(dqkv_ref[...], wqkv_buf[columns, :], ((1,), (1,)))
            return carry

        lax.fori_loop(0, width // 256, tile, 0)
        x = x_ref[...].astype(f32)
        inv = lax.rsqrt(jnp.mean(x * x, axis=1, keepdims=True) + epsilon)
        unit = x * inv
        part = grad_input_ref[...]
        vec_send[1:2, :] = jnp.sum(part * unit, axis=0, keepdims=True)
        scaled = part * gains_ref[1:2, :]
        grad_input_ref[...] = dmid_ref[...] + inv * (
            scaled - unit * jnp.mean(scaled * unit, axis=1, keepdims=True)
        )
        sums = jnp.sum(dqkv_ref[...].astype(f32), axis=0, keepdims=True)
        vec_send[0:1, :] = sums[:, :width]
        vec_send[3:4, 0 : 2 * KVH * HDIM] = sums[:, width:]
        vec_send[3:4, 2 * KVH * HDIM :] = jnp.zeros((1, width - 2 * KVH * HDIM), f32)
        vec_send[4:8, :] = jnp.zeros((4, width), f32)
        vec_plane[here] = vec_send[...]
        for copy in vec_copies["plane"]:
            copy.start()

    shard = width // 4
    half = shard // 2
    qkv_width = wqkv_hbm.shape[1]

    def half_grad(t, which):
        at = pl.ds(pl.multiple_of(t * shard + which * half, half), half)
        return (
            dot_f32(normed_turned[at, :], dqkv_ref[...]).astype(bf16),
            dot_f32(attn_turned[at, :], branch_ref[...]).astype(bf16),
        )

    half_sends = [remote(half_buf.at[t], attn_core.at[t], half_sems, t, links.partner) for t in range(4)]

    def other_half():
        def one(t, carry):
            left, right = half_grad(t, 1 - core)
            half_buf[t, :, :qkv_width] = left
            half_buf[t, :, qkv_width:] = right
            return carry

        lax.fori_loop(0, 4, one, 0)
        for copy in half_sends:
            copy.start()
        for copy in vec_comes["plane"]:
            copy.wait_recv()
        vec_core[core] = vec_plane[0] + vec_plane[1] + vec_plane[2] + vec_plane[3]
        vec_copies["core"][0].start()

    quarter = half // 2
    near_x, near_y, far = links.near[1:]

    def own_half():
        for copy in half_sends:
            copy.wait_send()
        for t in range(4):
            remote(attn_core.at[t], attn_core.at[t], half_sems, t, links.partner).wait_recv()
            load = pltpu.make_async_copy(attn_core.at[t], half_load, local_sems.at[3])
            load.start()
            left, right = half_grad(t, core)
            load.wait()
            half_buf[t, :, :qkv_width] = (left.astype(f32) + half_load[:, :qkv_width].astype(f32)).astype(bf16)
            half_buf[t, :, qkv_width:] = (right.astype(f32) + half_load[:, qkv_width:].astype(f32)).astype(bf16)
        for copy in first_sends:
            copy.start()
        vec_comes["core"][0].wait_recv()
        vec_line[line] = vec_core[0] + vec_core[1]
        for copy in vec_copies["line"]:
            copy.start()

    low_rows, high_rows = pl.ds(0, quarter), pl.ds(quarter, quarter)
    first_sends = [
        remote(half_buf.at[near_y, low_rows], plane_first.at[0], plane_sems, 0, links.plane[2]),
        remote(half_buf.at[far, low_rows], plane_first.at[1], plane_sems, 1, links.plane[2]),
        remote(half_buf.at[near_x, high_rows], plane_first.at[2], plane_sems, 2, links.plane[1]),
        remote(half_buf.at[far, high_rows], plane_first.at[3], plane_sems, 3, links.plane[1]),
    ]
    second_sends = [
        remote(plane_send.at[0], plane_second.at[0], plane_sems, 4, links.plane[1]),
        remote(plane_send.at[1], plane_second.at[1], plane_sems, 5, links.plane[2]),
    ]

    def plane_turn():
        for copy in first_sends:
            copy.wait_recv()
        plane_send[0] = (half_buf[near_x, 0:quarter].astype(f32) + plane_first[1].astype(f32)).astype(bf16)
        plane_send[1] = (
            half_buf[near_y, quarter : 2 * quarter].astype(f32) + plane_first[3].astype(f32)
        ).astype(bf16)
        for copy in second_sends:
            copy.start()

    def plane_end():
        for copy in second_sends + first_sends:
            copy.wait_send()
        for copy in second_sends:
            copy.wait_recv()
        for i in range(2):
            at = slice(i * quarter, (i + 1) * quarter)
            half_load[at, :] = (
                half_buf[here, at].astype(f32)
                + plane_first[2 * i].astype(f32)
                + plane_second[i].astype(f32)
            ).astype(bf16)
        store = pltpu.make_async_copy(half_load, attn_own, local_sems.at[3])
        store.start()
        for copy in vec_comes["line"]:
            copy.wait_recv()
        sums_ref[...] = vec_line[0] + vec_line[1] + vec_line[2] + vec_line[3]
        store.wait()

    def heads(lo, hi):
        return lambda: lax.fori_loop(lo, hi, head_back, 0)

    chain = [
        norm_back,
        attn_back,
        heads(0, 2),
        heads(2, 4),
        heads(4, 6),
        heads(6, 8),
        heads(8, 10),
        heads(10, 12),
        kv_send,
        input_back,
        other_half,
        own_half,
        None,
        plane_turn,
        None,
        plane_end,
    ]
    for n in range(len(pairs) + 8):
        service(n)
        if n < len(chain) and chain[n] is not None:
            chain[n]()

    for swap in swaps + kv_sends + mlp_sends:
        swap.wait_send()
    for copy in mlp_sends:
        copy.wait_recv()
    for name in vec_copies:
        for copy in vec_copies[name]:
            copy.wait_send()
    streams = (down, gate, up, attn)

    @pl.when(is_end)
    def _():
        for s in streams:
            s.close_end()

    @pl.when(is_mid)
    def _():
        for s in streams:
            s.close_mid()

    for s in streams:
        s.close_core()


def epilogue(
    lengths, starts, query, lse, trig, gains, x, cot, mid, part, normed, attn, mlp, kv, wqkv, wo, downs, gates, ups
):
    rows, width = x.shape
    bf16, f32 = jnp.bfloat16, jnp.float32
    any_space = pl.BlockSpec(memory_space=pl.ANY)
    vmem = pl.BlockSpec(memory_space=pltpu.VMEM)
    smem = pl.BlockSpec(memory_space=pltpu.SMEM)
    shape = jax.ShapeDtypeStruct
    wide = wqkv.shape[1] + width
    half = width // 8
    down_half = downs.shape[1]
    cols = gates.shape[3]
    down_size, gu_size, attn_size = 80, 16, 32
    down_pairs = down_half // (2 * down_size)
    gu_pairs = half // (2 * gu_size)
    attn_pairs = half // (2 * attn_size)
    down_chunk = (down_size, width)
    gu_chunk = (4, gu_size, cols)
    attn_chunk = (attn_size, wide)

    def line_buffers(pairs, chunk):
        return [shape((pairs, 2) + chunk, bf16), shape((pairs,) + chunk, bf16)]

    def sems(*n):
        return pltpu.SemaphoreType.DMA((2,) + n)

    outs = [
        shape((rows, width), f32),
        shape((8, width), f32),
        shape((2, down_half, width), bf16),
        shape((2, 4, half, cols), bf16),
        shape((2, 4, half, cols), bf16),
        shape((2, half, wide), bf16),
        shape((down_half, width), bf16),
        shape((4, half, cols), bf16),
        shape((4, half, cols), bf16),
        shape((4, half, wide), bf16),
        shape((half, wide), bf16),
        shape((3, rows, width), bf16),
    ]
    outs += line_buffers(down_pairs, down_chunk)
    outs += line_buffers(gu_pairs, gu_chunk) + line_buffers(gu_pairs, gu_chunk)
    outs += line_buffers(attn_pairs, attn_chunk)
    return pl.pallas_call(
        epilogue_kernel,
        name="epilogue",
        out_shape=tuple(outs),
        in_specs=[smem] * 2 + [vmem] * 4 + [any_space] * 13,
        out_specs=[vmem] * 2 + [any_space] * (len(outs) - 2),
        scratch_shapes=[
            pltpu.VMEM((4, rows, 4 * HDIM), bf16),
            pltpu.VMEM((KVH, HDIM, 4 * rows), bf16),
            pltpu.VMEM((4 * rows, rows), f32),
            pltpu.VMEM((HDIM, rows), f32),
            pltpu.VMEM((rows, width), f32),
            pltpu.VMEM((rows, width), bf16),
            pltpu.VMEM((rows, width), bf16),
            pltpu.VMEM((rows, wqkv.shape[1]), bf16),
            pltpu.VMEM((KVH, 4 * rows, HDIM), f32),
            pltpu.VMEM((KVH, 4 * rows, HDIM), f32),
            pltpu.VMEM((4, rows, 4 * HDIM), bf16),
            pltpu.VMEM((3, rows, 4 * HDIM), bf16),
            pltpu.VMEM((width, rows), bf16),
            pltpu.VMEM((width, rows), bf16),
            pltpu.VMEM((4, half, wide), bf16),
            pltpu.VMEM((half, wide), bf16),
            pltpu.VMEM((4, half // 2, wide), bf16),
            pltpu.VMEM((2, half // 2, wide), bf16),
            pltpu.VMEM((2, half // 2, wide), bf16),
            pltpu.VMEM((4, 8, width), f32),
            pltpu.VMEM((2, 8, width), f32),
            pltpu.VMEM((4, 8, width), f32),
            pltpu.VMEM((8, width), f32),
            pltpu.VMEM((4,) + down_chunk, bf16),
            pltpu.VMEM((2, 2) + down_chunk, bf16),
            pltpu.VMEM((4,) + gu_chunk, bf16),
            pltpu.VMEM((2, 2) + gu_chunk, bf16),
            pltpu.VMEM((2, 2) + gu_chunk, bf16),
            pltpu.VMEM((4,) + attn_chunk, bf16),
            pltpu.VMEM((2, 2) + attn_chunk, bf16),
            pltpu.SemaphoreType.DMA((4,)),
            pltpu.SemaphoreType.DMA((4,)),
            sems(3),
            pltpu.SemaphoreType.DMA((8,)),
            sems(3),
            sems(3),
            sems(4),
            sems(6),
            sems(7),
            sems(down_pairs, 11),
            sems(gu_pairs, 11),
            sems(gu_pairs, 11),
            sems(attn_pairs, 11),
        ],
        compiler_params=pltpu.CompilerParams(
            collective_id=1, has_side_effects=True, vmem_limit_bytes=63 * 2**20
        ),
    )(lengths, starts, query, lse, trig, gains, x, cot, mid, part, normed, attn, mlp, kv, wqkv, wo, downs, gates, ups)


class Place:
    def __init__(self):
        here = lax.axis_index("fsdp")
        self.near = [here, here + 1 - 2 * lax.rem(here, 2), lax.rem(here + 2, 4), 3 - here]


def feed_forward_kernel(
    x_ref, cot_ref, wgu, own_gu, down_hbm, act_ref, dgate_ref, dup_ref, norm_ref, mlp_ref, w_ref, down_ref, sems
):
    f32, bf16 = jnp.float32, jnp.bfloat16
    cores, line, others, kinds, thin, part = wgu.shape
    shard = own_gu.shape[1]

    @pl.when(pl.program_id(0) == 0)
    def _():
        near = Place().near
        copies = [pltpu.make_async_copy(down_hbm, down_ref, sems.at[0])]
        for g in range(kinds):
            at = pl.multiple_of(near[0] * shard, shard)
            copies.append(
                pltpu.make_async_copy(own_gu.at[g], w_ref.at[g, pl.ds(at, shard)], sems.at[1 + g])
            )
        n = 1 + kinds
        for d in range(1, 4):
            for c in range(cores):
                for z in range(line):
                    for g in range(kinds):
                        at = pl.multiple_of(near[d] * shard + (c * line + z) * thin, thin)
                        copies.append(
                            pltpu.make_async_copy(
                                wgu.at[c, z, d - 1, g], w_ref.at[g, pl.ds(at, thin)], sems.at[n]
                            )
                        )
                        n += 1
        for copy in copies:
            copy.start()
        for copy in copies:
            copy.wait()

    x, cot = x_ref[...], cot_ref[...]
    for lo in range(0, part, 512):
        at = slice(lo, min(lo + 512, part))
        gate = dot_f32(x, w_ref[0, :, at])
        up = dot_f32(x, w_ref[1, :, at])
        d_act = dot_f32(cot, down_ref[at, :], ((1,), (1,)))
        sig = jax.nn.sigmoid(gate)
        silu = gate * sig
        act_ref[:, at] = (silu * up).astype(bf16)
        dgate_ref[:, at] = (d_act * up * sig * (1.0 + gate * (1.0 - sig))).astype(bf16)
        dup_ref[:, at] = (d_act * silu).astype(bf16)
    for lo in range(0, x.shape[1], 512):
        at = slice(lo, lo + 512)
        norm_ref[:, at] = (
            dot_f32(dgate_ref[...], w_ref[0, at, :], ((1,), (1,)))
            + dot_f32(dup_ref[...], w_ref[1, at, :], ((1,), (1,)))
        ).astype(bf16)
        mlp_ref[:, at] = dot_f32(act_ref[...], down_ref[:, at]).astype(bf16)


def feed_forward(x, cot, wgu, own_gu, down):
    rows, width = x.shape
    part = down.shape[0]
    tile = rows // 4
    bf16 = jnp.bfloat16
    any_space = pl.BlockSpec(memory_space=pl.ANY)
    wide = pl.BlockSpec((tile, width), lambda i: (i, 0))
    hidden = pl.BlockSpec((tile, part), lambda i: (i, 0))
    shape = jax.ShapeDtypeStruct
    return pl.pallas_call(
        feed_forward_kernel,
        name="feed_forward",
        grid=(rows // tile,),
        out_shape=[shape((rows, part), bf16)] * 3 + [shape((rows, width), bf16)] * 2,
        in_specs=[wide, wide] + [any_space] * 3,
        out_specs=[hidden] * 3 + [wide] * 2,
        scratch_shapes=[
            pltpu.VMEM((2, width, part), bf16),
            pltpu.VMEM((part, width), bf16),
            pltpu.SemaphoreType.DMA((3 + wgu.shape[0] * wgu.shape[1] * wgu.shape[2] * wgu.shape[3],)),
        ],
        compiler_params=pltpu.CompilerParams(vmem_limit_bytes=62 * 2**20),
        cost_estimate=pl.CostEstimate(
            flops=12 * rows * width * part, bytes_accessed=10 * width * part, transcendentals=rows * part
        ),
    )(x, cot, wgu, own_gu, down)


def unfold_kernel(gate_ref, up_ref, gate_out, up_out):
    part = gate_ref.shape[3]
    for src, out in ((gate_ref, gate_out), (up_ref, up_out)):
        for t in range(src.shape[1]):
            out[:, t * part : (t + 1) * part] = src[0, t].astype(jnp.float32)


def unfold(gate, up):
    cores, shards, half, part = gate.shape
    tile = 32
    steps = half // tile
    block = pl.BlockSpec((1, shards, tile, part), lambda c, i: (c, 0, i, 0))
    out = pl.BlockSpec((tile, shards * part), lambda c, i: (c * steps + i, 0))
    return pl.pallas_call(
        unfold_kernel,
        name="unfold",
        grid=(cores, steps),
        out_shape=[jax.ShapeDtypeStruct((cores * half, shards * part), jnp.float32)] * 2,
        in_specs=[block, block],
        out_specs=[out, out],
        compiler_params=pltpu.CompilerParams(vmem_limit_bytes=32 * 2**20),
    )(gate, up)


def local(
    hidden_in,
    out_grad,
    doc_lengths,
    piece_starts,
    w_query,
    b_query,
    w_key,
    b_key,
    w_value,
    b_value,
    w_output,
    gain_attn,
    w_gate,
    w_up,
    w_down,
    gain_mlp,
):
    tok_rows = hidden_in.shape[0]
    model_width = hidden_in.shape[1]
    shard_count = lax.axis_size("fsdp")
    row_len = tok_rows * shard_count
    group_size = HEADS // KVH
    kv_width = KVH * HDIM
    ff_width = w_gate.shape[1]
    score_scale = 1.0 / HDIM**0.5
    local_pos = lax.axis_index("fsdp") * tok_rows + jnp.arange(tok_rows, dtype=jnp.int32)
    row_pos = jnp.arange(row_len, dtype=jnp.int32)
    lengths = doc_lengths[0]
    starts = piece_starts[0]
    query_doc, query_rel, query_piece = row_layout(local_pos, lengths, starts, PIECE)
    key_doc, unused_rel, key_piece = row_layout(row_pos, lengths, starts, PIECE)
    allowed = visible_pairs(query_doc, local_pos, query_piece, key_doc, row_pos, key_piece)
    cosine, sine = rope_tables(query_rel, HDIM)
    here = lax.axis_index("fsdp")
    core = lax.axis_index("rep") % 2
    line = lax.axis_size("rep") // 2
    low = jnp.bfloat16

    def gather_rows(weight):
        half = weight.shape[0] // 2
        mine = lax.dynamic_slice_in_dim(weight, core * half, half, 0)
        mine = jnp.stack([jnp.concatenate(p, axis=0) for p in gather_relative(mine, "fsdp")])
        both = core_halves(mine, core_swap(mine), core)
        rows = place([both[:, d] for d in range(shard_count)], here)
        return rows.reshape(2 * half * shard_count, weight.shape[1])

    qkv_full = gather_rows(jnp.concatenate([w_query, w_key, w_value], axis=1))
    query_full = qkv_full[:, :model_width]
    key_full = qkv_full[:, model_width : model_width + kv_width]
    value_full = qkv_full[:, model_width + kv_width :]
    output_full = gather_rows(w_output)
    vectors = lax.all_gather(
        jnp.concatenate([b_query, b_key, b_value, gain_attn, gain_mlp]), "fsdp", axis=0
    )
    cuts = [0]
    for vector in (b_query, b_key, b_value, gain_attn, gain_mlp):
        cuts.append(cuts[-1] + vector.shape[0])
    query_bias, key_bias, value_bias, attn_gain, mlp_gain = (
        vectors[:, cuts[i] : cuts[i + 1]].reshape(-1) for i in range(5)
    )

    part = ff_width // shard_count

    def exchange_columns(weight):
        half = weight.shape[0] // 2
        mine = lax.dynamic_slice_in_dim(weight, core * half, half, 0)
        got = []
        for d in range(shard_count):
            piece = lax.dynamic_slice_in_dim(mine, (here ^ d) * part, part, 1)
            got.append(piece if d == 0 else lax.ppermute(piece, "fsdp", xor_pairs(shard_count, d)))
        got = jnp.stack(got)
        both = core_halves(got, core_swap(got), core)
        rows = place([both[:, d] for d in range(shard_count)], here)
        return rows.reshape(2 * half * shard_count, part)

    gate_part = exchange_columns(w_gate)
    up_part = exchange_columns(w_up)
    cot_all = jnp.concatenate([h for p in gather_relative(out_grad, "fsdp") for h in p], axis=0)
    x_float = hidden_in.astype(jnp.float32)
    inv_first = lax.rsqrt(jnp.mean(x_float * x_float, axis=1, keepdims=True) + epsilon)
    unit_first = x_float * inv_first
    gain_first = attn_gain.astype(jnp.float32)
    normed_first = (unit_first * gain_first).astype(jnp.bfloat16)
    query_pre = mat_dot(normed_first, query_full) + query_bias.astype(jnp.float32)
    key_pre = mat_dot(normed_first, key_full) + key_bias.astype(jnp.float32)
    value_pre = mat_dot(normed_first, value_full) + value_bias.astype(jnp.float32)
    query_rot = rotate(query_pre.reshape(tok_rows, HEADS, HDIM), cosine, sine).astype(jnp.bfloat16)
    key_rot = (
        rotate(key_pre.reshape(tok_rows, KVH, HDIM), cosine, sine)
        .astype(jnp.bfloat16)
        .reshape(tok_rows, kv_width)
    )
    value_low = value_pre.astype(jnp.bfloat16)
    keys_row, values_row = (
        lax.all_gather(key_rot, "fsdp", axis=0, tiled=True),
        lax.all_gather(value_low, "fsdp", axis=0, tiled=True),
    )
    query_grouped = query_rot.reshape(tok_rows, KVH, group_size, HDIM)
    keys_grouped = keys_row.reshape(row_len, KVH, HDIM)
    values_grouped = values_row.reshape(row_len, KVH, HDIM)

    def masked_scores():
        raw_scores = (
            jnp.einsum(
                "tgjd,rgd->gjtr", query_grouped, keys_grouped, preferred_element_type=jnp.float32
            )
            * score_scale
        )
        return jnp.where(allowed[None, None], raw_scores, -1e30)

    scores = masked_scores()
    row_peak = jnp.max(scores, axis=3, keepdims=True)
    expo_vals = jnp.exp(scores - row_peak)
    row_total = jnp.sum(expo_vals, axis=3, keepdims=True)
    soft_probs = expo_vals / row_total
    log_total = row_peak + jnp.log(row_total)
    attn_heads = jnp.einsum(
        "gjtr,rgd->tgjd",
        soft_probs.astype(jnp.bfloat16),
        values_grouped,
        preferred_element_type=jnp.float32,
    )
    attn_low = attn_heads.reshape(tok_rows, model_width).astype(jnp.bfloat16)
    mid_state = x_float + mat_dot(attn_low, output_full)
    inv_second = lax.rsqrt(jnp.mean(mid_state * mid_state, axis=1, keepdims=True) + epsilon)
    unit_second = mid_state * inv_second
    gain_second = mlp_gain.astype(jnp.float32)
    normed_second = (unit_second * gain_second).astype(jnp.bfloat16)
    cot_float = out_grad.astype(jnp.float32)
    normed_all = jnp.concatenate([h for p in gather_relative(normed_second, "fsdp") for h in p], axis=0)
    gate_val = mat_dot(normed_all, gate_part)
    up_val = mat_dot(normed_all, up_part)
    sig_gate = jax.nn.sigmoid(gate_val)
    silu_gate = gate_val * sig_gate
    act_low = (silu_gate * up_val).astype(low)
    d_act = dot_right_t(cot_all, w_down)
    d_gate = (d_act * up_val * sig_gate * (1.0 + gate_val * (1.0 - sig_gate))).astype(low)
    d_up = (d_act * silu_gate).astype(low)
    mlp_part = mat_dot(act_low, w_down).reshape(shard_count, tok_rows, model_width)
    mlp_out = scatter_relative([mlp_part[d] for d in range(shard_count)], "fsdp")
    norm_part = (dot_right_t(d_gate, gate_part) + dot_right_t(d_up, up_part)).reshape(
        shard_count, tok_rows, model_width
    )
    partial_value = scatter_relative([norm_part[d] for d in range(shard_count)], "fsdp")

    def keep_half(grad):
        mine = lax.dynamic_index_in_dim(grad, core, 1, keepdims=False)
        other = lax.dynamic_index_in_dim(grad, 1 - core, 1, keepdims=False)
        return (mine.astype(jnp.float32) + core_swap(other).astype(jnp.float32)).astype(low)

    def both_cores(half):
        return core_halves(half, core_swap(half), core)

    down_grad = dot_left_t(act_low, cot_all).astype(low)
    half = part // 2
    down_half = keep_half(down_grad.reshape(1, 2, half, model_width))[0]
    wide = model_width // line
    down_parts = jnp.stack([down_half[:, q * wide : (q + 1) * wide] for q in range(line)])
    down_own = line_scatter(down_parts).astype(low)
    down_rows = line_gather(down_own)
    down_rows = jnp.concatenate([down_rows[q] for q in range(line)], axis=1)
    down_sums = both_cores(down_rows).reshape(part, model_width).astype(jnp.float32)

    rows = model_width // shard_count
    thin = rows // 2 // line

    def column_grad(d_value):
        grad = dot_left_t(normed_all, d_value).astype(low)
        kept = keep_half(grad.reshape(shard_count, 2, rows // 2, part))
        kept = kept.reshape(shard_count, line, thin, part).transpose(1, 0, 2, 3)
        own = line_scatter(kept).astype(low)
        got = []
        for d in range(shard_count):
            piece = pick(own, here ^ d)
            got.append(piece if d == 0 else lax.ppermute(piece, "fsdp", xor_pairs(shard_count, d)))
        got = place(got, here).transpose(1, 0, 2).reshape(thin, ff_width)
        full = line_gather(got).reshape(rows // 2, ff_width)
        return both_cores(full).reshape(rows, ff_width).astype(jnp.float32)

    grad_gate = column_grad(d_gate)
    grad_up = column_grad(d_up)
    output = mid_state + mlp_out
    d_gain_second = jnp.sum(partial_value * unit_second, axis=0)
    scaled_second = partial_value * gain_second
    d_mid = cot_float + inv_second * (
        scaled_second - unit_second * jnp.mean(scaled_second * unit_second, axis=1, keepdims=True)
    )
    d_branch_low = d_mid.astype(jnp.bfloat16)
    d_attn_low = dot_right_t(d_branch_low, output_full).astype(jnp.bfloat16)
    d_attn_grouped = d_attn_low.reshape(tok_rows, KVH, group_size, HDIM)
    scores = masked_scores()
    soft_back = jnp.exp(scores - log_total)
    probs_low = soft_back.astype(jnp.bfloat16)
    prob_grad = jnp.einsum(
        "tgjd,rgd->gjtr", d_attn_grouped, values_grouped, preferred_element_type=jnp.float32
    )
    row_delta = jnp.sum(soft_back * prob_grad, axis=3, keepdims=True)
    score_grad = (soft_back * (prob_grad - row_delta)).astype(jnp.bfloat16)
    dquery_rot = (
        jnp.einsum("gjtr,rgd->tgjd", score_grad, keys_grouped, preferred_element_type=jnp.float32)
        * score_scale
    )
    dquery_low = (
        unrotate(dquery_rot.reshape(tok_rows, HEADS, HDIM), cosine, sine)
        .reshape(tok_rows, model_width)
        .astype(jnp.bfloat16)
    )
    key_grad = (
        jnp.einsum("gjtr,tgjd->rgd", score_grad, query_grouped, preferred_element_type=jnp.float32)
        * score_scale
    )
    value_grad = jnp.einsum(
        "gjtr,tgjd->rgd", probs_low, d_attn_grouped, preferred_element_type=jnp.float32
    )
    kv_sums = lax.psum_scatter(
        jnp.concatenate(
            [
                key_grad.reshape(lax.axis_size("fsdp") * tok_rows, kv_width),
                value_grad.reshape(lax.axis_size("fsdp") * tok_rows, kv_width),
            ],
            axis=1,
        ).astype(jnp.bfloat16),
        "fsdp",
        scatter_dimension=0,
        tiled=True,
    ).astype(jnp.float32)
    dkey_low = (
        unrotate(kv_sums[:, :kv_width].reshape(tok_rows, KVH, HDIM), cosine, sine)
        .reshape(tok_rows, kv_width)
        .astype(jnp.bfloat16)
    )
    dvalue_low = kv_sums[:, kv_width:].astype(jnp.bfloat16)
    d_norm_first = (
        dot_right_t(dquery_low, query_full)
        + dot_right_t(dkey_low, key_full)
        + dot_right_t(dvalue_low, value_full)
    )
    attn_grads = jnp.concatenate(
        [
            dot_left_t(normed_first, dquery_low).astype(low),
            dot_left_t(normed_first, dkey_low).astype(low),
            dot_left_t(normed_first, dvalue_low).astype(low),
            dot_left_t(attn_low, d_branch_low).astype(low),
        ],
        axis=1,
    )
    attn_wide = attn_grads.shape[1]
    attn_kept = keep_half(attn_grads.reshape(shard_count, 2, rows // 2, attn_wide))
    attn_own = scatter_relative([pick(attn_kept, here ^ d) for d in range(shard_count)], "fsdp").astype(low)
    attn_own = line_scatter(attn_own.reshape(line, thin, attn_wide)).astype(low)
    attn_rows = line_gather(attn_own).reshape(rows // 2, attn_wide)
    attn_sums = both_cores(attn_rows).reshape(rows, attn_wide).astype(jnp.float32)
    d_gain_first = jnp.sum(d_norm_first * unit_first, axis=0)
    scaled_first = d_norm_first * gain_first
    grad_input = d_mid + inv_first * (
        scaled_first - unit_first * jnp.mean(scaled_first * unit_first, axis=1, keepdims=True)
    )
    bias_query = jnp.sum(dquery_low.astype(jnp.float32), axis=0)
    bias_key = jnp.sum(dkey_low.astype(jnp.float32), axis=0)
    bias_value = jnp.sum(dvalue_low.astype(jnp.float32), axis=0)
    small = (bias_query, bias_key, bias_value, d_gain_first, d_gain_second)
    summed = lax.psum(jnp.concatenate(small), ("rep", "fsdp"))
    outs = []
    at = 0
    for vector in small:
        size = vector.shape[0] // shard_count
        outs.append(lax.dynamic_slice_in_dim(summed, at + here * size, size, 0))
        at += vector.shape[0]
    bias_query, bias_key, bias_value, gain_first_sum, gain_second_sum = outs
    grad_query = attn_sums[:, :model_width]
    grad_key = attn_sums[:, model_width : model_width + kv_width]
    grad_value = attn_sums[:, model_width + kv_width : model_width + 2 * kv_width]
    grad_output = attn_sums[:, model_width + 2 * kv_width :]
    return (
        output,
        grad_input,
        grad_query,
        bias_query,
        grad_key,
        bias_key,
        grad_value,
        bias_value,
        grad_output,
        gain_first_sum,
        grad_gate,
        grad_up,
        down_sums,
        gain_second_sum,
    )


def local_fast(
    hidden_in,
    out_grad,
    doc_lengths,
    piece_starts,
    w_query,
    b_query,
    w_key,
    b_key,
    w_value,
    b_value,
    w_output,
    gain_attn,
    w_gate,
    w_up,
    w_down,
    gain_mlp,
):
    tok_rows = hidden_in.shape[0]
    model_width = hidden_in.shape[1]
    shard_count = lax.axis_size("fsdp")
    row_len = tok_rows * shard_count
    group_size = HEADS // KVH
    kv_width = KVH * HDIM
    ff_width = w_gate.shape[1]
    score_scale = 1.0 / HDIM**0.5
    row_pos = jnp.arange(row_len, dtype=jnp.int32)
    lengths = doc_lengths[0]
    starts = piece_starts[0]
    here = lax.axis_index("fsdp")
    core = lax.axis_index("rep") % 2
    line = lax.axis_size("rep") // 2
    line_pos = lax.axis_index("rep") // 2
    low = jnp.bfloat16
    part = ff_width // shard_count
    shard_rows = model_width // shard_count
    thin = shard_rows // 2 // line
    halves = jnp.arange(0, HDIM, 2).astype(jnp.float32) / HDIM
    inverse = rope_base ** (-halves)
    inverse = jnp.broadcast_to(jnp.concatenate([inverse, inverse])[None], (8, HDIM))

    def spread(vector, first, size):
        zeros = jnp.zeros((1, size), jnp.float32)
        return lax.dynamic_update_slice(
            zeros, vector.astype(jnp.float32)[None], (0, first + here * vector.shape[0])
        )

    kv_bias = spread(b_key, 0, model_width) + spread(b_value, kv_width, model_width)
    vec = jnp.concatenate(
        [
            spread(b_query, 0, model_width),
            spread(gain_attn, 0, model_width),
            spread(gain_mlp, 0, model_width),
            kv_bias,
            jnp.zeros((4, model_width), jnp.float32),
        ]
    )
    (
        normed_all,
        cot_all,
        wgu,
        own_gu,
        wqkv_full,
        output_full,
        kv_full,
        mid_state,
        normed_first,
        query_rot,
        attn_low,
        lse,
        trig,
        gains,
    ) = prologue(
        doc_lengths,
        piece_starts,
        hidden_in,
        out_grad,
        vec,
        inverse,
        jnp.concatenate([w_query, w_key, w_value], axis=1),
        w_output,
        w_gate,
        w_up,
    )
    cot_all = cot_all.reshape(row_len, model_width)
    normed_all = normed_all.reshape(row_len, model_width)
    act_low, d_gate, d_up, norm_part, mlp_part = feed_forward(normed_all, cot_all, wgu, own_gu, w_down)
    norm_part, act_low, d_gate, d_up = lax.optimization_barrier((norm_part, act_low, d_gate, d_up))
    norm_part = norm_part.reshape(shard_count, tok_rows, model_width)
    partial_value = scatter_relative([pick(norm_part, here ^ d) for d in range(shard_count)], "fsdp")
    down_part = dot_left_t(act_low, cot_all).astype(low).reshape(2, part // 2, model_width)
    gate_grads = [
        dot_left_t(normed_all, d_value).astype(low).reshape(shard_count, 2, shard_rows // 2, part)
        for d_value in (d_gate, d_up)
    ]
    mlp_part = mlp_part.reshape(shard_count, tok_rows, model_width)
    results = epilogue(
        doc_lengths,
        piece_starts,
        query_rot,
        lse,
        trig,
        gains,
        hidden_in,
        out_grad,
        mid_state,
        partial_value,
        normed_first,
        attn_low,
        mlp_part,
        kv_full,
        wqkv_full,
        output_full,
        down_part,
        gate_grads[0],
        gate_grads[1],
    )
    grad_input, sums, down_final, gate_final, up_final, attn_final = results[:6]
    mlp_land = results[11]
    output = mid_state + pick(mlp_part, here).astype(jnp.float32)
    for d in range(shard_count - 1):
        output = output + mlp_land[d].astype(jnp.float32)
    down_sums = down_final.reshape(part, model_width).astype(jnp.float32)
    grad_gate, grad_up = unfold(gate_final, up_final)
    attn_sums = attn_final.reshape(shard_rows, -1).astype(jnp.float32)
    ends = [0, model_width, model_width + kv_width, model_width + 2 * kv_width, 2 * (model_width + kv_width)]
    grad_query, grad_key, grad_value, grad_output = (attn_sums[:, ends[i] : ends[i + 1]] for i in range(4))

    def shard_of(row, first, size):
        return lax.dynamic_slice(sums, (row, first + here * (size // shard_count)), (1, size // shard_count))[0]

    return (
        output,
        grad_input,
        grad_query,
        shard_of(0, 0, model_width),
        grad_key,
        shard_of(3, 0, kv_width),
        grad_value,
        shard_of(3, kv_width, kv_width),
        grad_output,
        shard_of(1, 0, model_width),
        grad_gate,
        grad_up,
        down_sums,
        shard_of(2, 0, model_width),
    )


def solution(mesh):
    body = local_fast if mesh.shape["fsdp"] == 4 and mesh.shape["rep"] == 8 else local
    placed = (
        P(("rep", "fsdp"), None),
        P(("rep", "fsdp"), None),
        P("rep", None),
        P("rep", None),
        P("fsdp", None),
        P("fsdp"),
        P("fsdp", None),
        P("fsdp"),
        P("fsdp", None),
        P("fsdp"),
        P("fsdp", None),
        P("fsdp"),
        P("fsdp", None),
        P("fsdp", None),
        P("fsdp", None),
        P("fsdp"),
    )
    return jax.shard_map(
        body,
        mesh=mesh,
        in_specs=placed,
        out_specs=(
            P(("rep", "fsdp"), None),
            P(("rep", "fsdp"), None),
            P("fsdp", None),
            P("fsdp"),
            P("fsdp", None),
            P("fsdp"),
            P("fsdp", None),
            P("fsdp"),
            P("fsdp", None),
            P("fsdp"),
            P("fsdp", None),
            P("fsdp", None),
            P("fsdp", None),
            P("fsdp"),
        ),
        check_vma=False,
    )
```

```python
import jax
import jax.numpy as jnp
from jax import lax
from jax.experimental import pallas as pl
from jax.experimental.pallas import tpu as pltpu
from jax.sharding import PartitionSpec as P

HEADS = 12
KVH = 2
HDIM = 128
PIECE = 256


epsilon = 1e-06
rope_base = 1000000.0


def row_layout(positions, lengths, starts, piece_len):
    doc_ends = jnp.cumsum(lengths)
    passed = positions[:, None] >= doc_ends[None, :]
    doc_ids = jnp.sum(passed.astype(jnp.int32), axis=1, dtype=jnp.int32)
    offsets = jnp.sum(jnp.where(passed, lengths[None, :], 0), axis=1, dtype=jnp.int32)
    inside = (positions[:, None] >= starts[None, :]) & (
        positions[:, None] < starts[None, :] + piece_len
    )
    labels = jnp.arange(1, starts.shape[0] + 1, dtype=jnp.int32)
    piece_ids = jnp.sum(jnp.where(inside, labels[None, :], 0), axis=1, dtype=jnp.int32)
    return (doc_ids, positions - offsets, piece_ids)


def visible_pairs(query_doc, query_pos, query_piece, key_doc, key_pos, key_piece):
    same_doc = query_doc[:, None] == key_doc[None, :]
    causal = key_pos[None, :] <= query_pos[:, None]
    same_piece = (query_piece[:, None] == key_piece[None, :]) & (query_piece[:, None] > 0)
    return same_doc & (causal | same_piece)


def rope_tables(relative, head_dim):
    halves = jnp.arange(0, head_dim, 2).astype(jnp.float32) / head_dim
    inverse = rope_base ** (-halves)
    angles = relative.astype(jnp.float32)[:, None] * inverse[None, :]
    angles = jnp.concatenate([angles, angles], axis=1)
    return (jnp.cos(angles), jnp.sin(angles))


def rotate(values, cosine, sine):
    half_dim = values.shape[-1] // 2
    turned = jnp.concatenate([-values[..., half_dim:], values[..., :half_dim]], axis=-1)
    return values * cosine[:, None, :] + turned * sine[:, None, :]


def unrotate(grads, cosine, sine):
    half_dim = grads.shape[-1] // 2
    spun = grads * sine[:, None, :]
    turned_back = jnp.concatenate([spun[..., half_dim:], -spun[..., :half_dim]], axis=-1)
    return grads * cosine[:, None, :] + turned_back


def mat_dot(left, right):
    return jnp.dot(left, right, preferred_element_type=jnp.float32)


def dot_right_t(left, right):
    return lax.dot_general(
        left, right, (((1,), (1,)), ((), ())), preferred_element_type=jnp.float32
    )


def dot_left_t(left, right):
    return lax.dot_general(
        left, right, (((0,), (0,)), ((), ())), preferred_element_type=jnp.float32
    )


def xor_pairs(count, bit):
    return [(i, i ^ bit) for i in range(count)]


def bits_of(count):
    return [1 << k for k in range(count.bit_length() - 1)]


def gather_relative(block, axis):
    count = lax.axis_size(axis)
    bits = bits_of(count)
    half = block.shape[0] // 2
    halves = []
    for part, order in ((block[:half], bits), (block[half:], bits[::-1])):
        have = {0: part}
        for bit in order:
            fresh = {
                d ^ bit: lax.ppermute(piece, axis, xor_pairs(count, bit))
                for d, piece in have.items()
            }
            have.update(fresh)
        halves.append(have)
    return [(halves[0][d], halves[1][d]) for d in range(count)]


def scatter_relative(pieces, axis):
    count = lax.axis_size(axis)
    bits = bits_of(count)
    half = pieces[0].shape[0] // 2
    sums = []
    for lo, hi, order in ((0, half, bits[::-1]), (half, 2 * half, bits)):
        have = {d: pieces[d][lo:hi] for d in range(count)}
        for bit in order:
            come = {
                d ^ bit: lax.ppermute(have[d].astype(jnp.bfloat16), axis, xor_pairs(count, bit))
                for d in have
                if d & bit
            }
            have = {d: have[d].astype(jnp.float32) + come[d].astype(jnp.float32) for d in come}
        sums.append(have[0])
    return jnp.concatenate(sums, axis=0)


def core_swap(block):
    return lax.ppermute(block, "rep", xor_pairs(lax.axis_size("rep"), 1))


def line_pairs(lows, way):
    return [(2 * i + c, 2 * (i + way) + c) for i in lows for c in range(2)]


def pick(array, index):
    return lax.dynamic_index_in_dim(array, index, 0, keepdims=False)


def line_scatter(parts):
    count = lax.axis_size("rep") // 2
    here = lax.axis_index("rep") // 2
    arrived = [None, None]
    for step in range(1, count):
        sends = [
            pick(parts, jnp.clip(count - step + here, 0, count - 1)),
            pick(parts, jnp.clip(here - count + step, 0, count - 1)),
        ]
        for way in range(2):
            if arrived[way] is not None:
                sends[way] = (
                    sends[way].astype(jnp.float32) + arrived[way].astype(jnp.float32)
                ).astype(jnp.bfloat16)
        arrived = [
            lax.ppermute(sends[0], "rep", line_pairs(range(step), 1)),
            lax.ppermute(sends[1], "rep", line_pairs(range(count - step, count), -1)),
        ]
    own = pick(parts, here).astype(jnp.float32)
    return own + arrived[0].astype(jnp.float32) + arrived[1].astype(jnp.float32)


def line_gather(block):
    count = lax.axis_size("rep") // 2
    here = lax.axis_index("rep") // 2
    below, above = [block], [block]
    for step in range(1, count):
        below.append(lax.ppermute(below[-1], "rep", line_pairs(range(step - 1, count - 1), 1)))
        above.append(lax.ppermute(above[-1], "rep", line_pairs(range(1, count - step + 1), -1)))
    stacked = jnp.stack(below[:0:-1] + above)
    return lax.dynamic_slice_in_dim(stacked, count - 1 - here, count, 0)


def core_halves(mine, other, core):
    return jnp.where(core == 0, jnp.stack([mine, other]), jnp.stack([other, mine]))


def place(pieces, here):
    count = len(pieces)
    stacked = jnp.stack(pieces)
    return jnp.stack([pick(stacked, here ^ j) for j in range(count)])


MESH = pl.DeviceIdType.MESH
MASKED = -1e30


def dot_f32(left, right, dims=((1,), (0,))):
    return lax.dot_general(left, right, (dims, ((), ())), preferred_element_type=jnp.float32)


def layout_of(positions, lengths_ref, starts_ref):
    end = jnp.int32(0)
    doc = jnp.zeros_like(positions)
    before = jnp.zeros_like(positions)
    piece = jnp.zeros_like(positions)
    for i in range(lengths_ref.shape[1]):
        end = end + lengths_ref[0, i]
        passed = positions >= end
        doc = doc + jnp.where(passed, 1, 0)
        before = before + jnp.where(passed, lengths_ref[0, i], 0)
    for i in range(starts_ref.shape[1]):
        first = starts_ref[0, i]
        inside = (positions >= first) & (positions < first + PIECE)
        piece = piece + jnp.where(inside, i + 1, 0)
    return doc, positions - before, piece


def mask_bias(here, rows, row_len, lengths_ref, starts_ref):
    query_pos = here * rows + lax.broadcasted_iota(jnp.int32, (rows, 1), 0)
    key_pos = lax.broadcasted_iota(jnp.int32, (1, row_len), 1)
    query_doc, query_rel, query_piece = layout_of(query_pos, lengths_ref, starts_ref)
    key_doc, unused, key_piece = layout_of(key_pos, lengths_ref, starts_ref)
    allowed = (query_doc == key_doc) & (
        (key_pos <= query_pos) | ((query_piece == key_piece) & (query_piece > 0))
    )
    return jnp.where(allowed, 0.0, MASKED), query_rel


class Links:
    def __init__(self):
        self.here = lax.axis_index("fsdp")
        self.rep = lax.axis_index("rep")
        self.core = lax.rem(self.rep, 2)
        self.line = self.rep // 2
        reps = lax.axis_size("rep")
        here = self.here
        self.near = [here, here + 1 - 2 * lax.rem(here, 2), lax.rem(here + 2, 4), 3 - here]
        self.plane = [{"fsdp": index} for index in self.near]
        self.partner = {"rep": self.rep + 1 - 2 * self.core}
        self.up = {"rep": lax.rem(self.rep + 2, reps)}
        self.down = {"rep": lax.rem(self.rep + reps - 2, reps)}

    def greet(self, line=True):
        barrier = pltpu.get_barrier_semaphore()
        others = self.plane[1:] + ([self.partner, self.up, self.down] if line else [])
        for other in others:
            pl.semaphore_signal(barrier, inc=1, device_id=other, device_id_type=MESH)
        pl.semaphore_wait(barrier, len(others))


def remote(src, dst, sems, index, device):
    return pltpu.make_async_remote_copy(
        src_ref=src,
        dst_ref=dst,
        send_sem=sems.at[0, index],
        recv_sem=sems.at[1, index],
        device_id=device,
        device_id_type=MESH,
    )


class PlaneGather:
    def __init__(self, links, own, slot, rows, sems):
        x, y = links.plane[1], links.plane[2]
        here, near_x, near_y, far = links.near
        half = rows // 2

        def part(index, lo):
            return slot(index).at[pl.ds(lo, half)]

        self.first = [
            remote(own, slot(here), sems, 0, x),
            remote(own, slot(here), sems, 1, y),
        ]
        self.second = [
            remote(part(near_x, 0), part(near_x, 0), sems, 2, y),
            remote(part(near_y, half), part(near_y, half), sems, 3, x),
        ]
        self.come = [
            remote(slot(near_x), slot(near_x), sems, 0, x),
            remote(slot(near_y), slot(near_y), sems, 1, y),
            remote(part(far, 0), part(far, 0), sems, 2, y),
            remote(part(far, half), part(far, half), sems, 3, x),
        ]

    def start(self):
        for copy in self.first:
            copy.start()

    def hand_on(self):
        for i in range(2):
            self.come[i].wait_recv()
            self.second[i].start()

    def finish(self):
        for i in (2, 3):
            self.come[i].wait_recv()

    def drain(self):
        for copy in self.first + self.second:
            copy.wait_send()


def prologue_kernel(
    lengths_ref,
    starts_ref,
    x_ref,
    cot_ref,
    vec_ref,
    inverse_ref,
    wqkv_ref,
    wo_ref,
    gate_ref,
    up_ref,
    normed_all,
    cot_all,
    wgu,
    own_gu,
    wqkv_full,
    wo_full,
    kv_full,
    mid_ref,
    normed_first_ref,
    query_ref,
    attn_ref,
    lse_ref,
    trig_ref,
    gains_ref,
    vec_all,
    wqkv_buf,
    wo_buf,
    kv_buf,
    normed_buf,
    bias_ref,
    thin_buf,
    gu_ref,
    wide_buf,
    own_buf,
    cut_sems,
    local_sems,
    vec_sems,
    qkv_sems,
    qkv_core,
    wo_sems,
    wo_core,
    kv_sems,
    cot_sems,
    norm_sems,
    gu_sems,
    up_sems,
    down_sems,
    own_core,
    up_core,
    down_core,
):
    links = Links()
    here, core, line = links.here, links.core, links.line
    count = lax.axis_size("rep") // 2
    rows, width = x_ref.shape
    shard = wqkv_ref.shape[0]
    half = shard // 2
    links.greet()

    def shard_rows(ref, index):
        return ref.at[pl.ds(pl.multiple_of(index * shard, shard), shard)]

    own_copies = [
        pltpu.make_async_copy(wqkv_ref, shard_rows(wqkv_buf, here), local_sems.at[0]),
        pltpu.make_async_copy(wo_ref, shard_rows(wo_buf, here), local_sems.at[1]),
        pltpu.make_async_copy(cot_ref, cot_all.at[here], local_sems.at[2]),
        pltpu.make_async_copy(vec_ref, vec_all.at[here], local_sems.at[3]),
    ]

    vec_sends = [remote(vec_ref, vec_all.at[here], vec_sems, d - 1, links.plane[d]) for d in (1, 2, 3)]
    vec_comes = [
        remote(vec_ref, vec_all.at[links.near[d]], vec_sems, d - 1, links.plane[d]) for d in (1, 2, 3)
    ]

    def half_rows(ref, index, which):
        return ref.at[pl.ds(pl.multiple_of(index * shard + which * half, half), half)]

    def weight_gather(src, buf, sems, core_sems):
        gather = PlaneGather(
            links,
            src.at[pl.ds(pl.multiple_of(core * half, half), half)],
            lambda index: half_rows(buf, index, core),
            half,
            sems,
        )
        swaps = [
            remote(
                half_rows(buf, links.near[d], core),
                half_rows(buf, links.near[d], core),
                core_sems,
                d - 1,
                links.partner,
            )
            for d in (1, 2, 3)
        ]
        comes = [
            remote(
                half_rows(buf, links.near[d], 1 - core),
                half_rows(buf, links.near[d], 1 - core),
                core_sems,
                d - 1,
                links.partner,
            )
            for d in (1, 2, 3)
        ]
        return gather, swaps, comes

    qkv_gather, qkv_swaps, qkv_comes = weight_gather(wqkv_ref, wqkv_buf, qkv_sems, qkv_core)
    wo_gather, wo_swaps, wo_comes = weight_gather(wo_ref, wo_buf, wo_sems, wo_core)
    cot_gather = PlaneGather(links, cot_ref, lambda index: cot_all.at[index], rows, cot_sems)
    norm_gather = PlaneGather(links, normed_buf, lambda index: normed_all.at[index], rows, norm_sems)

    gu_sends = [
        remote(gu_ref.at[links.near[d]], wgu.at[core, line, d - 1], gu_sems, d - 1, links.plane[d])
        for d in (1, 2, 3)
    ]
    own_block = wgu.at[core, line]
    own_swap = remote(own_block, own_block, own_core, 0, links.partner)
    own_come = remote(wgu.at[1 - core, line], wgu.at[1 - core, line], own_core, 0, links.partner)

    class Hop:
        def __init__(self, k, way):
            sems = up_sems if way > 0 else down_sems
            core_sems = up_core if way > 0 else down_core
            device = links.up if way > 0 else links.down
            back = links.down if way > 0 else links.up
            sent = jnp.clip(line - way * (k - 1), 0, count - 1)
            come = jnp.clip(line - way * k, 0, count - 1)
            if way > 0:
                self.sends = (line <= count - 2) & (line >= k - 1)
                self.comes = line >= k
            else:
                self.sends = (line >= 1) & (line + k - 1 <= count - 1)
                self.comes = line + k <= count - 1
            self.send = remote(wgu.at[core, sent], wgu.at[core, sent], sems, k - 1, device)
            self.recv = remote(wgu.at[core, come], wgu.at[core, come], sems, k - 1, back)
            self.swap = remote(wgu.at[core, come], wgu.at[core, come], core_sems, k - 1, links.partner)
            self.swap_come = remote(
                wgu.at[1 - core, come], wgu.at[1 - core, come], core_sems, k - 1, links.partner
            )

    hops = [(Hop(k, 1), Hop(k, -1)) for k in range(1, count)]

    def start_hop(k):
        for hop in hops[k - 1]:
            pl.when(hop.sends)(hop.send.start)

    def take_hop(k):
        for hop in hops[k - 1]:

            @pl.when(hop.comes)
            def _():
                hop.recv.wait_recv()
                hop.swap.start()

    thin, part = gu_ref.shape[2:]
    first_row = pl.multiple_of(core * half + line * thin, thin)
    cuts = [
        pltpu.make_async_copy(ref.at[pl.ds(first_row, thin)], thin_buf.at[i], cut_sems.at[i])
        for i, ref in enumerate((gate_ref, up_ref))
    ] + [
        pltpu.make_async_copy(ref, wide_buf.at[i], cut_sems.at[2 + i])
        for i, ref in enumerate((gate_ref, up_ref))
    ]
    for copy in vec_sends + cuts:
        copy.start()
    qkv_gather.start()
    for copy in cuts[:2]:
        copy.wait()
    for t in range(4):
        gu_ref[t] = thin_buf[:, :, t * part : (t + 1) * part]
    for copy in own_copies:
        copy.start()

    bias, query_rel = mask_bias(here, rows, kv_buf.shape[0] * rows, lengths_ref, starts_ref)
    bias_ref[...] = bias
    angles = query_rel.astype(jnp.float32) * inverse_ref[0:1, :]
    lanes = lax.broadcasted_iota(jnp.int32, (1, HDIM), 1)
    cosine = jnp.cos(angles)
    sine = jnp.sin(angles) * jnp.where(lanes < HDIM // 2, -1.0, 1.0)
    trig_ref[0] = cosine
    trig_ref[1] = sine

    x_float = x_ref[...].astype(jnp.float32)
    unit = x_float * lax.rsqrt(jnp.mean(x_float * x_float, axis=1, keepdims=True) + epsilon)
    own_copies[3].wait()
    for copy in vec_comes:
        copy.wait_recv()
    gains_ref[...] = vec_all[0] + vec_all[1] + vec_all[2] + vec_all[3]
    normed_first_ref[...] = (unit * gains_ref[1:2, :]).astype(jnp.bfloat16)

    qkv_gather.hand_on()
    for swap in qkv_swaps[:2]:
        swap.start()
    for copy in gu_sends:
        copy.start()
    qkv_gather.finish()
    qkv_swaps[2].start()
    own_copies[0].wait()
    for copy in qkv_comes:
        copy.wait_recv()

    full_copy = pltpu.make_async_copy(wqkv_buf, wqkv_full, local_sems.at[4])
    full_copy.start()

    def rope(value):
        return value * trig_ref[0] + pltpu.roll(value, HDIM // 2, 1) * trig_ref[1]

    def project(first, bias_row):
        columns = pl.ds(pl.multiple_of(first, 2 * HDIM), 2 * HDIM)
        return dot_f32(normed_first_ref[...], wqkv_buf[:, columns]) + bias_row

    keys = project(width, gains_ref[3:4, 0 : 2 * HDIM])
    own_kv = kv_buf.at[here]
    for h in range(2):
        kv_buf[here, :, h * HDIM : (h + 1) * HDIM] = rope(keys[:, h * HDIM : (h + 1) * HDIM]).astype(
            jnp.bfloat16
        )
    values = project(width + 2 * HDIM, gains_ref[3:4, 2 * HDIM : 4 * HDIM])
    kv_buf[here, :, 2 * HDIM : 4 * HDIM] = values.astype(jnp.bfloat16)
    kv_sends = [remote(own_kv, own_kv, kv_sems, d - 1, links.plane[d]) for d in (1, 2, 3)]
    kv_comes = [
        remote(kv_buf.at[links.near[d]], kv_buf.at[links.near[d]], kv_sems, d - 1, links.plane[d])
        for d in (1, 2, 3)
    ]
    for copy in kv_sends:
        copy.start()
    wo_gather.start()

    def query_pair(pair, carry):
        columns = pl.ds(pl.multiple_of(pair * 2 * HDIM, 2 * HDIM), 2 * HDIM)
        got = project(pair * 2 * HDIM, gains_ref[0:1, columns])
        for h in range(2):
            where = pl.ds(pl.multiple_of(pair * 2 * HDIM + h * HDIM, HDIM), HDIM)
            query_ref[:, where] = rope(got[:, h * HDIM : (h + 1) * HDIM]).astype(jnp.bfloat16)
        return carry

    lax.fori_loop(0, HEADS // 2, query_pair, 0)
    for copy in cuts[2:]:
        copy.wait()
    for t in range(4):

        @pl.when(here == t)
        def _():
            own_buf[...] = wide_buf[:, :, t * part : (t + 1) * part]

    own_store = pltpu.make_async_copy(own_buf, own_gu, cut_sems.at[0])
    own_store.start()
    for copy in gu_sends:
        copy.wait_recv()
    start_hop(1)
    own_swap.start()
    for copy in kv_comes:
        copy.wait_recv()
    kv_copy = pltpu.make_async_copy(kv_buf, kv_full, local_sems.at[5])
    kv_copy.start()

    group = HEADS // KVH
    row_len = kv_buf.shape[0] * rows
    head_lane = lax.broadcasted_iota(jnp.int32, (1, HDIM), 1)

    def head_step(h, lse):
        columns = pl.ds(pl.multiple_of(h * HDIM, HDIM), HDIM)
        shared = h // group
        key = kv_buf[:, :, pl.ds(pl.multiple_of(shared * HDIM, HDIM), HDIM)].reshape(row_len, HDIM)
        value = kv_buf[:, :, pl.ds(pl.multiple_of((KVH + shared) * HDIM, HDIM), HDIM)].reshape(
            row_len, HDIM
        )
        scores = dot_f32(query_ref[:, columns], key, ((1,), (1,))) * (1.0 / HDIM**0.5) + bias_ref[...]
        peak = jnp.max(scores, axis=1, keepdims=True)
        expo = jnp.exp(scores - peak)
        total = jnp.sum(expo, axis=1, keepdims=True)
        mixed = dot_f32(expo.astype(jnp.bfloat16), value) / total
        attn_ref[:, columns] = mixed.astype(jnp.bfloat16)
        return jnp.where(head_lane == h, peak + jnp.log(total), lse)

    lse = lax.fori_loop(0, 2 * HEADS // 3, head_step, jnp.zeros((rows, HDIM), jnp.float32))
    wo_gather.hand_on()
    for swap in wo_swaps[:2]:
        swap.start()
    cot_gather.start()
    lse_ref[...] = lax.fori_loop(2 * HEADS // 3, HEADS, head_step, lse)
    take_hop(1)
    start_hop(2)
    wo_gather.finish()
    wo_swaps[2].start()
    own_copies[1].wait()
    for copy in wo_comes:
        copy.wait_recv()
    wo_copy = pltpu.make_async_copy(wo_buf, wo_full, local_sems.at[6])
    wo_copy.start()

    def out_columns(i, carry):
        columns = pl.ds(pl.multiple_of(i * 256, 256), 256)
        mid_ref[:, columns] = x_ref[:, columns].astype(jnp.float32) + dot_f32(
            attn_ref[...], wo_buf[:, columns]
        )
        return carry

    lax.fori_loop(0, width // 256, out_columns, 0)
    mid = mid_ref[...]
    unit = mid * lax.rsqrt(jnp.mean(mid * mid, axis=1, keepdims=True) + epsilon)
    normed_buf[...] = (unit * gains_ref[2:3, :]).astype(jnp.bfloat16)
    norm_gather.start()
    norm_copy = pltpu.make_async_copy(normed_buf, normed_all.at[here], local_sems.at[7])
    norm_copy.start()
    cot_gather.hand_on()
    take_hop(2)
    start_hop(3)
    norm_gather.hand_on()
    cot_gather.finish()
    take_hop(3)
    norm_gather.finish()

    own_copies[2].wait()
    own_store.wait()
    full_copy.wait()
    kv_copy.wait()
    wo_copy.wait()
    norm_copy.wait()
    for copy in vec_sends + gu_sends + qkv_swaps + wo_swaps + kv_sends + [own_swap]:
        copy.wait_send()
    own_come.wait_recv()
    for copy in wo_comes[:0]:
        copy.wait_recv()
    for gather in (qkv_gather, wo_gather, cot_gather, norm_gather):
        gather.drain()
    for pair in hops:
        for hop in pair:
            pl.when(hop.sends)(hop.send.wait_send)

            @pl.when(hop.comes)
            def _():
                hop.swap.wait_send()
                hop.swap_come.wait_recv()


def prologue(lengths, starts, x, cot, vec, inverse, wqkv, wo, gate, up):
    rows, width = x.shape
    shards = lax.axis_size("fsdp")
    count = lax.axis_size("rep") // 2
    shard = gate.shape[0]
    thin, part = shard // (2 * count), gate.shape[1] // shards
    bf16, f32 = jnp.bfloat16, jnp.float32
    any_space = pl.BlockSpec(memory_space=pl.ANY)
    vmem = pl.BlockSpec(memory_space=pltpu.VMEM)
    smem = pl.BlockSpec(memory_space=pltpu.SMEM)
    shape = jax.ShapeDtypeStruct

    def sems(n):
        return pltpu.SemaphoreType.DMA((2, n))

    return pl.pallas_call(
        prologue_kernel,
        name="prologue",
        out_shape=(
            shape((shards, rows, width), bf16),
            shape((shards, rows, width), bf16),
            shape((2, count, shards - 1, 2, thin, part), bf16),
            shape((2, shard, part), bf16),
            shape((width, wqkv.shape[1]), bf16),
            shape((width, width), bf16),
            shape((shards, rows, 4 * HDIM), bf16),
            shape((rows, width), f32),
            shape((rows, width), bf16),
            shape((rows, width), bf16),
            shape((rows, width), bf16),
            shape((rows, HDIM), f32),
            shape((2, rows, HDIM), f32),
            shape((8, width), f32),
        ),
        in_specs=[smem, smem, vmem, vmem, vmem, vmem] + [any_space] * 4,
        out_specs=[any_space] * 7 + [vmem] * 7,
        scratch_shapes=[
            pltpu.VMEM((shards, 8, width), f32),
            pltpu.VMEM((width, wqkv.shape[1]), bf16),
            pltpu.VMEM((width, width), bf16),
            pltpu.VMEM((shards, rows, 4 * HDIM), bf16),
            pltpu.VMEM((rows, width), bf16),
            pltpu.VMEM((rows, shards * rows), f32),
            pltpu.VMEM((2, thin, gate.shape[1]), bf16),
            pltpu.VMEM((shards, 2, thin, part), bf16),
            pltpu.VMEM((2, shard, gate.shape[1]), bf16),
            pltpu.VMEM((2, shard, part), bf16),
            pltpu.SemaphoreType.DMA((4,)),
            pltpu.SemaphoreType.DMA((8,)),
            sems(3),
            sems(4),
            sems(3),
            sems(4),
            sems(3),
            sems(3),
            sems(4),
            sems(4),
            sems(3),
            sems(count - 1),
            sems(count - 1),
            sems(1),
            sems(count - 1),
            sems(count - 1),
        ],
        compiler_params=pltpu.CompilerParams(
            collective_id=0, has_side_effects=True, vmem_limit_bytes=60 * 2**20
        ),
    )(lengths, starts, x, cot, vec, inverse, wqkv, wo, gate, up)


class Stream:
    def __init__(self, links, pairs, size, own, land_end, land_mid, final, loads, stage, sems, local_sems, targets):
        self.links, self.pairs, self.size = links, pairs, size
        self.own, self.land_end, self.land_mid, self.final = own, land_end, land_mid, final
        self.loads, self.stage, self.sems, self.local_sems = loads, stage, sems, local_sems
        self.targets = targets
        self.near = links.line // 2
        self.far = 1 - self.near
        self.busy = {}

    def rows(self, kind, p):
        return pl.ds(pl.multiple_of((kind * self.pairs + p) * self.size, self.size), self.size)

    def copy(self, src, dst, p, index, device):
        return pltpu.make_async_remote_copy(
            src_ref=src,
            dst_ref=dst,
            send_sem=self.sems.at[0, p, index],
            recv_sem=self.sems.at[1, p, index],
            device_id=device,
            device_id_type=MESH,
        )

    def load(self, refs, first):
        copies = [
            pltpu.make_async_copy(ref, self.loads.at[first + i], self.local_sems.at[first + i])
            for i, ref in enumerate(refs)
        ]
        for copy in copies:
            copy.start()

        def total():
            for copy in copies:
                copy.wait()
            out = self.loads[first].astype(jnp.float32)
            for i in range(1, len(refs)):
                out = out + self.loads[first + i].astype(jnp.float32)
            return out.astype(jnp.bfloat16)

        return total

    def free(self, role, which, p):
        for copy in self.busy.pop((role, which, p % 2), list)():
            copy.wait_send()

    def hold(self, role, which, p, make):
        copies = make()
        for copy in copies:
            copy.start()
        self.busy[(role, which, p % 2)] = make

    def finals(self, p, which):
        links = self.links
        near, far = self.rows(self.near, p), self.rows(self.far, p)
        ref_near, ref_far = self.final(links.core, near), self.final(links.core, far)
        plans = (
            (ref_near, 3, links.away),
            (ref_near, 4, links.toward),
            (ref_far, 5, links.away),
            (ref_near, 6, links.partner),
            (ref_far, 7, links.partner),
        )
        return [
            self.copy(ref, ref, p, index, device)
            for i, (ref, index, device) in enumerate(plans)
            if i in which
        ]

    def end_send(self, p):
        totals = [
            self.load(self.own(self.rows(kind, p)), first) for first, kind in ((0, self.far), (2, self.near))
        ]
        for which in range(2):
            self.free("end", which, p)
            self.stage[which, p % 2] = totals[which]()
            self.hold(
                "end",
                which,
                p,
                lambda which=which: [
                    self.copy(
                        self.stage.at[which, p % 2], self.land_end.at[p, which], p, which, self.links.toward
                    )
                ],
            )

    def pass_load(self, p):
        self.copy(self.land_end.at[p, 0], self.land_end.at[p, 0], p, 0, self.links.away).wait_recv()
        return self.load(self.own(self.rows(self.far, p)) + [self.land_end.at[p, 0]], 4)

    def mid_pass(self, p, total):
        self.free("mid", 0, p)
        self.stage[0, p % 2] = total()
        self.hold(
            "mid",
            0,
            p,
            lambda: [self.copy(self.stage.at[0, p % 2], self.land_mid.at[p], p, 2, self.links.toward)],
        )

    def sum_load(self, p):
        links = self.links
        self.copy(self.land_end.at[p, 1], self.land_end.at[p, 1], p, 1, links.away).wait_recv()
        self.copy(self.land_mid.at[p], self.land_mid.at[p], p, 2, links.toward).wait_recv()
        near = self.rows(self.near, p)
        return self.load(self.own(near) + [self.land_end.at[p, 1], self.land_mid.at[p]], 0)

    def mid_sum(self, p, total):
        links = self.links
        self.free("mid", 1, p)
        self.stage[1, p % 2] = total()
        self.own_copy(p).start()

        def sends():
            buf = self.stage.at[1, p % 2]
            near = self.rows(self.near, p)
            final = self.final(links.core, near)
            if self.targets:
                ref = self.target(links.core, near, links.here)
                return [
                    self.copy(buf.at[links.near[d]], ref, p, 7 + d, links.plane[d]) for d in (1, 2, 3)
                ]
            return [
                self.copy(buf, final, p, 3, links.away),
                self.copy(buf, final, p, 4, links.toward),
                self.copy(buf, final, p, 6, links.partner),
            ]

        self.hold("mid", 1, p, sends)

    def own_copy(self, p):
        links = self.links
        buf, near = self.stage.at[1, p % 2], self.rows(self.near, p)
        final = self.final(links.core, near)
        if self.targets:
            buf, final = buf.at[links.here], self.target(links.core, near, links.here)
        return pltpu.make_async_copy(buf, final, self.local_sems.at[7 + p % 2])

    def target(self, core, rows, source):
        return self.final(core, rows).at[source]

    def mid_out(self, p):
        links = self.links
        self.own_copy(p).wait()
        if not self.targets:
            return
        near = self.rows(self.near, p)
        for d in (1, 2, 3):
            ref = self.target(links.core, near, links.near[d])
            self.copy(ref, ref, p, 7 + d, links.plane[d]).wait_recv()
        for copy in self.finals(p, (0, 1, 3)):
            copy.start()

    def mid_far(self, p):
        far = self.final(self.links.core, self.rows(self.far, p))
        self.copy(far, far, p, 4, self.links.toward).wait_recv()
        for copy in self.finals(p, (2, 4)):
            copy.start()

    def end_take(self, p):
        for kind, index, out in ((self.near, 3, 3), (self.far, 5, 4)):
            ref = self.final(self.links.core, self.rows(kind, p))
            self.copy(ref, ref, p, index, self.links.toward).wait_recv()
            self.finals(p, (out,))[0].start()

    def close_mid(self):
        for key in [k for k in self.busy if k[0] == "mid"]:
            for copy in self.busy.pop(key)():
                copy.wait_send()
        for p in range(self.pairs):
            for copy in self.finals(p, (0, 1, 2, 3, 4) if self.targets else (2, 4)):
                copy.wait_send()

    def close_end(self):
        for key in [k for k in self.busy if k[0] == "end"]:
            for copy in self.busy.pop(key)():
                copy.wait_send()
        for p in range(self.pairs):
            for copy in self.finals(p, (3, 4)):
                copy.wait_send()

    def close_core(self):
        for p in range(self.pairs):
            for kind, index in ((self.near, 6), (self.far, 7)):
                ref = self.final(1 - self.links.core, self.rows(kind, p))
                self.copy(ref, ref, p, index, self.links.partner).wait_recv()


class WeightSum:
    def __init__(self, links, product, land, own, half_buf, load_buf, first, second, send, half_sems, plane_sems, sem):
        self.links, self.product, self.land, self.own = links, product, land, own
        self.half_buf, self.load_buf, self.first, self.second, self.send = half_buf, load_buf, first, second, send
        self.half_sems, self.sem = half_sems, sem
        self.quarter = half_buf.shape[1] // 2
        near_x, near_y, far = links.near[1:]
        low, high = pl.ds(0, self.quarter), pl.ds(self.quarter, self.quarter)
        self.first_sends = [
            remote(half_buf.at[near_y, low], first.at[0], plane_sems, 0, links.plane[2]),
            remote(half_buf.at[far, low], first.at[1], plane_sems, 1, links.plane[2]),
            remote(half_buf.at[near_x, high], first.at[2], plane_sems, 2, links.plane[1]),
            remote(half_buf.at[far, high], first.at[3], plane_sems, 3, links.plane[1]),
        ]
        self.second_sends = [
            remote(send.at[0], second.at[0], plane_sems, 4, links.plane[1]),
            remote(send.at[1], second.at[1], plane_sems, 5, links.plane[2]),
        ]
        self.half_sends = [
            remote(half_buf.at[t], land.at[t], half_sems, t, links.partner) for t in range(4)
        ]

    def other_half(self):
        def one(t, carry):
            self.half_buf[t] = self.product(t, 1 - self.links.core).astype(jnp.bfloat16)
            return carry

        lax.fori_loop(0, 4, one, 0)
        for copy in self.half_sends:
            copy.start()

    def own_half(self):
        for copy in self.half_sends:
            copy.wait_send()
            copy.wait_recv()

        def one(t, carry):
            load = pltpu.make_async_copy(self.land.at[t], self.load_buf, self.sem)
            load.start()
            got = self.product(t, self.links.core)
            load.wait()
            self.half_buf[t] = (got + self.load_buf[...].astype(jnp.float32)).astype(jnp.bfloat16)
            return carry

        lax.fori_loop(0, 4, one, 0)
        for copy in self.first_sends:
            copy.start()

    def plane_turn(self):
        for copy in self.first_sends:
            copy.wait_recv()
        near_x, near_y, far = self.links.near[1:]
        for i, near in ((0, near_x), (1, near_y)):
            at = slice(i * self.quarter, (i + 1) * self.quarter)
            self.send[i] = (
                self.half_buf[near, at].astype(jnp.float32) + self.first[2 * i + 1].astype(jnp.float32)
            ).astype(jnp.bfloat16)
        for copy in self.second_sends:
            copy.start()

    def plane_end(self):
        for copy in self.second_sends + self.first_sends:
            copy.wait_send()
        for copy in self.second_sends:
            copy.wait_recv()
        for i in range(2):
            at = slice(i * self.quarter, (i + 1) * self.quarter)
            self.load_buf[at, :] = (
                self.half_buf[self.links.here, at].astype(jnp.float32)
                + self.first[2 * i].astype(jnp.float32)
                + self.second[i].astype(jnp.float32)
            ).astype(jnp.bfloat16)
        store = pltpu.make_async_copy(self.load_buf, self.own, self.sem)
        store.start()
        store.wait()


def epilogue_kernel(
    lengths_ref,
    starts_ref,
    query_ref,
    lse_ref,
    trig_ref,
    gains_ref,
    x_hbm,
    cot_hbm,
    mid_hbm,
    normed_hbm,
    attn_hbm,
    kv_hbm,
    wqkv_hbm,
    wo_hbm,
    act_hbm,
    dgate_hbm,
    dup_hbm,
    normed_all,
    cot_all,
    w_hbm,
    down_hbm,
    grad_input_ref,
    sums_ref,
    down_final,
    gate_final,
    up_final,
    out_final,
    qkv_final,
    down_core,
    gate_core,
    up_core,
    out_core,
    qkv_core,
    out_own,
    qkv_own,
    mlp_land,
    mlp_own,
    norm_land,
    norm_parts,
    mlp_parts,
    down_own,
    gate_own,
    up_own,
    down_end,
    down_mid,
    gate_end,
    gate_mid,
    up_end,
    up_mid,
    out_end,
    out_mid,
    qkv_end,
    qkv_mid,
    kv_buf,
    key_turned,
    bias_ref,
    lse_turned,
    dmid_ref,
    branch_ref,
    dattn_ref,
    dqkv_ref,
    dkey_ref,
    dvalue_ref,
    kv_out,
    kv_land,
    normed_turned,
    attn_turned,
    out_half,
    out_load,
    out_first,
    out_second,
    out_send,
    qkv_half,
    qkv_load,
    qkv_first,
    qkv_second,
    qkv_send,
    vec_plane,
    vec_core,
    vec_line,
    vec_send,
    norm_own,
    down_loads,
    down_stage,
    gu_loads,
    gate_stage,
    out_loads,
    out_stage,
    qkv_loads,
    qkv_stage,
    local_sems,
    scope_sems,
    norm_sems,
    mlp_sems,
    load_sems,
    core_sems,
    kv_sems,
    half_sems,
    plane_sems,
    qkv_half_sems,
    qkv_plane_sems,
    vec_sems,
    down_sems,
    gate_sems,
    up_sems,
    out_sems,
    qkv_sems,
):
    links = Links()
    here, core, line = links.here, links.core, links.line
    rows, width = x_hbm.shape
    scale = 1.0 / HDIM**0.5
    group = HEADS // KVH
    bf16, f32 = jnp.bfloat16, jnp.float32
    step = 2 - 4 * (line // 2)
    links.toward = {"rep": links.rep + step}
    links.away = {"rep": links.rep - step}
    is_end = (line == 0) | (line == 3)
    is_mid = (line == 1) | (line == 2)

    barrier = pltpu.get_barrier_semaphore()
    line_others = [{"rep": 2 * lax.rem(line + j, 4) + core} for j in (1, 2, 3)]
    others = links.plane[1:] + [links.partner] + line_others
    for other in others:
        pl.semaphore_signal(barrier, inc=1, device_id=other, device_id_type=MESH)
    pl.semaphore_wait(barrier, len(others))

    fetches = [pltpu.make_async_copy(kv_hbm, kv_buf, local_sems.at[1])]
    fetches[0].start()
    core_comes = [
        remote(ref, ref, core_sems, i, links.partner) for i, ref in enumerate((down_core, gate_core, up_core))
    ]

    def stream(size, total, own, end, mid, final, loads, stage, sems, targets=False):
        return Stream(
            links, total // (2 * size), size, own, end, mid, final, loads, stage, sems, load_sems, targets
        )

    down = stream(
        down_stage.shape[2],
        down_core.shape[0],
        lambda r: [down_own.at[r], down_core.at[r]],
        down_end,
        down_mid,
        lambda c, r: down_final.at[c, r],
        down_loads,
        down_stage,
        down_sems,
    )
    gate = stream(
        gate_stage.shape[3],
        gate_core.shape[1],
        lambda r: [gate_own.at[:, r], gate_core.at[:, r]],
        gate_end,
        gate_mid,
        lambda c, r: gate_final.at[c, :, r],
        gu_loads,
        gate_stage,
        gate_sems,
        True,
    )
    up = stream(
        gate_stage.shape[3],
        up_core.shape[1],
        lambda r: [up_own.at[:, r], up_core.at[:, r]],
        up_end,
        up_mid,
        lambda c, r: up_final.at[c, :, r],
        gu_loads,
        gate_stage,
        up_sems,
        True,
    )
    up.busy = gate.busy
    out = stream(
        out_stage.shape[2],
        out_own.shape[0],
        lambda r: [out_own.at[r]],
        out_end,
        out_mid,
        lambda c, r: out_final.at[c, r],
        out_loads,
        out_stage,
        out_sems,
    )
    qkv = stream(
        qkv_stage.shape[2],
        qkv_own.shape[0],
        lambda r: [qkv_own.at[r]],
        qkv_end,
        qkv_mid,
        lambda c, r: qkv_final.at[c, r],
        qkv_loads,
        qkv_stage,
        qkv_sems,
    )
    streams = (down, gate, up, out, qkv)
    pairs = [(s, p) for s in streams for p in range(s.pairs)]

    def when(i):
        far = i + (4 if pairs[i][0].targets else 3)
        return {
            "end_send": i,
            "mid_pass": i + 1,
            "mid_sum": i + 2,
            "mid_out": i + 3,
            "mid_far": far,
            "end_take": far + 1,
        }

    def service(n):
        def due(action):
            return [pairs[i] for i in range(len(pairs)) if when(i)[action] == n]

        first = {0: down, down.pairs: gate, down.pairs + gate.pairs: up}
        if n in first:
            core_comes[list(first).index(n)].wait_recv()

        @pl.when(is_end)
        def _():
            for s, p in due("end_take"):
                s.end_take(p)
            for s, p in due("end_send"):
                s.end_send(p)

        @pl.when(is_mid)
        def _():
            for s, p in due("mid_far"):
                s.mid_far(p)
            for s, p in due("mid_out"):
                s.mid_out(p)
            sums = [(s, p, s.sum_load(p)) for s, p in due("mid_sum")]
            passes = [(s, p, s.pass_load(p)) for s, p in due("mid_pass")]
            for s, p, total in sums:
                s.mid_sum(p, total)
            for s, p, total in passes:
                s.mid_pass(p, total)

    def scoped(refs, body):
        def inner(*bufs):
            copies = [pltpu.make_async_copy(r, b, scope_sems.at[i]) for i, (r, b) in enumerate(zip(refs, bufs))]
            for copy in copies:
                copy.start()
            for copy in copies:
                copy.wait()
            body(*bufs)

        pl.run_scoped(inner, *[pltpu.VMEM(r.shape, r.dtype) for r in refs])

    def norm_back():
        for d in range(3):
            remote(norm_land.at[d], norm_land.at[d], norm_sems, d, links.plane[d + 1]).wait_recv()
        scoped((mid_hbm, norm_land, cot_hbm), norm_body)

    def norm_body(mid_ref, land_ref, cot_ref):
        mid = mid_ref[...]
        inv = lax.rsqrt(jnp.mean(mid * mid, axis=1, keepdims=True) + epsilon)
        unit = mid * inv
        part = norm_own[...]
        for d in range(3):
            part = part + land_ref[d].astype(f32)
        vec_send[2:3, :] = jnp.sum(part * unit, axis=0, keepdims=True)
        scaled = part * gains_ref[2:3, :]
        d_mid = cot_ref[...].astype(f32) + inv * (
            scaled - unit * jnp.mean(scaled * unit, axis=1, keepdims=True)
        )
        dmid_ref[...] = d_mid
        branch_ref[...] = d_mid.astype(bf16)
        query_pos = here * rows + lax.broadcasted_iota(jnp.int32, (1, rows), 1)
        key_pos = lax.broadcasted_iota(jnp.int32, (4 * rows, 1), 0)
        query_doc, unused, query_piece = layout_of(query_pos, lengths_ref, starts_ref)
        key_doc, unused, key_piece = layout_of(key_pos, lengths_ref, starts_ref)
        allowed = (query_doc == key_doc) & (
            (key_pos <= query_pos) | ((query_piece == key_piece) & (query_piece > 0))
        )
        bias_ref[...] = jnp.where(allowed, 0.0, MASKED)
        lse_turned[...] = lse_ref[...].T

    def attn_back():
        scoped((wo_hbm,), attn_body)

    def attn_body(wo_buf):
        scoped((normed_hbm, attn_hbm), turn_body)

        def tile(i, carry):
            columns = pl.ds(pl.multiple_of(i * 256, 256), 256)
            dattn_ref[:, columns] = dot_f32(branch_ref[...], wo_buf[columns, :], ((1,), (1,))).astype(bf16)
            return carry

        lax.fori_loop(0, width // 256, tile, 0)
        fetches[0].wait()
        for g in range(KVH):
            key_turned[g] = kv_buf[:, :, g * HDIM : (g + 1) * HDIM].reshape(4 * rows, HDIM).T
        dkey_ref[...] = jnp.zeros_like(dkey_ref)
        dvalue_ref[...] = jnp.zeros_like(dvalue_ref)

    def head_back(h, carry):
        columns = pl.ds(pl.multiple_of(h * HDIM, HDIM), HDIM)
        shared = h // group
        key = kv_buf[:, :, pl.ds(pl.multiple_of(shared * HDIM, HDIM), HDIM)].reshape(4 * rows, HDIM)
        value = kv_buf[:, :, pl.ds(pl.multiple_of((KVH + shared) * HDIM, HDIM), HDIM)].reshape(
            4 * rows, HDIM
        )
        query, d_out = query_ref[:, columns], dattn_ref[:, columns]
        scores = dot_f32(key, query, ((1,), (1,))) * scale + bias_ref[...]
        probs = jnp.exp(scores - lse_turned[pl.ds(h, 1), :])
        d_probs = dot_f32(value, d_out, ((1,), (1,)))
        delta = jnp.sum(probs * d_probs, axis=0, keepdims=True)
        d_scores = (probs * (d_probs - delta)).astype(bf16)
        dkey_ref[shared] += dot_f32(d_scores, query)
        dvalue_ref[shared] += dot_f32(probs.astype(bf16), d_out)
        d_query = dot_f32(key_turned[shared], d_scores).T * scale
        d_query = d_query * trig_ref[0] - pltpu.roll(d_query, HDIM // 2, 1) * trig_ref[1]
        dqkv_ref[:, columns] = d_query.astype(bf16)
        return carry

    kv_sends = [
        remote(kv_out.at[links.near[d]], kv_land.at[d - 1], kv_sems, d - 1, links.plane[d]) for d in (1, 2, 3)
    ]

    def kv_send():
        for g in range(KVH):
            kv_out[:, :, g * HDIM : (g + 1) * HDIM] = (
                (dkey_ref[g] * scale).astype(bf16).reshape(4, rows, HDIM)
            )
            kv_out[:, :, (KVH + g) * HDIM : (KVH + g + 1) * HDIM] = (
                dvalue_ref[g].astype(bf16).reshape(4, rows, HDIM)
            )
        for copy in kv_sends:
            copy.start()

    vec_copies = {
        "plane": [remote(vec_send, vec_plane.at[here], vec_sems, d - 1, links.plane[d]) for d in (1, 2, 3)],
        "core": [remote(vec_core.at[core], vec_core.at[core], vec_sems, 3, links.partner)],
        "line": [
            remote(vec_line.at[line], vec_line.at[line], vec_sems, 4 + j, line_others[j]) for j in range(3)
        ],
    }
    vec_comes = {
        "plane": [
            remote(vec_send, vec_plane.at[links.near[d]], vec_sems, d - 1, links.plane[d]) for d in (1, 2, 3)
        ],
        "core": [remote(vec_core.at[core], vec_core.at[1 - core], vec_sems, 3, links.partner)],
        "line": [
            remote(
                vec_line.at[line],
                vec_line.at[lax.rem(line + 3 - j, 4)],
                vec_sems,
                4 + j,
                line_others[2 - j],
            )
            for j in range(3)
        ],
    }

    def input_back():
        for d in (1, 2, 3):
            remote(kv_land.at[d - 1], kv_land.at[d - 1], kv_sems, d - 1, links.plane[d]).wait_recv()
        kv = kv_out[here].astype(f32)
        for d in range(3):
            kv = kv + kv_land[d].astype(f32)
        for g in range(KVH):
            d_key = kv[:, g * HDIM : (g + 1) * HDIM]
            d_key = d_key * trig_ref[0] - pltpu.roll(d_key, HDIM // 2, 1) * trig_ref[1]
            dqkv_ref[:, width + g * HDIM : width + (g + 1) * HDIM] = d_key.astype(bf16)
        dqkv_ref[:, width + KVH * HDIM :] = kv[:, KVH * HDIM :].astype(bf16)
        scoped((wqkv_hbm, x_hbm), input_body)

    def turn_body(normed_ref, attn_ref):
        normed_turned[...] = normed_ref[...].T
        attn_turned[...] = attn_ref[...].T

    def input_body(wqkv_buf, x_ref):
        def tile(i, carry):
            columns = pl.ds(pl.multiple_of(i * 256, 256), 256)
            grad_input_ref[:, columns] = dot_f32(dqkv_ref[...], wqkv_buf[columns, :], ((1,), (1,)))
            return carry

        lax.fori_loop(0, width // 256, tile, 0)
        x = x_ref[...].astype(f32)
        inv = lax.rsqrt(jnp.mean(x * x, axis=1, keepdims=True) + epsilon)
        unit = x * inv
        part = grad_input_ref[...]
        vec_send[1:2, :] = jnp.sum(part * unit, axis=0, keepdims=True)
        scaled = part * gains_ref[1:2, :]
        grad_input_ref[...] = dmid_ref[...] + inv * (
            scaled - unit * jnp.mean(scaled * unit, axis=1, keepdims=True)
        )
        sums = jnp.sum(dqkv_ref[...].astype(f32), axis=0, keepdims=True)
        vec_send[0:1, :] = sums[:, :width]
        vec_send[3:4, 0 : 2 * KVH * HDIM] = sums[:, width:]
        vec_send[3:4, 2 * KVH * HDIM :] = jnp.zeros((1, width - 2 * KVH * HDIM), f32)
        vec_send[4:8, :] = jnp.zeros((4, width), f32)
        vec_plane[here] = vec_send[...]
        for copy in vec_copies["plane"]:
            copy.start()

    shard = width // 4
    half = shard // 2

    def row_block(t, which):
        return pl.ds(pl.multiple_of(t * shard + which * half, half), half)

    out_sum = WeightSum(
        links,
        lambda t, which: dot_f32(attn_turned[row_block(t, which), :], branch_ref[...]),
        out_core,
        out_own,
        out_half,
        out_load,
        out_first,
        out_second,
        out_send,
        half_sems,
        plane_sems,
        local_sems.at[3],
    )
    qkv_sum = WeightSum(
        links,
        lambda t, which: dot_f32(normed_turned[row_block(t, which), :], dqkv_ref[...]),
        qkv_core,
        qkv_own,
        qkv_half,
        qkv_load,
        qkv_first,
        qkv_second,
        qkv_send,
        qkv_half_sems,
        qkv_plane_sems,
        local_sems.at[3],
    )

    def vec_core_step():
        for copy in vec_comes["plane"]:
            copy.wait_recv()
        vec_core[core] = vec_plane[0] + vec_plane[1] + vec_plane[2] + vec_plane[3]
        vec_copies["core"][0].start()

    def vec_line_step():
        vec_comes["core"][0].wait_recv()
        vec_line[line] = vec_core[0] + vec_core[1]
        for copy in vec_copies["line"]:
            copy.start()

    def vec_end():
        for copy in vec_comes["line"]:
            copy.wait_recv()
        sums_ref[...] = vec_line[0] + vec_line[1] + vec_line[2] + vec_line[3]

    done = [0]

    def tick():
        service(done[0])
        done[0] += 1

    def fetch(src, dst, i):
        return pltpu.make_async_copy(src, dst, scope_sems.at[i])

    def down_grads(act_buf, cot_buf, send_buf, keep_buf):
        loads = [fetch(act_hbm, act_buf, 0), fetch(cot_all, cot_buf, 1)]
        for load in loads:
            load.start()
        for load in loads:
            load.wait()
        units, cols = keep_buf.shape

        def product(which, out):
            at = pl.ds(pl.multiple_of(which * cols, cols), cols)
            for lo in range(0, units, 768):
                part = slice(lo, min(lo + 768, units))
                out[part, :] = dot_f32(act_buf[:, part], cot_buf[:, at], ((0,), (0,))).astype(bf16)

        product(1 - core, send_buf)
        send = remote(send_buf, down_core, core_sems, 0, links.partner)
        send.start()
        product(core, keep_buf)
        keep = fetch(keep_buf, down_own, 0)
        keep.start()
        keep.wait()
        send.wait_send()

    def column_grads(turned, value_buf, send_buf, keep_buf):
        def turn(normed_buf):
            load = fetch(normed_all, normed_buf, 1)
            load.start()
            load.wait()
            turned[...] = normed_buf[...].T.reshape(turned.shape)

        def product(which, out):
            left = turned[:, which].reshape(width // 2, turned.shape[3])
            cols = value_buf.shape[1]
            for lo in range(0, cols, 512):
                at = slice(lo, min(lo + 512, cols))
                out[:, :, at] = dot_f32(left, value_buf[:, at]).astype(bf16).reshape(4, width // 8, -1)

        load = fetch(dgate_hbm, value_buf, 0)
        load.start()
        pl.run_scoped(turn, pltpu.VMEM(normed_all.shape, bf16))
        for i, (land, own) in enumerate(((gate_core, gate_own), (up_core, up_own))):
            load.wait()
            send = remote(send_buf, land, core_sems, 1 + i, links.partner)
            product(1 - core, send_buf)
            send.start()
            tick()
            product(core, keep_buf)
            if i == 0:
                load = fetch(dup_hbm, value_buf, 0)
                load.start()
            keep = fetch(keep_buf, own, 1)
            keep.start()
            tick()
            keep.wait()
            send.wait_send()

    order = (1, 2, 3, 0)

    def token_sends(parts, land, sems):
        return [
            remote(parts.at[i], land.at[order[i] - 1], sems, order[i] - 1, links.plane[order[i]]) for i in range(3)
        ]

    def token_blocks(inputs, weights, product, sems, parts, land, keep, store, ticks):
        depth = 3 - len(inputs)

        def body(weight_buf, block_buf, send_buf):
            def block_loads(i):
                return [
                    fetch(ref.at[links.near[order[i]]], block_buf.at[i % depth, j], 2 * (i % depth) + j)
                    for j, ref in enumerate(inputs)
                ]

            load = pltpu.make_async_copy(weights, weight_buf, local_sems.at[2])
            load.start()
            for copy in block_loads(0):
                copy.start()
            load.wait()
            sends = token_sends(parts, land, sems)
            for i, d in enumerate(order):
                if i < 3 and depth > 1:
                    for copy in block_loads(i + 1):
                        copy.start()
                for copy in block_loads(i):
                    copy.wait()
                for lo in range(0, width, 512):
                    at = slice(lo, lo + 512)
                    got = product(block_buf.at[i % depth], weight_buf, at)
                    if d == 0 and store is None:
                        keep[:, at] = got
                    else:
                        send_buf[i % 2, :, at] = got.astype(bf16)
                if d or store is not None:
                    copy = fetch(send_buf.at[i % 2], parts.at[i] if d else store, 3)
                    copy.start()
                    copy.wait()
                if d:
                    sends[i].start()
                if i < 3 and depth == 1:
                    for copy in block_loads(i + 1):
                        copy.start()
                if i in ticks:
                    tick()

        pl.run_scoped(
            body,
            pltpu.VMEM(weights.shape, bf16),
            pltpu.VMEM((depth, len(inputs)) + inputs[0].shape[1:], bf16),
            pltpu.VMEM((2, rows, width), bf16),
        )

    def norm_product(block, weight, at):
        return dot_f32(block[0], weight[0, at, :], ((1,), (1,))) + dot_f32(
            block[1], weight[1, at, :], ((1,), (1,))
        )

    def mlp_product(block, weight, at):
        return dot_f32(block[0], weight[:, at])

    units = act_hbm.shape[1]

    def by_block(ref):
        return ref.reshape(4, rows, units)

    pl.run_scoped(
        down_grads,
        pltpu.VMEM(act_hbm.shape, bf16),
        pltpu.VMEM(cot_all.shape, bf16),
        pltpu.VMEM(down_own.shape, bf16),
        pltpu.VMEM(down_own.shape, bf16),
    )
    tick()
    token_blocks(
        (by_block(dgate_hbm), by_block(dup_hbm)), w_hbm, norm_product, norm_sems, norm_parts, norm_land, norm_own, None, (0, 1, 2, 3)
    )
    pl.run_scoped(
        column_grads,
        pltpu.VMEM((4, 2, width // 8, normed_all.shape[0]), bf16),
        pltpu.VMEM(dgate_hbm.shape, bf16),
        pltpu.VMEM(gate_own.shape, bf16),
        pltpu.VMEM(gate_own.shape, bf16),
    )
    norm_back()
    tick()
    attn_back()
    tick()
    out_sum.other_half()
    lax.fori_loop(0, 2, head_back, 0)
    tick()
    out_sum.own_half()
    lax.fori_loop(2, 4, head_back, 0)
    tick()
    lax.fori_loop(4, 7, head_back, 0)
    tick()
    out_sum.plane_turn()
    lax.fori_loop(7, 10, head_back, 0)
    tick()
    lax.fori_loop(10, 12, head_back, 0)
    kv_send()
    tick()
    out_sum.plane_end()
    tick()
    input_back()
    tick()
    qkv_sum.other_half()
    vec_core_step()
    tick()
    qkv_sum.own_half()
    vec_line_step()
    tick()
    qkv_sum.plane_turn()
    vec_end()
    tick()
    qkv_sum.plane_end()
    assert down.pairs + gate.pairs + up.pairs + out.pairs >= done[0]
    tick()
    token_blocks((by_block(act_hbm),), down_hbm, mlp_product, mlp_sems, mlp_parts, mlp_land, None, mlp_own, (0, 1, 2, 3))
    while done[0] <= len(pairs) + 3:
        tick()

    for copy in kv_sends + token_sends(norm_parts, norm_land, norm_sems) + token_sends(mlp_parts, mlp_land, mlp_sems):
        copy.wait_send()
    for d in range(3):
        remote(mlp_land.at[d], mlp_land.at[d], mlp_sems, d, links.plane[d + 1]).wait_recv()
    for name in vec_copies:
        for copy in vec_copies[name]:
            copy.wait_send()

    @pl.when(is_end)
    def _():
        for s in streams:
            s.close_end()

    @pl.when(is_mid)
    def _():
        for s in streams:
            s.close_mid()

    for s in streams:
        s.close_core()


def epilogue(lengths, starts, query, lse, trig, gains, *others):
    x, wqkv, act, normed_all, w_full = others[0], others[6], others[8], others[11], others[13]
    rows, width = x.shape
    bf16, f32 = jnp.bfloat16, jnp.float32
    any_space = pl.BlockSpec(memory_space=pl.ANY)
    vmem = pl.BlockSpec(memory_space=pltpu.VMEM)
    smem = pl.BlockSpec(memory_space=pltpu.SMEM)
    shape = jax.ShapeDtypeStruct
    half = width // 8
    cols = act.shape[1]
    down_size, gu_size, attn_size = 160, 16, 32
    down_pairs = cols // (2 * down_size)
    gu_pairs = half // (2 * gu_size)
    attn_pairs = half // (2 * attn_size)
    down_chunk = (down_size, width // 2)
    gu_chunk = (4, gu_size, cols)
    out_chunk, qkv_chunk = (attn_size, width), (attn_size, wqkv.shape[1])

    def line_buffers(pairs, chunk):
        return [shape((pairs, 2) + chunk, bf16), shape((pairs,) + chunk, bf16)]

    def sems(*n):
        return pltpu.SemaphoreType.DMA((2,) + n)

    def weight_buffers(cols):
        return [
            pltpu.VMEM((4, half, cols), bf16),
            pltpu.VMEM((half, cols), bf16),
            pltpu.VMEM((4, half // 2, cols), bf16),
            pltpu.VMEM((2, half // 2, cols), bf16),
            pltpu.VMEM((2, half // 2, cols), bf16),
        ]

    outs = [
        shape((rows, width), f32),
        shape((8, width), f32),
        shape((2, cols, width // 2), bf16),
        shape((2, 4, half, cols), bf16),
        shape((2, 4, half, cols), bf16),
        shape((2, half, width), bf16),
        shape((2, half, wqkv.shape[1]), bf16),
        shape((cols, width // 2), bf16),
        shape((4, half, cols), bf16),
        shape((4, half, cols), bf16),
        shape((4, half, width), bf16),
        shape((4, half, wqkv.shape[1]), bf16),
        shape((half, width), bf16),
        shape((half, wqkv.shape[1]), bf16),
        shape((3, rows, width), bf16),
        shape((rows, width), bf16),
        shape((3, rows, width), bf16),
        shape((3, rows, width), bf16),
        shape((3, rows, width), bf16),
        shape((cols, width // 2), bf16),
        shape((4, half, cols), bf16),
        shape((4, half, cols), bf16),
    ]
    outs += line_buffers(down_pairs, down_chunk)
    outs += line_buffers(gu_pairs, gu_chunk) + line_buffers(gu_pairs, gu_chunk)
    outs += line_buffers(attn_pairs, out_chunk) + line_buffers(attn_pairs, qkv_chunk)
    return pl.pallas_call(
        epilogue_kernel,
        name="epilogue",
        out_shape=tuple(outs),
        in_specs=[smem] * 2 + [vmem] * 4 + [any_space] * len(others),
        out_specs=[vmem] * 2 + [any_space] * (len(outs) - 2),
        scratch_shapes=[
            pltpu.VMEM((4, rows, 4 * HDIM), bf16),
            pltpu.VMEM((KVH, HDIM, 4 * rows), bf16),
            pltpu.VMEM((4 * rows, rows), f32),
            pltpu.VMEM((HDIM, rows), f32),
            pltpu.VMEM((rows, width), f32),
            pltpu.VMEM((rows, width), bf16),
            pltpu.VMEM((rows, width), bf16),
            pltpu.VMEM((rows, wqkv.shape[1]), bf16),
            pltpu.VMEM((KVH, 4 * rows, HDIM), f32),
            pltpu.VMEM((KVH, 4 * rows, HDIM), f32),
            pltpu.VMEM((4, rows, 4 * HDIM), bf16),
            pltpu.VMEM((3, rows, 4 * HDIM), bf16),
            pltpu.VMEM((width, rows), bf16),
            pltpu.VMEM((width, rows), bf16),
            *weight_buffers(width),
            *weight_buffers(wqkv.shape[1]),
            pltpu.VMEM((4, 8, width), f32),
            pltpu.VMEM((2, 8, width), f32),
            pltpu.VMEM((4, 8, width), f32),
            pltpu.VMEM((8, width), f32),
            pltpu.VMEM((rows, width), f32),
            pltpu.VMEM((7,) + down_chunk, bf16),
            pltpu.VMEM((2, 2) + down_chunk, bf16),
            pltpu.VMEM((7,) + gu_chunk, bf16),
            pltpu.VMEM((2, 2) + gu_chunk, bf16),
            pltpu.VMEM((7,) + out_chunk, bf16),
            pltpu.VMEM((2, 2) + out_chunk, bf16),
            pltpu.VMEM((7,) + qkv_chunk, bf16),
            pltpu.VMEM((2, 2) + qkv_chunk, bf16),
            pltpu.SemaphoreType.DMA((4,)),
            pltpu.SemaphoreType.DMA((4,)),
            sems(3),
            sems(3),
            pltpu.SemaphoreType.DMA((9,)),
            sems(3),
            sems(3),
            sems(4),
            sems(6),
            sems(4),
            sems(6),
            sems(7),
            sems(down_pairs, 11),
            sems(gu_pairs, 11),
            sems(gu_pairs, 11),
            sems(attn_pairs, 11),
            sems(attn_pairs, 11),
        ],
        compiler_params=pltpu.CompilerParams(
            collective_id=1, has_side_effects=True, vmem_limit_bytes=63 * 2**20
        ),
    )(lengths, starts, query, lse, trig, gains, *others)


class Place:
    def __init__(self):
        here = lax.axis_index("fsdp")
        self.near = [here, here + 1 - 2 * lax.rem(here, 2), lax.rem(here + 2, 4), 3 - here]


def feed_forward_kernel(
    x_ref, cot_ref, wgu, own_gu, down_hbm, act_ref, dgate_ref, dup_ref, w_hbm, w_ref, down_ref, sems
):
    f32, bf16 = jnp.float32, jnp.bfloat16
    cores, line, others, kinds, thin, part = wgu.shape
    shard = own_gu.shape[1]

    @pl.when(pl.program_id(0) == 0)
    def _():
        near = Place().near
        copies = [pltpu.make_async_copy(down_hbm, down_ref, sems.at[0])]
        for g in range(kinds):
            at = pl.multiple_of(near[0] * shard, shard)
            copies.append(
                pltpu.make_async_copy(own_gu.at[g], w_ref.at[g, pl.ds(at, shard)], sems.at[1 + g])
            )
        n = 1 + kinds
        for d in range(1, 4):
            for c in range(cores):
                for z in range(line):
                    for g in range(kinds):
                        at = pl.multiple_of(near[d] * shard + (c * line + z) * thin, thin)
                        copies.append(
                            pltpu.make_async_copy(
                                wgu.at[c, z, d - 1, g], w_ref.at[g, pl.ds(at, thin)], sems.at[n]
                            )
                        )
                        n += 1
        for copy in copies:
            copy.start()
        for copy in copies:
            copy.wait()
        pltpu.make_async_copy(w_ref, w_hbm, sems.at[0]).start()

    x, cot = x_ref[...], cot_ref[...]
    for lo in range(0, part, 512):
        at = slice(lo, min(lo + 512, part))
        gate = dot_f32(x, w_ref[0, :, at])
        up = dot_f32(x, w_ref[1, :, at])
        d_act = dot_f32(cot, down_ref[at, :], ((1,), (1,)))
        sig = jax.nn.sigmoid(gate)
        silu = gate * sig
        act_ref[:, at] = (silu * up).astype(bf16)
        dgate_ref[:, at] = (d_act * up * sig * (1.0 + gate * (1.0 - sig))).astype(bf16)
        dup_ref[:, at] = (d_act * silu).astype(bf16)

    @pl.when(pl.program_id(0) == pl.num_programs(0) - 1)
    def _():
        pltpu.make_async_copy(w_ref, w_hbm, sems.at[0]).wait()


def feed_forward(x, cot, wgu, own_gu, down):
    rows, width = x.shape
    part = down.shape[0]
    tile = rows // 4
    bf16 = jnp.bfloat16
    any_space = pl.BlockSpec(memory_space=pl.ANY)
    wide = pl.BlockSpec((tile, width), lambda i: (i, 0))
    hidden = pl.BlockSpec((tile, part), lambda i: (i, 0))
    shape = jax.ShapeDtypeStruct
    return pl.pallas_call(
        feed_forward_kernel,
        name="feed_forward",
        grid=(rows // tile,),
        out_shape=[shape((rows, part), bf16)] * 3 + [shape((2, width, part), bf16)],
        in_specs=[wide, wide] + [any_space] * 3,
        out_specs=[hidden] * 3 + [any_space],
        scratch_shapes=[
            pltpu.VMEM((2, width, part), bf16),
            pltpu.VMEM((part, width), bf16),
            pltpu.SemaphoreType.DMA((3 + wgu.shape[0] * wgu.shape[1] * wgu.shape[2] * wgu.shape[3],)),
        ],
        compiler_params=pltpu.CompilerParams(vmem_limit_bytes=62 * 2**20),
        cost_estimate=pl.CostEstimate(
            flops=6 * rows * width * part, bytes_accessed=10 * width * part, transcendentals=rows * part
        ),
    )(x, cot, wgu, own_gu, down)


def unfold_kernel(gate_ref, up_ref, out_ref, qkv_ref, gate_out, up_out, out_out, query_out, key_out, value_out):
    part = gate_ref.shape[3]
    for src, out in ((gate_ref, gate_out), (up_ref, up_out)):
        for t in range(src.shape[1]):
            out[:, t * part : (t + 1) * part] = src[0, t].astype(jnp.float32)
    out_out[...] = out_ref[0].astype(jnp.float32)
    first = 0
    for out in (query_out, key_out, value_out):
        out[...] = qkv_ref[0, :, first : first + out.shape[1]].astype(jnp.float32)
        first += out.shape[1]


def unfold(gate, up, out, qkv):
    cores, shards, half, part = gate.shape
    width = out.shape[2]
    narrow = KVH * HDIM
    tile = 32
    steps = half // tile
    wides = [shards * part] * 2 + [width, width, narrow, narrow]
    block = pl.BlockSpec((1, shards, tile, part), lambda c, i: (c, 0, i, 0))

    def flat(cols):
        return pl.BlockSpec((1, tile, cols), lambda c, i: (c, i, 0))

    return pl.pallas_call(
        unfold_kernel,
        name="unfold",
        grid=(cores, steps),
        out_shape=[jax.ShapeDtypeStruct((cores * half, wide), jnp.float32) for wide in wides],
        in_specs=[block, block, flat(width), flat(qkv.shape[2])],
        out_specs=[pl.BlockSpec((tile, wide), lambda c, i: (c * steps + i, 0)) for wide in wides],
        compiler_params=pltpu.CompilerParams(vmem_limit_bytes=32 * 2**20),
    )(gate, up, out, qkv)


def join_kernel(down_ref, out):
    cols = down_ref.shape[2]
    for c in range(2):
        out[:, c * cols : (c + 1) * cols] = down_ref[c].astype(jnp.float32)


def join(down):
    cores, rows, cols = down.shape
    tile = rows // 7
    return pl.pallas_call(
        join_kernel,
        name="join",
        grid=(rows // tile,),
        out_shape=jax.ShapeDtypeStruct((rows, cores * cols), jnp.float32),
        in_specs=[pl.BlockSpec((cores, tile, cols), lambda i: (0, i, 0))],
        out_specs=pl.BlockSpec((tile, cores * cols), lambda i: (i, 0)),
        compiler_params=pltpu.CompilerParams(vmem_limit_bytes=32 * 2**20),
    )(down)


def local(
    hidden_in,
    out_grad,
    doc_lengths,
    piece_starts,
    w_query,
    b_query,
    w_key,
    b_key,
    w_value,
    b_value,
    w_output,
    gain_attn,
    w_gate,
    w_up,
    w_down,
    gain_mlp,
):
    tok_rows = hidden_in.shape[0]
    model_width = hidden_in.shape[1]
    shard_count = lax.axis_size("fsdp")
    row_len = tok_rows * shard_count
    group_size = HEADS // KVH
    kv_width = KVH * HDIM
    ff_width = w_gate.shape[1]
    score_scale = 1.0 / HDIM**0.5
    local_pos = lax.axis_index("fsdp") * tok_rows + jnp.arange(tok_rows, dtype=jnp.int32)
    row_pos = jnp.arange(row_len, dtype=jnp.int32)
    lengths = doc_lengths[0]
    starts = piece_starts[0]
    query_doc, query_rel, query_piece = row_layout(local_pos, lengths, starts, PIECE)
    key_doc, unused_rel, key_piece = row_layout(row_pos, lengths, starts, PIECE)
    allowed = visible_pairs(query_doc, local_pos, query_piece, key_doc, row_pos, key_piece)
    cosine, sine = rope_tables(query_rel, HDIM)
    here = lax.axis_index("fsdp")
    core = lax.axis_index("rep") % 2
    line = lax.axis_size("rep") // 2
    low = jnp.bfloat16

    def gather_rows(weight):
        half = weight.shape[0] // 2
        mine = lax.dynamic_slice_in_dim(weight, core * half, half, 0)
        mine = jnp.stack([jnp.concatenate(p, axis=0) for p in gather_relative(mine, "fsdp")])
        both = core_halves(mine, core_swap(mine), core)
        rows = place([both[:, d] for d in range(shard_count)], here)
        return rows.reshape(2 * half * shard_count, weight.shape[1])

    qkv_full = gather_rows(jnp.concatenate([w_query, w_key, w_value], axis=1))
    query_full = qkv_full[:, :model_width]
    key_full = qkv_full[:, model_width : model_width + kv_width]
    value_full = qkv_full[:, model_width + kv_width :]
    output_full = gather_rows(w_output)
    vectors = lax.all_gather(
        jnp.concatenate([b_query, b_key, b_value, gain_attn, gain_mlp]), "fsdp", axis=0
    )
    cuts = [0]
    for vector in (b_query, b_key, b_value, gain_attn, gain_mlp):
        cuts.append(cuts[-1] + vector.shape[0])
    query_bias, key_bias, value_bias, attn_gain, mlp_gain = (
        vectors[:, cuts[i] : cuts[i + 1]].reshape(-1) for i in range(5)
    )

    part = ff_width // shard_count

    def exchange_columns(weight):
        half = weight.shape[0] // 2
        mine = lax.dynamic_slice_in_dim(weight, core * half, half, 0)
        got = []
        for d in range(shard_count):
            piece = lax.dynamic_slice_in_dim(mine, (here ^ d) * part, part, 1)
            got.append(piece if d == 0 else lax.ppermute(piece, "fsdp", xor_pairs(shard_count, d)))
        got = jnp.stack(got)
        both = core_halves(got, core_swap(got), core)
        rows = place([both[:, d] for d in range(shard_count)], here)
        return rows.reshape(2 * half * shard_count, part)

    gate_part = exchange_columns(w_gate)
    up_part = exchange_columns(w_up)
    cot_all = jnp.concatenate([h for p in gather_relative(out_grad, "fsdp") for h in p], axis=0)
    x_float = hidden_in.astype(jnp.float32)
    inv_first = lax.rsqrt(jnp.mean(x_float * x_float, axis=1, keepdims=True) + epsilon)
    unit_first = x_float * inv_first
    gain_first = attn_gain.astype(jnp.float32)
    normed_first = (unit_first * gain_first).astype(jnp.bfloat16)
    query_pre = mat_dot(normed_first, query_full) + query_bias.astype(jnp.float32)
    key_pre = mat_dot(normed_first, key_full) + key_bias.astype(jnp.float32)
    value_pre = mat_dot(normed_first, value_full) + value_bias.astype(jnp.float32)
    query_rot = rotate(query_pre.reshape(tok_rows, HEADS, HDIM), cosine, sine).astype(jnp.bfloat16)
    key_rot = (
        rotate(key_pre.reshape(tok_rows, KVH, HDIM), cosine, sine)
        .astype(jnp.bfloat16)
        .reshape(tok_rows, kv_width)
    )
    value_low = value_pre.astype(jnp.bfloat16)
    keys_row, values_row = (
        lax.all_gather(key_rot, "fsdp", axis=0, tiled=True),
        lax.all_gather(value_low, "fsdp", axis=0, tiled=True),
    )
    query_grouped = query_rot.reshape(tok_rows, KVH, group_size, HDIM)
    keys_grouped = keys_row.reshape(row_len, KVH, HDIM)
    values_grouped = values_row.reshape(row_len, KVH, HDIM)

    def masked_scores():
        raw_scores = (
            jnp.einsum(
                "tgjd,rgd->gjtr", query_grouped, keys_grouped, preferred_element_type=jnp.float32
            )
            * score_scale
        )
        return jnp.where(allowed[None, None], raw_scores, -1e30)

    scores = masked_scores()
    row_peak = jnp.max(scores, axis=3, keepdims=True)
    expo_vals = jnp.exp(scores - row_peak)
    row_total = jnp.sum(expo_vals, axis=3, keepdims=True)
    soft_probs = expo_vals / row_total
    log_total = row_peak + jnp.log(row_total)
    attn_heads = jnp.einsum(
        "gjtr,rgd->tgjd",
        soft_probs.astype(jnp.bfloat16),
        values_grouped,
        preferred_element_type=jnp.float32,
    )
    attn_low = attn_heads.reshape(tok_rows, model_width).astype(jnp.bfloat16)
    mid_state = x_float + mat_dot(attn_low, output_full)
    inv_second = lax.rsqrt(jnp.mean(mid_state * mid_state, axis=1, keepdims=True) + epsilon)
    unit_second = mid_state * inv_second
    gain_second = mlp_gain.astype(jnp.float32)
    normed_second = (unit_second * gain_second).astype(jnp.bfloat16)
    cot_float = out_grad.astype(jnp.float32)
    normed_all = jnp.concatenate([h for p in gather_relative(normed_second, "fsdp") for h in p], axis=0)
    gate_val = mat_dot(normed_all, gate_part)
    up_val = mat_dot(normed_all, up_part)
    sig_gate = jax.nn.sigmoid(gate_val)
    silu_gate = gate_val * sig_gate
    act_low = (silu_gate * up_val).astype(low)
    d_act = dot_right_t(cot_all, w_down)
    d_gate = (d_act * up_val * sig_gate * (1.0 + gate_val * (1.0 - sig_gate))).astype(low)
    d_up = (d_act * silu_gate).astype(low)
    mlp_part = mat_dot(act_low, w_down).reshape(shard_count, tok_rows, model_width)
    mlp_out = scatter_relative([mlp_part[d] for d in range(shard_count)], "fsdp")
    norm_part = (dot_right_t(d_gate, gate_part) + dot_right_t(d_up, up_part)).reshape(
        shard_count, tok_rows, model_width
    )
    partial_value = scatter_relative([norm_part[d] for d in range(shard_count)], "fsdp")

    def keep_half(grad):
        mine = lax.dynamic_index_in_dim(grad, core, 1, keepdims=False)
        other = lax.dynamic_index_in_dim(grad, 1 - core, 1, keepdims=False)
        return (mine.astype(jnp.float32) + core_swap(other).astype(jnp.float32)).astype(low)

    def both_cores(half):
        return core_halves(half, core_swap(half), core)

    down_grad = dot_left_t(act_low, cot_all).astype(low)
    half = part // 2
    down_half = keep_half(down_grad.reshape(1, 2, half, model_width))[0]
    wide = model_width // line
    down_parts = jnp.stack([down_half[:, q * wide : (q + 1) * wide] for q in range(line)])
    down_own = line_scatter(down_parts).astype(low)
    down_rows = line_gather(down_own)
    down_rows = jnp.concatenate([down_rows[q] for q in range(line)], axis=1)
    down_sums = both_cores(down_rows).reshape(part, model_width).astype(jnp.float32)

    rows = model_width // shard_count
    thin = rows // 2 // line

    def column_grad(d_value):
        grad = dot_left_t(normed_all, d_value).astype(low)
        kept = keep_half(grad.reshape(shard_count, 2, rows // 2, part))
        kept = kept.reshape(shard_count, line, thin, part).transpose(1, 0, 2, 3)
        own = line_scatter(kept).astype(low)
        got = []
        for d in range(shard_count):
            piece = pick(own, here ^ d)
            got.append(piece if d == 0 else lax.ppermute(piece, "fsdp", xor_pairs(shard_count, d)))
        got = place(got, here).transpose(1, 0, 2).reshape(thin, ff_width)
        full = line_gather(got).reshape(rows // 2, ff_width)
        return both_cores(full).reshape(rows, ff_width).astype(jnp.float32)

    grad_gate = column_grad(d_gate)
    grad_up = column_grad(d_up)
    output = mid_state + mlp_out
    d_gain_second = jnp.sum(partial_value * unit_second, axis=0)
    scaled_second = partial_value * gain_second
    d_mid = cot_float + inv_second * (
        scaled_second - unit_second * jnp.mean(scaled_second * unit_second, axis=1, keepdims=True)
    )
    d_branch_low = d_mid.astype(jnp.bfloat16)
    d_attn_low = dot_right_t(d_branch_low, output_full).astype(jnp.bfloat16)
    d_attn_grouped = d_attn_low.reshape(tok_rows, KVH, group_size, HDIM)
    scores = masked_scores()
    soft_back = jnp.exp(scores - log_total)
    probs_low = soft_back.astype(jnp.bfloat16)
    prob_grad = jnp.einsum(
        "tgjd,rgd->gjtr", d_attn_grouped, values_grouped, preferred_element_type=jnp.float32
    )
    row_delta = jnp.sum(soft_back * prob_grad, axis=3, keepdims=True)
    score_grad = (soft_back * (prob_grad - row_delta)).astype(jnp.bfloat16)
    dquery_rot = (
        jnp.einsum("gjtr,rgd->tgjd", score_grad, keys_grouped, preferred_element_type=jnp.float32)
        * score_scale
    )
    dquery_low = (
        unrotate(dquery_rot.reshape(tok_rows, HEADS, HDIM), cosine, sine)
        .reshape(tok_rows, model_width)
        .astype(jnp.bfloat16)
    )
    key_grad = (
        jnp.einsum("gjtr,tgjd->rgd", score_grad, query_grouped, preferred_element_type=jnp.float32)
        * score_scale
    )
    value_grad = jnp.einsum(
        "gjtr,tgjd->rgd", probs_low, d_attn_grouped, preferred_element_type=jnp.float32
    )
    kv_sums = lax.psum_scatter(
        jnp.concatenate(
            [
                key_grad.reshape(lax.axis_size("fsdp") * tok_rows, kv_width),
                value_grad.reshape(lax.axis_size("fsdp") * tok_rows, kv_width),
            ],
            axis=1,
        ).astype(jnp.bfloat16),
        "fsdp",
        scatter_dimension=0,
        tiled=True,
    ).astype(jnp.float32)
    dkey_low = (
        unrotate(kv_sums[:, :kv_width].reshape(tok_rows, KVH, HDIM), cosine, sine)
        .reshape(tok_rows, kv_width)
        .astype(jnp.bfloat16)
    )
    dvalue_low = kv_sums[:, kv_width:].astype(jnp.bfloat16)
    d_norm_first = (
        dot_right_t(dquery_low, query_full)
        + dot_right_t(dkey_low, key_full)
        + dot_right_t(dvalue_low, value_full)
    )
    attn_grads = jnp.concatenate(
        [
            dot_left_t(normed_first, dquery_low).astype(low),
            dot_left_t(normed_first, dkey_low).astype(low),
            dot_left_t(normed_first, dvalue_low).astype(low),
            dot_left_t(attn_low, d_branch_low).astype(low),
        ],
        axis=1,
    )
    attn_wide = attn_grads.shape[1]
    attn_kept = keep_half(attn_grads.reshape(shard_count, 2, rows // 2, attn_wide))
    attn_own = scatter_relative([pick(attn_kept, here ^ d) for d in range(shard_count)], "fsdp").astype(low)
    attn_own = line_scatter(attn_own.reshape(line, thin, attn_wide)).astype(low)
    attn_rows = line_gather(attn_own).reshape(rows // 2, attn_wide)
    attn_sums = both_cores(attn_rows).reshape(rows, attn_wide).astype(jnp.float32)
    d_gain_first = jnp.sum(d_norm_first * unit_first, axis=0)
    scaled_first = d_norm_first * gain_first
    grad_input = d_mid + inv_first * (
        scaled_first - unit_first * jnp.mean(scaled_first * unit_first, axis=1, keepdims=True)
    )
    bias_query = jnp.sum(dquery_low.astype(jnp.float32), axis=0)
    bias_key = jnp.sum(dkey_low.astype(jnp.float32), axis=0)
    bias_value = jnp.sum(dvalue_low.astype(jnp.float32), axis=0)
    small = (bias_query, bias_key, bias_value, d_gain_first, d_gain_second)
    summed = lax.psum(jnp.concatenate(small), ("rep", "fsdp"))
    outs = []
    at = 0
    for vector in small:
        size = vector.shape[0] // shard_count
        outs.append(lax.dynamic_slice_in_dim(summed, at + here * size, size, 0))
        at += vector.shape[0]
    bias_query, bias_key, bias_value, gain_first_sum, gain_second_sum = outs
    grad_query = attn_sums[:, :model_width]
    grad_key = attn_sums[:, model_width : model_width + kv_width]
    grad_value = attn_sums[:, model_width + kv_width : model_width + 2 * kv_width]
    grad_output = attn_sums[:, model_width + 2 * kv_width :]
    return (
        output,
        grad_input,
        grad_query,
        bias_query,
        grad_key,
        bias_key,
        grad_value,
        bias_value,
        grad_output,
        gain_first_sum,
        grad_gate,
        grad_up,
        down_sums,
        gain_second_sum,
    )


def local_fast(
    hidden_in,
    out_grad,
    doc_lengths,
    piece_starts,
    w_query,
    b_query,
    w_key,
    b_key,
    w_value,
    b_value,
    w_output,
    gain_attn,
    w_gate,
    w_up,
    w_down,
    gain_mlp,
):
    tok_rows = hidden_in.shape[0]
    model_width = hidden_in.shape[1]
    shard_count = lax.axis_size("fsdp")
    row_len = tok_rows * shard_count
    group_size = HEADS // KVH
    kv_width = KVH * HDIM
    ff_width = w_gate.shape[1]
    score_scale = 1.0 / HDIM**0.5
    row_pos = jnp.arange(row_len, dtype=jnp.int32)
    lengths = doc_lengths[0]
    starts = piece_starts[0]
    here = lax.axis_index("fsdp")
    core = lax.axis_index("rep") % 2
    line = lax.axis_size("rep") // 2
    line_pos = lax.axis_index("rep") // 2
    low = jnp.bfloat16
    part = ff_width // shard_count
    shard_rows = model_width // shard_count
    thin = shard_rows // 2 // line
    halves = jnp.arange(0, HDIM, 2).astype(jnp.float32) / HDIM
    inverse = rope_base ** (-halves)
    inverse = jnp.broadcast_to(jnp.concatenate([inverse, inverse])[None], (8, HDIM))

    def spread(vector, first, size):
        zeros = jnp.zeros((1, size), jnp.float32)
        return lax.dynamic_update_slice(
            zeros, vector.astype(jnp.float32)[None], (0, first + here * vector.shape[0])
        )

    kv_bias = spread(b_key, 0, model_width) + spread(b_value, kv_width, model_width)
    vec = jnp.concatenate(
        [
            spread(b_query, 0, model_width),
            spread(gain_attn, 0, model_width),
            spread(gain_mlp, 0, model_width),
            kv_bias,
            jnp.zeros((4, model_width), jnp.float32),
        ]
    )
    (
        normed_all,
        cot_all,
        wgu,
        own_gu,
        wqkv_full,
        output_full,
        kv_full,
        mid_state,
        normed_first,
        query_rot,
        attn_low,
        lse,
        trig,
        gains,
    ) = prologue(
        doc_lengths,
        piece_starts,
        hidden_in,
        out_grad,
        vec,
        inverse,
        jnp.concatenate([w_query, w_key, w_value], axis=1),
        w_output,
        w_gate,
        w_up,
    )
    cot_all = cot_all.reshape(row_len, model_width)
    normed_all = normed_all.reshape(row_len, model_width)
    act_low, d_gate, d_up, w_full = feed_forward(normed_all, cot_all, wgu, own_gu, w_down)
    results = epilogue(
        doc_lengths,
        piece_starts,
        query_rot,
        lse,
        trig,
        gains,
        hidden_in,
        out_grad,
        mid_state,
        normed_first,
        attn_low,
        kv_full,
        wqkv_full,
        output_full,
        act_low,
        d_gate,
        d_up,
        normed_all,
        cot_all,
        w_full,
        w_down,
    )
    grad_input, sums, down_final, gate_final, up_final, out_final, qkv_final = results[:7]
    mlp_land = results[14]
    output = mid_state + results[15].astype(jnp.float32)
    for d in range(shard_count - 1):
        output = output + mlp_land[d].astype(jnp.float32)
    down_sums = join(down_final)
    grad_gate, grad_up, grad_output, grad_query, grad_key, grad_value = unfold(
        gate_final, up_final, out_final, qkv_final
    )
    def shard_of(row, first, size):
        return lax.dynamic_slice(sums, (row, first + here * (size // shard_count)), (1, size // shard_count))[0]

    return (
        output,
        grad_input,
        grad_query,
        shard_of(0, 0, model_width),
        grad_key,
        shard_of(3, 0, kv_width),
        grad_value,
        shard_of(3, kv_width, kv_width),
        grad_output,
        shard_of(1, 0, model_width),
        grad_gate,
        grad_up,
        down_sums,
        shard_of(2, 0, model_width),
    )


def solution(mesh):
    body = local_fast if mesh.shape["fsdp"] == 4 and mesh.shape["rep"] == 8 else local
    placed = (
        P(("rep", "fsdp"), None),
        P(("rep", "fsdp"), None),
        P("rep", None),
        P("rep", None),
        P("fsdp", None),
        P("fsdp"),
        P("fsdp", None),
        P("fsdp"),
        P("fsdp", None),
        P("fsdp"),
        P("fsdp", None),
        P("fsdp"),
        P("fsdp", None),
        P("fsdp", None),
        P("fsdp", None),
        P("fsdp"),
    )
    return jax.shard_map(
        body,
        mesh=mesh,
        in_specs=placed,
        out_specs=(
            P(("rep", "fsdp"), None),
            P(("rep", "fsdp"), None),
            P("fsdp", None),
            P("fsdp"),
            P("fsdp", None),
            P("fsdp"),
            P("fsdp", None),
            P("fsdp"),
            P("fsdp", None),
            P("fsdp"),
            P("fsdp", None),
            P("fsdp", None),
            P("fsdp", None),
            P("fsdp"),
        ),
        check_vma=False,
    )
```

```python
import jax
import jax.numpy as jnp
import numpy as np
from jax import lax
from jax.experimental import pallas as pl
from jax.experimental.pallas import tpu as pltpu
from jax.sharding import PartitionSpec as P

HEADS = 12
KVH = 2
HDIM = 128
PIECE = 256


epsilon = 1e-06
rope_base = 1000000.0


def row_layout(positions, lengths, starts, piece_len):
    doc_ends = jnp.cumsum(lengths)
    passed = positions[:, None] >= doc_ends[None, :]
    doc_ids = jnp.sum(passed.astype(jnp.int32), axis=1, dtype=jnp.int32)
    offsets = jnp.sum(jnp.where(passed, lengths[None, :], 0), axis=1, dtype=jnp.int32)
    inside = (positions[:, None] >= starts[None, :]) & (
        positions[:, None] < starts[None, :] + piece_len
    )
    labels = jnp.arange(1, starts.shape[0] + 1, dtype=jnp.int32)
    piece_ids = jnp.sum(jnp.where(inside, labels[None, :], 0), axis=1, dtype=jnp.int32)
    return (doc_ids, positions - offsets, piece_ids)


def visible_pairs(query_doc, query_pos, query_piece, key_doc, key_pos, key_piece):
    same_doc = query_doc[:, None] == key_doc[None, :]
    causal = key_pos[None, :] <= query_pos[:, None]
    same_piece = (query_piece[:, None] == key_piece[None, :]) & (query_piece[:, None] > 0)
    return same_doc & (causal | same_piece)


def rope_tables(relative, head_dim):
    halves = jnp.arange(0, head_dim, 2).astype(jnp.float32) / head_dim
    inverse = rope_base ** (-halves)
    angles = relative.astype(jnp.float32)[:, None] * inverse[None, :]
    angles = jnp.concatenate([angles, angles], axis=1)
    return (jnp.cos(angles), jnp.sin(angles))


def rotate(values, cosine, sine):
    half_dim = values.shape[-1] // 2
    turned = jnp.concatenate([-values[..., half_dim:], values[..., :half_dim]], axis=-1)
    return values * cosine[:, None, :] + turned * sine[:, None, :]


def unrotate(grads, cosine, sine):
    half_dim = grads.shape[-1] // 2
    spun = grads * sine[:, None, :]
    turned_back = jnp.concatenate([spun[..., half_dim:], -spun[..., :half_dim]], axis=-1)
    return grads * cosine[:, None, :] + turned_back


def mat_dot(left, right):
    return jnp.dot(left, right, preferred_element_type=jnp.float32)


def dot_right_t(left, right):
    return lax.dot_general(
        left, right, (((1,), (1,)), ((), ())), preferred_element_type=jnp.float32
    )


def dot_left_t(left, right):
    return lax.dot_general(
        left, right, (((0,), (0,)), ((), ())), preferred_element_type=jnp.float32
    )


def xor_pairs(count, bit):
    return [(i, i ^ bit) for i in range(count)]


def bits_of(count):
    return [1 << k for k in range(count.bit_length() - 1)]


def gather_relative(block, axis):
    count = lax.axis_size(axis)
    bits = bits_of(count)
    half = block.shape[0] // 2
    halves = []
    for part, order in ((block[:half], bits), (block[half:], bits[::-1])):
        have = {0: part}
        for bit in order:
            fresh = {
                d ^ bit: lax.ppermute(piece, axis, xor_pairs(count, bit))
                for d, piece in have.items()
            }
            have.update(fresh)
        halves.append(have)
    return [(halves[0][d], halves[1][d]) for d in range(count)]


def scatter_relative(pieces, axis):
    count = lax.axis_size(axis)
    bits = bits_of(count)
    half = pieces[0].shape[0] // 2
    sums = []
    for lo, hi, order in ((0, half, bits[::-1]), (half, 2 * half, bits)):
        have = {d: pieces[d][lo:hi] for d in range(count)}
        for bit in order:
            come = {
                d ^ bit: lax.ppermute(have[d].astype(jnp.bfloat16), axis, xor_pairs(count, bit))
                for d in have
                if d & bit
            }
            have = {d: have[d].astype(jnp.float32) + come[d].astype(jnp.float32) for d in come}
        sums.append(have[0])
    return jnp.concatenate(sums, axis=0)


def core_swap(block):
    return lax.ppermute(block, "rep", xor_pairs(lax.axis_size("rep"), 1))


def line_pairs(lows, way):
    return [(2 * i + c, 2 * (i + way) + c) for i in lows for c in range(2)]


def pick(array, index):
    return lax.dynamic_index_in_dim(array, index, 0, keepdims=False)


def line_scatter(parts):
    count = lax.axis_size("rep") // 2
    here = lax.axis_index("rep") // 2
    arrived = [None, None]
    for step in range(1, count):
        sends = [
            pick(parts, jnp.clip(count - step + here, 0, count - 1)),
            pick(parts, jnp.clip(here - count + step, 0, count - 1)),
        ]
        for way in range(2):
            if arrived[way] is not None:
                sends[way] = (
                    sends[way].astype(jnp.float32) + arrived[way].astype(jnp.float32)
                ).astype(jnp.bfloat16)
        arrived = [
            lax.ppermute(sends[0], "rep", line_pairs(range(step), 1)),
            lax.ppermute(sends[1], "rep", line_pairs(range(count - step, count), -1)),
        ]
    own = pick(parts, here).astype(jnp.float32)
    return own + arrived[0].astype(jnp.float32) + arrived[1].astype(jnp.float32)


def line_gather(block):
    count = lax.axis_size("rep") // 2
    here = lax.axis_index("rep") // 2
    below, above = [block], [block]
    for step in range(1, count):
        below.append(lax.ppermute(below[-1], "rep", line_pairs(range(step - 1, count - 1), 1)))
        above.append(lax.ppermute(above[-1], "rep", line_pairs(range(1, count - step + 1), -1)))
    stacked = jnp.stack(below[:0:-1] + above)
    return lax.dynamic_slice_in_dim(stacked, count - 1 - here, count, 0)


def core_halves(mine, other, core):
    return jnp.where(core == 0, jnp.stack([mine, other]), jnp.stack([other, mine]))


def place(pieces, here):
    count = len(pieces)
    stacked = jnp.stack(pieces)
    return jnp.stack([pick(stacked, here ^ j) for j in range(count)])


MESH = pl.DeviceIdType.MESH
MASKED = -1e30


def dot_f32(left, right, dims=((1,), (0,))):
    return lax.dot_general(left, right, (dims, ((), ())), preferred_element_type=jnp.float32)


def layout_of(positions, lengths_ref, starts_ref):
    end = jnp.int32(0)
    doc = jnp.zeros_like(positions)
    before = jnp.zeros_like(positions)
    piece = jnp.zeros_like(positions)
    for i in range(lengths_ref.shape[1]):
        end = end + lengths_ref[0, i]
        passed = positions >= end
        doc = doc + jnp.where(passed, 1, 0)
        before = before + jnp.where(passed, lengths_ref[0, i], 0)
    for i in range(starts_ref.shape[1]):
        first = starts_ref[0, i]
        inside = (positions >= first) & (positions < first + PIECE)
        piece = piece + jnp.where(inside, i + 1, 0)
    return doc, positions - before, piece


def mask_bias(here, rows, row_len, lengths_ref, starts_ref):
    query_pos = here * rows + lax.broadcasted_iota(jnp.int32, (rows, 1), 0)
    key_pos = lax.broadcasted_iota(jnp.int32, (1, row_len), 1)
    query_doc, query_rel, query_piece = layout_of(query_pos, lengths_ref, starts_ref)
    key_doc, unused, key_piece = layout_of(key_pos, lengths_ref, starts_ref)
    allowed = (query_doc == key_doc) & (
        (key_pos <= query_pos) | ((query_piece == key_piece) & (query_piece > 0))
    )
    return jnp.where(allowed, 0.0, MASKED), query_rel


class Links:
    def __init__(self):
        self.here = lax.axis_index("fsdp")
        self.rep = lax.axis_index("rep")
        self.core = lax.rem(self.rep, 2)
        self.line = self.rep // 2
        reps = lax.axis_size("rep")
        here = self.here
        self.near = [here, here + 1 - 2 * lax.rem(here, 2), lax.rem(here + 2, 4), 3 - here]
        self.plane = [{"fsdp": index} for index in self.near]
        self.partner = {"rep": self.rep + 1 - 2 * self.core}
        self.up = {"rep": lax.rem(self.rep + 2, reps)}
        self.down = {"rep": lax.rem(self.rep + reps - 2, reps)}

    def greet(self, line=True):
        barrier = pltpu.get_barrier_semaphore()
        others = self.plane[1:] + ([self.partner, self.up, self.down] if line else [])
        for other in others:
            pl.semaphore_signal(barrier, inc=1, device_id=other, device_id_type=MESH)
        pl.semaphore_wait(barrier, len(others))


def remote(src, dst, sems, index, device):
    return pltpu.make_async_remote_copy(
        src_ref=src,
        dst_ref=dst,
        send_sem=sems.at[0, index],
        recv_sem=sems.at[1, index],
        device_id=device,
        device_id_type=MESH,
    )


class PlaneGather:
    def __init__(self, links, own, slot, rows, sems):
        x, y = links.plane[1], links.plane[2]
        here, near_x, near_y, far = links.near
        half = rows // 2

        def part(index, lo):
            return slot(index).at[pl.ds(lo, half)]

        self.first = [
            remote(own, slot(here), sems, 0, x),
            remote(own, slot(here), sems, 1, y),
        ]
        self.second = [
            remote(part(near_x, 0), part(near_x, 0), sems, 2, y),
            remote(part(near_y, half), part(near_y, half), sems, 3, x),
        ]
        self.come = [
            remote(slot(near_x), slot(near_x), sems, 0, x),
            remote(slot(near_y), slot(near_y), sems, 1, y),
            remote(part(far, 0), part(far, 0), sems, 2, y),
            remote(part(far, half), part(far, half), sems, 3, x),
        ]

    def start(self):
        for copy in self.first:
            copy.start()

    def hand_on(self):
        for i in range(2):
            self.come[i].wait_recv()
            self.second[i].start()

    def finish(self):
        for i in (2, 3):
            self.come[i].wait_recv()

    def drain(self):
        for copy in self.first + self.second:
            copy.wait_send()


def prologue_kernel(
    lengths_ref,
    starts_ref,
    x_ref,
    cot_ref,
    vec_ref,
    inverse_ref,
    wqkv_ref,
    wo_ref,
    gate_ref,
    up_ref,
    normed_all,
    cot_all,
    wgu,
    own_gu,
    wqkv_full,
    wo_full,
    kv_full,
    mid_ref,
    normed_first_ref,
    query_ref,
    attn_ref,
    lse_ref,
    trig_ref,
    gains_ref,
    vec_all,
    wqkv_buf,
    wo_buf,
    kv_buf,
    normed_buf,
    bias_ref,
    thin_buf,
    gu_ref,
    wide_buf,
    own_buf,
    cut_sems,
    local_sems,
    vec_sems,
    qkv_sems,
    qkv_core,
    wo_sems,
    wo_core,
    kv_sems,
    cot_sems,
    norm_sems,
    gu_sems,
    up_sems,
    down_sems,
    own_core,
    up_core,
    down_core,
):
    links = Links()
    here, core, line = links.here, links.core, links.line
    count = lax.axis_size("rep") // 2
    rows, width = x_ref.shape
    shard = wqkv_ref.shape[0]
    half = shard // 2
    links.greet()

    def shard_rows(ref, index):
        return ref.at[pl.ds(pl.multiple_of(index * shard, shard), shard)]

    own_copies = [
        pltpu.make_async_copy(wqkv_ref, shard_rows(wqkv_buf, here), local_sems.at[0]),
        pltpu.make_async_copy(wo_ref, shard_rows(wo_buf, here), local_sems.at[1]),
        pltpu.make_async_copy(cot_ref, cot_all.at[here], local_sems.at[2]),
        pltpu.make_async_copy(vec_ref, vec_all.at[here], local_sems.at[3]),
    ]

    vec_sends = [remote(vec_ref, vec_all.at[here], vec_sems, d - 1, links.plane[d]) for d in (1, 2, 3)]
    vec_comes = [
        remote(vec_ref, vec_all.at[links.near[d]], vec_sems, d - 1, links.plane[d]) for d in (1, 2, 3)
    ]

    def half_rows(ref, index, which):
        return ref.at[pl.ds(pl.multiple_of(index * shard + which * half, half), half)]

    def weight_gather(src, buf, sems, core_sems):
        gather = PlaneGather(
            links,
            src.at[pl.ds(pl.multiple_of(core * half, half), half)],
            lambda index: half_rows(buf, index, core),
            half,
            sems,
        )
        swaps = [
            remote(
                half_rows(buf, links.near[d], core),
                half_rows(buf, links.near[d], core),
                core_sems,
                d - 1,
                links.partner,
            )
            for d in (1, 2, 3)
        ]
        comes = [
            remote(
                half_rows(buf, links.near[d], 1 - core),
                half_rows(buf, links.near[d], 1 - core),
                core_sems,
                d - 1,
                links.partner,
            )
            for d in (1, 2, 3)
        ]
        return gather, swaps, comes

    qkv_gather, qkv_swaps, qkv_comes = weight_gather(wqkv_ref, wqkv_buf, qkv_sems, qkv_core)
    wo_gather, wo_swaps, wo_comes = weight_gather(wo_ref, wo_buf, wo_sems, wo_core)
    cot_gather = PlaneGather(links, cot_ref, lambda index: cot_all.at[index], rows, cot_sems)
    norm_gather = PlaneGather(links, normed_buf, lambda index: normed_all.at[index], rows, norm_sems)

    gu_sends = [
        remote(gu_ref.at[links.near[d]], wgu.at[core, line, d - 1], gu_sems, d - 1, links.plane[d])
        for d in (1, 2, 3)
    ]
    own_block = wgu.at[core, line]
    own_swap = remote(own_block, own_block, own_core, 0, links.partner)
    own_come = remote(wgu.at[1 - core, line], wgu.at[1 - core, line], own_core, 0, links.partner)

    class Hop:
        def __init__(self, k, way):
            sems = up_sems if way > 0 else down_sems
            core_sems = up_core if way > 0 else down_core
            device = links.up if way > 0 else links.down
            back = links.down if way > 0 else links.up
            sent = jnp.clip(line - way * (k - 1), 0, count - 1)
            come = jnp.clip(line - way * k, 0, count - 1)
            if way > 0:
                self.sends = (line <= count - 2) & (line >= k - 1)
                self.comes = line >= k
            else:
                self.sends = (line >= 1) & (line + k - 1 <= count - 1)
                self.comes = line + k <= count - 1
            self.send = remote(wgu.at[core, sent], wgu.at[core, sent], sems, k - 1, device)
            self.recv = remote(wgu.at[core, come], wgu.at[core, come], sems, k - 1, back)
            self.swap = remote(wgu.at[core, come], wgu.at[core, come], core_sems, k - 1, links.partner)
            self.swap_come = remote(
                wgu.at[1 - core, come], wgu.at[1 - core, come], core_sems, k - 1, links.partner
            )

    hops = [(Hop(k, 1), Hop(k, -1)) for k in range(1, count)]

    def start_hop(k):
        for hop in hops[k - 1]:
            pl.when(hop.sends)(hop.send.start)

    def take_hop(k):
        for hop in hops[k - 1]:

            @pl.when(hop.comes)
            def _():
                hop.recv.wait_recv()
                hop.swap.start()

    thin, part = gu_ref.shape[2:]
    first_row = pl.multiple_of(core * half + line * thin, thin)
    cuts = [
        pltpu.make_async_copy(ref.at[pl.ds(first_row, thin)], thin_buf.at[i], cut_sems.at[i])
        for i, ref in enumerate((gate_ref, up_ref))
    ] + [
        pltpu.make_async_copy(ref, wide_buf.at[i], cut_sems.at[2 + i])
        for i, ref in enumerate((gate_ref, up_ref))
    ]
    for copy in vec_sends + cuts:
        copy.start()
    qkv_gather.start()
    for copy in cuts[:2]:
        copy.wait()
    for t in range(4):
        gu_ref[t] = thin_buf[:, :, t * part : (t + 1) * part]
    for copy in own_copies:
        copy.start()

    bias, query_rel = mask_bias(here, rows, kv_buf.shape[0] * rows, lengths_ref, starts_ref)
    bias_ref[...] = bias
    angles = query_rel.astype(jnp.float32) * inverse_ref[0:1, :]
    lanes = lax.broadcasted_iota(jnp.int32, (1, HDIM), 1)
    cosine = jnp.cos(angles)
    sine = jnp.sin(angles) * jnp.where(lanes < HDIM // 2, -1.0, 1.0)
    trig_ref[0] = cosine
    trig_ref[1] = sine

    x_float = x_ref[...].astype(jnp.float32)
    unit = x_float * lax.rsqrt(jnp.mean(x_float * x_float, axis=1, keepdims=True) + epsilon)
    own_copies[3].wait()
    for copy in vec_comes:
        copy.wait_recv()
    gains_ref[...] = vec_all[0] + vec_all[1] + vec_all[2] + vec_all[3]
    normed_first_ref[...] = (unit * gains_ref[1:2, :]).astype(jnp.bfloat16)

    qkv_gather.hand_on()
    for swap in qkv_swaps[:2]:
        swap.start()
    for copy in gu_sends:
        copy.start()
    qkv_gather.finish()
    qkv_swaps[2].start()
    own_copies[0].wait()
    for copy in qkv_comes:
        copy.wait_recv()

    full_copy = pltpu.make_async_copy(wqkv_buf, wqkv_full, local_sems.at[4])
    full_copy.start()

    def rope(value):
        return value * trig_ref[0] + pltpu.roll(value, HDIM // 2, 1) * trig_ref[1]

    def project(first, bias_row):
        columns = pl.ds(pl.multiple_of(first, 2 * HDIM), 2 * HDIM)
        return dot_f32(normed_first_ref[...], wqkv_buf[:, columns]) + bias_row

    keys = project(width, gains_ref[3:4, 0 : 2 * HDIM])
    own_kv = kv_buf.at[here]
    for h in range(2):
        kv_buf[here, :, h * HDIM : (h + 1) * HDIM] = rope(keys[:, h * HDIM : (h + 1) * HDIM]).astype(
            jnp.bfloat16
        )
    values = project(width + 2 * HDIM, gains_ref[3:4, 2 * HDIM : 4 * HDIM])
    kv_buf[here, :, 2 * HDIM : 4 * HDIM] = values.astype(jnp.bfloat16)
    kv_sends = [remote(own_kv, own_kv, kv_sems, d - 1, links.plane[d]) for d in (1, 2, 3)]
    kv_comes = [
        remote(kv_buf.at[links.near[d]], kv_buf.at[links.near[d]], kv_sems, d - 1, links.plane[d])
        for d in (1, 2, 3)
    ]
    for copy in kv_sends:
        copy.start()
    wo_gather.start()

    def query_pair(pair, carry):
        columns = pl.ds(pl.multiple_of(pair * 2 * HDIM, 2 * HDIM), 2 * HDIM)
        got = project(pair * 2 * HDIM, gains_ref[0:1, columns])
        for h in range(2):
            where = pl.ds(pl.multiple_of(pair * 2 * HDIM + h * HDIM, HDIM), HDIM)
            query_ref[:, where] = rope(got[:, h * HDIM : (h + 1) * HDIM]).astype(jnp.bfloat16)
        return carry

    lax.fori_loop(0, HEADS // 2, query_pair, 0)
    for copy in cuts[2:]:
        copy.wait()
    for t in range(4):

        @pl.when(here == t)
        def _():
            own_buf[...] = wide_buf[:, :, t * part : (t + 1) * part]

    own_store = pltpu.make_async_copy(own_buf, own_gu, cut_sems.at[0])
    own_store.start()
    for copy in gu_sends:
        copy.wait_recv()
    start_hop(1)
    own_swap.start()
    for copy in kv_comes:
        copy.wait_recv()
    kv_copy = pltpu.make_async_copy(kv_buf, kv_full, local_sems.at[5])
    kv_copy.start()

    group = HEADS // KVH
    row_len = kv_buf.shape[0] * rows
    head_lane = lax.broadcasted_iota(jnp.int32, (1, HDIM), 1)

    def head_step(h, lse):
        columns = pl.ds(pl.multiple_of(h * HDIM, HDIM), HDIM)
        shared = h // group
        key = kv_buf[:, :, pl.ds(pl.multiple_of(shared * HDIM, HDIM), HDIM)].reshape(row_len, HDIM)
        value = kv_buf[:, :, pl.ds(pl.multiple_of((KVH + shared) * HDIM, HDIM), HDIM)].reshape(
            row_len, HDIM
        )
        scores = dot_f32(query_ref[:, columns], key, ((1,), (1,))) * (1.0 / HDIM**0.5) + bias_ref[...]
        peak = jnp.max(scores, axis=1, keepdims=True)
        expo = jnp.exp(scores - peak)
        total = jnp.sum(expo, axis=1, keepdims=True)
        mixed = dot_f32(expo.astype(jnp.bfloat16), value) / total
        attn_ref[:, columns] = mixed.astype(jnp.bfloat16)
        return jnp.where(head_lane == h, peak + jnp.log(total), lse)

    lse = lax.fori_loop(0, 2 * HEADS // 3, head_step, jnp.zeros((rows, HDIM), jnp.float32))
    wo_gather.hand_on()
    for swap in wo_swaps[:2]:
        swap.start()
    cot_gather.start()
    lse_ref[...] = lax.fori_loop(2 * HEADS // 3, HEADS, head_step, lse)
    take_hop(1)
    start_hop(2)
    wo_gather.finish()
    wo_swaps[2].start()
    own_copies[1].wait()
    for copy in wo_comes:
        copy.wait_recv()
    wo_copy = pltpu.make_async_copy(wo_buf, wo_full, local_sems.at[6])
    wo_copy.start()

    def out_columns(i, carry):
        columns = pl.ds(pl.multiple_of(i * 256, 256), 256)
        mid_ref[:, columns] = x_ref[:, columns].astype(jnp.float32) + dot_f32(
            attn_ref[...], wo_buf[:, columns]
        )
        return carry

    lax.fori_loop(0, width // 256, out_columns, 0)
    mid = mid_ref[...]
    unit = mid * lax.rsqrt(jnp.mean(mid * mid, axis=1, keepdims=True) + epsilon)
    normed_buf[...] = (unit * gains_ref[2:3, :]).astype(jnp.bfloat16)
    norm_gather.start()
    norm_copy = pltpu.make_async_copy(normed_buf, normed_all.at[here], local_sems.at[7])
    norm_copy.start()
    cot_gather.hand_on()
    take_hop(2)
    start_hop(3)
    norm_gather.hand_on()
    cot_gather.finish()
    take_hop(3)
    norm_gather.finish()

    own_copies[2].wait()
    own_store.wait()
    full_copy.wait()
    kv_copy.wait()
    wo_copy.wait()
    norm_copy.wait()
    for copy in vec_sends + gu_sends + qkv_swaps + wo_swaps + kv_sends + [own_swap]:
        copy.wait_send()
    own_come.wait_recv()
    for copy in wo_comes[:0]:
        copy.wait_recv()
    for gather in (qkv_gather, wo_gather, cot_gather, norm_gather):
        gather.drain()
    for pair in hops:
        for hop in pair:
            pl.when(hop.sends)(hop.send.wait_send)

            @pl.when(hop.comes)
            def _():
                hop.swap.wait_send()
                hop.swap_come.wait_recv()


def prologue(lengths, starts, x, cot, vec, inverse, wqkv, wo, gate, up):
    rows, width = x.shape
    shards = lax.axis_size("fsdp")
    count = lax.axis_size("rep") // 2
    shard = gate.shape[0]
    thin, part = shard // (2 * count), gate.shape[1] // shards
    bf16, f32 = jnp.bfloat16, jnp.float32
    any_space = pl.BlockSpec(memory_space=pl.ANY)
    vmem = pl.BlockSpec(memory_space=pltpu.VMEM)
    smem = pl.BlockSpec(memory_space=pltpu.SMEM)
    shape = jax.ShapeDtypeStruct

    def sems(n):
        return pltpu.SemaphoreType.DMA((2, n))

    return pl.pallas_call(
        prologue_kernel,
        name="prologue",
        out_shape=(
            shape((shards, rows, width), bf16),
            shape((shards, rows, width), bf16),
            shape((2, count, shards - 1, 2, thin, part), bf16),
            shape((2, shard, part), bf16),
            shape((width, wqkv.shape[1]), bf16),
            shape((width, width), bf16),
            shape((shards, rows, 4 * HDIM), bf16),
            shape((rows, width), f32),
            shape((rows, width), bf16),
            shape((rows, width), bf16),
            shape((rows, width), bf16),
            shape((rows, HDIM), f32),
            shape((2, rows, HDIM), f32),
            shape((8, width), f32),
        ),
        in_specs=[smem, smem, vmem, vmem, vmem, vmem] + [any_space] * 4,
        out_specs=[any_space] * 7 + [vmem] * 7,
        scratch_shapes=[
            pltpu.VMEM((shards, 8, width), f32),
            pltpu.VMEM((width, wqkv.shape[1]), bf16),
            pltpu.VMEM((width, width), bf16),
            pltpu.VMEM((shards, rows, 4 * HDIM), bf16),
            pltpu.VMEM((rows, width), bf16),
            pltpu.VMEM((rows, shards * rows), f32),
            pltpu.VMEM((2, thin, gate.shape[1]), bf16),
            pltpu.VMEM((shards, 2, thin, part), bf16),
            pltpu.VMEM((2, shard, gate.shape[1]), bf16),
            pltpu.VMEM((2, shard, part), bf16),
            pltpu.SemaphoreType.DMA((4,)),
            pltpu.SemaphoreType.DMA((8,)),
            sems(3),
            sems(4),
            sems(3),
            sems(4),
            sems(3),
            sems(3),
            sems(4),
            sems(4),
            sems(3),
            sems(count - 1),
            sems(count - 1),
            sems(1),
            sems(count - 1),
            sems(count - 1),
        ],
        compiler_params=pltpu.CompilerParams(
            collective_id=0, has_side_effects=True, vmem_limit_bytes=60 * 2**20
        ),
    )(lengths, starts, x, cot, vec, inverse, wqkv, wo, gate, up)


class Stream:
    def __init__(self, links, pairs, size, own, land_end, land_mid, final, loads, stage, sems, local_sems, targets):
        self.links, self.pairs, self.size = links, pairs, size
        self.own, self.land_end, self.land_mid, self.final = own, land_end, land_mid, final
        self.loads, self.stage, self.sems, self.local_sems = loads, stage, sems, local_sems
        self.targets = targets
        self.near = links.line // 2
        self.far = 1 - self.near
        self.busy = {}

    def rows(self, kind, p):
        return pl.ds(pl.multiple_of((kind * self.pairs + p) * self.size, self.size), self.size)

    def copy(self, src, dst, p, index, device):
        return pltpu.make_async_remote_copy(
            src_ref=src,
            dst_ref=dst,
            send_sem=self.sems.at[0, p, index],
            recv_sem=self.sems.at[1, p, index],
            device_id=device,
            device_id_type=MESH,
        )

    def load(self, refs, first):
        copies = [
            pltpu.make_async_copy(ref, self.loads.at[first + i], self.local_sems.at[first + i])
            for i, ref in enumerate(refs)
        ]
        for copy in copies:
            copy.start()

        def total():
            for copy in copies:
                copy.wait()
            out = self.loads[first].astype(jnp.float32)
            for i in range(1, len(refs)):
                out = out + self.loads[first + i].astype(jnp.float32)
            return out.astype(jnp.bfloat16)

        return total

    def free(self, role, which, p):
        for copy in self.busy.pop((role, which, p % 2), list)():
            copy.wait_send()

    def hold(self, role, which, p, make):
        copies = make()
        for copy in copies:
            copy.start()
        self.busy[(role, which, p % 2)] = make

    def finals(self, p, which):
        links = self.links
        near, far = self.rows(self.near, p), self.rows(self.far, p)
        ref_near, ref_far = self.final(links.core, near), self.final(links.core, far)
        plans = (
            (ref_near, 3, links.away),
            (ref_near, 4, links.toward),
            (ref_far, 5, links.away),
            (ref_near, 6, links.partner),
            (ref_far, 7, links.partner),
        )
        return [
            self.copy(ref, ref, p, index, device)
            for i, (ref, index, device) in enumerate(plans)
            if i in which
        ]

    def end_send(self, p):
        totals = [
            self.load(self.own(self.rows(kind, p)), first) for first, kind in ((0, self.far), (2, self.near))
        ]
        for which in range(2):
            self.free("end", which, p)
            self.stage[which, p % 2] = totals[which]()
            self.hold(
                "end",
                which,
                p,
                lambda which=which: [
                    self.copy(
                        self.stage.at[which, p % 2], self.land_end.at[p, which], p, which, self.links.toward
                    )
                ],
            )

    def pass_load(self, p):
        self.copy(self.land_end.at[p, 0], self.land_end.at[p, 0], p, 0, self.links.away).wait_recv()
        return self.load(self.own(self.rows(self.far, p)) + [self.land_end.at[p, 0]], 4)

    def mid_pass(self, p, total):
        self.free("mid", 0, p)
        self.stage[0, p % 2] = total()
        self.hold(
            "mid",
            0,
            p,
            lambda: [self.copy(self.stage.at[0, p % 2], self.land_mid.at[p], p, 2, self.links.toward)],
        )

    def sum_load(self, p):
        links = self.links
        self.copy(self.land_end.at[p, 1], self.land_end.at[p, 1], p, 1, links.away).wait_recv()
        self.copy(self.land_mid.at[p], self.land_mid.at[p], p, 2, links.toward).wait_recv()
        near = self.rows(self.near, p)
        return self.load(self.own(near) + [self.land_end.at[p, 1], self.land_mid.at[p]], 0)

    def mid_sum(self, p, total):
        links = self.links
        self.free("mid", 1, p)
        self.stage[1, p % 2] = total()
        self.own_copy(p).start()

        def sends():
            buf = self.stage.at[1, p % 2]
            near = self.rows(self.near, p)
            final = self.final(links.core, near)
            if self.targets:
                ref = self.target(links.core, near, links.here)
                return [
                    self.copy(buf.at[links.near[d]], ref, p, 7 + d, links.plane[d]) for d in (1, 2, 3)
                ]
            return [
                self.copy(buf, final, p, 3, links.away),
                self.copy(buf, final, p, 4, links.toward),
                self.copy(buf, final, p, 6, links.partner),
            ]

        self.hold("mid", 1, p, sends)

    def own_copy(self, p):
        links = self.links
        buf, near = self.stage.at[1, p % 2], self.rows(self.near, p)
        final = self.final(links.core, near)
        if self.targets:
            buf, final = buf.at[links.here], self.target(links.core, near, links.here)
        return pltpu.make_async_copy(buf, final, self.local_sems.at[7 + p % 2])

    def target(self, core, rows, source):
        return self.final(core, rows).at[source]

    def mid_out(self, p):
        links = self.links
        self.own_copy(p).wait()
        if not self.targets:
            return
        near = self.rows(self.near, p)
        for d in (1, 2, 3):
            ref = self.target(links.core, near, links.near[d])
            self.copy(ref, ref, p, 7 + d, links.plane[d]).wait_recv()
        for copy in self.finals(p, (0, 1, 3)):
            copy.start()

    def mid_far(self, p):
        far = self.final(self.links.core, self.rows(self.far, p))
        self.copy(far, far, p, 4, self.links.toward).wait_recv()
        for copy in self.finals(p, (2, 4)):
            copy.start()

    def end_take(self, p):
        for kind, index, out in ((self.near, 3, 3), (self.far, 5, 4)):
            ref = self.final(self.links.core, self.rows(kind, p))
            self.copy(ref, ref, p, index, self.links.toward).wait_recv()
            self.finals(p, (out,))[0].start()

    def close_mid(self):
        for key in [k for k in self.busy if k[0] == "mid"]:
            for copy in self.busy.pop(key)():
                copy.wait_send()
        for p in range(self.pairs):
            for copy in self.finals(p, (0, 1, 2, 3, 4) if self.targets else (2, 4)):
                copy.wait_send()

    def close_end(self):
        for key in [k for k in self.busy if k[0] == "end"]:
            for copy in self.busy.pop(key)():
                copy.wait_send()
        for p in range(self.pairs):
            for copy in self.finals(p, (3, 4)):
                copy.wait_send()

    def close_core(self):
        for p in range(self.pairs):
            for kind, index in ((self.near, 6), (self.far, 7)):
                ref = self.final(1 - self.links.core, self.rows(kind, p))
                self.copy(ref, ref, p, index, self.links.partner).wait_recv()


class WeightSum:
    def __init__(self, links, product, land, own, half_buf, load_buf, first, second, send, half_sems, plane_sems, sem):
        self.links, self.product, self.land, self.own = links, product, land, own
        self.half_buf, self.load_buf, self.first, self.second, self.send = half_buf, load_buf, first, second, send
        self.half_sems, self.sem = half_sems, sem
        self.quarter = half_buf.shape[1] // 2
        near_x, near_y, far = links.near[1:]
        low, high = pl.ds(0, self.quarter), pl.ds(self.quarter, self.quarter)
        self.first_sends = [
            remote(half_buf.at[near_y, low], first.at[0], plane_sems, 0, links.plane[2]),
            remote(half_buf.at[far, low], first.at[1], plane_sems, 1, links.plane[2]),
            remote(half_buf.at[near_x, high], first.at[2], plane_sems, 2, links.plane[1]),
            remote(half_buf.at[far, high], first.at[3], plane_sems, 3, links.plane[1]),
        ]
        self.second_sends = [
            remote(send.at[0], second.at[0], plane_sems, 4, links.plane[1]),
            remote(send.at[1], second.at[1], plane_sems, 5, links.plane[2]),
        ]
        self.half_sends = [
            remote(half_buf.at[t], land.at[t], half_sems, t, links.partner) for t in range(4)
        ]

    def other_half(self):
        def one(t, carry):
            self.half_buf[t] = self.product(t, 1 - self.links.core).astype(jnp.bfloat16)
            return carry

        lax.fori_loop(0, 4, one, 0)
        for copy in self.half_sends:
            copy.start()

    def own_half(self):
        for copy in self.half_sends:
            copy.wait_send()
            copy.wait_recv()

        def one(t, carry):
            load = pltpu.make_async_copy(self.land.at[t], self.load_buf, self.sem)
            load.start()
            got = self.product(t, self.links.core)
            load.wait()
            self.half_buf[t] = (got + self.load_buf[...].astype(jnp.float32)).astype(jnp.bfloat16)
            return carry

        lax.fori_loop(0, 4, one, 0)
        for copy in self.first_sends:
            copy.start()

    def plane_turn(self):
        for copy in self.first_sends:
            copy.wait_recv()
        near_x, near_y, far = self.links.near[1:]
        for i, near in ((0, near_x), (1, near_y)):
            at = slice(i * self.quarter, (i + 1) * self.quarter)
            self.send[i] = (
                self.half_buf[near, at].astype(jnp.float32) + self.first[2 * i + 1].astype(jnp.float32)
            ).astype(jnp.bfloat16)
        for copy in self.second_sends:
            copy.start()

    def plane_end(self):
        for copy in self.second_sends + self.first_sends:
            copy.wait_send()
        for copy in self.second_sends:
            copy.wait_recv()
        for i in range(2):
            at = slice(i * self.quarter, (i + 1) * self.quarter)
            self.load_buf[at, :] = (
                self.half_buf[self.links.here, at].astype(jnp.float32)
                + self.first[2 * i].astype(jnp.float32)
                + self.second[i].astype(jnp.float32)
            ).astype(jnp.bfloat16)
        store = pltpu.make_async_copy(self.load_buf, self.own, self.sem)
        store.start()
        store.wait()


def epilogue_kernel(
    lengths_ref,
    starts_ref,
    query_ref,
    lse_ref,
    trig_ref,
    gains_ref,
    x_hbm,
    cot_hbm,
    mid_hbm,
    normed_hbm,
    attn_hbm,
    kv_hbm,
    wqkv_hbm,
    wo_hbm,
    act_hbm,
    dgate_hbm,
    dup_hbm,
    normed_all,
    cot_all,
    w_hbm,
    down_hbm,
    grad_input_ref,
    sums_ref,
    down_final,
    gate_final,
    up_final,
    out_final,
    qkv_final,
    down_core,
    gate_core,
    up_core,
    out_core,
    qkv_core,
    out_own,
    qkv_own,
    mlp_land,
    mlp_own,
    norm_land,
    norm_parts,
    mlp_parts,
    down_own,
    gate_own,
    up_own,
    down_end,
    down_mid,
    gate_end,
    gate_mid,
    up_end,
    up_mid,
    out_end,
    out_mid,
    qkv_end,
    qkv_mid,
    kv_buf,
    key_turned,
    bias_ref,
    lse_turned,
    dmid_ref,
    branch_ref,
    dattn_ref,
    dqkv_ref,
    dkey_ref,
    dvalue_ref,
    kv_out,
    kv_land,
    normed_turned,
    attn_turned,
    out_half,
    out_load,
    out_first,
    out_second,
    out_send,
    qkv_half,
    qkv_load,
    qkv_first,
    qkv_second,
    qkv_send,
    vec_plane,
    vec_core,
    vec_line,
    vec_send,
    norm_own,
    down_loads,
    down_stage,
    gu_loads,
    gate_stage,
    out_loads,
    out_stage,
    qkv_loads,
    qkv_stage,
    local_sems,
    scope_sems,
    norm_sems,
    mlp_sems,
    load_sems,
    core_sems,
    kv_sems,
    half_sems,
    plane_sems,
    qkv_half_sems,
    qkv_plane_sems,
    vec_sems,
    down_sems,
    gate_sems,
    up_sems,
    out_sems,
    qkv_sems,
):
    links = Links()
    here, core, line = links.here, links.core, links.line
    rows, width = x_hbm.shape
    scale = 1.0 / HDIM**0.5
    group = HEADS // KVH
    bf16, f32 = jnp.bfloat16, jnp.float32
    step = 2 - 4 * (line // 2)
    links.toward = {"rep": links.rep + step}
    links.away = {"rep": links.rep - step}
    is_end = (line == 0) | (line == 3)
    is_mid = (line == 1) | (line == 2)

    barrier = pltpu.get_barrier_semaphore()
    line_others = [{"rep": 2 * lax.rem(line + j, 4) + core} for j in (1, 2, 3)]
    others = links.plane[1:] + [links.partner] + line_others
    for other in others:
        pl.semaphore_signal(barrier, inc=1, device_id=other, device_id_type=MESH)
    pl.semaphore_wait(barrier, len(others))

    fetches = [pltpu.make_async_copy(kv_hbm, kv_buf, local_sems.at[1])]
    fetches[0].start()
    core_comes = [
        remote(ref, ref, core_sems, i, links.partner) for i, ref in enumerate((down_core, gate_core, up_core))
    ]

    def stream(size, total, own, end, mid, final, loads, stage, sems, targets=False):
        return Stream(
            links, total // (2 * size), size, own, end, mid, final, loads, stage, sems, load_sems, targets
        )

    down = stream(
        down_stage.shape[2],
        down_core.shape[0],
        lambda r: [down_own.at[r], down_core.at[r]],
        down_end,
        down_mid,
        lambda c, r: down_final.at[c, r],
        down_loads,
        down_stage,
        down_sems,
    )
    gate = stream(
        gate_stage.shape[3],
        gate_core.shape[1],
        lambda r: [gate_own.at[:, r], gate_core.at[:, r]],
        gate_end,
        gate_mid,
        lambda c, r: gate_final.at[c, :, r],
        gu_loads,
        gate_stage,
        gate_sems,
        True,
    )
    up = stream(
        gate_stage.shape[3],
        up_core.shape[1],
        lambda r: [up_own.at[:, r], up_core.at[:, r]],
        up_end,
        up_mid,
        lambda c, r: up_final.at[c, :, r],
        gu_loads,
        gate_stage,
        up_sems,
        True,
    )
    up.busy = gate.busy
    out = stream(
        out_stage.shape[2],
        out_own.shape[0],
        lambda r: [out_own.at[r]],
        out_end,
        out_mid,
        lambda c, r: out_final.at[c, r],
        out_loads,
        out_stage,
        out_sems,
    )
    qkv = stream(
        qkv_stage.shape[2],
        qkv_own.shape[0],
        lambda r: [qkv_own.at[r]],
        qkv_end,
        qkv_mid,
        lambda c, r: qkv_final.at[c, r],
        qkv_loads,
        qkv_stage,
        qkv_sems,
    )
    streams = (down, gate, up, out, qkv)
    pairs = [(s, p) for s in streams for p in range(s.pairs)]

    def when(i):
        far = i + (4 if pairs[i][0].targets else 3)
        return {
            "end_send": i,
            "mid_pass": i + 1,
            "mid_sum": i + 2,
            "mid_out": i + 3,
            "mid_far": far,
            "end_take": far + 1,
        }

    def service(n):
        def due(action):
            return [pairs[i] for i in range(len(pairs)) if when(i)[action] == n]

        first = {0: down, down.pairs: gate, down.pairs + gate.pairs: up}
        if n in first:
            core_comes[list(first).index(n)].wait_recv()

        @pl.when(is_end)
        def _():
            for s, p in due("end_take"):
                s.end_take(p)
            for s, p in due("end_send"):
                s.end_send(p)

        @pl.when(is_mid)
        def _():
            for s, p in due("mid_far"):
                s.mid_far(p)
            for s, p in due("mid_out"):
                s.mid_out(p)
            sums = [(s, p, s.sum_load(p)) for s, p in due("mid_sum")]
            passes = [(s, p, s.pass_load(p)) for s, p in due("mid_pass")]
            for s, p, total in sums:
                s.mid_sum(p, total)
            for s, p, total in passes:
                s.mid_pass(p, total)

    def scoped(refs, body):
        def inner(*bufs):
            copies = [pltpu.make_async_copy(r, b, scope_sems.at[i]) for i, (r, b) in enumerate(zip(refs, bufs))]
            for copy in copies:
                copy.start()
            for copy in copies:
                copy.wait()
            body(*bufs)

        pl.run_scoped(inner, *[pltpu.VMEM(r.shape, r.dtype) for r in refs])

    def norm_back():
        for d in range(3):
            remote(norm_land.at[d], norm_land.at[d], norm_sems, d, links.plane[d + 1]).wait_recv()
        scoped((mid_hbm, norm_land, cot_hbm), norm_body)

    def norm_body(mid_ref, land_ref, cot_ref):
        mid = mid_ref[...]
        inv = lax.rsqrt(jnp.mean(mid * mid, axis=1, keepdims=True) + epsilon)
        unit = mid * inv
        part = norm_own[...]
        for d in range(3):
            part = part + land_ref[d].astype(f32)
        vec_send[2:3, :] = jnp.sum(part * unit, axis=0, keepdims=True)
        scaled = part * gains_ref[2:3, :]
        d_mid = cot_ref[...].astype(f32) + inv * (
            scaled - unit * jnp.mean(scaled * unit, axis=1, keepdims=True)
        )
        dmid_ref[...] = d_mid
        branch_ref[...] = d_mid.astype(bf16)
        query_pos = here * rows + lax.broadcasted_iota(jnp.int32, (1, rows), 1)
        key_pos = lax.broadcasted_iota(jnp.int32, (4 * rows, 1), 0)
        query_doc, unused, query_piece = layout_of(query_pos, lengths_ref, starts_ref)
        key_doc, unused, key_piece = layout_of(key_pos, lengths_ref, starts_ref)
        allowed = (query_doc == key_doc) & (
            (key_pos <= query_pos) | ((query_piece == key_piece) & (query_piece > 0))
        )
        bias_ref[...] = jnp.where(allowed, 0.0, MASKED)
        lse_turned[...] = lse_ref[...].T

    def attn_back():
        scoped((wo_hbm,), attn_body)

    def attn_body(wo_buf):
        scoped((normed_hbm, attn_hbm), turn_body)

        def tile(i, carry):
            columns = pl.ds(pl.multiple_of(i * 256, 256), 256)
            dattn_ref[:, columns] = dot_f32(branch_ref[...], wo_buf[columns, :], ((1,), (1,))).astype(bf16)
            return carry

        lax.fori_loop(0, width // 256, tile, 0)
        fetches[0].wait()
        for g in range(KVH):
            key_turned[g] = kv_buf[:, :, g * HDIM : (g + 1) * HDIM].reshape(4 * rows, HDIM).T
        dkey_ref[...] = jnp.zeros_like(dkey_ref)
        dvalue_ref[...] = jnp.zeros_like(dvalue_ref)

    def head_back(h, carry):
        columns = pl.ds(pl.multiple_of(h * HDIM, HDIM), HDIM)
        shared = h // group
        key = kv_buf[:, :, pl.ds(pl.multiple_of(shared * HDIM, HDIM), HDIM)].reshape(4 * rows, HDIM)
        value = kv_buf[:, :, pl.ds(pl.multiple_of((KVH + shared) * HDIM, HDIM), HDIM)].reshape(
            4 * rows, HDIM
        )
        query, d_out = query_ref[:, columns], dattn_ref[:, columns]
        scores = dot_f32(key, query, ((1,), (1,))) * scale + bias_ref[...]
        probs = jnp.exp(scores - lse_turned[pl.ds(h, 1), :])
        d_probs = dot_f32(value, d_out, ((1,), (1,)))
        delta = jnp.sum(probs * d_probs, axis=0, keepdims=True)
        d_scores = (probs * (d_probs - delta)).astype(bf16)
        dkey_ref[shared] += dot_f32(d_scores, query)
        dvalue_ref[shared] += dot_f32(probs.astype(bf16), d_out)
        d_query = dot_f32(key_turned[shared], d_scores).T * scale
        d_query = d_query * trig_ref[0] - pltpu.roll(d_query, HDIM // 2, 1) * trig_ref[1]
        dqkv_ref[:, columns] = d_query.astype(bf16)
        return carry

    kv_sends = [
        remote(kv_out.at[links.near[d]], kv_land.at[d - 1], kv_sems, d - 1, links.plane[d]) for d in (1, 2, 3)
    ]

    def kv_send():
        for g in range(KVH):
            kv_out[:, :, g * HDIM : (g + 1) * HDIM] = (
                (dkey_ref[g] * scale).astype(bf16).reshape(4, rows, HDIM)
            )
            kv_out[:, :, (KVH + g) * HDIM : (KVH + g + 1) * HDIM] = (
                dvalue_ref[g].astype(bf16).reshape(4, rows, HDIM)
            )
        for copy in kv_sends:
            copy.start()

    vec_copies = {
        "plane": [remote(vec_send, vec_plane.at[here], vec_sems, d - 1, links.plane[d]) for d in (1, 2, 3)],
        "core": [remote(vec_core.at[core], vec_core.at[core], vec_sems, 3, links.partner)],
        "line": [
            remote(vec_line.at[line], vec_line.at[line], vec_sems, 4 + j, line_others[j]) for j in range(3)
        ],
    }
    vec_comes = {
        "plane": [
            remote(vec_send, vec_plane.at[links.near[d]], vec_sems, d - 1, links.plane[d]) for d in (1, 2, 3)
        ],
        "core": [remote(vec_core.at[core], vec_core.at[1 - core], vec_sems, 3, links.partner)],
        "line": [
            remote(
                vec_line.at[line],
                vec_line.at[lax.rem(line + 3 - j, 4)],
                vec_sems,
                4 + j,
                line_others[2 - j],
            )
            for j in range(3)
        ],
    }

    def input_back():
        for d in (1, 2, 3):
            remote(kv_land.at[d - 1], kv_land.at[d - 1], kv_sems, d - 1, links.plane[d]).wait_recv()
        kv = kv_out[here].astype(f32)
        for d in range(3):
            kv = kv + kv_land[d].astype(f32)
        for g in range(KVH):
            d_key = kv[:, g * HDIM : (g + 1) * HDIM]
            d_key = d_key * trig_ref[0] - pltpu.roll(d_key, HDIM // 2, 1) * trig_ref[1]
            dqkv_ref[:, width + g * HDIM : width + (g + 1) * HDIM] = d_key.astype(bf16)
        dqkv_ref[:, width + KVH * HDIM :] = kv[:, KVH * HDIM :].astype(bf16)
        scoped((wqkv_hbm, x_hbm), input_body)

    def turn_body(normed_ref, attn_ref):
        normed_turned[...] = normed_ref[...].T
        attn_turned[...] = attn_ref[...].T

    def input_body(wqkv_buf, x_ref):
        def tile(i, carry):
            columns = pl.ds(pl.multiple_of(i * 256, 256), 256)
            grad_input_ref[:, columns] = dot_f32(dqkv_ref[...], wqkv_buf[columns, :], ((1,), (1,)))
            return carry

        lax.fori_loop(0, width // 256, tile, 0)
        x = x_ref[...].astype(f32)
        inv = lax.rsqrt(jnp.mean(x * x, axis=1, keepdims=True) + epsilon)
        unit = x * inv
        part = grad_input_ref[...]
        vec_send[1:2, :] = jnp.sum(part * unit, axis=0, keepdims=True)
        scaled = part * gains_ref[1:2, :]
        grad_input_ref[...] = dmid_ref[...] + inv * (
            scaled - unit * jnp.mean(scaled * unit, axis=1, keepdims=True)
        )
        sums = jnp.sum(dqkv_ref[...].astype(f32), axis=0, keepdims=True)
        vec_send[0:1, :] = sums[:, :width]
        vec_send[3:4, 0 : 2 * KVH * HDIM] = sums[:, width:]
        vec_send[3:4, 2 * KVH * HDIM :] = jnp.zeros((1, width - 2 * KVH * HDIM), f32)
        vec_send[4:8, :] = jnp.zeros((4, width), f32)
        vec_plane[here] = vec_send[...]
        for copy in vec_copies["plane"]:
            copy.start()

    shard = width // 4
    half = shard // 2

    def row_block(t, which):
        return pl.ds(pl.multiple_of(t * shard + which * half, half), half)

    out_sum = WeightSum(
        links,
        lambda t, which: dot_f32(attn_turned[row_block(t, which), :], branch_ref[...]),
        out_core,
        out_own,
        out_half,
        out_load,
        out_first,
        out_second,
        out_send,
        half_sems,
        plane_sems,
        local_sems.at[3],
    )
    qkv_sum = WeightSum(
        links,
        lambda t, which: dot_f32(normed_turned[row_block(t, which), :], dqkv_ref[...]),
        qkv_core,
        qkv_own,
        qkv_half,
        qkv_load,
        qkv_first,
        qkv_second,
        qkv_send,
        qkv_half_sems,
        qkv_plane_sems,
        local_sems.at[3],
    )

    def vec_core_step():
        for copy in vec_comes["plane"]:
            copy.wait_recv()
        vec_core[core] = vec_plane[0] + vec_plane[1] + vec_plane[2] + vec_plane[3]
        vec_copies["core"][0].start()

    def vec_line_step():
        vec_comes["core"][0].wait_recv()
        vec_line[line] = vec_core[0] + vec_core[1]
        for copy in vec_copies["line"]:
            copy.start()

    def vec_end():
        for copy in vec_comes["line"]:
            copy.wait_recv()
        sums_ref[...] = vec_line[0] + vec_line[1] + vec_line[2] + vec_line[3]

    done = [0]

    def tick():
        service(done[0])
        done[0] += 1

    def fetch(src, dst, i):
        return pltpu.make_async_copy(src, dst, scope_sems.at[i])

    def down_grads(act_buf, cot_buf, send_buf, keep_buf):
        loads = [fetch(act_hbm, act_buf, 0), fetch(cot_all, cot_buf, 1)]
        for load in loads:
            load.start()
        for load in loads:
            load.wait()
        units, cols = keep_buf.shape

        def product(which, out):
            at = pl.ds(pl.multiple_of(which * cols, cols), cols)
            for lo in range(0, units, 768):
                part = slice(lo, min(lo + 768, units))
                out[part, :] = dot_f32(act_buf[:, part], cot_buf[:, at], ((0,), (0,))).astype(bf16)

        product(1 - core, send_buf)
        send = remote(send_buf, down_core, core_sems, 0, links.partner)
        send.start()
        product(core, keep_buf)
        keep = fetch(keep_buf, down_own, 0)
        keep.start()
        keep.wait()
        send.wait_send()

    def column_grads(turned, value_buf, send_buf, keep_buf):
        def turn(normed_buf):
            load = fetch(normed_all, normed_buf, 1)
            load.start()
            load.wait()
            turned[...] = normed_buf[...].T.reshape(turned.shape)

        def product(which, out):
            left = turned[:, which].reshape(width // 2, turned.shape[3])
            cols = value_buf.shape[1]
            for lo in range(0, cols, 512):
                at = slice(lo, min(lo + 512, cols))
                out[:, :, at] = dot_f32(left, value_buf[:, at]).astype(bf16).reshape(4, width // 8, -1)

        load = fetch(dgate_hbm, value_buf, 0)
        load.start()
        pl.run_scoped(turn, pltpu.VMEM(normed_all.shape, bf16))
        for i, (land, own) in enumerate(((gate_core, gate_own), (up_core, up_own))):
            load.wait()
            send = remote(send_buf, land, core_sems, 1 + i, links.partner)
            product(1 - core, send_buf)
            send.start()
            tick()
            product(core, keep_buf)
            if i == 0:
                load = fetch(dup_hbm, value_buf, 0)
                load.start()
            keep = fetch(keep_buf, own, 1)
            keep.start()
            tick()
            keep.wait()
            send.wait_send()

    order = (1, 2, 3, 0)

    def token_sends(parts, land, sems):
        return [
            remote(parts.at[i], land.at[order[i] - 1], sems, order[i] - 1, links.plane[order[i]]) for i in range(3)
        ]

    def token_blocks(inputs, weights, product, sems, parts, land, keep, store, ticks):
        depth = 3 - len(inputs)

        def body(weight_buf, block_buf, send_buf):
            def block_loads(i):
                return [
                    fetch(ref.at[links.near[order[i]]], block_buf.at[i % depth, j], 2 * (i % depth) + j)
                    for j, ref in enumerate(inputs)
                ]

            load = pltpu.make_async_copy(weights, weight_buf, local_sems.at[2])
            load.start()
            for copy in block_loads(0):
                copy.start()
            load.wait()
            sends = token_sends(parts, land, sems)
            for i, d in enumerate(order):
                if i < 3 and depth > 1:
                    for copy in block_loads(i + 1):
                        copy.start()
                for copy in block_loads(i):
                    copy.wait()
                for lo in range(0, width, 512):
                    at = slice(lo, lo + 512)
                    got = product(block_buf.at[i % depth], weight_buf, at)
                    if d == 0 and store is None:
                        keep[:, at] = got
                    else:
                        send_buf[i % 2, :, at] = got.astype(bf16)
                if d or store is not None:
                    copy = fetch(send_buf.at[i % 2], parts.at[i] if d else store, 3)
                    copy.start()
                    copy.wait()
                if d:
                    sends[i].start()
                if i < 3 and depth == 1:
                    for copy in block_loads(i + 1):
                        copy.start()
                if i in ticks:
                    tick()

        pl.run_scoped(
            body,
            pltpu.VMEM(weights.shape, bf16),
            pltpu.VMEM((depth, len(inputs)) + inputs[0].shape[1:], bf16),
            pltpu.VMEM((2, rows, width), bf16),
        )

    def norm_product(block, weight, at):
        return dot_f32(block[0], weight[0, at, :], ((1,), (1,))) + dot_f32(
            block[1], weight[1, at, :], ((1,), (1,))
        )

    def mlp_product(block, weight, at):
        return dot_f32(block[0], weight[:, at])

    units = act_hbm.shape[1]

    def by_block(ref):
        return ref.reshape(4, rows, units)

    pl.run_scoped(
        down_grads,
        pltpu.VMEM(act_hbm.shape, bf16),
        pltpu.VMEM(cot_all.shape, bf16),
        pltpu.VMEM(down_own.shape, bf16),
        pltpu.VMEM(down_own.shape, bf16),
    )
    tick()
    token_blocks(
        (by_block(dgate_hbm), by_block(dup_hbm)), w_hbm, norm_product, norm_sems, norm_parts, norm_land, norm_own, None, (0, 1, 2, 3)
    )
    pl.run_scoped(
        column_grads,
        pltpu.VMEM((4, 2, width // 8, normed_all.shape[0]), bf16),
        pltpu.VMEM(dgate_hbm.shape, bf16),
        pltpu.VMEM(gate_own.shape, bf16),
        pltpu.VMEM(gate_own.shape, bf16),
    )
    norm_back()
    tick()
    attn_back()
    tick()
    out_sum.other_half()
    lax.fori_loop(0, 2, head_back, 0)
    tick()
    out_sum.own_half()
    lax.fori_loop(2, 4, head_back, 0)
    tick()
    lax.fori_loop(4, 7, head_back, 0)
    tick()
    out_sum.plane_turn()
    lax.fori_loop(7, 10, head_back, 0)
    tick()
    lax.fori_loop(10, 12, head_back, 0)
    kv_send()
    tick()
    out_sum.plane_end()
    tick()
    input_back()
    tick()
    qkv_sum.other_half()
    vec_core_step()
    tick()
    qkv_sum.own_half()
    vec_line_step()
    tick()
    qkv_sum.plane_turn()
    vec_end()
    tick()
    qkv_sum.plane_end()
    assert down.pairs + gate.pairs + up.pairs + out.pairs >= done[0]
    tick()
    token_blocks((by_block(act_hbm),), down_hbm, mlp_product, mlp_sems, mlp_parts, mlp_land, None, mlp_own, (0, 1, 2, 3))
    while done[0] <= len(pairs) + 3:
        tick()

    for copy in kv_sends + token_sends(norm_parts, norm_land, norm_sems) + token_sends(mlp_parts, mlp_land, mlp_sems):
        copy.wait_send()
    for d in range(3):
        remote(mlp_land.at[d], mlp_land.at[d], mlp_sems, d, links.plane[d + 1]).wait_recv()
    for name in vec_copies:
        for copy in vec_copies[name]:
            copy.wait_send()

    @pl.when(is_end)
    def _():
        for s in streams:
            s.close_end()

    @pl.when(is_mid)
    def _():
        for s in streams:
            s.close_mid()

    for s in streams:
        s.close_core()


def epilogue(lengths, starts, query, lse, trig, gains, *others):
    x, wqkv, act, normed_all, w_full = others[0], others[6], others[8], others[11], others[13]
    rows, width = x.shape
    bf16, f32 = jnp.bfloat16, jnp.float32
    any_space = pl.BlockSpec(memory_space=pl.ANY)
    vmem = pl.BlockSpec(memory_space=pltpu.VMEM)
    smem = pl.BlockSpec(memory_space=pltpu.SMEM)
    shape = jax.ShapeDtypeStruct
    half = width // 8
    cols = act.shape[1]
    down_size, gu_size, attn_size = 160, 16, 32
    down_pairs = cols // (2 * down_size)
    gu_pairs = half // (2 * gu_size)
    attn_pairs = half // (2 * attn_size)
    down_chunk = (down_size, width // 2)
    gu_chunk = (4, gu_size, cols)
    out_chunk, qkv_chunk = (attn_size, width), (attn_size, wqkv.shape[1])

    def line_buffers(pairs, chunk):
        return [shape((pairs, 2) + chunk, bf16), shape((pairs,) + chunk, bf16)]

    def sems(*n):
        return pltpu.SemaphoreType.DMA((2,) + n)

    def weight_buffers(cols):
        return [
            pltpu.VMEM((4, half, cols), bf16),
            pltpu.VMEM((half, cols), bf16),
            pltpu.VMEM((4, half // 2, cols), bf16),
            pltpu.VMEM((2, half // 2, cols), bf16),
            pltpu.VMEM((2, half // 2, cols), bf16),
        ]

    outs = [
        shape((rows, width), f32),
        shape((8, width), f32),
        shape((2, cols, width // 2), bf16),
        shape((2, 4, half, cols), bf16),
        shape((2, 4, half, cols), bf16),
        shape((2, half, width), bf16),
        shape((2, half, wqkv.shape[1]), bf16),
        shape((cols, width // 2), bf16),
        shape((4, half, cols), bf16),
        shape((4, half, cols), bf16),
        shape((4, half, width), bf16),
        shape((4, half, wqkv.shape[1]), bf16),
        shape((half, width), bf16),
        shape((half, wqkv.shape[1]), bf16),
        shape((3, rows, width), bf16),
        shape((rows, width), bf16),
        shape((3, rows, width), bf16),
        shape((3, rows, width), bf16),
        shape((3, rows, width), bf16),
        shape((cols, width // 2), bf16),
        shape((4, half, cols), bf16),
        shape((4, half, cols), bf16),
    ]
    outs += line_buffers(down_pairs, down_chunk)
    outs += line_buffers(gu_pairs, gu_chunk) + line_buffers(gu_pairs, gu_chunk)
    outs += line_buffers(attn_pairs, out_chunk) + line_buffers(attn_pairs, qkv_chunk)
    return pl.pallas_call(
        epilogue_kernel,
        name="epilogue",
        out_shape=tuple(outs),
        in_specs=[smem] * 2 + [vmem] * 4 + [any_space] * len(others),
        out_specs=[vmem] * 2 + [any_space] * (len(outs) - 2),
        scratch_shapes=[
            pltpu.VMEM((4, rows, 4 * HDIM), bf16),
            pltpu.VMEM((KVH, HDIM, 4 * rows), bf16),
            pltpu.VMEM((4 * rows, rows), f32),
            pltpu.VMEM((HDIM, rows), f32),
            pltpu.VMEM((rows, width), f32),
            pltpu.VMEM((rows, width), bf16),
            pltpu.VMEM((rows, width), bf16),
            pltpu.VMEM((rows, wqkv.shape[1]), bf16),
            pltpu.VMEM((KVH, 4 * rows, HDIM), f32),
            pltpu.VMEM((KVH, 4 * rows, HDIM), f32),
            pltpu.VMEM((4, rows, 4 * HDIM), bf16),
            pltpu.VMEM((3, rows, 4 * HDIM), bf16),
            pltpu.VMEM((width, rows), bf16),
            pltpu.VMEM((width, rows), bf16),
            *weight_buffers(width),
            *weight_buffers(wqkv.shape[1]),
            pltpu.VMEM((4, 8, width), f32),
            pltpu.VMEM((2, 8, width), f32),
            pltpu.VMEM((4, 8, width), f32),
            pltpu.VMEM((8, width), f32),
            pltpu.VMEM((rows, width), f32),
            pltpu.VMEM((7,) + down_chunk, bf16),
            pltpu.VMEM((2, 2) + down_chunk, bf16),
            pltpu.VMEM((7,) + gu_chunk, bf16),
            pltpu.VMEM((2, 2) + gu_chunk, bf16),
            pltpu.VMEM((7,) + out_chunk, bf16),
            pltpu.VMEM((2, 2) + out_chunk, bf16),
            pltpu.VMEM((7,) + qkv_chunk, bf16),
            pltpu.VMEM((2, 2) + qkv_chunk, bf16),
            pltpu.SemaphoreType.DMA((4,)),
            pltpu.SemaphoreType.DMA((4,)),
            sems(3),
            sems(3),
            pltpu.SemaphoreType.DMA((9,)),
            sems(3),
            sems(3),
            sems(4),
            sems(6),
            sems(4),
            sems(6),
            sems(7),
            sems(down_pairs, 11),
            sems(gu_pairs, 11),
            sems(gu_pairs, 11),
            sems(attn_pairs, 11),
            sems(attn_pairs, 11),
        ],
        compiler_params=pltpu.CompilerParams(
            collective_id=1, has_side_effects=True, vmem_limit_bytes=63 * 2**20
        ),
    )(lengths, starts, query, lse, trig, gains, *others)


class Place:
    def __init__(self):
        here = lax.axis_index("fsdp")
        self.near = [here, here + 1 - 2 * lax.rem(here, 2), lax.rem(here + 2, 4), 3 - here]


def feed_forward_kernel(
    x_ref, cot_ref, wgu, own_gu, down_hbm, act_ref, dgate_ref, dup_ref, w_hbm, w_ref, down_ref, d_act_ref, sems
):
    f32, bf16 = jnp.float32, jnp.bfloat16
    cores, line, others, kinds, thin, part = wgu.shape
    shard = own_gu.shape[1]

    def weight_copies():
        near = Place().near
        copies = []
        for g in range(kinds):
            at = pl.multiple_of(near[0] * shard, shard)
            copies.append(
                pltpu.make_async_copy(own_gu.at[g], w_ref.at[g, pl.ds(at, shard)], sems.at[1 + g])
            )
        n = 1 + kinds
        for d in range(1, 4):
            for c in range(cores):
                for z in range(line):
                    for g in range(kinds):
                        at = pl.multiple_of(near[d] * shard + (c * line + z) * thin, thin)
                        copies.append(
                            pltpu.make_async_copy(
                                wgu.at[c, z, d - 1, g], w_ref.at[g, pl.ds(at, thin)], sems.at[n]
                            )
                        )
                        n += 1
        return copies

    @pl.when(pl.program_id(0) == 0)
    def _():
        down_copy = pltpu.make_async_copy(down_hbm, down_ref, sems.at[0])
        down_copy.start()
        for copy in weight_copies():
            copy.start()
        down_copy.wait()

    x, cot = x_ref[...], cot_ref[...]
    pieces = [slice(lo, min(lo + 512, part)) for lo in range(0, part, 512)]
    for at in pieces:
        d_act_ref[:, at] = dot_f32(cot, down_ref[at, :], ((1,), (1,)))

    @pl.when(pl.program_id(0) == 0)
    def _():
        for copy in weight_copies():
            copy.wait()
        pltpu.make_async_copy(w_ref, w_hbm, sems.at[0]).start()

    for at in pieces:
        gate = dot_f32(x, w_ref[0, :, at])
        up = dot_f32(x, w_ref[1, :, at])
        d_act = d_act_ref[:, at]
        sig = jax.nn.sigmoid(gate)
        silu = gate * sig
        act_ref[:, at] = (silu * up).astype(bf16)
        dgate_ref[:, at] = (d_act * up * sig * (1.0 + gate * (1.0 - sig))).astype(bf16)
        dup_ref[:, at] = (d_act * silu).astype(bf16)

    @pl.when(pl.program_id(0) == pl.num_programs(0) - 1)
    def _():
        pltpu.make_async_copy(w_ref, w_hbm, sems.at[0]).wait()


def feed_forward(x, cot, wgu, own_gu, down):
    rows, width = x.shape
    part = down.shape[0]
    tile = rows // 4
    bf16 = jnp.bfloat16
    any_space = pl.BlockSpec(memory_space=pl.ANY)
    wide = pl.BlockSpec((tile, width), lambda i: (i, 0))
    hidden = pl.BlockSpec((tile, part), lambda i: (i, 0))
    shape = jax.ShapeDtypeStruct
    return pl.pallas_call(
        feed_forward_kernel,
        name="feed_forward",
        grid=(rows // tile,),
        out_shape=[shape((rows, part), bf16)] * 3 + [shape((2, width, part), bf16)],
        in_specs=[wide, wide] + [any_space] * 3,
        out_specs=[hidden] * 3 + [any_space],
        scratch_shapes=[
            pltpu.VMEM((2, width, part), bf16),
            pltpu.VMEM((part, width), bf16),
            pltpu.VMEM((tile, part), jnp.float32),
            pltpu.SemaphoreType.DMA((3 + wgu.shape[0] * wgu.shape[1] * wgu.shape[2] * wgu.shape[3],)),
        ],
        compiler_params=pltpu.CompilerParams(vmem_limit_bytes=62 * 2**20),
        cost_estimate=pl.CostEstimate(
            flops=6 * rows * width * part, bytes_accessed=10 * width * part, transcendentals=rows * part
        ),
    )(x, cot, wgu, own_gu, down)


def unfold_kernel(gate_ref, up_ref, out_ref, qkv_ref, gate_out, up_out, out_out, query_out, key_out, value_out):
    part = gate_ref.shape[3]
    for src, out in ((gate_ref, gate_out), (up_ref, up_out)):
        for t in range(src.shape[1]):
            out[:, t * part : (t + 1) * part] = src[0, t].astype(jnp.float32)
    out_out[...] = out_ref[0].astype(jnp.float32)
    first = 0
    for out in (query_out, key_out, value_out):
        out[...] = qkv_ref[0, :, first : first + out.shape[1]].astype(jnp.float32)
        first += out.shape[1]


def unfold(gate, up, out, qkv):
    cores, shards, half, part = gate.shape
    width = out.shape[2]
    narrow = KVH * HDIM
    tile = 32
    steps = half // tile
    wides = [shards * part] * 2 + [width, width, narrow, narrow]
    block = pl.BlockSpec((1, shards, tile, part), lambda c, i: (c, 0, i, 0))

    def flat(cols):
        return pl.BlockSpec((1, tile, cols), lambda c, i: (c, i, 0))

    return pl.pallas_call(
        unfold_kernel,
        name="unfold",
        grid=(cores, steps),
        out_shape=[jax.ShapeDtypeStruct((cores * half, wide), jnp.float32) for wide in wides],
        in_specs=[block, block, flat(width), flat(qkv.shape[2])],
        out_specs=[pl.BlockSpec((tile, wide), lambda c, i: (c * steps + i, 0)) for wide in wides],
        compiler_params=pltpu.CompilerParams(vmem_limit_bytes=32 * 2**20),
    )(gate, up, out, qkv)


def join_kernel(down_ref, out):
    cols = down_ref.shape[2]
    for c in range(2):
        out[:, c * cols : (c + 1) * cols] = down_ref[c].astype(jnp.float32)


def join(down):
    cores, rows, cols = down.shape
    tile = rows // 7
    return pl.pallas_call(
        join_kernel,
        name="join",
        grid=(rows // tile,),
        out_shape=jax.ShapeDtypeStruct((rows, cores * cols), jnp.float32),
        in_specs=[pl.BlockSpec((cores, tile, cols), lambda i: (0, i, 0))],
        out_specs=pl.BlockSpec((tile, cores * cols), lambda i: (i, 0)),
        compiler_params=pltpu.CompilerParams(vmem_limit_bytes=32 * 2**20),
    )(down)


def local(
    hidden_in,
    out_grad,
    doc_lengths,
    piece_starts,
    w_query,
    b_query,
    w_key,
    b_key,
    w_value,
    b_value,
    w_output,
    gain_attn,
    w_gate,
    w_up,
    w_down,
    gain_mlp,
):
    tok_rows = hidden_in.shape[0]
    model_width = hidden_in.shape[1]
    shard_count = lax.axis_size("fsdp")
    row_len = tok_rows * shard_count
    group_size = HEADS // KVH
    kv_width = KVH * HDIM
    ff_width = w_gate.shape[1]
    score_scale = 1.0 / HDIM**0.5
    local_pos = lax.axis_index("fsdp") * tok_rows + jnp.arange(tok_rows, dtype=jnp.int32)
    row_pos = jnp.arange(row_len, dtype=jnp.int32)
    lengths = doc_lengths[0]
    starts = piece_starts[0]
    query_doc, query_rel, query_piece = row_layout(local_pos, lengths, starts, PIECE)
    key_doc, unused_rel, key_piece = row_layout(row_pos, lengths, starts, PIECE)
    allowed = visible_pairs(query_doc, local_pos, query_piece, key_doc, row_pos, key_piece)
    cosine, sine = rope_tables(query_rel, HDIM)
    here = lax.axis_index("fsdp")
    core = lax.axis_index("rep") % 2
    line = lax.axis_size("rep") // 2
    low = jnp.bfloat16

    def gather_rows(weight):
        half = weight.shape[0] // 2
        mine = lax.dynamic_slice_in_dim(weight, core * half, half, 0)
        mine = jnp.stack([jnp.concatenate(p, axis=0) for p in gather_relative(mine, "fsdp")])
        both = core_halves(mine, core_swap(mine), core)
        rows = place([both[:, d] for d in range(shard_count)], here)
        return rows.reshape(2 * half * shard_count, weight.shape[1])

    qkv_full = gather_rows(jnp.concatenate([w_query, w_key, w_value], axis=1))
    query_full = qkv_full[:, :model_width]
    key_full = qkv_full[:, model_width : model_width + kv_width]
    value_full = qkv_full[:, model_width + kv_width :]
    output_full = gather_rows(w_output)
    vectors = lax.all_gather(
        jnp.concatenate([b_query, b_key, b_value, gain_attn, gain_mlp]), "fsdp", axis=0
    )
    cuts = [0]
    for vector in (b_query, b_key, b_value, gain_attn, gain_mlp):
        cuts.append(cuts[-1] + vector.shape[0])
    query_bias, key_bias, value_bias, attn_gain, mlp_gain = (
        vectors[:, cuts[i] : cuts[i + 1]].reshape(-1) for i in range(5)
    )

    part = ff_width // shard_count

    def exchange_columns(weight):
        half = weight.shape[0] // 2
        mine = lax.dynamic_slice_in_dim(weight, core * half, half, 0)
        got = []
        for d in range(shard_count):
            piece = lax.dynamic_slice_in_dim(mine, (here ^ d) * part, part, 1)
            got.append(piece if d == 0 else lax.ppermute(piece, "fsdp", xor_pairs(shard_count, d)))
        got = jnp.stack(got)
        both = core_halves(got, core_swap(got), core)
        rows = place([both[:, d] for d in range(shard_count)], here)
        return rows.reshape(2 * half * shard_count, part)

    gate_part = exchange_columns(w_gate)
    up_part = exchange_columns(w_up)
    cot_all = jnp.concatenate([h for p in gather_relative(out_grad, "fsdp") for h in p], axis=0)
    x_float = hidden_in.astype(jnp.float32)
    inv_first = lax.rsqrt(jnp.mean(x_float * x_float, axis=1, keepdims=True) + epsilon)
    unit_first = x_float * inv_first
    gain_first = attn_gain.astype(jnp.float32)
    normed_first = (unit_first * gain_first).astype(jnp.bfloat16)
    query_pre = mat_dot(normed_first, query_full) + query_bias.astype(jnp.float32)
    key_pre = mat_dot(normed_first, key_full) + key_bias.astype(jnp.float32)
    value_pre = mat_dot(normed_first, value_full) + value_bias.astype(jnp.float32)
    query_rot = rotate(query_pre.reshape(tok_rows, HEADS, HDIM), cosine, sine).astype(jnp.bfloat16)
    key_rot = (
        rotate(key_pre.reshape(tok_rows, KVH, HDIM), cosine, sine)
        .astype(jnp.bfloat16)
        .reshape(tok_rows, kv_width)
    )
    value_low = value_pre.astype(jnp.bfloat16)
    keys_row, values_row = (
        lax.all_gather(key_rot, "fsdp", axis=0, tiled=True),
        lax.all_gather(value_low, "fsdp", axis=0, tiled=True),
    )
    query_grouped = query_rot.reshape(tok_rows, KVH, group_size, HDIM)
    keys_grouped = keys_row.reshape(row_len, KVH, HDIM)
    values_grouped = values_row.reshape(row_len, KVH, HDIM)

    def masked_scores():
        raw_scores = (
            jnp.einsum(
                "tgjd,rgd->gjtr", query_grouped, keys_grouped, preferred_element_type=jnp.float32
            )
            * score_scale
        )
        return jnp.where(allowed[None, None], raw_scores, -1e30)

    scores = masked_scores()
    row_peak = jnp.max(scores, axis=3, keepdims=True)
    expo_vals = jnp.exp(scores - row_peak)
    row_total = jnp.sum(expo_vals, axis=3, keepdims=True)
    soft_probs = expo_vals / row_total
    log_total = row_peak + jnp.log(row_total)
    attn_heads = jnp.einsum(
        "gjtr,rgd->tgjd",
        soft_probs.astype(jnp.bfloat16),
        values_grouped,
        preferred_element_type=jnp.float32,
    )
    attn_low = attn_heads.reshape(tok_rows, model_width).astype(jnp.bfloat16)
    mid_state = x_float + mat_dot(attn_low, output_full)
    inv_second = lax.rsqrt(jnp.mean(mid_state * mid_state, axis=1, keepdims=True) + epsilon)
    unit_second = mid_state * inv_second
    gain_second = mlp_gain.astype(jnp.float32)
    normed_second = (unit_second * gain_second).astype(jnp.bfloat16)
    cot_float = out_grad.astype(jnp.float32)
    normed_all = jnp.concatenate([h for p in gather_relative(normed_second, "fsdp") for h in p], axis=0)
    gate_val = mat_dot(normed_all, gate_part)
    up_val = mat_dot(normed_all, up_part)
    sig_gate = jax.nn.sigmoid(gate_val)
    silu_gate = gate_val * sig_gate
    act_low = (silu_gate * up_val).astype(low)
    d_act = dot_right_t(cot_all, w_down)
    d_gate = (d_act * up_val * sig_gate * (1.0 + gate_val * (1.0 - sig_gate))).astype(low)
    d_up = (d_act * silu_gate).astype(low)
    mlp_part = mat_dot(act_low, w_down).reshape(shard_count, tok_rows, model_width)
    mlp_out = scatter_relative([mlp_part[d] for d in range(shard_count)], "fsdp")
    norm_part = (dot_right_t(d_gate, gate_part) + dot_right_t(d_up, up_part)).reshape(
        shard_count, tok_rows, model_width
    )
    partial_value = scatter_relative([norm_part[d] for d in range(shard_count)], "fsdp")

    def keep_half(grad):
        mine = lax.dynamic_index_in_dim(grad, core, 1, keepdims=False)
        other = lax.dynamic_index_in_dim(grad, 1 - core, 1, keepdims=False)
        return (mine.astype(jnp.float32) + core_swap(other).astype(jnp.float32)).astype(low)

    def both_cores(half):
        return core_halves(half, core_swap(half), core)

    down_grad = dot_left_t(act_low, cot_all).astype(low)
    half = part // 2
    down_half = keep_half(down_grad.reshape(1, 2, half, model_width))[0]
    wide = model_width // line
    down_parts = jnp.stack([down_half[:, q * wide : (q + 1) * wide] for q in range(line)])
    down_own = line_scatter(down_parts).astype(low)
    down_rows = line_gather(down_own)
    down_rows = jnp.concatenate([down_rows[q] for q in range(line)], axis=1)
    down_sums = both_cores(down_rows).reshape(part, model_width).astype(jnp.float32)

    rows = model_width // shard_count
    thin = rows // 2 // line

    def column_grad(d_value):
        grad = dot_left_t(normed_all, d_value).astype(low)
        kept = keep_half(grad.reshape(shard_count, 2, rows // 2, part))
        kept = kept.reshape(shard_count, line, thin, part).transpose(1, 0, 2, 3)
        own = line_scatter(kept).astype(low)
        got = []
        for d in range(shard_count):
            piece = pick(own, here ^ d)
            got.append(piece if d == 0 else lax.ppermute(piece, "fsdp", xor_pairs(shard_count, d)))
        got = place(got, here).transpose(1, 0, 2).reshape(thin, ff_width)
        full = line_gather(got).reshape(rows // 2, ff_width)
        return both_cores(full).reshape(rows, ff_width).astype(jnp.float32)

    grad_gate = column_grad(d_gate)
    grad_up = column_grad(d_up)
    output = mid_state + mlp_out
    d_gain_second = jnp.sum(partial_value * unit_second, axis=0)
    scaled_second = partial_value * gain_second
    d_mid = cot_float + inv_second * (
        scaled_second - unit_second * jnp.mean(scaled_second * unit_second, axis=1, keepdims=True)
    )
    d_branch_low = d_mid.astype(jnp.bfloat16)
    d_attn_low = dot_right_t(d_branch_low, output_full).astype(jnp.bfloat16)
    d_attn_grouped = d_attn_low.reshape(tok_rows, KVH, group_size, HDIM)
    scores = masked_scores()
    soft_back = jnp.exp(scores - log_total)
    probs_low = soft_back.astype(jnp.bfloat16)
    prob_grad = jnp.einsum(
        "tgjd,rgd->gjtr", d_attn_grouped, values_grouped, preferred_element_type=jnp.float32
    )
    row_delta = jnp.sum(soft_back * prob_grad, axis=3, keepdims=True)
    score_grad = (soft_back * (prob_grad - row_delta)).astype(jnp.bfloat16)
    dquery_rot = (
        jnp.einsum("gjtr,rgd->tgjd", score_grad, keys_grouped, preferred_element_type=jnp.float32)
        * score_scale
    )
    dquery_low = (
        unrotate(dquery_rot.reshape(tok_rows, HEADS, HDIM), cosine, sine)
        .reshape(tok_rows, model_width)
        .astype(jnp.bfloat16)
    )
    key_grad = (
        jnp.einsum("gjtr,tgjd->rgd", score_grad, query_grouped, preferred_element_type=jnp.float32)
        * score_scale
    )
    value_grad = jnp.einsum(
        "gjtr,tgjd->rgd", probs_low, d_attn_grouped, preferred_element_type=jnp.float32
    )
    kv_sums = lax.psum_scatter(
        jnp.concatenate(
            [
                key_grad.reshape(lax.axis_size("fsdp") * tok_rows, kv_width),
                value_grad.reshape(lax.axis_size("fsdp") * tok_rows, kv_width),
            ],
            axis=1,
        ).astype(jnp.bfloat16),
        "fsdp",
        scatter_dimension=0,
        tiled=True,
    ).astype(jnp.float32)
    dkey_low = (
        unrotate(kv_sums[:, :kv_width].reshape(tok_rows, KVH, HDIM), cosine, sine)
        .reshape(tok_rows, kv_width)
        .astype(jnp.bfloat16)
    )
    dvalue_low = kv_sums[:, kv_width:].astype(jnp.bfloat16)
    d_norm_first = (
        dot_right_t(dquery_low, query_full)
        + dot_right_t(dkey_low, key_full)
        + dot_right_t(dvalue_low, value_full)
    )
    attn_grads = jnp.concatenate(
        [
            dot_left_t(normed_first, dquery_low).astype(low),
            dot_left_t(normed_first, dkey_low).astype(low),
            dot_left_t(normed_first, dvalue_low).astype(low),
            dot_left_t(attn_low, d_branch_low).astype(low),
        ],
        axis=1,
    )
    attn_wide = attn_grads.shape[1]
    attn_kept = keep_half(attn_grads.reshape(shard_count, 2, rows // 2, attn_wide))
    attn_own = scatter_relative([pick(attn_kept, here ^ d) for d in range(shard_count)], "fsdp").astype(low)
    attn_own = line_scatter(attn_own.reshape(line, thin, attn_wide)).astype(low)
    attn_rows = line_gather(attn_own).reshape(rows // 2, attn_wide)
    attn_sums = both_cores(attn_rows).reshape(rows, attn_wide).astype(jnp.float32)
    d_gain_first = jnp.sum(d_norm_first * unit_first, axis=0)
    scaled_first = d_norm_first * gain_first
    grad_input = d_mid + inv_first * (
        scaled_first - unit_first * jnp.mean(scaled_first * unit_first, axis=1, keepdims=True)
    )
    bias_query = jnp.sum(dquery_low.astype(jnp.float32), axis=0)
    bias_key = jnp.sum(dkey_low.astype(jnp.float32), axis=0)
    bias_value = jnp.sum(dvalue_low.astype(jnp.float32), axis=0)
    small = (bias_query, bias_key, bias_value, d_gain_first, d_gain_second)
    summed = lax.psum(jnp.concatenate(small), ("rep", "fsdp"))
    outs = []
    at = 0
    for vector in small:
        size = vector.shape[0] // shard_count
        outs.append(lax.dynamic_slice_in_dim(summed, at + here * size, size, 0))
        at += vector.shape[0]
    bias_query, bias_key, bias_value, gain_first_sum, gain_second_sum = outs
    grad_query = attn_sums[:, :model_width]
    grad_key = attn_sums[:, model_width : model_width + kv_width]
    grad_value = attn_sums[:, model_width + kv_width : model_width + 2 * kv_width]
    grad_output = attn_sums[:, model_width + 2 * kv_width :]
    return (
        output,
        grad_input,
        grad_query,
        bias_query,
        grad_key,
        bias_key,
        grad_value,
        bias_value,
        grad_output,
        gain_first_sum,
        grad_gate,
        grad_up,
        down_sums,
        gain_second_sum,
    )


def local_fast(
    hidden_in,
    out_grad,
    doc_lengths,
    piece_starts,
    w_query,
    b_query,
    w_key,
    b_key,
    w_value,
    b_value,
    w_output,
    gain_attn,
    w_gate,
    w_up,
    w_down,
    gain_mlp,
):
    tok_rows = hidden_in.shape[0]
    model_width = hidden_in.shape[1]
    shard_count = lax.axis_size("fsdp")
    row_len = tok_rows * shard_count
    group_size = HEADS // KVH
    kv_width = KVH * HDIM
    ff_width = w_gate.shape[1]
    score_scale = 1.0 / HDIM**0.5
    row_pos = jnp.arange(row_len, dtype=jnp.int32)
    lengths = doc_lengths[0]
    starts = piece_starts[0]
    here = lax.axis_index("fsdp")
    core = lax.axis_index("rep") % 2
    line = lax.axis_size("rep") // 2
    line_pos = lax.axis_index("rep") // 2
    low = jnp.bfloat16
    part = ff_width // shard_count
    shard_rows = model_width // shard_count
    thin = shard_rows // 2 // line
    inverse = rope_base ** (-np.arange(0, HDIM, 2) / HDIM)
    inverse = np.tile(np.concatenate([inverse, inverse]).astype(np.float32)[None], (8, 1))

    def spread(vector, first, size):
        zeros = jnp.zeros((1, size), jnp.float32)
        return lax.dynamic_update_slice(
            zeros, vector.astype(jnp.float32)[None], (0, first + here * vector.shape[0])
        )

    kv_bias = spread(b_key, 0, model_width) + spread(b_value, kv_width, model_width)
    vec = jnp.concatenate(
        [
            spread(b_query, 0, model_width),
            spread(gain_attn, 0, model_width),
            spread(gain_mlp, 0, model_width),
            kv_bias,
            jnp.zeros((4, model_width), jnp.float32),
        ]
    )
    (
        normed_all,
        cot_all,
        wgu,
        own_gu,
        wqkv_full,
        output_full,
        kv_full,
        mid_state,
        normed_first,
        query_rot,
        attn_low,
        lse,
        trig,
        gains,
    ) = prologue(
        doc_lengths,
        piece_starts,
        hidden_in,
        out_grad,
        vec,
        inverse,
        jnp.concatenate([w_query, w_key, w_value], axis=1),
        w_output,
        w_gate,
        w_up,
    )
    cot_all = cot_all.reshape(row_len, model_width)
    normed_all = normed_all.reshape(row_len, model_width)
    act_low, d_gate, d_up, w_full = feed_forward(normed_all, cot_all, wgu, own_gu, w_down)
    results = epilogue(
        doc_lengths,
        piece_starts,
        query_rot,
        lse,
        trig,
        gains,
        hidden_in,
        out_grad,
        mid_state,
        normed_first,
        attn_low,
        kv_full,
        wqkv_full,
        output_full,
        act_low,
        d_gate,
        d_up,
        normed_all,
        cot_all,
        w_full,
        w_down,
    )
    grad_input, sums, down_final, gate_final, up_final, out_final, qkv_final = results[:7]
    mlp_land = results[14]
    output = mid_state + results[15].astype(jnp.float32)
    for d in range(shard_count - 1):
        output = output + mlp_land[d].astype(jnp.float32)
    down_sums = join(down_final)
    grad_gate, grad_up, grad_output, grad_query, grad_key, grad_value = unfold(
        gate_final, up_final, out_final, qkv_final
    )
    def shard_of(row, first, size):
        return lax.dynamic_slice(sums, (row, first + here * (size // shard_count)), (1, size // shard_count))[0]

    return (
        output,
        grad_input,
        grad_query,
        shard_of(0, 0, model_width),
        grad_key,
        shard_of(3, 0, kv_width),
        grad_value,
        shard_of(3, kv_width, kv_width),
        grad_output,
        shard_of(1, 0, model_width),
        grad_gate,
        grad_up,
        down_sums,
        shard_of(2, 0, model_width),
    )


def solution(mesh):
    body = local_fast if mesh.shape["fsdp"] == 4 and mesh.shape["rep"] == 8 else local
    placed = (
        P(("rep", "fsdp"), None),
        P(("rep", "fsdp"), None),
        P("rep", None),
        P("rep", None),
        P("fsdp", None),
        P("fsdp"),
        P("fsdp", None),
        P("fsdp"),
        P("fsdp", None),
        P("fsdp"),
        P("fsdp", None),
        P("fsdp"),
        P("fsdp", None),
        P("fsdp", None),
        P("fsdp", None),
        P("fsdp"),
    )
    return jax.shard_map(
        body,
        mesh=mesh,
        in_specs=placed,
        out_specs=(
            P(("rep", "fsdp"), None),
            P(("rep", "fsdp"), None),
            P("fsdp", None),
            P("fsdp"),
            P("fsdp", None),
            P("fsdp"),
            P("fsdp", None),
            P("fsdp"),
            P("fsdp", None),
            P("fsdp"),
            P("fsdp", None),
            P("fsdp", None),
            P("fsdp", None),
            P("fsdp"),
        ),
        check_vma=False,
    )
```
